32 devices in a mesh: tok: 8 (over z, y), feat: 4 (over x, core).
Axes of the slice: x: 2, y: 2, z: 4, core: 2. Of those that a mesh axis runs over, the one named last changes fastest.
Arguments:
- tokens: bfloat16 [8192, 2048], P('tok', 'feat'), as said below
- gain_attn: float32 [2048], P('feat'), may hold values from 0.5 to 1.5
- w_query: bfloat16 [2048, 2048], P('tok', 'feat'), may hold values from -0.125 to 0.125
- w_key: bfloat16 [2048, 2048], P('tok', 'feat'), may hold values from -0.125 to 0.125
- w_value: bfloat16 [2048, 2048], P('tok', 'feat'), may hold values from -0.125 to 0.125
- w_out: bfloat16 [2048, 2048], P('feat', 'tok'), may hold values from -1.5 to 1.5
- gain_ffn: float32 [2048], P('feat'), may hold values from 0.5 to 1.5
- w_gate: bfloat16 [2048, 8192], P('tok', 'feat'), may hold values from -0.125 to 0.125
- w_up: bfloat16 [2048, 8192], P('tok', 'feat'), may hold values from -0.125 to 0.125
- w_down: bfloat16 [8192, 2048], P('feat', 'tok'), may hold values from -0.125 to 0.125
- cotangent: bfloat16 [8192, 2048], P('tok', 'feat'), as said below
Outputs:
- result: bfloat16 [8192, 2048], P('tok', 'feat')
- input_grad: bfloat16 [8192, 2048], P('tok', 'feat')
- gain_attn_grad: float32 [2048], P('feat')
- gain_ffn_grad: float32 [2048], P('feat')
- query_grad: float32 [2048, 2048], P('tok', 'feat')
- key_grad: float32 [2048, 2048], P('tok', 'feat')
- value_grad: float32 [2048, 2048], P('tok', 'feat')
- out_grad: float32 [2048, 2048], P('feat', 'tok')
- gate_grad: float32 [2048, 8192], P('tok', 'feat')
- up_grad: float32 [2048, 8192], P('tok', 'feat')
- down_grad: float32 [8192, 2048], P('feat', 'tok')
The draws below stay inside these ranges and needn't reach their ends.
Inputs may be any that keep to these rules, and one draw needn't show every extreme that they name: `tokens`: real-valued activations. `cotangent`: real-valued output gradients.
All inputs are finite; a program needn't handle non-finite values.
Results may differ from the reference program's by a relative error of at most 0.019.
Values may be sent and summed in bfloat16 or wider, within the bound.
A program may use at most 256 MiB of HBM per device.

```python
import math
import jax
import jax.numpy as jnp
from jax import lax

D = 2048
H = 32
HD = 64
FF = 8192
LEN = 1024
TOKENS = 8192


def draw_tokens(key, part):
    key_col = jax.random.fold_in(jax.random.fold_in(key, 17), 0)
    key_base = jax.random.fold_in(jax.random.fold_in(key, 17), 2)
    columns = jnp.arange(D, dtype=jnp.float32)
    col_scale = jnp.sqrt(0.5 + 1.5 * columns / D) * jnp.exp(jax.random.uniform(key_col, (D,), jnp.float32, -0.5, 0.5))
    base = jnp.clip(jax.random.normal(key_base, (TOKENS, D), jnp.float32), -4.0, 4.0)
    return (base * col_scale[None, :]).astype(jnp.bfloat16)


def draw_cotangent(key, part):
    key_base = jax.random.fold_in(key, 29)
    places = jnp.arange(TOKENS, dtype=jnp.float32)[:, None] / TOKENS
    ramped = 1.0 + 2.0 * places
    base = jnp.clip(jax.random.normal(key_base, (TOKENS, D), jnp.float32), -4.0, 4.0)
    return (base * ramped).astype(jnp.bfloat16)


def level_of(rng, extent, cuts, least, largest):
    level = 1.0
    for position, blocks in cuts:
        draws = jax.random.uniform(jax.random.fold_in(jax.random.fold_in(rng, 6), position), (blocks,), jnp.float32, least / len(cuts), largest / len(cuts))
        level = level * jnp.repeat(jnp.exp(draws), extent[position] // blocks).reshape((-1,) + (1,) * (len(extent) - 1 - position))
    return level


def centred(own_key, dims, spread, bound, shards=(), held_as=jnp.bfloat16):
    loudness = level_of(own_key, dims, shards, -0.22, 0.18) if shards else 1.0
    entries = jax.random.normal(own_key, dims, jnp.float32) * spread * loudness
    return jnp.minimum(jnp.maximum(entries, -bound), bound).astype(held_as)


def setup_inputs(seed: int = 0) -> dict:
    keys = jax.random.split(jax.random.key(seed), 12)
    tokens = draw_tokens(jax.random.fold_in(keys[11], 71), 0)
    gain_attn = jnp.clip(1.0 + 0.1 * jax.random.normal(keys[1], (D,), jnp.float32), 0.5, 1.5)
    w_query = centred(keys[2], (D, D), D ** -0.5, 0.125, ((0, 8), (1, 4)))
    w_key = centred(keys[3], (D, D), D ** -0.5, 0.125, ((0, 8), (1, 4)))
    w_value = centred(keys[4], (D, D), D ** -0.5, 0.125, ((0, 8), (1, 4)))
    w_out = centred(keys[5], (D, D), (max(D // 128, 4)) ** -0.5, 1.5, ((0, 4), (1, 8)))
    gain_ffn = jnp.clip(1.0 + 0.1 * jax.random.normal(keys[6], (D,), jnp.float32), 0.5, 1.5)
    w_gate = centred(keys[7], (D, FF), D ** -0.5, 0.125, ((0, 8), (1, 4)))
    w_up = centred(keys[8], (D, FF), D ** -0.5, 0.125, ((0, 8), (1, 4)))
    w_down = centred(keys[9], (FF, D), (FF // 4) ** -0.5, 0.125, ((0, 4), (1, 8)))
    cotangent = draw_cotangent(jax.random.fold_in(keys[11], 71), 0)
    return dict(tokens=tokens, gain_attn=gain_attn, w_query=w_query, w_key=w_key, w_value=w_value, w_out=w_out, gain_ffn=gain_ffn, w_gate=w_gate, w_up=w_up, w_down=w_down, cotangent=cotangent)


EPSILON = 1e-05
HIGHEST_PRECISION = lax.Precision.HIGHEST

@jax.custom_vjp
def low(v):
    return lax.optimization_barrier(v.astype(jnp.bfloat16)).astype(jnp.float32)

@jax.custom_vjp
def low_back(v):
    return v

def low_keep(v):
    return (low(v), None)

def low_pass(kept, grad):
    return (grad,)

def back_keep(v):
    return (v, None)

def back_low(kept, grad):
    return (low(grad),)
low.defvjp(low_keep, low_pass)
low_back.defvjp(back_keep, back_low)

def matmul(left, right):
    return jnp.dot(left, right, precision=HIGHEST_PRECISION)

def attend_one(pieces):
    queries, key_rows, value_rows = pieces
    scores = low_back(jnp.einsum('qhd,khd->hqk', queries, key_rows, precision=HIGHEST_PRECISION) * HD ** (-0.5))
    places = jnp.arange(LEN)
    scores = jnp.where(places[:, None] >= places[None, :], scores, -1e+30)
    probs = low(jax.nn.softmax(scores, axis=-1))
    return jnp.einsum('hqk,khd->qhd', probs, value_rows, precision=HIGHEST_PRECISION)

def split_heads(values):
    return values.reshape(values.shape[0] // LEN, LEN, H, HD)

def forward(residual, gain_attn, w_query, w_key, w_value, w_out, gain_ffn, w_gate, w_up, w_down):
    factor_one = lax.rsqrt(lax.optimization_barrier(jnp.mean(residual * residual, axis=1, keepdims=True)) + EPSILON)
    normed = low(residual * factor_one * gain_attn)
    queries = low(low_back(matmul(normed, w_query)))
    key_rows = low(low_back(matmul(normed, w_key)))
    value_rows = low(low_back(matmul(normed, w_value)))
    attended = lax.map(jax.checkpoint(attend_one), (split_heads(queries), split_heads(key_rows), split_heads(value_rows)))
    attended = low(low_back(attended.reshape(residual.shape[0], D)))
    middle = residual + low_back(matmul(attended, w_out))
    factor_two = lax.rsqrt(lax.optimization_barrier(jnp.mean(middle * middle, axis=1, keepdims=True)) + EPSILON)
    normed_two = low(middle * factor_two * gain_ffn)
    gate = low_back(matmul(normed_two, w_gate))
    upward = low_back(matmul(normed_two, w_up))
    hidden = low(gate * jax.nn.sigmoid(gate) * upward)
    return middle + low_back(matmul(hidden, w_down))

def reference(tokens, gain_attn, w_query, w_key, w_value, w_out, gain_ffn, w_gate, w_up, w_down, cotangent):
    weights = tuple((weight.astype(jnp.float32) for weight in (gain_attn, w_query, w_key, w_value, w_out, gain_ffn, w_gate, w_up, w_down)))
    sequences = tokens.shape[0] // LEN
    group_seqs = math.gcd(sequences, max(1, 4096 // LEN))
    group_rows = group_seqs * LEN
    groups = sequences // group_seqs
    inputs = tokens.reshape(groups, group_rows, D)
    grad_inputs = cotangent.reshape(groups, group_rows, D)

    def advance(running, segments):
        segment, grad_segment = segments
        outcome, pullback = jax.vjp(forward, segment.astype(jnp.float32), *weights)
        gradients = pullback(grad_segment.astype(jnp.float32))
        running = tuple((total + part_grad for total, part_grad in zip(running, gradients[1:])))
        return (running, (outcome.astype(jnp.bfloat16), gradients[0].astype(jnp.bfloat16)))
    initial = tuple((jnp.zeros(weight.shape, jnp.float32) for weight in weights))
    totals, (outputs, grad_rows) = lax.scan(advance, initial, (inputs, grad_inputs))
    return (outputs.reshape(-1, D), grad_rows.reshape(-1, D), totals[0], totals[5], totals[1], totals[2], totals[3], totals[4], totals[6], totals[7], totals[8])
```

```python
import jax
import jax.numpy as jnp
from jax import lax
from jax.sharding import PartitionSpec as P

HD = 64
LEN = 1024
EPSILON = 1e-05
BF16 = jnp.bfloat16
F32 = jnp.float32


def left_trans(left, right):
    return lax.dot_general(
        left, right, (((0,), (0,)), ((), ())), preferred_element_type=F32
    )


def right_trans(left, right):
    return lax.dot_general(
        left, right, (((1,), (1,)), ((), ())), preferred_element_type=F32
    )


def product(left, right):
    return jnp.dot(left, right, preferred_element_type=F32)


class Tok:
    def __init__(self, size):
        self.size = size
        self.ring = size // 2

    def coords(self):
        me = lax.axis_index("tok")
        return me // 2, me % 2

    def up(self, value):
        pairs = [(i, (i + 2) % self.size) for i in range(self.size)]
        return lax.ppermute(value, "tok", pairs)

    def down(self, value):
        pairs = [(i, (i - 2) % self.size) for i in range(self.size)]
        return lax.ppermute(value, "tok", pairs)

    def swap(self, value):
        return lax.ppermute(value, "tok", [(i, i ^ 1) for i in range(self.size)])

    def gather(self, shard):
        pieces = []
        for step in range(self.ring):
            pieces += [shard, self.swap(shard)]
            if step < self.ring - 1:
                shard = self.up(shard)
        return pieces

    def scatter(self, piece):
        total = None
        for step in reversed(range(self.ring)):
            arrived = self.swap(piece(2 * step + 1).astype(BF16))
            mine = piece(2 * step) + arrived.astype(F32)
            if total is not None:
                mine = mine + self.down(total.astype(BF16)).astype(F32)
            total = mine
        return total


def x_swap(value):
    return lax.ppermute(value, "feat", [(i, i ^ 2) for i in range(4)])


def core_swap(value):
    return lax.ppermute(value, "feat", [(i, i ^ 1) for i in range(4)])


def feat_gather(shard):
    far = x_swap(shard)
    return [shard, core_swap(shard), far, core_swap(far)]


def feat_scatter(piece):
    third = core_swap(piece(3).astype(BF16)).astype(F32)
    far = (piece(2) + third).astype(BF16)
    far = x_swap(far).astype(F32)
    first = core_swap(piece(1).astype(BF16)).astype(F32)
    return piece(0) + first + far


def split_heads(values):
    return values.reshape(values.shape[0] // LEN, LEN, values.shape[1] // HD, HD)


def causal_scores(query_block, key_block, offset):
    block_rows = query_block.shape[1]
    key_count = key_block.shape[1]
    scores = jnp.einsum(
        "sqhd,skhd->shqk", query_block, key_block, preferred_element_type=F32
    ) * HD ** (-0.5)
    allowed = (offset + jnp.arange(block_rows))[:, None] >= jnp.arange(key_count)[None, :]
    return jnp.where(allowed, scores, -1e30)


def attend(queries, key_rows, value_rows):
    query_heads, key_heads, value_heads = (
        split_heads(queries),
        split_heads(key_rows),
        split_heads(value_rows),
    )
    block_rows = min(512, LEN)
    outputs = []
    log_sums = []
    for offset in range(0, LEN, block_rows):
        block_end = offset + block_rows
        scores = causal_scores(query_heads[:, offset:block_end], key_heads[:, :block_end], offset)
        highest = jnp.max(scores, axis=-1, keepdims=True)
        exponent = jnp.exp(scores - highest)
        denominator = jnp.sum(exponent, axis=-1, keepdims=True)
        probs = (exponent / denominator).astype(BF16)
        outputs.append(
            jnp.einsum(
                "shqk,skhd->sqhd",
                probs,
                value_heads[:, :block_end],
                preferred_element_type=F32,
            )
        )
        log_sums.append((highest + jnp.log(denominator))[..., 0])
    attended = jnp.concatenate(outputs, axis=1).astype(BF16).reshape(queries.shape)
    return (attended, jnp.concatenate(log_sums, axis=2))


def attend_back(queries, key_rows, value_rows, log_sums, grad_attended):
    query_heads, key_heads, value_heads = (
        split_heads(queries),
        split_heads(key_rows),
        split_heads(value_rows),
    )
    grad_heads = split_heads(grad_attended)
    block_rows = min(512, LEN)
    factor = HD ** (-0.5)
    query_parts = []
    grad_keys = jnp.zeros(key_heads.shape, F32)
    grad_values = jnp.zeros(value_heads.shape, F32)
    for offset in range(0, LEN, block_rows):
        block_end = offset + block_rows
        query_block = query_heads[:, offset:block_end]
        grad_block = grad_heads[:, offset:block_end]
        scores = causal_scores(query_block, key_heads[:, :block_end], offset)
        probs = jnp.exp(scores - log_sums[:, :, offset:block_end, None])
        grad_probs = jnp.einsum(
            "sqhd,skhd->shqk",
            grad_block,
            value_heads[:, :block_end],
            preferred_element_type=F32,
        )
        inner = jnp.sum(probs * grad_probs, axis=-1, keepdims=True)
        grad_scores = (probs * (grad_probs - inner)).astype(BF16)
        query_parts.append(
            jnp.einsum(
                "shqk,skhd->sqhd",
                grad_scores,
                key_heads[:, :block_end],
                preferred_element_type=F32,
            )
            * factor
        )
        key_term = (
            jnp.einsum(
                "shqk,sqhd->skhd", grad_scores, query_block, preferred_element_type=F32
            )
            * factor
        )
        grad_keys = grad_keys.at[:, :block_end].add(key_term)
        value_term = jnp.einsum(
            "shqk,sqhd->skhd",
            probs.astype(BF16),
            grad_block,
            preferred_element_type=F32,
        )
        grad_values = grad_values.at[:, :block_end].add(value_term)
    shape = queries.shape
    grad_queries = jnp.concatenate(query_parts, axis=1).astype(BF16).reshape(shape)
    return (
        grad_queries,
        grad_keys.astype(BF16).reshape(shape),
        grad_values.astype(BF16).reshape(shape),
    )


def program(
    tok_size,
    tokens, gain_attn, w_query, w_key, w_value, w_out, gain_ffn, w_gate, w_up, w_down, cotangent
):
    tok = Tok(tok_size)
    ring = tok.ring
    place, member = tok.coords()
    feat = lax.axis_index("feat")
    rows, wide = tokens.shape
    model = 4 * wide
    unit = model // ring
    half = unit // 2
    per = wide // unit
    quarter = rows // 4
    hidden_wide = w_gate.shape[1]

    def swap_halves(block):
        turned = jnp.concatenate([block[..., half:], block[..., :half]], axis=-1)
        return jnp.where(member == 0, block, turned)

    def to_rotated(slots):
        stacked = jnp.stack(slots)
        if per > 1:
            lead = stacked.reshape(4, -1, per, unit)
            stacked = jnp.moveaxis(lead, 2, 1).reshape(4 * per, -1, unit)
        blocks = []
        for step in range(ring):
            source = (place - step) % ring
            index = ((source // per) ^ feat) * per + source % per
            block = lax.dynamic_index_in_dim(stacked, index, 0, keepdims=False)
            blocks.append(swap_halves(block))
        return jnp.concatenate(blocks, axis=-1)

    def slot_of(rotated, r):
        lead = rotated.reshape(-1, ring, unit)
        blocks = []
        for inside in range(per):
            source = (feat ^ r) * per + inside
            step = (place - source) % ring
            block = lax.dynamic_index_in_dim(lead, step, 1, keepdims=False)
            blocks.append(swap_halves(block))
        return jnp.concatenate(blocks, axis=-1)

    def row_block(values, r):
        return lax.dynamic_slice_in_dim(values, (feat ^ r) * quarter, quarter, 0)

    def natural_rows(blocks):
        stacked = jnp.stack(blocks)
        return jnp.concatenate(
            [lax.dynamic_index_in_dim(stacked, feat ^ j, 0, keepdims=False) for j in range(4)]
        )

    qkv = jnp.concatenate(tok.gather(jnp.concatenate([w_query, w_key, w_value], axis=1)), axis=0)
    out_proj = jnp.concatenate(tok.gather(w_out), axis=1)
    gate_up = jnp.concatenate(tok.gather(jnp.concatenate([w_gate, w_up], axis=1)), axis=0)
    down_proj = jnp.concatenate(tok.gather(w_down), axis=1)

    gains = lax.all_gather(jnp.stack([gain_attn, gain_ffn]), "feat")
    gains_slots = [lax.dynamic_index_in_dim(gains, feat ^ r, 0, keepdims=False) for r in range(4)]
    gains_rot = to_rotated(gains_slots)
    gain_one, gain_two = gains_rot[0], gains_rot[1]
    x_all = to_rotated(feat_gather(tokens)).astype(F32)
    cot_slots = feat_gather(cotangent)
    cot_nat = to_rotated(cot_slots)
    cot_rows = jnp.concatenate([row_block(cot_nat, r) for r in range(4)])

    factor_one = lax.rsqrt(jnp.mean(x_all * x_all, axis=1, keepdims=True) + EPSILON)
    normed = (x_all * factor_one * gain_one).astype(BF16)
    projected = product(normed, qkv).astype(BF16)
    queries = projected[:, :wide]
    key_rows = projected[:, wide : 2 * wide]
    value_rows = projected[:, 2 * wide :]
    attended, log_sums = attend(queries, key_rows, value_rows)
    mixed = feat_scatter(lambda r: product(row_block(attended, r), out_proj))
    middle = row_block(x_all, 0) + mixed
    factor_two = lax.rsqrt(jnp.mean(middle * middle, axis=1, keepdims=True) + EPSILON)
    normed_own = (middle * factor_two * gain_two).astype(BF16)
    normed_two = jnp.concatenate(feat_gather(normed_own))

    both = product(normed_two, gate_up)
    gate, upward = both[:, :hidden_wide], both[:, hidden_wide:]
    sigma = jax.nn.sigmoid(gate)
    hidden = (gate * sigma * upward).astype(BF16)
    grad_hidden = right_trans(cot_rows, down_proj)
    grad_gate = (grad_hidden * upward * sigma * (1.0 + gate * (1.0 - sigma))).astype(BF16)
    grad_up = (grad_hidden * gate * sigma).astype(BF16)
    grad_both = jnp.concatenate([grad_gate, grad_up], axis=1)

    def columns(values, i):
        return values[:, i * half : (i + 1) * half]

    down_grad = tok.scatter(lambda i: left_trans(hidden, columns(cot_rows, i)))
    both_grad = tok.scatter(lambda i: left_trans(columns(normed_two, i), grad_both))
    gate_grad, up_grad = both_grad[:, :hidden_wide], both_grad[:, hidden_wide:]

    grad_normed_two = feat_scatter(
        lambda r: right_trans(grad_both[r * quarter : (r + 1) * quarter], gate_up)
    )
    weighted = gain_two * grad_normed_two
    inner = jnp.mean(weighted * middle, axis=1, keepdims=True)
    grad_middle = (
        cot_rows[:quarter].astype(F32)
        + factor_two * weighted
        - middle * (factor_two * factor_two * factor_two * inner)
    )
    gain_ffn_part = jnp.sum(grad_normed_two * middle * factor_two, axis=0)

    out_rows = product(hidden, down_proj)
    out_rows = jnp.concatenate([out_rows[:quarter] + middle, out_rows[quarter:]])
    out_blocks = [out_rows[r * quarter : (r + 1) * quarter] for r in range(4)]
    outcome = feat_scatter(lambda r: natural_rows([slot_of(block, r) for block in out_blocks]))

    grad_mid_rows = natural_rows(feat_gather(grad_middle.astype(BF16)))
    grad_attended = right_trans(grad_mid_rows, out_proj).astype(BF16)
    out_grad = tok.scatter(lambda i: left_trans(attended, columns(grad_mid_rows, i)))
    grad_queries, grad_keys, grad_values = attend_back(
        queries, key_rows, value_rows, log_sums, grad_attended
    )
    grad_proj = jnp.concatenate([grad_queries, grad_keys, grad_values], axis=1)
    qkv_grad = tok.scatter(lambda i: left_trans(columns(normed, i), grad_proj))

    grad_normed = right_trans(grad_proj, qkv)
    inner_part = jnp.sum(grad_normed * gain_one * x_all, axis=1)
    inner_one = lax.psum(inner_part, "feat")
    gain_attn_part = jnp.sum(grad_normed * x_all * factor_one, axis=0)
    carried = grad_normed * gain_one * factor_one
    own_rows = jax.nn.one_hot(feat, 4, dtype=F32)
    spread = jnp.concatenate([own_rows[j] * grad_middle for j in range(4)])
    carried = carried + spread
    gathered_grad = feat_scatter(lambda r: slot_of(carried, r))
    one = factor_one[:, 0]
    input_grad = gathered_grad - tokens.astype(F32) * (one * one * one * inner_one / model)[:, None]

    parts = jnp.stack([gain_attn_part, gain_ffn_part])
    owned = jnp.stack([slot_of(parts, r) for r in range(4)])
    own_all = jnp.concatenate(
        [lax.dynamic_index_in_dim(owned, feat ^ j, 0, keepdims=False) for j in range(4)], axis=-1
    )
    gain_sums = lax.psum(own_all, ("tok", "feat"))
    gain_grads = lax.dynamic_slice_in_dim(gain_sums, feat * wide, wide, 1)
    return (
        outcome.astype(BF16),
        input_grad.astype(BF16),
        gain_grads[0],
        gain_grads[1],
        qkv_grad[:, :wide],
        qkv_grad[:, wide : 2 * wide],
        qkv_grad[:, 2 * wide :],
        out_grad,
        gate_grad,
        up_grad,
        down_grad,
    )


def solution(mesh):
    in_specs = (
        P("tok", "feat"),
        P("feat"),
        P("tok", "feat"),
        P("tok", "feat"),
        P("tok", "feat"),
        P("feat", "tok"),
        P("feat"),
        P("tok", "feat"),
        P("tok", "feat"),
        P("feat", "tok"),
        P("tok", "feat"),
    )
    out_specs = (
        P("tok", "feat"),
        P("tok", "feat"),
        P("feat"),
        P("feat"),
        P("tok", "feat"),
        P("tok", "feat"),
        P("tok", "feat"),
        P("feat", "tok"),
        P("tok", "feat"),
        P("tok", "feat"),
        P("feat", "tok"),
    )

    def on_device(*arrays):
        return program(mesh.shape["tok"], *arrays)

    return jax.shard_map(
        on_device, mesh=mesh, in_specs=in_specs, out_specs=out_specs, check_vma=False
    )
```

```python
import jax
import jax.numpy as jnp
from jax import lax
from jax.experimental import pallas as pl
from jax.experimental.pallas import tpu as pltpu
from jax.sharding import PartitionSpec as P

HD = 64
LEN = 1024
EPSILON = 1e-05
BF16 = jnp.bfloat16
F32 = jnp.float32
MESH = pl.DeviceIdType.MESH
VMEM = 48 << 20
CHUNKS = 2
FORWARD_BLOCK = 512
BACK_BLOCK = 256


def left_trans(left, right):
    return lax.dot_general(
        left, right, (((0,), (0,)), ((), ())), preferred_element_type=F32
    )


def right_trans(left, right):
    return lax.dot_general(
        left, right, (((1,), (1,)), ((), ())), preferred_element_type=F32
    )


def product(left, right):
    return jnp.dot(left, right, preferred_element_type=F32)


def causal_tile(scores):
    size = scores.shape[0]
    key = lax.broadcasted_iota(jnp.int32, scores.shape, 0)
    query = lax.broadcasted_iota(jnp.int32, scores.shape, 1)
    return jnp.where(key <= query, scores, -1e30)


def head_parts(packed_ref, head, width):
    columns = [slice(part * width + head * HD, part * width + (head + 1) * HD) for part in range(3)]
    query, key, value = [packed_ref[:, part] for part in columns]
    return query * HD ** (-0.5), key, value


def attend_kernel(packed_ref, out_ref, lse_ref):
    width = out_ref.shape[1]
    for head in range(width // HD):
        query, key, value = head_parts(packed_ref, head, width)
        query = query.astype(BF16)
        value_t = value.T
        for top in range(0, LEN, FORWARD_BLOCK):
            keys = top + FORWARD_BLOCK
            scores = right_trans(key[:keys], query[top:keys])
            last = causal_tile(scores[top:])
            scores = jnp.concatenate([scores[:top], last]) if top else last
            highest = jnp.max(scores, axis=0, keepdims=True)
            exponent = jnp.exp(scores - highest)
            total = jnp.sum(exponent, axis=0, keepdims=True)
            mixed = product(value_t[:, :keys], exponent.astype(BF16)) / total
            out_ref[top:keys, head * HD : (head + 1) * HD] = mixed.T.astype(BF16)
            lse_ref[0, 0, head : head + 1, top:keys] = highest + jnp.log(total)


def attend_back_kernel(packed_ref, out_ref, grad_ref, lse_ref, grads_ref, key_acc, value_acc):
    width = out_ref.shape[1]
    for head in range(width // HD):
        lanes = slice(head * HD, (head + 1) * HD)
        query, key, value = head_parts(packed_ref, head, width)
        query = query.astype(BF16)
        key_t = key.T
        grad = grad_ref[:, lanes]
        inner = (out_ref[:, lanes].astype(F32) * grad.astype(F32)).T
        inner = jnp.sum(inner, axis=0, keepdims=True)
        for top in reversed(range(0, LEN, BACK_BLOCK)):
            keys = top + BACK_BLOCK
            scores = right_trans(key[:keys], query[top:keys])
            last = causal_tile(scores[top:])
            scores = jnp.concatenate([scores[:top], last]) if top else last
            probs = jnp.exp(scores - lse_ref[0, 0, head : head + 1, top:keys])
            grad_probs = right_trans(value[:keys], grad[top:keys])
            grad_scores = (probs * (grad_probs - inner[:, top:keys])).astype(BF16)
            value_term = product(probs.astype(BF16), grad[top:keys])
            key_term = product(grad_scores, query[top:keys])
            if keys == LEN:
                value_acc[...] = value_term
                key_acc[...] = key_term
            else:
                value_acc[:keys] += value_term
                key_acc[:keys] += key_term
            grad_query = product(key_t[:, :keys], grad_scores) * HD ** (-0.5)
            grads_ref[top:keys, lanes] = grad_query.T.astype(BF16)
        grads_ref[:, width + head * HD : width + (head + 1) * HD] = key_acc[...].astype(BF16)
        grads_ref[:, 2 * width + head * HD : 2 * width + (head + 1) * HD] = value_acc[...].astype(
            BF16
        )


def attend(packed):
    rows, columns = packed.shape
    width = 2 * HD
    sequences, pairs = rows // LEN, columns // (3 * width)
    return pl.pallas_call(
        attend_kernel,
        grid=(sequences, pairs),
        out_shape=(
            jax.ShapeDtypeStruct((rows, pairs * width), BF16),
            jax.ShapeDtypeStruct((sequences, pairs, 2, LEN), F32),
        ),
        in_specs=[pl.BlockSpec((LEN, 3 * width), lambda s, p: (s, p))],
        out_specs=(
            pl.BlockSpec((LEN, width), lambda s, p: (s, p)),
            pl.BlockSpec((1, 1, 2, LEN), lambda s, p: (s, p, 0, 0)),
        ),
        compiler_params=pltpu.CompilerParams(vmem_limit_bytes=VMEM),
        cost_estimate=pl.CostEstimate(
            flops=4 * rows * LEN * pairs * width // 2,
            transcendentals=rows * LEN * pairs,
            bytes_accessed=2 * rows * columns * 2,
        ),
        name="attend",
    )(packed)


def attend_back(packed, attended, grad_attended, lse):
    rows, columns = packed.shape
    width = 2 * HD
    sequences, pairs = rows // LEN, columns // (3 * width)
    narrow = pl.BlockSpec((LEN, width), lambda s, p: (s, p))
    return pl.pallas_call(
        attend_back_kernel,
        grid=(sequences, pairs),
        out_shape=jax.ShapeDtypeStruct((rows, columns), BF16),
        in_specs=[
            pl.BlockSpec((LEN, 3 * width), lambda s, p: (s, p)),
            narrow,
            narrow,
            pl.BlockSpec((1, 1, 2, LEN), lambda s, p: (s, p, 0, 0)),
        ],
        out_specs=pl.BlockSpec((LEN, 3 * width), lambda s, p: (s, p)),
        scratch_shapes=[pltpu.VMEM((LEN, HD), F32)] * 2,
        compiler_params=pltpu.CompilerParams(vmem_limit_bytes=VMEM),
        cost_estimate=pl.CostEstimate(
            flops=10 * rows * LEN * pairs * width // 2,
            transcendentals=rows * LEN * pairs,
            bytes_accessed=3 * rows * columns * 2,
        ),
        name="attend_back",
    )(packed, attended, grad_attended, lse)


SPREAD = (
    (0, 0, "y", None),
    (0, 1, "x", None),
    (0, 0, "x", None),
    (0, 1, "y", None),
    (0, 0, "core", None),
    (0, 1, "core", None),
    (4, 0, "x", 0),
    (2, 1, "y", 1),
    (4, 0, "core", 0),
    (2, 1, "core", 1),
    (2, 0, "core", 2),
    (4, 1, "core", 3),
    (6, 0, "core", 6),
    (6, 1, "core", 7),
)
BIT = {"y": 4, "x": 2, "core": 1}


def neighbours():
    token, feat = lax.axis_index("tok"), lax.axis_index("feat")
    return {
        "y": (token + 1 - 2 * lax.rem(token, 2), feat),
        "x": (token, lax.rem(feat + 2, 4)),
        "core": (token, feat + 1 - 2 * lax.rem(feat, 2)),
    }


def owner(r):
    member, slot = lax.rem(lax.axis_index("tok"), 2), lax.axis_index("feat")
    if r & 4:
        member = 1 - member
    if r & 2:
        slot = lax.rem(slot + 2, 4)
    if r & 1:
        slot = slot + 1 - 2 * lax.rem(slot, 2)
    return member, slot


def greet():
    barrier = pltpu.get_barrier_semaphore()
    for peer in neighbours().values():
        pl.semaphore_signal(barrier, inc=1, device_id=peer, device_id_type=MESH)
    pl.semaphore_wait(barrier, 3)


class Spread:
    def __init__(self, own, region, send, recv):
        self.own, self.region, self.send, self.recv = own, region, send, recv
        self.peers = neighbours()

    def copy(self, k):
        r, half, way, _ = SPREAD[k]
        source = self.own(half) if r == 0 else self.region(r, half)
        return pltpu.make_async_remote_copy(
            source, self.region(r, half), self.send.at[k], self.recv.at[k],
            device_id=self.peers[way], device_id_type=MESH,
        )

    def arrival(self, k):
        r, half, way, _ = SPREAD[k]
        place = self.region(r ^ BIT[way], half)
        return pltpu.make_async_remote_copy(
            place, place, self.send.at[k], self.recv.at[k],
            device_id=self.peers[way], device_id_type=MESH,
        )

    def start(self, half):
        for k, (r, which, _, after) in enumerate(SPREAD):
            if after is None and which == half:
                self.copy(k).start()

    def forward(self):
        for first in range(8):
            if first in (4, 5):
                continue
            self.arrival(first).wait_recv()
            for k, (_, _, _, after) in enumerate(SPREAD):
                if after == first:
                    self.copy(k).start()

    def finish(self):
        for k, (_, _, way, _) in enumerate(SPREAD):
            if way == "core":
                self.arrival(k).wait_recv()
        for k in range(len(SPREAD)):
            self.copy(k).wait_send()


SPREAD_SEMS = [pltpu.SemaphoreType.DMA((len(SPREAD),))] * 2


class Collect:
    def __init__(self, part, size, parts, near, from_x, from_y, last_y, last_x, sems):
        self.part, self.size, self.half = part, size, size // 2
        self.parts, self.near = parts, near
        self.from_x, self.from_y, self.last_y, self.last_x = from_x, from_y, last_y, last_x
        self.load, self.send, self.recv = sems
        self.peers = neighbours()

    @staticmethod
    def scratch(size, columns):
        half = size // 2
        return [
            pltpu.VMEM((4, size, columns), BF16),
            pltpu.VMEM((4, size, columns), BF16),
            pltpu.VMEM((2, half, columns), BF16),
            pltpu.VMEM((2, half, columns), BF16),
            pltpu.VMEM((half, columns), BF16),
            pltpu.VMEM((half, columns), BF16),
            pltpu.SemaphoreType.DMA((4,)),
            pltpu.SemaphoreType.DMA((10,)),
            pltpu.SemaphoreType.DMA((10,)),
        ]

    def remote(self, k, source, target, way):
        return pltpu.make_async_remote_copy(
            source, target, self.send.at[k], self.recv.at[k],
            device_id=self.peers[way], device_id_type=MESH,
        )

    def copy(self, k):
        low, high = pl.ds(0, self.half), pl.ds(self.half, self.half)
        if k < 4:
            return self.remote(k, self.part(2 * k + 1), self.near.at[k], "core")
        if k < 6:
            return self.remote(k, self.parts.at[(1, 3)[k - 4], low], self.from_x.at[k - 4], "x")
        if k < 8:
            return self.remote(k, self.parts.at[(2, 3)[k - 6], high], self.from_y.at[k - 6], "y")
        if k == 8:
            return self.remote(k, self.parts.at[2, low], self.last_y, "y")
        return self.remote(k, self.parts.at[1, high], self.last_x, "x")

    def add(self, index, start, count, other):
        step = 32

        def body(i, carry):
            here = pl.ds(pl.multiple_of(start + i * step, step), step)
            there = pl.ds(pl.multiple_of(i * step, step), step)
            total = self.parts[index, here].astype(F32) + other[there].astype(F32)
            self.parts[index, here] = total.astype(BF16)
            return carry

        lax.fori_loop(0, count // step, body, 0)

    def run(self):
        for k in (3, 1, 2, 0):
            self.copy(k).start()
        loads = [
            pltpu.make_async_copy(self.part(2 * k), self.parts.at[k], self.load.at[k])
            for k in range(4)
        ]
        for k in (3, 1, 2, 0):
            loads[k].start()
        for k, following in ((3, (5, 7)), (1, (4,)), (2, (6,)), (0, ())):
            loads[k].wait()
            self.copy(k).wait_recv()
            self.add(k, 0, self.size, self.near.at[k])
            for after in following:
                self.copy(after).start()
        self.copy(5).wait_recv()
        self.add(2, 0, self.half, self.from_x.at[1])
        self.copy(8).start()
        self.copy(7).wait_recv()
        self.add(1, self.half, self.half, self.from_y.at[1])
        self.copy(9).start()

    def total(self, half, rows):
        first, last = (self.from_x, self.last_y) if half == 0 else (self.from_y, self.last_x)
        own = self.parts[0, pl.ds(pl.multiple_of(half * self.half + rows.start, 32), rows.size)]
        return own.astype(F32) + first[0, rows].astype(F32) + last[rows].astype(F32)

    def ready(self, half):
        for k in ((4, 8) if half == 0 else (6, 9)):
            self.copy(k).wait_recv()

    def finish(self):
        for k in range(10):
            self.copy(k).wait_send()


def loop_rows(count, body):
    def step(i, carry):
        body(pl.ds(pl.multiple_of(i * 32, 32), 32))
        return carry

    lax.fori_loop(0, count // 32, step, 0)


def call(kernel, identity, operands, spaces, outputs, out_spaces, scratch, cost):
    return pl.pallas_call(
        kernel,
        out_shape=outputs,
        in_specs=[pl.BlockSpec(memory_space=space) for space in spaces],
        out_specs=jax.tree.map(lambda space: pl.BlockSpec(memory_space=space), out_spaces),
        scratch_shapes=scratch,
        compiler_params=pltpu.CompilerParams(
            collective_id=identity, has_side_effects=True, vmem_limit_bytes=VMEM
        ),
        cost_estimate=pl.CostEstimate(flops=cost, bytes_accessed=cost // 100, transcendentals=0),
        name=kernel.__name__,
    )(*operands)


def gather_block(identity, shard):
    rows, wide = shard.shape
    half = rows // 2

    def gather_input(shard_ref, out_ref, local, send, recv):
        greet()

        def region(r, which):
            member, slot = owner(r)
            return out_ref.at[
                pl.ds(pl.multiple_of(member * rows + which * half, half), half),
                pl.ds(pl.multiple_of(slot * wide, wide), wide),
            ]

        spread = Spread(
            lambda which: shard_ref.at[pl.ds(which * half, half)], region, send, recv
        )
        spread.start(0)
        spread.start(1)
        copies = [
            pltpu.make_async_copy(
                shard_ref.at[pl.ds(which * half, half)], region(0, which), local.at[which]
            )
            for which in range(2)
        ]
        for copy in copies:
            copy.start()
        spread.forward()
        spread.finish()
        for copy in copies:
            copy.wait()

    return call(
        gather_input, identity, (shard,), (pl.ANY,),
        jax.ShapeDtypeStruct((2 * rows, 4 * wide), shard.dtype), pl.ANY,
        [pltpu.SemaphoreType.DMA((2,))] + SPREAD_SEMS, 40_000_000_000,
    )


def scatter_block(identity, terms):
    rows, wide = terms.shape[0] // 2, terms.shape[1] // 4

    def scatter_output(terms_ref, out_ref, *scratch):
        greet()

        def part(r):
            member, slot = owner(r)
            return terms_ref.at[
                pl.ds(pl.multiple_of(member * rows, rows), rows),
                pl.ds(pl.multiple_of(slot * wide, wide), wide),
            ]

        collect = Collect(part, rows, *scratch[:6], scratch[6:])
        collect.run()
        for which in range(2):
            collect.ready(which)

            def body(here):
                there = pl.ds(pl.multiple_of(which * (rows // 2) + here.start, 32), 32)
                out_ref[there] = collect.total(which, here).astype(BF16)

            loop_rows(rows // 2, body)
        collect.finish()

    return call(
        scatter_output, identity, (terms,), (pl.ANY,),
        jax.ShapeDtypeStruct((rows, wide), BF16), pltpu.VMEM,
        Collect.scratch(rows, wide), 30_000_000_000,
    )


def row_parts(terms_ref, quarter):
    def part(r):
        member, slot = owner(r)
        return terms_ref.at[pl.ds(pl.multiple_of((member * 4 + slot) * quarter, quarter), quarter)]

    return part


def row_region(out_ref, quarter):
    half = quarter // 2

    def region(r, which):
        member, slot = owner(r)
        start = (member * 4 + slot) * quarter + which * half
        return out_ref.at[pl.ds(pl.multiple_of(start, half), half)]

    return region


def middle_norm(identity, terms, x_all, gain):
    total, model = terms.shape
    quarter = total // 8
    half = quarter // 2

    def middle_step(
        terms_ref, x_ref, gain_ref, out_ref, middle_ref, factor_ref,
        x_own, normed, local, send, recv, *scratch
    ):
        greet()
        x_copy = pltpu.make_async_copy(row_parts(x_ref, quarter)(0), x_own, local.at[0])
        x_copy.start()
        collect = Collect(row_parts(terms_ref, quarter), quarter, *scratch[:6], scratch[6:])
        region = row_region(out_ref, quarter)
        spread = Spread(
            lambda which: normed.at[pl.ds(which * half, half)], region, send, recv
        )
        collect.run()
        x_copy.wait()
        copies = []
        for which in range(2):
            collect.ready(which)

            def body(here):
                there = pl.ds(pl.multiple_of(which * half + here.start, 32), 32)
                middle = collect.total(which, here) + x_own[there].astype(F32)
                mean = jnp.mean(middle * middle, axis=1, keepdims=True)
                factor = lax.rsqrt(mean + EPSILON)
                middle_ref[there] = middle
                factor_ref[there] = jnp.broadcast_to(factor, (32, 128))
                normed[there] = (middle * factor * gain_ref[...]).astype(BF16)

            loop_rows(half, body)
            spread.start(which)
            copy = pltpu.make_async_copy(
                normed.at[pl.ds(which * half, half)], region(0, which), local.at[1 + which]
            )
            copy.start()
            copies.append(copy)
        spread.forward()
        spread.finish()
        collect.finish()
        for copy in copies:
            copy.wait()

    return call(
        middle_step, identity, (terms, x_all, gain), (pl.ANY, pl.ANY, pltpu.VMEM),
        (
            jax.ShapeDtypeStruct((total, model), BF16),
            jax.ShapeDtypeStruct((quarter, model), F32),
            jax.ShapeDtypeStruct((quarter, 128), F32),
        ),
        (pl.ANY, pltpu.VMEM, pltpu.VMEM),
        [
            pltpu.VMEM((quarter, model), BF16),
            pltpu.VMEM((quarter, model), BF16),
            pltpu.SemaphoreType.DMA((3,)),
        ]
        + SPREAD_SEMS
        + Collect.scratch(quarter, model),
        70_000_000_000,
    )


def middle_back(identity, terms, cot, middle, factor, gain):
    total, model = terms.shape
    quarter = total // 8
    half = quarter // 2

    def middle_back_step(
        terms_ref, cot_ref, middle_ref, factor_ref, gain_ref, out_ref, grad_ref, gain_grad_ref,
        cot_own, rounded, local, send, recv, *scratch
    ):
        greet()
        cot_copy = pltpu.make_async_copy(row_parts(cot_ref, quarter)(0), cot_own, local.at[0])
        cot_copy.start()
        collect = Collect(row_parts(terms_ref, quarter), quarter, *scratch[:6], scratch[6:])
        region = row_region(out_ref, quarter)
        spread = Spread(
            lambda which: rounded.at[pl.ds(which * half, half)], region, send, recv
        )
        collect.run()
        cot_copy.wait()
        gain_grad_ref[...] = jnp.zeros_like(gain_grad_ref)
        copies = []
        for which in range(2):
            collect.ready(which)

            def body(here):
                there = pl.ds(pl.multiple_of(which * half + here.start, 32), 32)
                grad_normed = collect.total(which, here)
                values = middle_ref[there]
                factor = factor_ref[there][:, :1]
                weighted = gain_ref[...] * grad_normed
                inner = jnp.mean(weighted * values, axis=1, keepdims=True)
                grad = (
                    cot_own[there].astype(F32)
                    + factor * weighted
                    - values * (factor * factor * factor * inner)
                )
                grad_ref[there] = grad
                rounded[there] = grad.astype(BF16)
                gain_grad_ref[...] += jnp.sum(grad_normed * values * factor, axis=0, keepdims=True)

            loop_rows(half, body)
            spread.start(which)
            copy = pltpu.make_async_copy(
                rounded.at[pl.ds(which * half, half)], region(0, which), local.at[1 + which]
            )
            copy.start()
            copies.append(copy)
        spread.forward()
        spread.finish()
        collect.finish()
        for copy in copies:
            copy.wait()

    return call(
        middle_back_step, identity, (terms, cot, middle, factor, gain),
        (pl.ANY, pl.ANY, pltpu.VMEM, pltpu.VMEM, pltpu.VMEM),
        (
            jax.ShapeDtypeStruct((total, model), BF16),
            jax.ShapeDtypeStruct((quarter, model), F32),
            jax.ShapeDtypeStruct((1, model), F32),
        ),
        (pl.ANY, pltpu.VMEM, pltpu.VMEM),
        [
            pltpu.VMEM((quarter, model), BF16),
            pltpu.VMEM((quarter, model), BF16),
            pltpu.SemaphoreType.DMA((3,)),
        ]
        + SPREAD_SEMS
        + Collect.scratch(quarter, model),
        70_000_000_000,
    )


def input_terms(grad_packed, qkv, x_all, gain, grad_middle, own):
    total, columns = grad_packed.shape
    model = x_all.shape[1]
    tile = grad_middle.shape[0]

    def input_terms_step(own_ref, grad_ref, qkv_ref, x_ref, gain_ref, middle_ref, out_ref, gain_grad_ref):
        step = pl.program_id(0)
        grad_normed = right_trans(grad_ref[...], qkv_ref[...])
        values = x_ref[...].astype(F32)
        factor = lax.rsqrt(jnp.mean(values * values, axis=1, keepdims=True) + EPSILON)
        weighted = grad_normed * gain_ref[...]
        inner = jnp.mean(weighted * values, axis=1, keepdims=True)
        terms = factor * weighted - values * (factor * factor * factor * inner)

        @pl.when(step == own_ref[0])
        def _():
            out_ref[...] = (terms + middle_ref[...]).astype(BF16)

        @pl.when(step != own_ref[0])
        def _():
            out_ref[...] = terms.astype(BF16)

        @pl.when(step == 0)
        def _():
            gain_grad_ref[...] = jnp.zeros_like(gain_grad_ref)

        gain_grad_ref[...] += jnp.sum(grad_normed * values * factor, axis=0, keepdims=True)

    return pl.pallas_call(
        input_terms_step,
        grid_spec=pltpu.PrefetchScalarGridSpec(
            num_scalar_prefetch=1,
            grid=(total // tile,),
            in_specs=[
                pl.BlockSpec((tile, columns), lambda i, own: (i, 0)),
                pl.BlockSpec((model, columns), lambda i, own: (0, 0)),
                pl.BlockSpec((tile, model), lambda i, own: (i, 0)),
                pl.BlockSpec((1, model), lambda i, own: (0, 0)),
                pl.BlockSpec((tile, model), lambda i, own: (0, 0)),
            ],
            out_specs=[
                pl.BlockSpec((tile, model), lambda i, own: (i, 0)),
                pl.BlockSpec((1, model), lambda i, own: (0, 0)),
            ],
        ),
        out_shape=[
            jax.ShapeDtypeStruct((total, model), BF16),
            jax.ShapeDtypeStruct((1, model), F32),
        ],
        compiler_params=pltpu.CompilerParams(vmem_limit_bytes=VMEM),
        cost_estimate=pl.CostEstimate(
            flops=2 * total * columns * model,
            transcendentals=total,
            bytes_accessed=6 * total * model,
        ),
        name="input_terms",
    )(own, grad_packed, qkv, x_all, gain, grad_middle)


def program(
    tok_size,
    tokens, gain_attn, w_query, w_key, w_value, w_out, gain_ffn, w_gate, w_up, w_down, cotangent
):
    token = lax.axis_index("tok")
    feat = lax.axis_index("feat")
    member = token % 2
    rows, wide = tokens.shape
    model = 4 * wide
    quarter = rows // 4
    groups = [list(range(i, tok_size, 2)) for i in range(2)]
    pair_width = 2 * HD

    def swap(value):
        return lax.ppermute(value, "tok", [(i, i ^ 1) for i in range(tok_size)])

    def x_swap(value):
        return lax.ppermute(value, "feat", [(i, i ^ 2) for i in range(4)])

    def core_swap(value):
        return lax.ppermute(value, "feat", [(i, i ^ 1) for i in range(4)])

    def mine(values, axis):
        size = values.shape[axis] // 2
        return lax.dynamic_slice_in_dim(values, member * size, size, axis)

    def theirs(values, axis):
        size = values.shape[axis] // 2
        return lax.dynamic_slice_in_dim(values, (1 - member) * size, size, axis)

    def ordered(own, other, axis):
        first = jnp.where(member == 0, own, other)
        second = jnp.where(member == 0, other, own)
        return jnp.concatenate([first, second], axis=axis)

    def weight_start(shard, hidden_axis):
        return ordered(
            mine(shard, hidden_axis), swap(theirs(shard, hidden_axis)), 1 - hidden_axis
        )

    def ring_gather(shard, axis):
        return lax.all_gather(shard, "tok", axis=axis, tiled=True, axis_index_groups=groups)

    def ring_scatter(terms, axis):
        return lax.psum_scatter(
            terms, "tok", scatter_dimension=axis, tiled=True, axis_index_groups=groups
        )

    def weight_finish(total, hidden_axis):
        axis = 1 - hidden_axis
        other = swap(theirs(total, axis))
        return ordered(mine(total, axis), other, hidden_axis).astype(F32)

    def add_own_rows(values, own):
        start = (member * 4 + feat) * quarter
        here = lax.dynamic_slice_in_dim(values, start, quarter, 0)
        here = (here.astype(F32) + own).astype(BF16)
        return lax.dynamic_update_slice_in_dim(values, here, start, 0)

    packed_weights = []
    starts = [weight_start(w, 1) for w in (w_query, w_key, w_value)]
    heads_wide = starts[0].shape[1]
    for left in range(0, heads_wide, pair_width):
        packed_weights += [w[:, left : left + pair_width] for w in starts]
    qkv_start = jnp.concatenate(packed_weights, axis=1)
    out_start = weight_start(w_out, 0)
    tokens_after, qkv_start, out_start = lax.optimization_barrier((tokens, qkv_start, out_start))
    qkv = ring_gather(qkv_start, 0)
    out_proj = ring_gather(out_start, 1)
    x_all = gather_block(0, tokens_after)
    w_gate, w_up, w_down, cotangent, x_all = lax.optimization_barrier(
        (w_gate, w_up, w_down, cotangent, x_all)
    )
    gate_start = weight_start(w_gate, 1)
    up_start = weight_start(w_up, 1)
    down_start = weight_start(w_down, 0)
    hidden_wide = down_start.shape[0]
    chunk = hidden_wide // CHUNKS
    gate_up, down_proj = [], []
    for c in range(CHUNKS):
        part = slice(c * chunk, (c + 1) * chunk)
        gate_up.append(
            ring_gather(jnp.concatenate([gate_start[:, part], up_start[:, part]], axis=1), 0)
        )
        down_proj.append(ring_gather(down_start[part], 1))
    cot_rows = gather_block(1, cotangent)

    gains = jnp.stack([gain_attn, gain_ffn])
    gains = jnp.stack([gains, core_swap(gains)])
    gains = jnp.concatenate([gains, x_swap(gains)])
    gains = jnp.concatenate(
        [lax.dynamic_index_in_dim(gains, feat ^ j, 0, keepdims=False) for j in range(4)], axis=1
    )
    gain_one, gain_two = gains[:1], gains[1:]

    x_wide = x_all.astype(F32)
    factor_one = lax.rsqrt(jnp.mean(x_wide * x_wide, axis=1, keepdims=True) + EPSILON)
    normed = (x_wide * factor_one * gain_one).astype(BF16)
    packed = product(normed, qkv).astype(BF16)
    attended, log_sums = attend(packed)
    normed_two, middle, factor_two = middle_norm(
        2, product(attended, out_proj).astype(BF16), x_all, gain_two
    )

    out_rows = 0.0
    grad_normed_two = 0.0
    gate_grads, up_grads, down_grads = [], [], []
    for c in range(CHUNKS):
        both = product(normed_two, gate_up[c])
        gate, upward = both[:, :chunk], both[:, chunk:]
        sigma = jax.nn.sigmoid(gate)
        hidden = (gate * sigma * upward).astype(BF16)
        grad_hidden = right_trans(cot_rows, down_proj[c])
        grad_gate = (grad_hidden * upward * sigma * (1.0 + gate * (1.0 - sigma))).astype(BF16)
        grad_up = (grad_hidden * gate * sigma).astype(BF16)
        grad_both = jnp.concatenate([grad_gate, grad_up], axis=1)
        grad_normed_two = grad_normed_two + right_trans(grad_both, gate_up[c])
        down_grads.append(ring_scatter(left_trans(hidden, cot_rows).astype(BF16), 1))
        both_grad = ring_scatter(left_trans(normed_two, grad_both).astype(BF16), 0)
        gate_grads.append(both_grad[:, :chunk])
        up_grads.append(both_grad[:, chunk:])
        out_rows = out_rows + product(hidden, down_proj[c])
    gate_grad = weight_finish(jnp.concatenate(gate_grads, axis=1), 1)
    up_grad = weight_finish(jnp.concatenate(up_grads, axis=1), 1)
    down_grad = weight_finish(jnp.concatenate(down_grads, axis=0), 0)
    grad_mid_rows, grad_middle, gain_ffn_part = middle_back(
        3, grad_normed_two.astype(BF16), cot_rows, middle, factor_two, gain_two
    )
    outcome = scatter_block(4, add_own_rows(out_rows.astype(BF16), middle))

    grad_attended = right_trans(grad_mid_rows, out_proj).astype(BF16)
    out_grad = weight_finish(
        ring_scatter(left_trans(attended, grad_mid_rows).astype(BF16), 1), 0
    )
    grad_packed = attend_back(packed, attended, grad_attended, log_sums)
    qkv_grad = ring_scatter(left_trans(normed, grad_packed).astype(BF16), 0)
    part_grads = []
    for part in range(3):
        columns = [
            qkv_grad[:, left + part * pair_width : left + (part + 1) * pair_width]
            for left in range(0, 3 * heads_wide, 3 * pair_width)
        ]
        part_grads.append(weight_finish(jnp.concatenate(columns, axis=1), 1))
    own = (member * 4 + feat).astype(jnp.int32).reshape(1)
    terms, gain_attn_part = input_terms(grad_packed, qkv, x_all, gain_one, grad_middle, own)
    input_grad = scatter_block(5, terms)

    sums = jnp.concatenate([gain_attn_part, gain_ffn_part])
    for change in (core_swap, x_swap):
        sums = sums + change(sums)
    bit = 1
    while bit < tok_size:
        sums = sums + lax.ppermute(sums, "tok", [(i, i ^ bit) for i in range(tok_size)])
        bit *= 2
    gain_grads = lax.dynamic_slice_in_dim(sums, feat * wide, wide, 1)
    return (
        outcome,
        input_grad,
        gain_grads[0],
        gain_grads[1],
        *part_grads,
        out_grad,
        gate_grad,
        up_grad,
        down_grad,
    )


def solution(mesh):
    in_specs = (
        P("tok", "feat"),
        P("feat"),
        P("tok", "feat"),
        P("tok", "feat"),
        P("tok", "feat"),
        P("feat", "tok"),
        P("feat"),
        P("tok", "feat"),
        P("tok", "feat"),
        P("feat", "tok"),
        P("tok", "feat"),
    )
    out_specs = (
        P("tok", "feat"),
        P("tok", "feat"),
        P("feat"),
        P("feat"),
        P("tok", "feat"),
        P("tok", "feat"),
        P("tok", "feat"),
        P("feat", "tok"),
        P("tok", "feat"),
        P("tok", "feat"),
        P("feat", "tok"),
    )

    def on_device(*arrays):
        return program(mesh.shape["tok"], *arrays)

    return jax.shard_map(
        on_device, mesh=mesh, in_specs=in_specs, out_specs=out_specs, check_vma=False
    )
```

```python
import jax
import jax.numpy as jnp
from jax import lax
from jax.experimental import pallas as pl
from jax.experimental.pallas import tpu as pltpu
from jax.sharding import PartitionSpec as P

HD = 64
LEN = 1024
EPSILON = 1e-05
BF16 = jnp.bfloat16
F32 = jnp.float32
MESH = pl.DeviceIdType.MESH
VMEM = 48 << 20
CHUNKS = 2
FORWARD_BLOCK = 512
BACK_BLOCK = 256


def left_trans(left, right):
    return lax.dot_general(
        left, right, (((0,), (0,)), ((), ())), preferred_element_type=F32
    )


def right_trans(left, right):
    return lax.dot_general(
        left, right, (((1,), (1,)), ((), ())), preferred_element_type=F32
    )


def product(left, right):
    return jnp.dot(left, right, preferred_element_type=F32)


def causal_tile(scores):
    size = scores.shape[0]
    key = lax.broadcasted_iota(jnp.int32, scores.shape, 0)
    query = lax.broadcasted_iota(jnp.int32, scores.shape, 1)
    return jnp.where(key <= query, scores, -1e30)


def head_parts(packed_ref, head, width):
    columns = [slice(part * width + head * HD, part * width + (head + 1) * HD) for part in range(3)]
    query, key, value = [packed_ref[:, part] for part in columns]
    return query * HD ** (-0.5), key, value


def attend_kernel(packed_ref, out_ref, lse_ref):
    width = out_ref.shape[1]
    for head in range(width // HD):
        query, key, value = head_parts(packed_ref, head, width)
        query = query.astype(BF16)
        value_t = value.T
        for top in range(0, LEN, FORWARD_BLOCK):
            keys = top + FORWARD_BLOCK
            scores = right_trans(key[:keys], query[top:keys])
            last = causal_tile(scores[top:])
            scores = jnp.concatenate([scores[:top], last]) if top else last
            highest = jnp.max(scores, axis=0, keepdims=True)
            exponent = jnp.exp(scores - highest)
            total = jnp.sum(exponent, axis=0, keepdims=True)
            mixed = product(value_t[:, :keys], exponent.astype(BF16)) / total
            out_ref[top:keys, head * HD : (head + 1) * HD] = mixed.T.astype(BF16)
            lse_ref[0, 0, head : head + 1, top:keys] = highest + jnp.log(total)


def attend_back_kernel(packed_ref, out_ref, grad_ref, lse_ref, grads_ref, key_acc, value_acc):
    width = out_ref.shape[1]
    for head in range(width // HD):
        lanes = slice(head * HD, (head + 1) * HD)
        query, key, value = head_parts(packed_ref, head, width)
        query = query.astype(BF16)
        key_t = key.T
        grad = grad_ref[:, lanes]
        inner = (out_ref[:, lanes].astype(F32) * grad.astype(F32)).T
        inner = jnp.sum(inner, axis=0, keepdims=True)
        for top in reversed(range(0, LEN, BACK_BLOCK)):
            keys = top + BACK_BLOCK
            scores = right_trans(key[:keys], query[top:keys])
            last = causal_tile(scores[top:])
            scores = jnp.concatenate([scores[:top], last]) if top else last
            probs = jnp.exp(scores - lse_ref[0, 0, head : head + 1, top:keys])
            grad_probs = right_trans(value[:keys], grad[top:keys])
            grad_scores = (probs * (grad_probs - inner[:, top:keys])).astype(BF16)
            value_term = product(probs.astype(BF16), grad[top:keys])
            key_term = product(grad_scores, query[top:keys])
            if keys == LEN:
                value_acc[...] = value_term
                key_acc[...] = key_term
            else:
                value_acc[:keys] += value_term
                key_acc[:keys] += key_term
            grad_query = product(key_t[:, :keys], grad_scores) * HD ** (-0.5)
            grads_ref[top:keys, lanes] = grad_query.T.astype(BF16)
        grads_ref[:, width + head * HD : width + (head + 1) * HD] = key_acc[...].astype(BF16)
        grads_ref[:, 2 * width + head * HD : 2 * width + (head + 1) * HD] = value_acc[...].astype(
            BF16
        )


def attend(packed):
    rows, columns = packed.shape
    width = 2 * HD
    sequences, pairs = rows // LEN, columns // (3 * width)
    return pl.pallas_call(
        attend_kernel,
        grid=(sequences, pairs),
        out_shape=(
            jax.ShapeDtypeStruct((rows, pairs * width), BF16),
            jax.ShapeDtypeStruct((sequences, pairs, 2, LEN), F32),
        ),
        in_specs=[pl.BlockSpec((LEN, 3 * width), lambda s, p: (s, p))],
        out_specs=(
            pl.BlockSpec((LEN, width), lambda s, p: (s, p)),
            pl.BlockSpec((1, 1, 2, LEN), lambda s, p: (s, p, 0, 0)),
        ),
        compiler_params=pltpu.CompilerParams(vmem_limit_bytes=VMEM),
        cost_estimate=pl.CostEstimate(
            flops=4 * rows * LEN * pairs * width // 2,
            transcendentals=rows * LEN * pairs,
            bytes_accessed=2 * rows * columns * 2,
        ),
        name="attend",
    )(packed)


def attend_back(packed, attended, grad_attended, lse):
    rows, columns = packed.shape
    width = 2 * HD
    sequences, pairs = rows // LEN, columns // (3 * width)
    narrow = pl.BlockSpec((LEN, width), lambda s, p: (s, p))
    return pl.pallas_call(
        attend_back_kernel,
        grid=(sequences, pairs),
        out_shape=jax.ShapeDtypeStruct((rows, columns), BF16),
        in_specs=[
            pl.BlockSpec((LEN, 3 * width), lambda s, p: (s, p)),
            narrow,
            narrow,
            pl.BlockSpec((1, 1, 2, LEN), lambda s, p: (s, p, 0, 0)),
        ],
        out_specs=pl.BlockSpec((LEN, 3 * width), lambda s, p: (s, p)),
        scratch_shapes=[pltpu.VMEM((LEN, HD), F32)] * 2,
        compiler_params=pltpu.CompilerParams(vmem_limit_bytes=VMEM),
        cost_estimate=pl.CostEstimate(
            flops=10 * rows * LEN * pairs * width // 2,
            transcendentals=rows * LEN * pairs,
            bytes_accessed=3 * rows * columns * 2,
        ),
        name="attend_back",
    )(packed, attended, grad_attended, lse)


SPREAD = (
    (0, 0, "y", None),
    (0, 1, "x", None),
    (0, 0, "x", None),
    (0, 1, "y", None),
    (0, 0, "core", None),
    (0, 1, "core", None),
    (4, 0, "x", 0),
    (2, 1, "y", 1),
    (4, 0, "core", 0),
    (2, 1, "core", 1),
    (2, 0, "core", 2),
    (4, 1, "core", 3),
    (6, 0, "core", 6),
    (6, 1, "core", 7),
)
BIT = {"y": 4, "x": 2, "core": 1}


def neighbours():
    token, feat = lax.axis_index("tok"), lax.axis_index("feat")
    return {
        "y": (token + 1 - 2 * lax.rem(token, 2), feat),
        "x": (token, lax.rem(feat + 2, 4)),
        "core": (token, feat + 1 - 2 * lax.rem(feat, 2)),
    }


def owner(r):
    member, slot = lax.rem(lax.axis_index("tok"), 2), lax.axis_index("feat")
    if r & 4:
        member = 1 - member
    if r & 2:
        slot = lax.rem(slot + 2, 4)
    if r & 1:
        slot = slot + 1 - 2 * lax.rem(slot, 2)
    return member, slot


def greet():
    barrier = pltpu.get_barrier_semaphore()
    for peer in neighbours().values():
        pl.semaphore_signal(barrier, inc=1, device_id=peer, device_id_type=MESH)
    pl.semaphore_wait(barrier, 3)


class Spread:
    def __init__(self, own, region, send, recv):
        self.own, self.region, self.send, self.recv = own, region, send, recv
        self.peers = neighbours()

    def copy(self, k):
        r, half, way, _ = SPREAD[k]
        source = self.own(half) if r == 0 else self.region(r, half)
        return pltpu.make_async_remote_copy(
            source, self.region(r, half), self.send.at[k], self.recv.at[k],
            device_id=self.peers[way], device_id_type=MESH,
        )

    def arrival(self, k):
        r, half, way, _ = SPREAD[k]
        place = self.region(r ^ BIT[way], half)
        return pltpu.make_async_remote_copy(
            place, place, self.send.at[k], self.recv.at[k],
            device_id=self.peers[way], device_id_type=MESH,
        )

    def start(self, half):
        for k, (r, which, _, after) in enumerate(SPREAD):
            if after is None and which == half:
                self.copy(k).start()

    def forward(self):
        for first in range(8):
            if first in (4, 5):
                continue
            self.arrival(first).wait_recv()
            for k, (_, _, _, after) in enumerate(SPREAD):
                if after == first:
                    self.copy(k).start()

    def finish(self):
        for k, (_, _, way, _) in enumerate(SPREAD):
            if way == "core":
                self.arrival(k).wait_recv()
        for k in range(len(SPREAD)):
            self.copy(k).wait_send()


SPREAD_SEMS = [pltpu.SemaphoreType.DMA((len(SPREAD),))] * 2


class Collect:
    def __init__(self, part, size, parts, near, from_x, from_y, last_y, last_x, sems):
        self.part, self.size, self.half = part, size, size // 2
        self.parts, self.near = parts, near
        self.from_x, self.from_y, self.last_y, self.last_x = from_x, from_y, last_y, last_x
        self.load, self.send, self.recv = sems
        self.peers = neighbours()

    @staticmethod
    def scratch(size, columns):
        half = size // 2
        return [
            pltpu.VMEM((4, size, columns), BF16),
            pltpu.VMEM((4, size, columns), BF16),
            pltpu.VMEM((2, half, columns), BF16),
            pltpu.VMEM((2, half, columns), BF16),
            pltpu.VMEM((half, columns), BF16),
            pltpu.VMEM((half, columns), BF16),
            pltpu.SemaphoreType.DMA((4,)),
            pltpu.SemaphoreType.DMA((10,)),
            pltpu.SemaphoreType.DMA((10,)),
        ]

    def remote(self, k, source, target, way):
        return pltpu.make_async_remote_copy(
            source, target, self.send.at[k], self.recv.at[k],
            device_id=self.peers[way], device_id_type=MESH,
        )

    def copy(self, k):
        low, high = pl.ds(0, self.half), pl.ds(self.half, self.half)
        if k < 4:
            return self.remote(k, self.part(2 * k + 1), self.near.at[k], "core")
        if k < 6:
            return self.remote(k, self.parts.at[(1, 3)[k - 4], low], self.from_x.at[k - 4], "x")
        if k < 8:
            return self.remote(k, self.parts.at[(2, 3)[k - 6], high], self.from_y.at[k - 6], "y")
        if k == 8:
            return self.remote(k, self.parts.at[2, low], self.last_y, "y")
        return self.remote(k, self.parts.at[1, high], self.last_x, "x")

    def add(self, index, start, count, other):
        step = 32

        def body(i, carry):
            here = pl.ds(pl.multiple_of(start + i * step, step), step)
            there = pl.ds(pl.multiple_of(i * step, step), step)
            total = self.parts[index, here].astype(F32) + other[there].astype(F32)
            self.parts[index, here] = total.astype(BF16)
            return carry

        lax.fori_loop(0, count // step, body, 0)

    def run(self):
        for k in (3, 1, 2, 0):
            self.copy(k).start()
        loads = [
            pltpu.make_async_copy(self.part(2 * k), self.parts.at[k], self.load.at[k])
            for k in range(4)
        ]
        for k in (3, 1, 2, 0):
            loads[k].start()
        for k, following in ((3, (5, 7)), (1, (4,)), (2, (6,)), (0, ())):
            loads[k].wait()
            self.copy(k).wait_recv()
            self.add(k, 0, self.size, self.near.at[k])
            for after in following:
                self.copy(after).start()
        self.copy(5).wait_recv()
        self.add(2, 0, self.half, self.from_x.at[1])
        self.copy(8).start()
        self.copy(7).wait_recv()
        self.add(1, self.half, self.half, self.from_y.at[1])
        self.copy(9).start()

    def total(self, half, rows):
        first, last = (self.from_x, self.last_y) if half == 0 else (self.from_y, self.last_x)
        own = self.parts[0, pl.ds(pl.multiple_of(half * self.half + rows.start, 32), rows.size)]
        return own.astype(F32) + first[0, rows].astype(F32) + last[rows].astype(F32)

    def ready(self, half):
        for k in ((4, 8) if half == 0 else (6, 9)):
            self.copy(k).wait_recv()

    def finish(self):
        for k in range(10):
            self.copy(k).wait_send()


def loop_rows(count, body):
    def step(i, carry):
        body(pl.ds(pl.multiple_of(i * 32, 32), 32))
        return carry

    lax.fori_loop(0, count // 32, step, 0)


def call(kernel, identity, operands, spaces, outputs, out_spaces, scratch, cost):
    return pl.pallas_call(
        kernel,
        out_shape=outputs,
        in_specs=[pl.BlockSpec(memory_space=space) for space in spaces],
        out_specs=jax.tree.map(lambda space: pl.BlockSpec(memory_space=space), out_spaces),
        scratch_shapes=scratch,
        compiler_params=pltpu.CompilerParams(
            collective_id=identity, has_side_effects=True, vmem_limit_bytes=VMEM
        ),
        cost_estimate=pl.CostEstimate(flops=cost, bytes_accessed=cost // 100, transcendentals=0),
        name=kernel.__name__,
    )(*operands)


def gather_blocks(identity, *shards):
    rows, wide = shards[0].shape
    half = rows // 2
    count = len(shards)

    def gather_inputs(*refs):
        greet()
        local = refs[2 * count]
        spreads, copies = [], []
        for i in range(count):
            shard_ref, out_ref = refs[i], refs[count + i]

            def own(which, shard_ref=shard_ref):
                return shard_ref.at[pl.ds(which * half, half)]

            def region(r, which, out_ref=out_ref):
                member, slot = owner(r)
                return out_ref.at[
                    pl.ds(pl.multiple_of(member * rows + which * half, half), half),
                    pl.ds(pl.multiple_of(slot * wide, wide), wide),
                ]

            sems = refs[2 * count + 1 + 2 * i : 2 * count + 3 + 2 * i]
            spreads.append(Spread(own, region, *sems))
            for which in range(2):
                copies.append(
                    pltpu.make_async_copy(own(which), region(0, which), local.at[i, which])
                )
        spreads[0].start(0)
        spreads[0].start(1)
        for copy in copies:
            copy.start()
        for i in range(count):
            spreads[i].forward()
            if i + 1 < count:
                spreads[i + 1].start(0)
                spreads[i + 1].start(1)
        for spread in spreads:
            spread.finish()
        for copy in copies:
            copy.wait()

    return call(
        gather_inputs, identity, shards, (pl.ANY,) * count,
        [jax.ShapeDtypeStruct((2 * rows, 4 * wide), shard.dtype) for shard in shards],
        [pl.ANY] * count,
        [pltpu.SemaphoreType.DMA((count, 2))] + SPREAD_SEMS * count, 80_000_000_000,
    )


def scatter_block(identity, terms):
    rows, wide = terms.shape[0] // 2, terms.shape[1] // 4

    def scatter_output(terms_ref, out_ref, *scratch):
        greet()

        def part(r):
            member, slot = owner(r)
            return terms_ref.at[
                pl.ds(pl.multiple_of(member * rows, rows), rows),
                pl.ds(pl.multiple_of(slot * wide, wide), wide),
            ]

        collect = Collect(part, rows, *scratch[:6], scratch[6:])
        collect.run()
        for which in range(2):
            collect.ready(which)

            def body(here):
                there = pl.ds(pl.multiple_of(which * (rows // 2) + here.start, 32), 32)
                out_ref[there] = collect.total(which, here).astype(BF16)

            loop_rows(rows // 2, body)
        collect.finish()

    return call(
        scatter_output, identity, (terms,), (pl.ANY,),
        jax.ShapeDtypeStruct((rows, wide), BF16), pltpu.VMEM,
        Collect.scratch(rows, wide), 30_000_000_000,
    )


def row_parts(terms_ref, quarter):
    def part(r):
        member, slot = owner(r)
        return terms_ref.at[pl.ds(pl.multiple_of((member * 4 + slot) * quarter, quarter), quarter)]

    return part


def row_region(out_ref, quarter):
    half = quarter // 2

    def region(r, which):
        member, slot = owner(r)
        start = (member * 4 + slot) * quarter + which * half
        return out_ref.at[pl.ds(pl.multiple_of(start, half), half)]

    return region


def middle_norm(identity, terms, x_all, gain):
    total, model = terms.shape
    quarter = total // 8
    half = quarter // 2

    def middle_step(
        terms_ref, x_ref, gain_ref, out_ref, middle_ref, factor_ref,
        x_own, normed, local, send, recv, *scratch
    ):
        greet()
        x_copy = pltpu.make_async_copy(row_parts(x_ref, quarter)(0), x_own, local.at[0])
        x_copy.start()
        collect = Collect(row_parts(terms_ref, quarter), quarter, *scratch[:6], scratch[6:])
        region = row_region(out_ref, quarter)
        spread = Spread(
            lambda which: normed.at[pl.ds(which * half, half)], region, send, recv
        )
        collect.run()
        x_copy.wait()
        copies = []
        for which in range(2):
            collect.ready(which)

            def body(here):
                there = pl.ds(pl.multiple_of(which * half + here.start, 32), 32)
                middle = collect.total(which, here) + x_own[there].astype(F32)
                mean = jnp.mean(middle * middle, axis=1, keepdims=True)
                factor = lax.rsqrt(mean + EPSILON)
                middle_ref[there] = middle
                factor_ref[there] = jnp.broadcast_to(factor, (32, 128))
                normed[there] = (middle * factor * gain_ref[...]).astype(BF16)

            loop_rows(half, body)
            spread.start(which)
            copy = pltpu.make_async_copy(
                normed.at[pl.ds(which * half, half)], region(0, which), local.at[1 + which]
            )
            copy.start()
            copies.append(copy)
        spread.forward()
        spread.finish()
        collect.finish()
        for copy in copies:
            copy.wait()

    return call(
        middle_step, identity, (terms, x_all, gain), (pl.ANY, pl.ANY, pltpu.VMEM),
        (
            jax.ShapeDtypeStruct((total, model), BF16),
            jax.ShapeDtypeStruct((quarter, model), F32),
            jax.ShapeDtypeStruct((quarter, 128), F32),
        ),
        (pl.ANY, pltpu.VMEM, pltpu.VMEM),
        [
            pltpu.VMEM((quarter, model), BF16),
            pltpu.VMEM((quarter, model), BF16),
            pltpu.SemaphoreType.DMA((3,)),
        ]
        + SPREAD_SEMS
        + Collect.scratch(quarter, model),
        70_000_000_000,
    )


def middle_back(identity, terms, cot, middle, factor, gain):
    total, model = terms.shape
    quarter = total // 8
    half = quarter // 2

    def middle_back_step(
        terms_ref, cot_ref, middle_ref, factor_ref, gain_ref, out_ref, grad_ref, gain_grad_ref,
        cot_own, rounded, local, send, recv, *scratch
    ):
        greet()
        cot_copy = pltpu.make_async_copy(row_parts(cot_ref, quarter)(0), cot_own, local.at[0])
        cot_copy.start()
        collect = Collect(row_parts(terms_ref, quarter), quarter, *scratch[:6], scratch[6:])
        region = row_region(out_ref, quarter)
        spread = Spread(
            lambda which: rounded.at[pl.ds(which * half, half)], region, send, recv
        )
        collect.run()
        cot_copy.wait()
        gain_grad_ref[...] = jnp.zeros_like(gain_grad_ref)
        copies = []
        for which in range(2):
            collect.ready(which)

            def body(here):
                there = pl.ds(pl.multiple_of(which * half + here.start, 32), 32)
                grad_normed = collect.total(which, here)
                values = middle_ref[there]
                factor = factor_ref[there][:, :1]
                weighted = gain_ref[...] * grad_normed
                inner = jnp.mean(weighted * values, axis=1, keepdims=True)
                grad = (
                    cot_own[there].astype(F32)
                    + factor * weighted
                    - values * (factor * factor * factor * inner)
                )
                grad_ref[there] = grad
                rounded[there] = grad.astype(BF16)
                gain_grad_ref[...] += jnp.sum(grad_normed * values * factor, axis=0, keepdims=True)

            loop_rows(half, body)
            spread.start(which)
            copy = pltpu.make_async_copy(
                rounded.at[pl.ds(which * half, half)], region(0, which), local.at[1 + which]
            )
            copy.start()
            copies.append(copy)
        spread.forward()
        spread.finish()
        collect.finish()
        for copy in copies:
            copy.wait()

    return call(
        middle_back_step, identity, (terms, cot, middle, factor, gain),
        (pl.ANY, pl.ANY, pltpu.VMEM, pltpu.VMEM, pltpu.VMEM),
        (
            jax.ShapeDtypeStruct((total, model), BF16),
            jax.ShapeDtypeStruct((quarter, model), F32),
            jax.ShapeDtypeStruct((1, model), F32),
        ),
        (pl.ANY, pltpu.VMEM, pltpu.VMEM),
        [
            pltpu.VMEM((quarter, model), BF16),
            pltpu.VMEM((quarter, model), BF16),
            pltpu.SemaphoreType.DMA((3,)),
        ]
        + SPREAD_SEMS
        + Collect.scratch(quarter, model),
        70_000_000_000,
    )


def input_terms(grad_packed, weights, x_all, gain, grad_middle, own):
    total, columns = grad_packed.shape
    model = x_all.shape[1]
    tile = grad_middle.shape[0]

    def input_terms_step(own_ref, grad_ref, qkv_ref, x_ref, gain_ref, middle_ref, out_ref, gain_grad_ref):
        step = pl.program_id(0)
        grad_normed = right_trans(grad_ref[...], qkv_ref[...])
        values = x_ref[...].astype(F32)
        factor = lax.rsqrt(jnp.mean(values * values, axis=1, keepdims=True) + EPSILON)
        weighted = grad_normed * gain_ref[...]
        inner = jnp.mean(weighted * values, axis=1, keepdims=True)
        terms = factor * weighted - values * (factor * factor * factor * inner)

        @pl.when(step == own_ref[0])
        def _():
            out_ref[...] = (terms + middle_ref[...]).astype(BF16)

        @pl.when(step != own_ref[0])
        def _():
            out_ref[...] = terms.astype(BF16)

        @pl.when(step == 0)
        def _():
            gain_grad_ref[...] = jnp.zeros_like(gain_grad_ref)

        gain_grad_ref[...] += jnp.sum(grad_normed * values * factor, axis=0, keepdims=True)

    return pl.pallas_call(
        input_terms_step,
        grid_spec=pltpu.PrefetchScalarGridSpec(
            num_scalar_prefetch=1,
            grid=(total // tile,),
            in_specs=[
                pl.BlockSpec((tile, columns), lambda i, own: (i, 0)),
                pl.BlockSpec((model, columns), lambda i, own: (0, 0)),
                pl.BlockSpec((tile, model), lambda i, own: (i, 0)),
                pl.BlockSpec((1, model), lambda i, own: (0, 0)),
                pl.BlockSpec((tile, model), lambda i, own: (0, 0)),
            ],
            out_specs=[
                pl.BlockSpec((tile, model), lambda i, own: (i, 0)),
                pl.BlockSpec((1, model), lambda i, own: (0, 0)),
            ],
        ),
        out_shape=[
            jax.ShapeDtypeStruct((total, model), BF16),
            jax.ShapeDtypeStruct((1, model), F32),
        ],
        compiler_params=pltpu.CompilerParams(vmem_limit_bytes=VMEM),
        cost_estimate=pl.CostEstimate(
            flops=2 * total * columns * model,
            transcendentals=total,
            bytes_accessed=6 * total * model,
        ),
        name="input_terms",
    )(own, grad_packed, weights, x_all, gain, grad_middle)


def program(
    tok_size,
    tokens, gain_attn, w_query, w_key, w_value, w_out, gain_ffn, w_gate, w_up, w_down, cotangent
):
    token = lax.axis_index("tok")
    feat = lax.axis_index("feat")
    member = token % 2
    rows, wide = tokens.shape
    model = 4 * wide
    quarter = rows // 4
    groups = [list(range(i, tok_size, 2)) for i in range(2)]
    pair_width = 2 * HD

    def swap(value):
        return lax.ppermute(value, "tok", [(i, i ^ 1) for i in range(tok_size)])

    def x_swap(value):
        return lax.ppermute(value, "feat", [(i, i ^ 2) for i in range(4)])

    def core_swap(value):
        return lax.ppermute(value, "feat", [(i, i ^ 1) for i in range(4)])

    def halves(weight, own):
        size = weight.shape[1] // 2
        start = member if own else 1 - member
        return lax.dynamic_slice_in_dim(weight, start * size, size, 1)

    def pair_blocks(weights, select):
        own = select([halves(w, True) for w in weights])
        other = swap(select([halves(w, False) for w in weights]))
        return jnp.where(
            member == 0,
            jnp.concatenate([own, other]),
            jnp.concatenate([other, own]),
        )

    def ring_gather(shard):
        return lax.all_gather(shard, "tok", axis=0, tiled=True, axis_index_groups=groups)

    def ring_scatter(terms):
        return lax.psum_scatter(
            terms, "tok", scatter_dimension=0, tiled=True, axis_index_groups=groups
        )

    def pair_finish(total):
        size = total.shape[0] // 2
        own = lax.dynamic_slice_in_dim(total, member * size, size, 0)
        other = swap(lax.dynamic_slice_in_dim(total, (1 - member) * size, size, 0))
        first = jnp.where(member == 0, own, other)
        second = jnp.where(member == 0, other, own)
        return first, second

    def add_own_rows(values, own):
        start = (member * 4 + feat) * quarter
        here = lax.dynamic_slice_in_dim(values, start, quarter, 0)
        here = (here.astype(F32) + own).astype(BF16)
        return lax.dynamic_update_slice_in_dim(values, here, start, 0)

    def attention_columns(parts):
        heads_wide = parts[0].shape[1]
        packed = []
        for left in range(0, heads_wide, pair_width):
            packed += [part[:, left : left + pair_width] for part in parts[:3]]
        return jnp.concatenate(packed + [parts[3]], axis=1)

    def chunk_columns(c):
        def select(parts):
            size = parts[0].shape[1] // CHUNKS
            return jnp.concatenate([part[:, c * size : (c + 1) * size] for part in parts], axis=1)

        return select

    attention_start = pair_blocks((w_query, w_key, w_value, w_out.T), attention_columns)
    feed_starts = [
        pair_blocks((w_gate, w_up, w_down.T), chunk_columns(c)) for c in range(CHUNKS)
    ]
    tokens_after, attention_start = lax.optimization_barrier((tokens, attention_start))
    attention_weights = ring_gather(attention_start)
    x_all, cot_rows = gather_blocks(0, tokens_after, cotangent)
    feed_weights = [ring_gather(start) for start in feed_starts]
    heads_wide = w_query.shape[1] // 2
    qkv = attention_weights[:, : 3 * heads_wide]
    out_proj = attention_weights[:, 3 * heads_wide :]
    chunk = w_gate.shape[1] // 2 // CHUNKS

    gains = jnp.stack([gain_attn, gain_ffn])
    gains = jnp.stack([gains, core_swap(gains)])
    gains = jnp.concatenate([gains, x_swap(gains)])
    gains = jnp.concatenate(
        [lax.dynamic_index_in_dim(gains, feat ^ j, 0, keepdims=False) for j in range(4)], axis=1
    )
    gain_one, gain_two = gains[:1], gains[1:]

    x_wide = x_all.astype(F32)
    factor_one = lax.rsqrt(jnp.mean(x_wide * x_wide, axis=1, keepdims=True) + EPSILON)
    normed = (x_wide * factor_one * gain_one).astype(BF16)
    packed = product(normed, qkv).astype(BF16)
    attended, log_sums = attend(packed)
    normed_two, middle, factor_two = middle_norm(
        2, right_trans(attended, out_proj).astype(BF16), x_all, gain_two
    )

    out_rows = 0.0
    grad_normed_two = 0.0
    feed_sums = []
    for c in range(CHUNKS):
        if c:
            feed_weights[c], feed_terms = lax.optimization_barrier((feed_weights[c], feed_terms))
            feed_sums.append(ring_scatter(feed_terms))
        gate_up, down_proj = feed_weights[c][:, : 2 * chunk], feed_weights[c][:, 2 * chunk :]
        both = product(normed_two, gate_up)
        gate, upward = both[:, :chunk], both[:, chunk:]
        sigma = jax.nn.sigmoid(gate)
        hidden = (gate * sigma * upward).astype(BF16)
        grad_hidden = product(cot_rows, down_proj)
        grad_gate = (grad_hidden * upward * sigma * (1.0 + gate * (1.0 - sigma))).astype(BF16)
        grad_up = (grad_hidden * gate * sigma).astype(BF16)
        grad_both = jnp.concatenate([grad_gate, grad_up], axis=1)
        grad_normed_two = grad_normed_two + right_trans(grad_both, gate_up)
        if c + 1 == CHUNKS:
            grad_normed_two = grad_normed_two.astype(BF16)
        feed_terms = jnp.concatenate(
            [
                left_trans(normed_two, grad_both).astype(BF16),
                left_trans(cot_rows, hidden).astype(BF16),
            ],
            axis=1,
        )
        out_rows = out_rows + right_trans(hidden, down_proj)
    grad_normed_two, feed_terms = lax.optimization_barrier((grad_normed_two, feed_terms))
    feed_sums.append(ring_scatter(feed_terms))

    grad_mid_rows, grad_middle, gain_ffn_part = middle_back(
        3, grad_normed_two, cot_rows, middle, factor_two, gain_two
    )

    grad_mid_rows, feed_sums[0] = lax.optimization_barrier((grad_mid_rows, feed_sums[0]))
    grad_attended = product(grad_mid_rows, out_proj).astype(BF16)
    grad_packed = attend_back(packed, attended, grad_attended, log_sums)
    attention_terms = jnp.concatenate(
        [
            left_trans(normed, grad_packed).astype(BF16),
            left_trans(grad_mid_rows, attended).astype(BF16),
        ],
        axis=1,
    )
    attention_terms, grad_packed = lax.optimization_barrier((attention_terms, grad_packed))
    attention_grads = pair_finish(ring_scatter(attention_terms))
    part_grads = []
    for part in range(3):
        columns = [
            grads[:, left + part * pair_width : left + (part + 1) * pair_width]
            for grads in attention_grads
            for left in range(0, 3 * heads_wide, 3 * pair_width)
        ]
        part_grads.append(jnp.concatenate(columns, axis=1).astype(F32))
    out_grad = (
        jnp.concatenate([grads[:, 3 * heads_wide :] for grads in attention_grads], axis=1)
        .astype(F32)
        .T
    )
    own = (member * 4 + feat).astype(jnp.int32).reshape(1)
    terms, gain_attn_part = input_terms(grad_packed, attention_weights, x_all, gain_one, grad_middle, own)
    input_grad = scatter_block(5, terms)
    out_rows = add_own_rows(out_rows.astype(BF16), middle)
    out_rows, feed_sums[1] = lax.optimization_barrier((out_rows, feed_sums[1]))
    outcome = scatter_block(4, out_rows)
    feed_grads = [pair_finish(total) for total in feed_sums]

    def feed_grad(part):
        columns = slice(part * chunk, (part + 1) * chunk)
        return jnp.concatenate(
            [feed_grads[c][which][:, columns] for which in range(2) for c in range(CHUNKS)],
            axis=1,
        ).astype(F32)

    gate_grad, up_grad, down_grad = feed_grad(0), feed_grad(1), feed_grad(2).T

    sums = jnp.concatenate([gain_attn_part, gain_ffn_part])
    for change in (core_swap, x_swap):
        sums = sums + change(sums)
    bit = 1
    while bit < tok_size:
        sums = sums + lax.ppermute(sums, "tok", [(i, i ^ bit) for i in range(tok_size)])
        bit *= 2
    gain_grads = lax.dynamic_slice_in_dim(sums, feat * wide, wide, 1)
    return (
        outcome,
        input_grad,
        gain_grads[0],
        gain_grads[1],
        *part_grads,
        out_grad,
        gate_grad,
        up_grad,
        down_grad,
    )


def solution(mesh):
    in_specs = (
        P("tok", "feat"),
        P("feat"),
        P("tok", "feat"),
        P("tok", "feat"),
        P("tok", "feat"),
        P("feat", "tok"),
        P("feat"),
        P("tok", "feat"),
        P("tok", "feat"),
        P("feat", "tok"),
        P("tok", "feat"),
    )
    out_specs = (
        P("tok", "feat"),
        P("tok", "feat"),
        P("feat"),
        P("feat"),
        P("tok", "feat"),
        P("tok", "feat"),
        P("tok", "feat"),
        P("feat", "tok"),
        P("tok", "feat"),
        P("tok", "feat"),
        P("feat", "tok"),
    )

    def on_device(*arrays):
        return program(mesh.shape["tok"], *arrays)

    return jax.shard_map(
        on_device, mesh=mesh, in_specs=in_specs, out_specs=out_specs, check_vma=False
    )
```

```python
import jax
import jax.numpy as jnp
from jax import lax
from jax.experimental import pallas as pl
from jax.experimental.pallas import tpu as pltpu
from jax.sharding import PartitionSpec as P

HD = 64
LEN = 1024
EPSILON = 1e-05
BF16 = jnp.bfloat16
F32 = jnp.float32
MESH = pl.DeviceIdType.MESH
VMEM = 48 << 20
CHUNKS = 2
FORWARD_BLOCK = 512
BACK_BLOCK = 256


def left_trans(left, right):
    return lax.dot_general(
        left, right, (((0,), (0,)), ((), ())), preferred_element_type=F32
    )


def right_trans(left, right):
    return lax.dot_general(
        left, right, (((1,), (1,)), ((), ())), preferred_element_type=F32
    )


def product(left, right):
    return jnp.dot(left, right, preferred_element_type=F32)


def causal_tile(scores):
    size = scores.shape[0]
    key = lax.broadcasted_iota(jnp.int32, scores.shape, 0)
    query = lax.broadcasted_iota(jnp.int32, scores.shape, 1)
    return jnp.where(key <= query, scores, -1e30)


def head_parts(packed_ref, head, width):
    columns = [slice(part * width + head * HD, part * width + (head + 1) * HD) for part in range(3)]
    query, key, value = [packed_ref[:, part] for part in columns]
    return query * HD ** (-0.5), key, value


def attend_kernel(packed_ref, out_ref, lse_ref):
    width = out_ref.shape[1]
    for head in range(width // HD):
        query, key, value = head_parts(packed_ref, head, width)
        query = query.astype(BF16)
        value_t = value.T
        for top in range(0, LEN, FORWARD_BLOCK):
            keys = top + FORWARD_BLOCK
            scores = right_trans(key[:keys], query[top:keys])
            last = causal_tile(scores[top:])
            scores = jnp.concatenate([scores[:top], last]) if top else last
            highest = jnp.max(scores, axis=0, keepdims=True)
            exponent = jnp.exp(scores - highest)
            total = jnp.sum(exponent, axis=0, keepdims=True)
            mixed = product(value_t[:, :keys], exponent.astype(BF16)) / total
            out_ref[top:keys, head * HD : (head + 1) * HD] = mixed.T.astype(BF16)
            lse_ref[0, 0, head : head + 1, top:keys] = highest + jnp.log(total)


def attend_back_kernel(packed_ref, out_ref, grad_ref, lse_ref, grads_ref, key_acc, value_acc):
    width = out_ref.shape[1]
    for head in range(width // HD):
        lanes = slice(head * HD, (head + 1) * HD)
        query, key, value = head_parts(packed_ref, head, width)
        query = query.astype(BF16)
        key_t = key.T
        grad = grad_ref[:, lanes]
        inner = (out_ref[:, lanes].astype(F32) * grad.astype(F32)).T
        inner = jnp.sum(inner, axis=0, keepdims=True)
        for top in reversed(range(0, LEN, BACK_BLOCK)):
            keys = top + BACK_BLOCK
            scores = right_trans(key[:keys], query[top:keys])
            last = causal_tile(scores[top:])
            scores = jnp.concatenate([scores[:top], last]) if top else last
            probs = jnp.exp(scores - lse_ref[0, 0, head : head + 1, top:keys])
            grad_probs = right_trans(value[:keys], grad[top:keys])
            grad_scores = (probs * (grad_probs - inner[:, top:keys])).astype(BF16)
            value_term = product(probs.astype(BF16), grad[top:keys])
            key_term = product(grad_scores, query[top:keys])
            if keys == LEN:
                value_acc[...] = value_term
                key_acc[...] = key_term
            else:
                value_acc[:keys] += value_term
                key_acc[:keys] += key_term
            grad_query = product(key_t[:, :keys], grad_scores) * HD ** (-0.5)
            grads_ref[top:keys, lanes] = grad_query.T.astype(BF16)
        grads_ref[:, width + head * HD : width + (head + 1) * HD] = key_acc[...].astype(BF16)
        grads_ref[:, 2 * width + head * HD : 2 * width + (head + 1) * HD] = value_acc[...].astype(
            BF16
        )


def attend(packed):
    rows, columns = packed.shape
    width = 2 * HD
    sequences, pairs = rows // LEN, columns // (3 * width)
    return pl.pallas_call(
        attend_kernel,
        grid=(sequences, pairs),
        out_shape=(
            jax.ShapeDtypeStruct((rows, pairs * width), BF16),
            jax.ShapeDtypeStruct((sequences, pairs, 2, LEN), F32),
        ),
        in_specs=[pl.BlockSpec((LEN, 3 * width), lambda s, p: (s, p))],
        out_specs=(
            pl.BlockSpec((LEN, width), lambda s, p: (s, p)),
            pl.BlockSpec((1, 1, 2, LEN), lambda s, p: (s, p, 0, 0)),
        ),
        compiler_params=pltpu.CompilerParams(vmem_limit_bytes=VMEM),
        cost_estimate=pl.CostEstimate(
            flops=4 * rows * LEN * pairs * width // 2,
            transcendentals=rows * LEN * pairs,
            bytes_accessed=2 * rows * columns * 2,
        ),
        name="attend",
    )(packed)


def attend_back(packed, attended, grad_attended, lse):
    rows, columns = packed.shape
    width = 2 * HD
    sequences, pairs = rows // LEN, columns // (3 * width)
    narrow = pl.BlockSpec((LEN, width), lambda s, p: (s, p))
    return pl.pallas_call(
        attend_back_kernel,
        grid=(sequences, pairs),
        out_shape=jax.ShapeDtypeStruct((rows, columns), BF16),
        in_specs=[
            pl.BlockSpec((LEN, 3 * width), lambda s, p: (s, p)),
            narrow,
            narrow,
            pl.BlockSpec((1, 1, 2, LEN), lambda s, p: (s, p, 0, 0)),
        ],
        out_specs=pl.BlockSpec((LEN, 3 * width), lambda s, p: (s, p)),
        scratch_shapes=[pltpu.VMEM((LEN, HD), F32)] * 2,
        compiler_params=pltpu.CompilerParams(vmem_limit_bytes=VMEM),
        cost_estimate=pl.CostEstimate(
            flops=10 * rows * LEN * pairs * width // 2,
            transcendentals=rows * LEN * pairs,
            bytes_accessed=3 * rows * columns * 2,
        ),
        name="attend_back",
    )(packed, attended, grad_attended, lse)


SPREAD = (
    (0, 0, "y", None),
    (0, 1, "x", None),
    (0, 0, "x", None),
    (0, 1, "y", None),
    (0, 0, "core", None),
    (0, 1, "core", None),
    (4, 0, "x", 0),
    (2, 1, "y", 1),
    (4, 0, "core", 0),
    (2, 1, "core", 1),
    (2, 0, "core", 2),
    (4, 1, "core", 3),
    (6, 0, "core", 6),
    (6, 1, "core", 7),
)
BIT = {"y": 4, "x": 2, "core": 1}


def neighbours():
    token, feat = lax.axis_index("tok"), lax.axis_index("feat")
    return {
        "y": (token + 1 - 2 * lax.rem(token, 2), feat),
        "x": (token, lax.rem(feat + 2, 4)),
        "core": (token, feat + 1 - 2 * lax.rem(feat, 2)),
    }


def owner(r):
    member, slot = lax.rem(lax.axis_index("tok"), 2), lax.axis_index("feat")
    if r & 4:
        member = 1 - member
    if r & 2:
        slot = lax.rem(slot + 2, 4)
    if r & 1:
        slot = slot + 1 - 2 * lax.rem(slot, 2)
    return member, slot


def greet(others=()):
    barrier = pltpu.get_barrier_semaphore()
    peers = [*neighbours().values(), *others]
    for peer in peers:
        pl.semaphore_signal(barrier, inc=1, device_id=peer, device_id_type=MESH)
    pl.semaphore_wait(barrier, len(peers))


def ring_peer(ring, distance):
    token = lax.axis_index("tok")
    return lax.rem(token + 2 * distance, 2 * ring), lax.axis_index("feat")


class SumAll:
    def __init__(self, ring, ref, steps, arrived, slots, send, recv):
        self.ring, self.ref = ring, ref
        self.steps, self.arrived, self.slots = steps, arrived, slots
        self.send, self.recv = send, recv
        self.place = lax.div(lax.axis_index("tok"), 2)
        self.peers = neighbours()

    @staticmethod
    def scratch(ring, shape):
        return [
            pltpu.VMEM((3, *shape), F32),
            pltpu.VMEM((3, *shape), F32),
            pltpu.VMEM((ring, *shape), F32),
            pltpu.SemaphoreType.DMA((2 + ring,)),
            pltpu.SemaphoreType.DMA((2 + ring,)),
        ]

    def copy(self, k):
        if k < 3:
            source = self.ref if k == 0 else self.steps.at[k - 1]
            target, peer = self.arrived.at[k], self.peers[("core", "x", "y")[k]]
        else:
            source, target = self.steps.at[2], self.slots.at[self.place]
            peer = ring_peer(self.ring, k - 2)
        return pltpu.make_async_remote_copy(
            source, target, self.send.at[k], self.recv.at[k],
            device_id=peer, device_id_type=MESH,
        )

    def start(self):
        self.copy(0).start()

    def step(self, k):
        self.copy(k).wait_recv()
        before = self.ref[...] if k == 0 else self.steps[k - 1]
        self.steps[k] = before + self.arrived[k]
        if k < 2:
            self.copy(k + 1).start()
        else:
            for distance in range(1, self.ring):
                self.copy(2 + distance).start()
            self.slots[self.place] = self.steps[2]

    def finish(self):
        for distance in range(1, self.ring):
            source = lax.rem(self.place + self.ring - distance, self.ring)
            k = 2 + distance
            pltpu.make_async_remote_copy(
                self.slots.at[source], self.slots.at[source], self.send.at[k], self.recv.at[k],
                device_id=ring_peer(self.ring, distance), device_id_type=MESH,
            ).wait_recv()
        for k in range(2 + self.ring):
            self.copy(k).wait_send()
        total = self.slots[0]
        for place in range(1, self.ring):
            total = total + self.slots[place]
        return total


class Spread:
    def __init__(self, own, region, send, recv):
        self.own, self.region, self.send, self.recv = own, region, send, recv
        self.peers = neighbours()

    def copy(self, k):
        r, half, way, _ = SPREAD[k]
        source = self.own(half) if r == 0 else self.region(r, half)
        return pltpu.make_async_remote_copy(
            source, self.region(r, half), self.send.at[k], self.recv.at[k],
            device_id=self.peers[way], device_id_type=MESH,
        )

    def arrival(self, k):
        r, half, way, _ = SPREAD[k]
        place = self.region(r ^ BIT[way], half)
        return pltpu.make_async_remote_copy(
            place, place, self.send.at[k], self.recv.at[k],
            device_id=self.peers[way], device_id_type=MESH,
        )

    def start(self, half):
        for k, (r, which, _, after) in enumerate(SPREAD):
            if after is None and which == half:
                self.copy(k).start()

    def forward(self):
        for first in range(8):
            if first in (4, 5):
                continue
            self.arrival(first).wait_recv()
            for k, (_, _, _, after) in enumerate(SPREAD):
                if after == first:
                    self.copy(k).start()

    def finish(self):
        for k, (_, _, way, _) in enumerate(SPREAD):
            if way == "core":
                self.arrival(k).wait_recv()
        for k in range(len(SPREAD)):
            self.copy(k).wait_send()


SPREAD_SEMS = [pltpu.SemaphoreType.DMA((len(SPREAD),))] * 2


class Collect:
    def __init__(self, part, size, parts, near, from_x, from_y, last_y, last_x, sems):
        self.part, self.size, self.half = part, size, size // 2
        self.parts, self.near = parts, near
        self.from_x, self.from_y, self.last_y, self.last_x = from_x, from_y, last_y, last_x
        self.load, self.send, self.recv = sems
        self.peers = neighbours()

    @staticmethod
    def scratch(size, columns):
        half = size // 2
        return [
            pltpu.VMEM((4, size, columns), BF16),
            pltpu.VMEM((4, size, columns), BF16),
            pltpu.VMEM((2, half, columns), BF16),
            pltpu.VMEM((2, half, columns), BF16),
            pltpu.VMEM((half, columns), BF16),
            pltpu.VMEM((half, columns), BF16),
            pltpu.SemaphoreType.DMA((4,)),
            pltpu.SemaphoreType.DMA((10,)),
            pltpu.SemaphoreType.DMA((10,)),
        ]

    def remote(self, k, source, target, way):
        return pltpu.make_async_remote_copy(
            source, target, self.send.at[k], self.recv.at[k],
            device_id=self.peers[way], device_id_type=MESH,
        )

    def copy(self, k):
        low, high = pl.ds(0, self.half), pl.ds(self.half, self.half)
        if k < 4:
            return self.remote(k, self.part(2 * k + 1), self.near.at[k], "core")
        if k < 6:
            return self.remote(k, self.parts.at[(1, 3)[k - 4], low], self.from_x.at[k - 4], "x")
        if k < 8:
            return self.remote(k, self.parts.at[(2, 3)[k - 6], high], self.from_y.at[k - 6], "y")
        if k == 8:
            return self.remote(k, self.parts.at[2, low], self.last_y, "y")
        return self.remote(k, self.parts.at[1, high], self.last_x, "x")

    def add(self, index, start, count, other):
        step = 32

        def body(i, carry):
            here = pl.ds(pl.multiple_of(start + i * step, step), step)
            there = pl.ds(pl.multiple_of(i * step, step), step)
            total = self.parts[index, here].astype(F32) + other[there].astype(F32)
            self.parts[index, here] = total.astype(BF16)
            return carry

        lax.fori_loop(0, count // step, body, 0)

    def loads(self, k):
        return pltpu.make_async_copy(self.part(2 * k), self.parts.at[k], self.load.at[k])

    def start(self):
        for k in (3, 1, 2, 0):
            self.copy(k).start()
        for k in (3, 1, 2, 0):
            self.loads(k).start()

    def first(self):
        for k, following in ((3, (5, 7)), (1, (4,)), (2, (6,)), (0, ())):
            self.loads(k).wait()
            self.copy(k).wait_recv()
            self.add(k, 0, self.size, self.near.at[k])
            for after in following:
                self.copy(after).start()

    def second(self):
        self.copy(5).wait_recv()
        self.add(2, 0, self.half, self.from_x.at[1])
        self.copy(8).start()
        self.copy(7).wait_recv()
        self.add(1, self.half, self.half, self.from_y.at[1])
        self.copy(9).start()

    def total(self, half, rows):
        first, last = (self.from_x, self.last_y) if half == 0 else (self.from_y, self.last_x)
        own = self.parts[0, pl.ds(pl.multiple_of(half * self.half + rows.start, 32), rows.size)]
        return own.astype(F32) + first[0, rows].astype(F32) + last[rows].astype(F32)

    def ready(self, half):
        for k in ((4, 8) if half == 0 else (6, 9)):
            self.copy(k).wait_recv()

    def finish(self):
        for k in range(10):
            self.copy(k).wait_send()


def loop_rows(count, body):
    def step(i, carry):
        body(pl.ds(pl.multiple_of(i * 32, 32), 32))
        return carry

    lax.fori_loop(0, count // 32, step, 0)


def call(kernel, identity, operands, spaces, outputs, out_spaces, scratch, cost):
    return pl.pallas_call(
        kernel,
        out_shape=outputs,
        in_specs=[pl.BlockSpec(memory_space=space) for space in spaces],
        out_specs=jax.tree.map(lambda space: pl.BlockSpec(memory_space=space), out_spaces),
        scratch_shapes=scratch,
        compiler_params=pltpu.CompilerParams(
            collective_id=identity, has_side_effects=True, vmem_limit_bytes=VMEM
        ),
        cost_estimate=pl.CostEstimate(flops=cost, bytes_accessed=cost // 100, transcendentals=0),
        name=kernel.__name__,
    )(*operands)


class PairSwap:
    def __init__(self, sources, out_ref, pieces, local, send, recv):
        self.sources, self.out, self.pieces = sources, out_ref, pieces
        self.local, self.send, self.recv = local, send, recv
        self.peer = neighbours()["y"]
        self.member = lax.rem(lax.axis_index("tok"), 2)

    def block(self, i, half):
        source, start, width, _ = self.pieces[i]
        ref = self.sources[source]
        offset = half * (ref.shape[1] // 2) + start
        return ref.at[:, pl.ds(pl.multiple_of(offset, 128), width)]

    def place(self, i, member):
        _, _, width, column = self.pieces[i]
        rows = self.out.shape[0] // 2
        return self.out.at[pl.ds(pl.multiple_of(member * rows, rows), rows), pl.ds(column, width)]

    def remote(self, i, source, member):
        return pltpu.make_async_remote_copy(
            source, self.place(i, member), self.send.at[i], self.recv.at[i],
            device_id=self.peer, device_id_type=MESH,
        )

    def own(self, i):
        return pltpu.make_async_copy(
            self.block(i, self.member), self.place(i, self.member), self.local.at[i]
        )

    def away(self, i):
        return self.remote(i, self.block(i, 1 - self.member), self.member)

    def start(self):
        for i in range(len(self.pieces)):
            self.away(i).start()
        for i in range(len(self.pieces)):
            self.own(i).start()

    def finish(self):
        for i in range(len(self.pieces)):
            other = 1 - self.member
            self.remote(i, self.place(i, other), other).wait_recv()
            self.away(i).wait_send()
            self.own(i).wait()


def swap_and_gather(identity, weights, pieces, shard=None):
    count = len(weights)
    size = weights[0].shape[0]
    columns = sum(piece[2] for piece in pieces)
    operands = tuple(weights)
    outputs = [jax.ShapeDtypeStruct((2 * size, columns), weights[0].dtype)]
    scratch = [pltpu.SemaphoreType.DMA((len(pieces),))] * 3
    if shard is not None:
        rows, wide = shard.shape
        half = rows // 2
        operands += (shard,)
        outputs.append(jax.ShapeDtypeStruct((2 * rows, 4 * wide), shard.dtype))
        scratch += [pltpu.SemaphoreType.DMA((2,))] + SPREAD_SEMS

    def swap_gather(*refs):
        sources, refs = refs[:count], refs[count:]
        if shard is not None:
            shard_ref, start_ref, out_ref, *sems = refs
        else:
            start_ref, *sems = refs
        greet()
        pair = PairSwap(sources, start_ref, pieces, *sems[:3])
        pair.start()
        if shard is None:
            pair.finish()
            return

        def own(which):
            return shard_ref.at[pl.ds(which * half, half)]

        def region(r, which):
            member, slot = owner(r)
            return out_ref.at[
                pl.ds(pl.multiple_of(member * rows + which * half, half), half),
                pl.ds(pl.multiple_of(slot * wide, wide), wide),
            ]

        spread = Spread(own, region, *sems[4:])
        spread.start(0)
        spread.start(1)
        copies = [
            pltpu.make_async_copy(own(which), region(0, which), sems[3].at[which])
            for which in range(2)
        ]
        for copy in copies:
            copy.start()
        spread.forward()
        spread.finish()
        pair.finish()
        for copy in copies:
            copy.wait()

    return call(
        swap_gather, identity, operands, (pl.ANY,) * len(operands),
        outputs, [pl.ANY] * len(outputs), scratch,
        15_000_000_000 if shard is None else 50_000_000_000,
    )


def scatter_blocks(identity, ring, vector, *terms):
    rows, wide = terms[0].shape[0] // 2, terms[0].shape[1] // 4
    count = len(terms)

    def scatter_outputs(vector_ref, *refs):
        greet([ring_peer(ring, distance) for distance in range(1, ring)])
        small_ref = refs[2 * count]
        scratch = refs[2 * count + 1 :]
        small = SumAll(ring, vector_ref, *scratch[:5])
        collects = []
        for i in range(count):

            def part(r, terms_ref=refs[i]):
                member, slot = owner(r)
                return terms_ref.at[
                    pl.ds(pl.multiple_of(member * rows, rows), rows),
                    pl.ds(pl.multiple_of(slot * wide, wide), wide),
                ]

            mine = scratch[5 + 9 * i : 5 + 9 * (i + 1)]
            collects.append(Collect(part, rows, *mine[:6], mine[6:]))
        small.start()
        for collect in collects:
            collect.start()
        small.step(0)
        for collect in collects:
            collect.first()
        small.step(1)
        for collect in collects:
            collect.second()
        small.step(2)
        for collect, out_ref in zip(collects, refs[count:]):
            for which in range(2):
                collect.ready(which)

                def body(here, collect=collect, out_ref=out_ref):
                    there = pl.ds(pl.multiple_of(which * (rows // 2) + here.start, 32), 32)
                    out_ref[there] = collect.total(which, here).astype(BF16)

                loop_rows(rows // 2, body)
        for collect in collects:
            collect.finish()
        scratch[1][0] = small.finish()
        start = pl.multiple_of(lax.axis_index("feat") * wide, wide)
        small_ref[...] = scratch[1][0, :, pl.ds(start, wide)]

    return call(
        scatter_outputs, identity, (vector, *terms), (pltpu.VMEM,) + (pl.ANY,) * count,
        [jax.ShapeDtypeStruct((rows, wide), BF16)] * count
        + [jax.ShapeDtypeStruct((vector.shape[0], wide), F32)],
        [pltpu.VMEM] * (count + 1),
        SumAll.scratch(ring, vector.shape) + Collect.scratch(rows, wide) * count,
        30_000_000_000 * count,
    )


def row_parts(terms_ref, quarter):
    def part(r):
        member, slot = owner(r)
        return terms_ref.at[pl.ds(pl.multiple_of((member * 4 + slot) * quarter, quarter), quarter)]

    return part


def row_region(out_ref, quarter):
    half = quarter // 2

    def region(r, which):
        member, slot = owner(r)
        start = (member * 4 + slot) * quarter + which * half
        return out_ref.at[pl.ds(pl.multiple_of(start, half), half)]

    return region


def middle_norm(identity, terms, x_all, gain):
    total, model = terms.shape
    quarter = total // 8
    half = quarter // 2

    def middle_step(
        terms_ref, x_ref, gain_ref, out_ref, middle_ref, factor_ref,
        x_own, normed, local, send, recv, *scratch
    ):
        greet()
        x_copy = pltpu.make_async_copy(row_parts(x_ref, quarter)(0), x_own, local.at[0])
        x_copy.start()
        collect = Collect(row_parts(terms_ref, quarter), quarter, *scratch[:6], scratch[6:])
        region = row_region(out_ref, quarter)
        spread = Spread(
            lambda which: normed.at[pl.ds(which * half, half)], region, send, recv
        )
        collect.start()
        collect.first()
        collect.second()
        x_copy.wait()
        copies = []
        for which in range(2):
            collect.ready(which)

            def body(here):
                there = pl.ds(pl.multiple_of(which * half + here.start, 32), 32)
                middle = collect.total(which, here) + x_own[there].astype(F32)
                mean = jnp.mean(middle * middle, axis=1, keepdims=True)
                factor = lax.rsqrt(mean + EPSILON)
                middle_ref[there] = middle
                factor_ref[there] = jnp.broadcast_to(factor, (32, 128))
                normed[there] = (middle * factor * gain_ref[...]).astype(BF16)

            loop_rows(half, body)
            spread.start(which)
            copy = pltpu.make_async_copy(
                normed.at[pl.ds(which * half, half)], region(0, which), local.at[1 + which]
            )
            copy.start()
            copies.append(copy)
        spread.forward()
        spread.finish()
        collect.finish()
        for copy in copies:
            copy.wait()

    return call(
        middle_step, identity, (terms, x_all, gain), (pl.ANY, pl.ANY, pltpu.VMEM),
        (
            jax.ShapeDtypeStruct((total, model), BF16),
            jax.ShapeDtypeStruct((quarter, model), F32),
            jax.ShapeDtypeStruct((quarter, 128), F32),
        ),
        (pl.ANY, pltpu.VMEM, pltpu.VMEM),
        [
            pltpu.VMEM((quarter, model), BF16),
            pltpu.VMEM((quarter, model), BF16),
            pltpu.SemaphoreType.DMA((3,)),
        ]
        + SPREAD_SEMS
        + Collect.scratch(quarter, model),
        70_000_000_000,
    )


def middle_back(identity, terms, cot, middle, factor, gain):
    total, model = terms.shape
    quarter = total // 8
    half = quarter // 2

    def middle_back_step(
        terms_ref, cot_ref, middle_ref, factor_ref, gain_ref, out_ref, grad_ref, gain_grad_ref,
        cot_own, rounded, local, send, recv, *scratch
    ):
        greet()
        cot_copy = pltpu.make_async_copy(row_parts(cot_ref, quarter)(0), cot_own, local.at[0])
        cot_copy.start()
        collect = Collect(row_parts(terms_ref, quarter), quarter, *scratch[:6], scratch[6:])
        region = row_region(out_ref, quarter)
        spread = Spread(
            lambda which: rounded.at[pl.ds(which * half, half)], region, send, recv
        )
        collect.start()
        collect.first()
        collect.second()
        cot_copy.wait()
        gain_grad_ref[...] = jnp.zeros_like(gain_grad_ref)
        copies = []
        for which in range(2):
            collect.ready(which)

            def body(here):
                there = pl.ds(pl.multiple_of(which * half + here.start, 32), 32)
                grad_normed = collect.total(which, here)
                values = middle_ref[there]
                factor = factor_ref[there][:, :1]
                weighted = gain_ref[...] * grad_normed
                inner = jnp.mean(weighted * values, axis=1, keepdims=True)
                grad = (
                    cot_own[there].astype(F32)
                    + factor * weighted
                    - values * (factor * factor * factor * inner)
                )
                grad_ref[there] = grad
                rounded[there] = grad.astype(BF16)
                gain_grad_ref[...] += jnp.sum(grad_normed * values * factor, axis=0, keepdims=True)

            loop_rows(half, body)
            spread.start(which)
            copy = pltpu.make_async_copy(
                rounded.at[pl.ds(which * half, half)], region(0, which), local.at[1 + which]
            )
            copy.start()
            copies.append(copy)
        spread.forward()
        spread.finish()
        collect.finish()
        for copy in copies:
            copy.wait()

    return call(
        middle_back_step, identity, (terms, cot, middle, factor, gain),
        (pl.ANY, pl.ANY, pltpu.VMEM, pltpu.VMEM, pltpu.VMEM),
        (
            jax.ShapeDtypeStruct((total, model), BF16),
            jax.ShapeDtypeStruct((quarter, model), F32),
            jax.ShapeDtypeStruct((1, model), F32),
        ),
        (pl.ANY, pltpu.VMEM, pltpu.VMEM),
        [
            pltpu.VMEM((quarter, model), BF16),
            pltpu.VMEM((quarter, model), BF16),
            pltpu.SemaphoreType.DMA((3,)),
        ]
        + SPREAD_SEMS
        + Collect.scratch(quarter, model),
        70_000_000_000,
    )


def assemble(plan, flipped_out, totals, others):
    count = len(totals)
    size = others[0].shape[0]
    shapes = []
    for index, pieces in enumerate(plan):
        wide = 2 * sum(piece[2] for piece in pieces)
        shapes.append((size, wide) if index < flipped_out else (wide, size))

    def assemble_grads(*refs):
        member = lax.rem(lax.axis_index("tok"), 2)
        outs = refs[2 * count :]
        for index, pieces in enumerate(plan):
            half = sum(piece[2] for piece in pieces)
            for source, column, width, target in pieces:
                own_rows = pl.ds(pl.multiple_of(member * size, size), size)
                own = refs[source][own_rows, column : column + width]
                other = refs[count + source][:, column : column + width]
                for which, block in ((member, own), (1 - member, other)):
                    start = pl.multiple_of(which * half + target, 128)
                    if index < flipped_out:
                        outs[index][:, pl.ds(start, width)] = block.astype(F32)
                    else:
                        outs[index][pl.ds(start, width), :] = block.astype(F32).T

    return pl.pallas_call(
        assemble_grads,
        out_shape=[jax.ShapeDtypeStruct(shape, F32) for shape in shapes],
        in_specs=[pl.BlockSpec(memory_space=pltpu.VMEM)] * (2 * count),
        out_specs=[pl.BlockSpec(memory_space=pltpu.VMEM)] * len(plan),
        compiler_params=pltpu.CompilerParams(vmem_limit_bytes=VMEM),
        cost_estimate=pl.CostEstimate(
            flops=0, transcendentals=0, bytes_accessed=8 * size * 2 * sum(t.shape[1] for t in totals)
        ),
        name="assemble_grads",
    )(*totals, *others)


def input_terms(grad_packed, weights, x_all, gain, grad_middle, own):
    total, columns = grad_packed.shape
    model = x_all.shape[1]
    tile = grad_middle.shape[0]

    def input_terms_step(own_ref, grad_ref, qkv_ref, x_ref, gain_ref, middle_ref, out_ref, gain_grad_ref):
        step = pl.program_id(0)
        grad_normed = right_trans(grad_ref[...], qkv_ref[...])
        values = x_ref[...].astype(F32)
        factor = lax.rsqrt(jnp.mean(values * values, axis=1, keepdims=True) + EPSILON)
        weighted = grad_normed * gain_ref[...]
        inner = jnp.mean(weighted * values, axis=1, keepdims=True)
        terms = factor * weighted - values * (factor * factor * factor * inner)

        @pl.when(step == own_ref[0])
        def _():
            out_ref[...] = (terms + middle_ref[...]).astype(BF16)

        @pl.when(step != own_ref[0])
        def _():
            out_ref[...] = terms.astype(BF16)

        @pl.when(step == 0)
        def _():
            gain_grad_ref[...] = jnp.zeros_like(gain_grad_ref)

        gain_grad_ref[...] += jnp.sum(grad_normed * values * factor, axis=0, keepdims=True)

    return pl.pallas_call(
        input_terms_step,
        grid_spec=pltpu.PrefetchScalarGridSpec(
            num_scalar_prefetch=1,
            grid=(total // tile,),
            in_specs=[
                pl.BlockSpec((tile, columns), lambda i, own: (i, 0)),
                pl.BlockSpec((model, columns), lambda i, own: (0, 0)),
                pl.BlockSpec((tile, model), lambda i, own: (i, 0)),
                pl.BlockSpec((1, model), lambda i, own: (0, 0)),
                pl.BlockSpec((tile, model), lambda i, own: (0, 0)),
            ],
            out_specs=[
                pl.BlockSpec((tile, model), lambda i, own: (i, 0)),
                pl.BlockSpec((1, model), lambda i, own: (0, 0)),
            ],
        ),
        out_shape=[
            jax.ShapeDtypeStruct((total, model), BF16),
            jax.ShapeDtypeStruct((1, model), F32),
        ],
        compiler_params=pltpu.CompilerParams(vmem_limit_bytes=VMEM),
        cost_estimate=pl.CostEstimate(
            flops=2 * total * columns * model,
            transcendentals=total,
            bytes_accessed=6 * total * model,
        ),
        name="input_terms",
    )(own, grad_packed, weights, x_all, gain, grad_middle)


def feed_forward(normed, cot, weights, chunk):
    total, model = normed.shape
    tile = 512
    part = 256 if chunk % 256 == 0 else 128

    def feed_step(normed_ref, cot_ref, gate_ref, up_ref, down_ref, hidden_ref, grads_ref):
        for left in range(0, chunk, part):
            here = slice(left, left + part)
            gate = product(normed_ref[...], gate_ref[:, here])
            upward = product(normed_ref[...], up_ref[:, here])
            grad_hidden = product(cot_ref[...], down_ref[:, here])
            sigma = jax.nn.sigmoid(gate)
            active = gate * sigma
            hidden_ref[:, here] = (active * upward).astype(BF16)
            grads_ref[:, here] = (
                grad_hidden * upward * (sigma + active * (1.0 - sigma))
            ).astype(BF16)
            grads_ref[:, chunk + left : chunk + left + part] = (grad_hidden * active).astype(BF16)

    rows = pl.BlockSpec((tile, model), lambda i: (i, 0))

    def weight(part):
        return pl.BlockSpec((model, chunk), lambda i: (0, part), pipeline_mode=pl.Buffered(1))

    return pl.pallas_call(
        feed_step,
        grid=(total // tile,),
        in_specs=[rows, rows, weight(0), weight(1), weight(2)],
        out_specs=[
            pl.BlockSpec((tile, chunk), lambda i: (i, 0)),
            pl.BlockSpec((tile, 2 * chunk), lambda i: (i, 0)),
        ],
        out_shape=[
            jax.ShapeDtypeStruct((total, chunk), BF16),
            jax.ShapeDtypeStruct((total, 2 * chunk), BF16),
        ],
        compiler_params=pltpu.CompilerParams(vmem_limit_bytes=VMEM),
        cost_estimate=pl.CostEstimate(
            flops=6 * total * chunk * model,
            transcendentals=total * chunk,
            bytes_accessed=4 * total * model + 6 * chunk * (model + total),
        ),
        name="feed_forward",
    )(normed, cot, weights, weights, weights)


def columns_back(left, weights, place, base=None, own=None, middle=None):
    total, inner = left.shape
    model = weights.shape[0]
    tile, part = 512, 512

    def columns_step(own_ref, left_ref, right_ref, *refs):
        out_ref = refs[-1]
        for start in range(0, model, part):
            here = slice(start, start + part)
            value = right_trans(left_ref[...], right_ref[here, :])
            if base is not None:
                value = value + refs[0][:, here].astype(F32)
            out_ref[:, here] = value.astype(BF16)
        if middle is not None:
            middle_ref = refs[-2]
            size = middle_ref.shape[0]
            inside = own_ref[0] * size - pl.program_id(0) * tile

            @pl.when((inside >= 0) & (inside < tile))
            def _():
                rows = pl.ds(pl.multiple_of(inside, size), size)
                out_ref[rows, :] = (out_ref[rows, :].astype(F32) + middle_ref[...]).astype(BF16)

    in_specs = [
        pl.BlockSpec((tile, inner), lambda i, own: (i, 0)),
        pl.BlockSpec((model, inner), lambda i, own: (0, place), pipeline_mode=pl.Buffered(1)),
    ]
    operands = [own, left, weights]
    if base is not None:
        in_specs.append(pl.BlockSpec((tile, model), lambda i, own: (i, 0)))
        operands.append(base)
    if middle is not None:
        in_specs.append(pl.BlockSpec(middle.shape, lambda i, own: (0, 0)))
        operands.append(middle)
    return pl.pallas_call(
        columns_step,
        grid_spec=pltpu.PrefetchScalarGridSpec(
            num_scalar_prefetch=1,
            grid=(total // tile,),
            in_specs=in_specs,
            out_specs=pl.BlockSpec((tile, model), lambda i, own: (i, 0)),
        ),
        out_shape=jax.ShapeDtypeStruct((total, model), BF16),
        compiler_params=pltpu.CompilerParams(vmem_limit_bytes=VMEM),
        cost_estimate=pl.CostEstimate(
            flops=2 * total * model * inner,
            transcendentals=0,
            bytes_accessed=2 * total * model + 2 * (total + model) * inner,
        ),
        name="columns_back",
    )(*operands)


def program(
    tok_size,
    tokens, gain_attn, w_query, w_key, w_value, w_out, gain_ffn, w_gate, w_up, w_down, cotangent
):
    token = lax.axis_index("tok")
    feat = lax.axis_index("feat")
    member = token % 2
    rows, wide = tokens.shape
    model = 4 * wide
    quarter = rows // 4
    groups = [list(range(i, tok_size, 2)) for i in range(2)]
    pair_width = 2 * HD

    def swap(value):
        return lax.ppermute(value, "tok", [(i, i ^ 1) for i in range(tok_size)])

    def x_swap(value):
        return lax.ppermute(value, "feat", [(i, i ^ 2) for i in range(4)])

    def core_swap(value):
        return lax.ppermute(value, "feat", [(i, i ^ 1) for i in range(4)])

    def ring_gather(shard):
        return lax.all_gather(shard, "tok", axis=0, tiled=True, axis_index_groups=groups)

    def ring_scatter(terms):
        return lax.psum_scatter(
            terms, "tok", scatter_dimension=0, tiled=True, axis_index_groups=groups
        )

    def other_half(total):
        size = total.shape[0] // 2
        return swap(lax.dynamic_slice_in_dim(total, (1 - member) * size, size, 0))

    heads_wide = w_query.shape[1] // 2
    chunk = w_gate.shape[1] // 2 // CHUNKS
    attention_pieces = [
        (part, left, pair_width, 3 * left + part * pair_width)
        for left in range(0, heads_wide, pair_width)
        for part in range(3)
    ]
    attention_pieces.append((3, 0, heads_wide, 3 * heads_wide))
    (attention_start,) = swap_and_gather(0, (w_query, w_key, w_value, w_out.T), attention_pieces)
    feed = (w_gate, w_up, w_down.T)
    tokens_after, attention_start = lax.optimization_barrier((tokens, attention_start))
    attention_weights = ring_gather(attention_start)
    feed_weights = []
    wholes = []
    for c, shard in enumerate((tokens_after, cotangent)):
        if c:
            shard, wholes[0] = lax.optimization_barrier((shard, wholes[0]))
        pieces = [(part, c * chunk, chunk, part * chunk) for part in range(3)]
        start, whole = swap_and_gather(1 + c, feed, pieces, shard)
        wholes.append(whole)
        feed_weights.append(ring_gather(start))
    x_all, cot_rows = wholes
    qkv = attention_weights[:, : 3 * heads_wide]
    out_proj = attention_weights[:, 3 * heads_wide :]

    gains = jnp.stack([gain_attn, gain_ffn])
    gains = jnp.stack([gains, core_swap(gains)])
    gains = jnp.concatenate([gains, x_swap(gains)])
    gains = jnp.concatenate(
        [lax.dynamic_index_in_dim(gains, feat ^ j, 0, keepdims=False) for j in range(4)], axis=1
    )
    gain_one, gain_two = gains[:1], gains[1:]

    x_wide = x_all.astype(F32)
    factor_one = lax.rsqrt(jnp.mean(x_wide * x_wide, axis=1, keepdims=True) + EPSILON)
    normed = (x_wide * factor_one * gain_one).astype(BF16)
    packed = product(normed, qkv).astype(BF16)
    attended, log_sums = attend(packed)
    normed_two, middle, factor_two = middle_norm(
        3, right_trans(attended, out_proj).astype(BF16), x_all, gain_two
    )

    own = (member * 4 + feat).astype(jnp.int32).reshape(1)
    feed_sums = []
    grad_normed_two = out_rows = None
    for c in range(CHUNKS):
        if c:
            feed_weights[c], feed_terms, grad_normed_two, out_rows = lax.optimization_barrier(
                (feed_weights[c], feed_terms, grad_normed_two, out_rows)
            )
            feed_sums.append(ring_scatter(feed_terms))
        hidden, grad_both = feed_forward(normed_two, cot_rows, feed_weights[c], chunk)
        grad_normed_two = columns_back(grad_both, feed_weights[c], 0, grad_normed_two, own)
        feed_terms = jnp.concatenate(
            [
                left_trans(normed_two, grad_both).astype(BF16),
                left_trans(cot_rows, hidden).astype(BF16),
            ],
            axis=1,
        )
        if c + 1 < CHUNKS:
            out_rows = columns_back(hidden, feed_weights[c], 2, out_rows, own)
    grad_normed_two, feed_terms = lax.optimization_barrier((grad_normed_two, feed_terms))
    feed_sums.append(ring_scatter(feed_terms))
    grad_mid_rows, grad_middle, gain_ffn_part = middle_back(
        4, grad_normed_two, cot_rows, middle, factor_two, gain_two
    )

    grad_mid_rows, feed_sums[0] = lax.optimization_barrier((grad_mid_rows, feed_sums[0]))
    grad_attended = product(grad_mid_rows, out_proj).astype(BF16)
    grad_packed = attend_back(packed, attended, grad_attended, log_sums)
    first_other = other_half(feed_sums[0])
    grad_packed, first_other = lax.optimization_barrier((grad_packed, first_other))
    attention_terms = jnp.concatenate(
        [
            left_trans(normed, grad_packed).astype(BF16),
            left_trans(grad_mid_rows, attended).astype(BF16),
        ],
        axis=1,
    )
    attention_terms, grad_packed = lax.optimization_barrier((attention_terms, grad_packed))
    attention_sum = ring_scatter(attention_terms)
    terms, gain_attn_part = input_terms(grad_packed, attention_weights, x_all, gain_one, grad_middle, own)
    hidden, terms = lax.optimization_barrier((hidden, terms))
    out_rows = columns_back(hidden, feed_weights[-1], 2, out_rows, own, middle)
    out_rows, feed_sums[1] = lax.optimization_barrier((out_rows, feed_sums[1]))
    outcome, input_grad, gain_grads = scatter_blocks(
        5, tok_size // 2, jnp.concatenate([gain_attn_part, gain_ffn_part]), out_rows, terms
    )
    outcome, attention_sum = lax.optimization_barrier((outcome, attention_sum))

    feed_plan = [
        [(c, part * chunk, chunk, c * chunk) for c in range(CHUNKS)] for part in range(3)
    ]
    gate_grad, up_grad, down_grad = assemble(
        feed_plan, 2, feed_sums, [first_other, other_half(feed_sums[1])]
    )
    attention_plan = [
        [
            (0, 3 * left + part * pair_width, pair_width, left)
            for left in range(0, heads_wide, pair_width)
        ]
        for part in range(3)
    ]
    attention_plan.append([(0, 3 * heads_wide, heads_wide, 0)])
    part_grads = assemble(attention_plan, 3, [attention_sum], [other_half(attention_sum)])
    return (
        outcome,
        input_grad,
        gain_grads[0],
        gain_grads[1],
        *part_grads,
        gate_grad,
        up_grad,
        down_grad,
    )


def solution(mesh):
    in_specs = (
        P("tok", "feat"),
        P("feat"),
        P("tok", "feat"),
        P("tok", "feat"),
        P("tok", "feat"),
        P("feat", "tok"),
        P("feat"),
        P("tok", "feat"),
        P("tok", "feat"),
        P("feat", "tok"),
        P("tok", "feat"),
    )
    out_specs = (
        P("tok", "feat"),
        P("tok", "feat"),
        P("feat"),
        P("feat"),
        P("tok", "feat"),
        P("tok", "feat"),
        P("tok", "feat"),
        P("feat", "tok"),
        P("tok", "feat"),
        P("tok", "feat"),
        P("feat", "tok"),
    )

    def on_device(*arrays):
        return program(mesh.shape["tok"], *arrays)

    return jax.shard_map(
        on_device, mesh=mesh, in_specs=in_specs, out_specs=out_specs, check_vma=False
    )
```

```python
import jax
import jax.numpy as jnp
from jax import lax
from jax.experimental import pallas as pl
from jax.experimental.pallas import tpu as pltpu
from jax.sharding import PartitionSpec as P

HD = 64
LEN = 1024
EPSILON = 1e-05
BF16 = jnp.bfloat16
F32 = jnp.float32
MESH = pl.DeviceIdType.MESH
HBM = pltpu.MemorySpace.HBM
VMEM = 48 << 20
FORWARD_BLOCK = 512
BACK_BLOCK = 256
WHOLE_VMEM = 62 << 20
CHUNKS = (3, 1)


def left_trans(left, right):
    return lax.dot_general(
        left, right, (((0,), (0,)), ((), ())), preferred_element_type=F32
    )


def right_trans(left, right):
    return lax.dot_general(
        left, right, (((1,), (1,)), ((), ())), preferred_element_type=F32
    )


def product(left, right):
    return jnp.dot(left, right, preferred_element_type=F32)


def causal_tile(scores):
    size = scores.shape[0]
    key = lax.broadcasted_iota(jnp.int32, scores.shape, 0)
    query = lax.broadcasted_iota(jnp.int32, scores.shape, 1)
    return jnp.where(key <= query, scores, -1e30)


def head_parts(packed_ref, head, width):
    columns = [slice(part * width + head * HD, part * width + (head + 1) * HD) for part in range(3)]
    query, key, value = [packed_ref[:, part] for part in columns]
    return query * HD ** (-0.5), key, value


def attend_kernel(packed_ref, out_ref, lse_ref):
    width = out_ref.shape[1]
    for head in range(width // HD):
        query, key, value = head_parts(packed_ref, head, width)
        query = query.astype(BF16)
        value_t = value.T
        for top in range(0, LEN, FORWARD_BLOCK):
            keys = top + FORWARD_BLOCK
            scores = right_trans(key[:keys], query[top:keys])
            last = causal_tile(scores[top:])
            scores = jnp.concatenate([scores[:top], last]) if top else last
            highest = jnp.max(scores, axis=0, keepdims=True)
            exponent = jnp.exp(scores - highest)
            total = jnp.sum(exponent, axis=0, keepdims=True)
            mixed = product(value_t[:, :keys], exponent.astype(BF16)) / total
            out_ref[top:keys, head * HD : (head + 1) * HD] = mixed.T.astype(BF16)
            lse_ref[0, 0, head : head + 1, top:keys] = highest + jnp.log(total)


def attend_back_kernel(packed_ref, out_ref, grad_ref, lse_ref, grads_ref, key_acc, value_acc):
    width = out_ref.shape[1]
    for head in range(width // HD):
        lanes = slice(head * HD, (head + 1) * HD)
        query, key, value = head_parts(packed_ref, head, width)
        query = query.astype(BF16)
        key_t = key.T
        grad = grad_ref[:, lanes]
        inner = (out_ref[:, lanes].astype(F32) * grad.astype(F32)).T
        inner = jnp.sum(inner, axis=0, keepdims=True)
        for top in reversed(range(0, LEN, BACK_BLOCK)):
            keys = top + BACK_BLOCK
            scores = right_trans(key[:keys], query[top:keys])
            last = causal_tile(scores[top:])
            scores = jnp.concatenate([scores[:top], last]) if top else last
            probs = jnp.exp(scores - lse_ref[0, 0, head : head + 1, top:keys])
            grad_probs = right_trans(value[:keys], grad[top:keys])
            grad_scores = (probs * (grad_probs - inner[:, top:keys])).astype(BF16)
            value_term = product(probs.astype(BF16), grad[top:keys])
            key_term = product(grad_scores, query[top:keys])
            if keys == LEN:
                value_acc[...] = value_term
                key_acc[...] = key_term
            else:
                value_acc[:keys] += value_term
                key_acc[:keys] += key_term
            grad_query = product(key_t[:, :keys], grad_scores) * HD ** (-0.5)
            grads_ref[top:keys, lanes] = grad_query.T.astype(BF16)
        grads_ref[:, width + head * HD : width + (head + 1) * HD] = key_acc[...].astype(BF16)
        grads_ref[:, 2 * width + head * HD : 2 * width + (head + 1) * HD] = value_acc[...].astype(
            BF16
        )


def attend(packed):
    rows, columns = packed.shape
    width = 2 * HD
    sequences, pairs = rows // LEN, columns // (3 * width)
    return pl.pallas_call(
        attend_kernel,
        grid=(sequences, pairs),
        out_shape=(
            jax.ShapeDtypeStruct((rows, pairs * width), BF16),
            jax.ShapeDtypeStruct((sequences, pairs, 2, LEN), F32),
        ),
        in_specs=[pl.BlockSpec((LEN, 3 * width), lambda s, p: (s, p))],
        out_specs=(
            pl.BlockSpec((LEN, width), lambda s, p: (s, p)),
            pl.BlockSpec((1, 1, 2, LEN), lambda s, p: (s, p, 0, 0)),
        ),
        compiler_params=pltpu.CompilerParams(vmem_limit_bytes=VMEM),
        cost_estimate=pl.CostEstimate(
            flops=4 * rows * LEN * pairs * width // 2,
            transcendentals=rows * LEN * pairs,
            bytes_accessed=2 * rows * columns * 2,
        ),
        name="attend",
    )(packed)


def attend_back(packed, attended, grad_attended, lse):
    rows, columns = packed.shape
    width = 2 * HD
    sequences, pairs = rows // LEN, columns // (3 * width)
    narrow = pl.BlockSpec((LEN, width), lambda s, p: (s, p))
    return pl.pallas_call(
        attend_back_kernel,
        grid=(sequences, pairs),
        out_shape=jax.ShapeDtypeStruct((rows, columns), BF16),
        in_specs=[
            pl.BlockSpec((LEN, 3 * width), lambda s, p: (s, p)),
            narrow,
            narrow,
            pl.BlockSpec((1, 1, 2, LEN), lambda s, p: (s, p, 0, 0)),
        ],
        out_specs=pl.BlockSpec((LEN, 3 * width), lambda s, p: (s, p)),
        scratch_shapes=[pltpu.VMEM((LEN, HD), F32)] * 2,
        compiler_params=pltpu.CompilerParams(vmem_limit_bytes=VMEM),
        cost_estimate=pl.CostEstimate(
            flops=10 * rows * LEN * pairs * width // 2,
            transcendentals=rows * LEN * pairs,
            bytes_accessed=3 * rows * columns * 2,
        ),
        name="attend_back",
    )(packed, attended, grad_attended, lse)


SPREAD = (
    (0, 0, "y", None),
    (0, 1, "x", None),
    (0, 0, "x", None),
    (0, 1, "y", None),
    (0, 0, "core", None),
    (0, 1, "core", None),
    (4, 0, "x", 0),
    (2, 1, "y", 1),
    (4, 0, "core", 0),
    (2, 1, "core", 1),
    (2, 0, "core", 2),
    (4, 1, "core", 3),
    (6, 0, "core", 6),
    (6, 1, "core", 7),
)
BIT = {"y": 4, "x": 2, "core": 1}


def neighbours():
    token, feat = lax.axis_index("tok"), lax.axis_index("feat")
    return {
        "y": (token + 1 - 2 * lax.rem(token, 2), feat),
        "x": (token, lax.rem(feat + 2, 4)),
        "core": (token, feat + 1 - 2 * lax.rem(feat, 2)),
    }


def owner(r):
    member, slot = lax.rem(lax.axis_index("tok"), 2), lax.axis_index("feat")
    if r & 4:
        member = 1 - member
    if r & 2:
        slot = lax.rem(slot + 2, 4)
    if r & 1:
        slot = slot + 1 - 2 * lax.rem(slot, 2)
    return member, slot


def greet(others=()):
    barrier = pltpu.get_barrier_semaphore()
    peers = [*neighbours().values(), *others]
    for peer in peers:
        pl.semaphore_signal(barrier, inc=1, device_id=peer, device_id_type=MESH)
    pl.semaphore_wait(barrier, len(peers))


def ring_peer(ring, distance):
    token = lax.axis_index("tok")
    return lax.rem(token + 2 * distance, 2 * ring), lax.axis_index("feat")


class SumAll:
    def __init__(self, ring, ref, steps, arrived, slots, send, recv):
        self.ring, self.ref = ring, ref
        self.steps, self.arrived, self.slots = steps, arrived, slots
        self.send, self.recv = send, recv
        self.place = lax.div(lax.axis_index("tok"), 2)
        self.peers = neighbours()

    @staticmethod
    def scratch(ring, shape):
        return [
            pltpu.VMEM((3, *shape), F32),
            pltpu.VMEM((3, *shape), F32),
            pltpu.VMEM((ring, *shape), F32),
            pltpu.SemaphoreType.DMA((2 + ring,)),
            pltpu.SemaphoreType.DMA((2 + ring,)),
        ]

    def copy(self, k):
        if k < 3:
            source = self.ref if k == 0 else self.steps.at[k - 1]
            target, peer = self.arrived.at[k], self.peers[("core", "x", "y")[k]]
        else:
            source, target = self.steps.at[2], self.slots.at[self.place]
            peer = ring_peer(self.ring, k - 2)
        return pltpu.make_async_remote_copy(
            source, target, self.send.at[k], self.recv.at[k],
            device_id=peer, device_id_type=MESH,
        )

    def start(self):
        self.copy(0).start()

    def step(self, k):
        self.copy(k).wait_recv()
        before = self.ref[...] if k == 0 else self.steps[k - 1]
        self.steps[k] = before + self.arrived[k]
        if k < 2:
            self.copy(k + 1).start()
        else:
            for distance in range(1, self.ring):
                self.copy(2 + distance).start()
            self.slots[self.place] = self.steps[2]

    def finish(self):
        for distance in range(1, self.ring):
            source = lax.rem(self.place + self.ring - distance, self.ring)
            k = 2 + distance
            pltpu.make_async_remote_copy(
                self.slots.at[source], self.slots.at[source], self.send.at[k], self.recv.at[k],
                device_id=ring_peer(self.ring, distance), device_id_type=MESH,
            ).wait_recv()
        for k in range(2 + self.ring):
            self.copy(k).wait_send()
        total = self.slots[0]
        for place in range(1, self.ring):
            total = total + self.slots[place]
        return total


class Spread:
    def __init__(self, own, region, send, recv):
        self.own, self.region, self.send, self.recv = own, region, send, recv
        self.peers = neighbours()

    def copy(self, k):
        r, half, way, _ = SPREAD[k]
        source = self.own(half) if r == 0 else self.region(r, half)
        return pltpu.make_async_remote_copy(
            source, self.region(r, half), self.send.at[k], self.recv.at[k],
            device_id=self.peers[way], device_id_type=MESH,
        )

    def arrival(self, k):
        r, half, way, _ = SPREAD[k]
        place = self.region(r ^ BIT[way], half)
        return pltpu.make_async_remote_copy(
            place, place, self.send.at[k], self.recv.at[k],
            device_id=self.peers[way], device_id_type=MESH,
        )

    def start(self, half):
        for k, (r, which, _, after) in enumerate(SPREAD):
            if after is None and which == half:
                self.copy(k).start()

    def forward(self):
        for first in range(8):
            if first in (4, 5):
                continue
            self.arrival(first).wait_recv()
            for k, (_, _, _, after) in enumerate(SPREAD):
                if after == first:
                    self.copy(k).start()

    def finish(self):
        for k, (_, _, way, _) in enumerate(SPREAD):
            if way == "core":
                self.arrival(k).wait_recv()
        for k in range(len(SPREAD)):
            self.copy(k).wait_send()


SPREAD_SEMS = [pltpu.SemaphoreType.DMA((len(SPREAD),))] * 2


class Collect:
    def __init__(self, part, size, parts, near, from_x, from_y, last_y, last_x, sems):
        self.part, self.size, self.half = part, size, size // 2
        self.parts, self.near = parts, near
        self.from_x, self.from_y, self.last_y, self.last_x = from_x, from_y, last_y, last_x
        self.load, self.send, self.recv = sems
        self.peers = neighbours()

    @staticmethod
    def scratch(size, columns):
        half = size // 2
        return [
            pltpu.VMEM((4, size, columns), BF16),
            pltpu.VMEM((4, size, columns), BF16),
            pltpu.VMEM((2, half, columns), BF16),
            pltpu.VMEM((2, half, columns), BF16),
            pltpu.VMEM((half, columns), BF16),
            pltpu.VMEM((half, columns), BF16),
            pltpu.SemaphoreType.DMA((4,)),
            pltpu.SemaphoreType.DMA((10,)),
            pltpu.SemaphoreType.DMA((10,)),
        ]

    def remote(self, k, source, target, way):
        return pltpu.make_async_remote_copy(
            source, target, self.send.at[k], self.recv.at[k],
            device_id=self.peers[way], device_id_type=MESH,
        )

    def copy(self, k):
        low, high = pl.ds(0, self.half), pl.ds(self.half, self.half)
        if k < 4:
            return self.remote(k, self.part(2 * k + 1), self.near.at[k], "core")
        if k < 6:
            return self.remote(k, self.parts.at[(1, 3)[k - 4], low], self.from_x.at[k - 4], "x")
        if k < 8:
            return self.remote(k, self.parts.at[(2, 3)[k - 6], high], self.from_y.at[k - 6], "y")
        if k == 8:
            return self.remote(k, self.parts.at[2, low], self.last_y, "y")
        return self.remote(k, self.parts.at[1, high], self.last_x, "x")

    def add(self, index, start, count, other):
        step = 32

        def body(i, carry):
            here = pl.ds(pl.multiple_of(start + i * step, step), step)
            there = pl.ds(pl.multiple_of(i * step, step), step)
            total = self.parts[index, here].astype(F32) + other[there].astype(F32)
            self.parts[index, here] = total.astype(BF16)
            return carry

        lax.fori_loop(0, count // step, body, 0)

    def loads(self, k):
        return pltpu.make_async_copy(self.part(2 * k), self.parts.at[k], self.load.at[k])

    def start(self):
        for k in (3, 1, 2, 0):
            self.copy(k).start()
        for k in (3, 1, 2, 0):
            self.loads(k).start()

    def first(self):
        for k, following in ((3, (5, 7)), (1, (4,)), (2, (6,)), (0, ())):
            self.loads(k).wait()
            self.copy(k).wait_recv()
            self.add(k, 0, self.size, self.near.at[k])
            for after in following:
                self.copy(after).start()

    def second(self):
        self.copy(5).wait_recv()
        self.add(2, 0, self.half, self.from_x.at[1])
        self.copy(8).start()
        self.copy(7).wait_recv()
        self.add(1, self.half, self.half, self.from_y.at[1])
        self.copy(9).start()

    def total(self, half, rows):
        first, last = (self.from_x, self.last_y) if half == 0 else (self.from_y, self.last_x)
        own = self.parts[0, pl.ds(pl.multiple_of(half * self.half + rows.start, 32), rows.size)]
        return own.astype(F32) + first[0, rows].astype(F32) + last[rows].astype(F32)

    def ready(self, half):
        for k in ((4, 8) if half == 0 else (6, 9)):
            self.copy(k).wait_recv()

    def finish(self):
        for k in range(10):
            self.copy(k).wait_send()


def loop_rows(count, body):
    def step(i, carry):
        body(pl.ds(pl.multiple_of(i * 32, 32), 32))
        return carry

    lax.fori_loop(0, count // 32, step, 0)


def call(kernel, identity, operands, spaces, outputs, out_spaces, scratch, cost):
    return pl.pallas_call(
        kernel,
        out_shape=outputs,
        in_specs=[pl.BlockSpec(memory_space=space) for space in spaces],
        out_specs=jax.tree.map(lambda space: pl.BlockSpec(memory_space=space), out_spaces),
        scratch_shapes=scratch,
        compiler_params=pltpu.CompilerParams(
            collective_id=identity, has_side_effects=True, vmem_limit_bytes=VMEM
        ),
        cost_estimate=pl.CostEstimate(flops=cost, bytes_accessed=cost // 100, transcendentals=0),
        name=kernel.__name__,
    )(*operands)


class PairSwap:
    def __init__(self, sources, out_ref, pieces, local, send, recv):
        self.sources, self.out, self.pieces = sources, out_ref, pieces
        self.local, self.send, self.recv = local, send, recv
        self.peer = neighbours()["y"]
        self.member = lax.rem(lax.axis_index("tok"), 2)

    def block(self, i, half):
        source, start, width, _ = self.pieces[i]
        ref = self.sources[source]
        offset = half * (ref.shape[1] // 2) + start
        return ref.at[:, pl.ds(pl.multiple_of(offset, 128), width)]

    def place(self, i, member):
        _, _, width, column = self.pieces[i]
        rows = self.out.shape[0] // 2
        return self.out.at[pl.ds(pl.multiple_of(member * rows, rows), rows), pl.ds(column, width)]

    def remote(self, i, source, member):
        return pltpu.make_async_remote_copy(
            source, self.place(i, member), self.send.at[i], self.recv.at[i],
            device_id=self.peer, device_id_type=MESH,
        )

    def own(self, i):
        return pltpu.make_async_copy(
            self.block(i, self.member), self.place(i, self.member), self.local.at[i]
        )

    def away(self, i):
        return self.remote(i, self.block(i, 1 - self.member), self.member)

    def start(self):
        for i in range(len(self.pieces)):
            self.away(i).start()
        for i in range(len(self.pieces)):
            self.own(i).start()

    def finish(self):
        for i in range(len(self.pieces)):
            other = 1 - self.member
            self.remote(i, self.place(i, other), other).wait_recv()
            self.away(i).wait_send()
            self.own(i).wait()


def swap_and_gather(identity, weights, pieces, shard=None):
    count = len(weights)
    size = weights[0].shape[0]
    columns = sum(piece[2] for piece in pieces)
    operands = tuple(weights)
    outputs = [jax.ShapeDtypeStruct((2 * size, columns), weights[0].dtype)]
    scratch = [pltpu.SemaphoreType.DMA((len(pieces),))] * 3
    if shard is not None:
        rows, wide = shard.shape
        half = rows // 2
        operands += (shard,)
        outputs.append(jax.ShapeDtypeStruct((2 * rows, 4 * wide), shard.dtype))
        scratch += [pltpu.SemaphoreType.DMA((2,))] + SPREAD_SEMS

    def swap_gather(*refs):
        sources, refs = refs[:count], refs[count:]
        if shard is not None:
            shard_ref, start_ref, out_ref, *sems = refs
        else:
            start_ref, *sems = refs
        greet()
        pair = PairSwap(sources, start_ref, pieces, *sems[:3])
        pair.start()
        if shard is None:
            pair.finish()
            return

        def own(which):
            return shard_ref.at[pl.ds(which * half, half)]

        def region(r, which):
            member, slot = owner(r)
            return out_ref.at[
                pl.ds(pl.multiple_of(member * rows + which * half, half), half),
                pl.ds(pl.multiple_of(slot * wide, wide), wide),
            ]

        spread = Spread(own, region, *sems[4:])
        spread.start(0)
        spread.start(1)
        copies = [
            pltpu.make_async_copy(own(which), region(0, which), sems[3].at[which])
            for which in range(2)
        ]
        for copy in copies:
            copy.start()
        spread.forward()
        spread.finish()
        pair.finish()
        for copy in copies:
            copy.wait()

    return call(
        swap_gather, identity, operands, (pl.ANY,) * len(operands),
        outputs, [pl.ANY] * len(outputs), scratch,
        15_000_000_000 if shard is None else 50_000_000_000,
    )


def scatter_blocks(identity, ring, vector, *terms):
    rows, wide = terms[0].shape[0] // 2, terms[0].shape[1] // 4
    count = len(terms)

    def scatter_outputs(vector_ref, *refs):
        greet([ring_peer(ring, distance) for distance in range(1, ring)])
        small_ref = refs[2 * count]
        scratch = refs[2 * count + 1 :]
        small = SumAll(ring, vector_ref, *scratch[:5])
        collects = []
        for i in range(count):

            def part(r, terms_ref=refs[i]):
                member, slot = owner(r)
                return terms_ref.at[
                    pl.ds(pl.multiple_of(member * rows, rows), rows),
                    pl.ds(pl.multiple_of(slot * wide, wide), wide),
                ]

            mine = scratch[5 + 9 * i : 5 + 9 * (i + 1)]
            collects.append(Collect(part, rows, *mine[:6], mine[6:]))
        small.start()
        for collect in collects:
            collect.start()
        small.step(0)
        for collect in collects:
            collect.first()
        small.step(1)
        for collect in collects:
            collect.second()
        small.step(2)
        for collect, out_ref in zip(collects, refs[count:]):
            for which in range(2):
                collect.ready(which)

                def body(here, collect=collect, out_ref=out_ref):
                    there = pl.ds(pl.multiple_of(which * (rows // 2) + here.start, 32), 32)
                    out_ref[there] = collect.total(which, here).astype(BF16)

                loop_rows(rows // 2, body)
        for collect in collects:
            collect.finish()
        scratch[1][0] = small.finish()
        start = pl.multiple_of(lax.axis_index("feat") * wide, wide)
        small_ref[...] = scratch[1][0, :, pl.ds(start, wide)]

    return call(
        scatter_outputs, identity, (vector, *terms), (pltpu.VMEM,) + (pl.ANY,) * count,
        [jax.ShapeDtypeStruct((rows, wide), BF16)] * count
        + [jax.ShapeDtypeStruct((vector.shape[0], wide), F32)],
        [pltpu.VMEM] * (count + 1),
        SumAll.scratch(ring, vector.shape) + Collect.scratch(rows, wide) * count,
        30_000_000_000 * count,
    )


def row_parts(terms_ref, quarter):
    def part(r):
        member, slot = owner(r)
        return terms_ref.at[pl.ds(pl.multiple_of((member * 4 + slot) * quarter, quarter), quarter)]

    return part


def row_region(out_ref, quarter):
    half = quarter // 2

    def region(r, which):
        member, slot = owner(r)
        start = (member * 4 + slot) * quarter + which * half
        return out_ref.at[pl.ds(pl.multiple_of(start, half), half)]

    return region


def middle_norm(identity, terms, x_all, gain):
    total, model = terms.shape
    quarter = total // 8
    half = quarter // 2

    def middle_step(
        terms_ref, x_ref, gain_ref, out_ref, middle_ref, factor_ref,
        x_own, normed, local, send, recv, *scratch
    ):
        greet()
        x_copy = pltpu.make_async_copy(row_parts(x_ref, quarter)(0), x_own, local.at[0])
        x_copy.start()
        collect = Collect(row_parts(terms_ref, quarter), quarter, *scratch[:6], scratch[6:])
        region = row_region(out_ref, quarter)
        spread = Spread(
            lambda which: normed.at[pl.ds(which * half, half)], region, send, recv
        )
        collect.start()
        collect.first()
        collect.second()
        x_copy.wait()
        copies = []
        for which in range(2):
            collect.ready(which)

            def body(here):
                there = pl.ds(pl.multiple_of(which * half + here.start, 32), 32)
                middle = collect.total(which, here) + x_own[there].astype(F32)
                mean = jnp.mean(middle * middle, axis=1, keepdims=True)
                factor = lax.rsqrt(mean + EPSILON)
                middle_ref[there] = middle
                factor_ref[there] = jnp.broadcast_to(factor, (32, 128))
                normed[there] = (middle * factor * gain_ref[...]).astype(BF16)

            loop_rows(half, body)
            spread.start(which)
            copy = pltpu.make_async_copy(
                normed.at[pl.ds(which * half, half)], region(0, which), local.at[1 + which]
            )
            copy.start()
            copies.append(copy)
        spread.forward()
        spread.finish()
        collect.finish()
        for copy in copies:
            copy.wait()

    return call(
        middle_step, identity, (terms, x_all, gain), (pl.ANY, pl.ANY, pltpu.VMEM),
        (
            jax.ShapeDtypeStruct((total, model), BF16),
            jax.ShapeDtypeStruct((quarter, model), F32),
            jax.ShapeDtypeStruct((quarter, 128), F32),
        ),
        (pl.ANY, pltpu.VMEM, pltpu.VMEM),
        [
            pltpu.VMEM((quarter, model), BF16),
            pltpu.VMEM((quarter, model), BF16),
            pltpu.SemaphoreType.DMA((3,)),
        ]
        + SPREAD_SEMS
        + Collect.scratch(quarter, model),
        70_000_000_000,
    )


def middle_back(identity, terms, cot, middle, factor, gain):
    total, model = terms.shape
    quarter = total // 8
    half = quarter // 2

    def middle_back_step(
        terms_ref, cot_ref, middle_ref, factor_ref, gain_ref, out_ref, grad_ref, gain_grad_ref,
        cot_own, rounded, local, send, recv, *scratch
    ):
        greet()
        cot_copy = pltpu.make_async_copy(row_parts(cot_ref, quarter)(0), cot_own, local.at[0])
        cot_copy.start()
        collect = Collect(row_parts(terms_ref, quarter), quarter, *scratch[:6], scratch[6:])
        region = row_region(out_ref, quarter)
        spread = Spread(
            lambda which: rounded.at[pl.ds(which * half, half)], region, send, recv
        )
        collect.start()
        collect.first()
        collect.second()
        cot_copy.wait()
        gain_grad_ref[...] = jnp.zeros_like(gain_grad_ref)
        copies = []
        for which in range(2):
            collect.ready(which)

            def body(here):
                there = pl.ds(pl.multiple_of(which * half + here.start, 32), 32)
                grad_normed = collect.total(which, here)
                values = middle_ref[there]
                factor = factor_ref[there][:, :1]
                weighted = gain_ref[...] * grad_normed
                inner = jnp.mean(weighted * values, axis=1, keepdims=True)
                grad = (
                    cot_own[there].astype(F32)
                    + factor * weighted
                    - values * (factor * factor * factor * inner)
                )
                grad_ref[there] = grad
                rounded[there] = grad.astype(BF16)
                gain_grad_ref[...] += jnp.sum(grad_normed * values * factor, axis=0, keepdims=True)

            loop_rows(half, body)
            spread.start(which)
            copy = pltpu.make_async_copy(
                rounded.at[pl.ds(which * half, half)], region(0, which), local.at[1 + which]
            )
            copy.start()
            copies.append(copy)
        spread.forward()
        spread.finish()
        collect.finish()
        for copy in copies:
            copy.wait()

    return call(
        middle_back_step, identity, (terms, cot, middle, factor, gain),
        (pl.ANY, pl.ANY, pltpu.VMEM, pltpu.VMEM, pltpu.VMEM),
        (
            jax.ShapeDtypeStruct((total, model), BF16),
            jax.ShapeDtypeStruct((quarter, model), F32),
            jax.ShapeDtypeStruct((1, model), F32),
        ),
        (pl.ANY, pltpu.VMEM, pltpu.VMEM),
        [
            pltpu.VMEM((quarter, model), BF16),
            pltpu.VMEM((quarter, model), BF16),
            pltpu.SemaphoreType.DMA((3,)),
        ]
        + SPREAD_SEMS
        + Collect.scratch(quarter, model),
        70_000_000_000,
    )


def assemble(plan, flipped_out, totals, others, passed=()):
    count = len(totals)
    size = others[0].shape[0]
    shapes = []
    for index, pieces in enumerate(plan):
        wide = 2 * sum(piece[2] for piece in pieces)
        shapes.append((size, wide) if index < flipped_out else (wide, size))

    def assemble_grads(*refs):
        member = lax.rem(lax.axis_index("tok"), 2)
        outs = refs[2 * count + len(passed) :]
        for i in range(len(passed)):
            outs[len(plan) + i][...] = refs[2 * count + i][...]
        for index, pieces in enumerate(plan):
            half = sum(piece[2] for piece in pieces)
            for source, column, width, target in pieces:
                own_rows = pl.ds(pl.multiple_of(member * size, size), size)
                own = refs[source][own_rows, column : column + width]
                other = refs[count + source][:, column : column + width]
                for which, block in ((member, own), (1 - member, other)):
                    start = pl.multiple_of(which * half + target, 128)
                    if index < flipped_out:
                        outs[index][:, pl.ds(start, width)] = block.astype(F32)
                    else:
                        outs[index][pl.ds(start, width), :] = block.astype(F32).T

    return pl.pallas_call(
        assemble_grads,
        out_shape=[jax.ShapeDtypeStruct(shape, F32) for shape in shapes]
        + [jax.ShapeDtypeStruct(array.shape, array.dtype) for array in passed],
        in_specs=[pl.BlockSpec(memory_space=pltpu.VMEM)] * (2 * count + len(passed)),
        out_specs=[pl.BlockSpec(memory_space=pltpu.VMEM)] * (len(plan) + len(passed)),
        compiler_params=pltpu.CompilerParams(vmem_limit_bytes=VMEM),
        cost_estimate=pl.CostEstimate(
            flops=0, transcendentals=0, bytes_accessed=8 * size * 2 * sum(t.shape[1] for t in totals)
        ),
        name="assemble_grads",
    )(*totals, *others, *passed)


def input_terms(grad_packed, weights, x_all, gain, grad_middle, own):
    total, columns = grad_packed.shape
    model = x_all.shape[1]
    tile = grad_middle.shape[0]

    def input_terms_step(own_ref, grad_ref, qkv_ref, x_ref, gain_ref, middle_ref, out_ref, gain_grad_ref):
        step = pl.program_id(0)
        grad_normed = right_trans(grad_ref[...], qkv_ref[...])
        values = x_ref[...].astype(F32)
        factor = lax.rsqrt(jnp.mean(values * values, axis=1, keepdims=True) + EPSILON)
        weighted = grad_normed * gain_ref[...]
        inner = jnp.mean(weighted * values, axis=1, keepdims=True)
        terms = factor * weighted - values * (factor * factor * factor * inner)

        @pl.when(step == own_ref[0])
        def _():
            out_ref[...] = (terms + middle_ref[...]).astype(BF16)

        @pl.when(step != own_ref[0])
        def _():
            out_ref[...] = terms.astype(BF16)

        @pl.when(step == 0)
        def _():
            gain_grad_ref[...] = jnp.zeros_like(gain_grad_ref)

        gain_grad_ref[...] += jnp.sum(grad_normed * values * factor, axis=0, keepdims=True)

    return pl.pallas_call(
        input_terms_step,
        grid_spec=pltpu.PrefetchScalarGridSpec(
            num_scalar_prefetch=1,
            grid=(total // tile,),
            in_specs=[
                pl.BlockSpec((tile, columns), lambda i, own: (i, 0)),
                pl.BlockSpec((model, columns), lambda i, own: (0, 0)),
                pl.BlockSpec((tile, model), lambda i, own: (i, 0)),
                pl.BlockSpec((1, model), lambda i, own: (0, 0)),
                pl.BlockSpec((tile, model), lambda i, own: (0, 0)),
            ],
            out_specs=[
                pl.BlockSpec((tile, model), lambda i, own: (i, 0)),
                pl.BlockSpec((1, model), lambda i, own: (0, 0)),
            ],
        ),
        out_shape=[
            jax.ShapeDtypeStruct((total, model), BF16),
            jax.ShapeDtypeStruct((1, model), F32),
        ],
        compiler_params=pltpu.CompilerParams(vmem_limit_bytes=VMEM),
        cost_estimate=pl.CostEstimate(
            flops=2 * total * columns * model,
            transcendentals=total,
            bytes_accessed=6 * total * model,
        ),
        name="input_terms",
    )(own, grad_packed, weights, x_all, gain, grad_middle)


def feed_forward(normed, cot, weights, chunk):
    total, model = normed.shape
    tile = 512
    part = 256 if chunk % 256 == 0 else 128

    def feed_step(normed_ref, cot_ref, gate_ref, up_ref, down_ref, hidden_ref, grads_ref):
        for left in range(0, chunk, part):
            here = slice(left, left + part)
            gate = product(normed_ref[...], gate_ref[:, here])
            upward = product(normed_ref[...], up_ref[:, here])
            grad_hidden = product(cot_ref[...], down_ref[:, here])
            sigma = jax.nn.sigmoid(gate)
            active = gate * sigma
            hidden_ref[:, here] = (active * upward).astype(BF16)
            grads_ref[:, here] = (
                grad_hidden * upward * (sigma + active * (1.0 - sigma))
            ).astype(BF16)
            grads_ref[:, chunk + left : chunk + left + part] = (grad_hidden * active).astype(BF16)

    rows = pl.BlockSpec((tile, model), lambda i: (i, 0))

    def weight(part):
        return pl.BlockSpec((model, chunk), lambda i: (0, part), pipeline_mode=pl.Buffered(1))

    return pl.pallas_call(
        feed_step,
        grid=(total // tile,),
        in_specs=[rows, rows, weight(0), weight(1), weight(2)],
        out_specs=[
            pl.BlockSpec((tile, chunk), lambda i: (i, 0)),
            pl.BlockSpec((tile, 2 * chunk), lambda i: (i, 0)),
        ],
        out_shape=[
            jax.ShapeDtypeStruct((total, chunk), BF16),
            jax.ShapeDtypeStruct((total, 2 * chunk), BF16),
        ],
        compiler_params=pltpu.CompilerParams(vmem_limit_bytes=VMEM),
        cost_estimate=pl.CostEstimate(
            flops=6 * total * chunk * model,
            transcendentals=total * chunk,
            bytes_accessed=4 * total * model + 6 * chunk * (model + total),
        ),
        name="feed_forward",
    )(normed, cot, weights, weights, weights)


def columns_back(left, weights, place, base=None, own=None, middle=None):
    total, inner = left.shape
    model = weights.shape[0]
    tile, part = 512, 512

    def columns_step(own_ref, left_ref, right_ref, *refs):
        out_ref = refs[-1]
        for start in range(0, model, part):
            here = slice(start, start + part)
            value = right_trans(left_ref[...], right_ref[here, :])
            if base is not None:
                value = value + refs[0][:, here].astype(F32)
            out_ref[:, here] = value.astype(BF16)
        if middle is not None:
            middle_ref = refs[-2]
            size = middle_ref.shape[0]
            inside = own_ref[0] * size - pl.program_id(0) * tile

            @pl.when((inside >= 0) & (inside < tile))
            def _():
                rows = pl.ds(pl.multiple_of(inside, size), size)
                out_ref[rows, :] = (out_ref[rows, :].astype(F32) + middle_ref[...]).astype(BF16)

    in_specs = [
        pl.BlockSpec((tile, inner), lambda i, own: (i, 0)),
        pl.BlockSpec((model, inner), lambda i, own: (0, place), pipeline_mode=pl.Buffered(1)),
    ]
    operands = [own, left, weights]
    if base is not None:
        in_specs.append(pl.BlockSpec((tile, model), lambda i, own: (i, 0)))
        operands.append(base)
    if middle is not None:
        in_specs.append(pl.BlockSpec(middle.shape, lambda i, own: (0, 0)))
        operands.append(middle)
    return pl.pallas_call(
        columns_step,
        grid_spec=pltpu.PrefetchScalarGridSpec(
            num_scalar_prefetch=1,
            grid=(total // tile,),
            in_specs=in_specs,
            out_specs=pl.BlockSpec((tile, model), lambda i, own: (i, 0)),
        ),
        out_shape=jax.ShapeDtypeStruct((total, model), BF16),
        compiler_params=pltpu.CompilerParams(vmem_limit_bytes=VMEM),
        cost_estimate=pl.CostEstimate(
            flops=2 * total * model * inner,
            transcendentals=0,
            bytes_accessed=2 * total * model + 2 * (total + model) * inner,
        ),
        name="columns_back",
    )(*operands)


def program(
    tok_size,
    tokens, gain_attn, w_query, w_key, w_value, w_out, gain_ffn, w_gate, w_up, w_down, cotangent
):
    token = lax.axis_index("tok")
    feat = lax.axis_index("feat")
    member = token % 2
    rows, wide = tokens.shape
    model = 4 * wide
    quarter = rows // 4
    groups = [list(range(i, tok_size, 2)) for i in range(2)]
    pair_width = 2 * HD

    def swap(value):
        return lax.ppermute(value, "tok", [(i, i ^ 1) for i in range(tok_size)])

    def x_swap(value):
        return lax.ppermute(value, "feat", [(i, i ^ 2) for i in range(4)])

    def core_swap(value):
        return lax.ppermute(value, "feat", [(i, i ^ 1) for i in range(4)])

    def ring_gather(shard):
        return lax.all_gather(shard, "tok", axis=0, tiled=True, axis_index_groups=groups)

    def ring_scatter(terms):
        return lax.psum_scatter(
            terms, "tok", scatter_dimension=0, tiled=True, axis_index_groups=groups
        )

    def other_half(total):
        size = total.shape[0] // 2
        return swap(lax.dynamic_slice_in_dim(total, (1 - member) * size, size, 0))

    heads_wide = w_query.shape[1] // 2
    hidden_wide = w_gate.shape[1] // 2
    chunks = [hidden_wide * part // sum(CHUNKS) for part in CHUNKS]
    lefts = [sum(chunks[:c]) for c in range(len(chunks))]
    attention_pieces = [
        (part, left, pair_width, 3 * left + part * pair_width)
        for left in range(0, heads_wide, pair_width)
        for part in range(3)
    ]
    attention_pieces.append((3, 0, heads_wide, 3 * heads_wide))
    (attention_start,) = swap_and_gather(0, (w_query, w_key, w_value, w_out.T), attention_pieces)
    feed = (w_gate, w_up, w_down.T)
    tokens_after, attention_start = lax.optimization_barrier((tokens, attention_start))
    attention_weights = ring_gather(attention_start)
    feed_weights = []
    wholes = []
    for c, shard in enumerate((tokens_after, cotangent)):
        if c:
            shard, wholes[0] = lax.optimization_barrier((shard, wholes[0]))
        pieces = [(part, lefts[c], chunks[c], part * chunks[c]) for part in range(3)]
        start, whole = swap_and_gather(1 + c, feed, pieces, shard)
        wholes.append(whole)
        feed_weights.append(ring_gather(start))
    x_all, cot_rows = wholes
    qkv = attention_weights[:, : 3 * heads_wide]
    out_proj = attention_weights[:, 3 * heads_wide :]

    gains = jnp.stack([gain_attn, gain_ffn])
    gains = jnp.stack([gains, core_swap(gains)])
    gains = jnp.concatenate([gains, x_swap(gains)])
    gains = jnp.concatenate(
        [lax.dynamic_index_in_dim(gains, feat ^ j, 0, keepdims=False) for j in range(4)], axis=1
    )
    gain_one, gain_two = gains[:1], gains[1:]

    x_wide = x_all.astype(F32)
    factor_one = lax.rsqrt(jnp.mean(x_wide * x_wide, axis=1, keepdims=True) + EPSILON)
    normed = (x_wide * factor_one * gain_one).astype(BF16)
    packed = product(normed, qkv).astype(BF16)
    attended, log_sums = attend(packed)
    normed_two, middle, factor_two = middle_norm(
        3, right_trans(attended, out_proj).astype(BF16), x_all, gain_two
    )

    own = (member * 4 + feat).astype(jnp.int32).reshape(1)
    feed_sums = []
    grad_normed_two = out_rows = None

    def terms_of(grad_both, hidden):
        return jnp.concatenate(
            [
                left_trans(normed_two, grad_both).astype(BF16),
                left_trans(cot_rows, hidden).astype(BF16),
            ],
            axis=1,
        )

    hiddens = []
    for c in range(len(chunks)):
        if c:
            feed_weights[c], grad_normed_two = lax.optimization_barrier(
                (feed_weights[c], grad_normed_two)
            )
        hidden, grad_both = feed_forward(normed_two, cot_rows, feed_weights[c], chunks[c])
        hiddens.append(hidden)
        if c + 1 < len(chunks):
            feed_terms = terms_of(grad_both, hidden)
            feed_terms, grad_both = lax.optimization_barrier((feed_terms, grad_both))
            feed_sums.append(ring_scatter(feed_terms))
        grad_normed_two = columns_back(grad_both, feed_weights[c], 0, grad_normed_two, own)
    grad_mid_rows, grad_middle, gain_ffn_part = middle_back(
        4, grad_normed_two, cot_rows, middle, factor_two, gain_two
    )

    hidden, grad_both, grad_mid_rows = lax.optimization_barrier((hidden, grad_both, grad_mid_rows))
    feed_terms = terms_of(grad_both, hidden)
    grad_mid_rows, feed_terms = lax.optimization_barrier((grad_mid_rows, feed_terms))
    feed_sums.append(ring_scatter(feed_terms))

    grad_attended = product(grad_mid_rows, out_proj).astype(BF16)
    grad_packed = attend_back(packed, attended, grad_attended, log_sums)
    attention_terms = jnp.concatenate(
        [
            left_trans(normed, grad_packed).astype(BF16),
            left_trans(grad_mid_rows, attended).astype(BF16),
        ],
        axis=1,
    )
    attention_terms, grad_packed = lax.optimization_barrier((attention_terms, grad_packed))
    attention_sum = ring_scatter(attention_terms)
    terms, gain_attn_part = input_terms(grad_packed, attention_weights, x_all, gain_one, grad_middle, own)
    hiddens[0], terms, feed_sums[0] = lax.optimization_barrier((hiddens[0], terms, feed_sums[0]))
    for c in range(len(chunks)):
        last = middle if c + 1 == len(chunks) else None
        out_rows = columns_back(hiddens[c], feed_weights[c], 2, out_rows, own, last)
    outcome, input_grad, gain_grads = scatter_blocks(
        5, tok_size // 2, jnp.concatenate([gain_attn_part, gain_ffn_part]), out_rows, terms
    )
    feed_others = [other_half(feed_sums[0])]
    outcome, feed_sums[1] = lax.optimization_barrier((outcome, feed_sums[1]))
    feed_others.append(other_half(feed_sums[1]))
    feed_others[1], attention_sum = lax.optimization_barrier((feed_others[1], attention_sum))
    feed_plan = [
        [(c, part * chunks[c], chunks[c], lefts[c]) for c in range(len(chunks))]
        for part in range(3)
    ]
    gate_grad, up_grad, down_grad, outcome, input_grad = assemble(
        feed_plan, 2, feed_sums, feed_others, (outcome, input_grad)
    )
    attention_plan = [
        [
            (0, 3 * left + part * pair_width, pair_width, left)
            for left in range(0, heads_wide, pair_width)
        ]
        for part in range(3)
    ]
    attention_plan.append([(0, 3 * heads_wide, heads_wide, 0)])
    attention_other = other_half(attention_sum)
    attention_other, gate_grad, up_grad, down_grad, outcome, input_grad = lax.optimization_barrier(
        (attention_other, gate_grad, up_grad, down_grad, outcome, input_grad)
    )
    part_grads = assemble(attention_plan, 3, [attention_sum], [attention_other])
    return (
        outcome,
        input_grad,
        gain_grads[0],
        gain_grads[1],
        *part_grads,
        gate_grad,
        up_grad,
        down_grad,
    )


def solution(mesh):
    in_specs = (
        P("tok", "feat"),
        P("feat"),
        P("tok", "feat"),
        P("tok", "feat"),
        P("tok", "feat"),
        P("feat", "tok"),
        P("feat"),
        P("tok", "feat"),
        P("tok", "feat"),
        P("feat", "tok"),
        P("tok", "feat"),
    )
    out_specs = (
        P("tok", "feat"),
        P("tok", "feat"),
        P("feat"),
        P("feat"),
        P("tok", "feat"),
        P("tok", "feat"),
        P("tok", "feat"),
        P("feat", "tok"),
        P("tok", "feat"),
        P("tok", "feat"),
        P("feat", "tok"),
    )

    def on_device(*arrays):
        return program(mesh.shape["tok"], *arrays)

    return jax.shard_map(
        on_device, mesh=mesh, in_specs=in_specs, out_specs=out_specs, check_vma=False
    )
```

```python
import jax
import jax.numpy as jnp
from jax import lax
from jax.experimental import pallas as pl
from jax.experimental.pallas import tpu as pltpu
from jax.sharding import PartitionSpec as P

HD = 64
LEN = 1024
EPSILON = 1e-05
BF16 = jnp.bfloat16
F32 = jnp.float32
MESH = pl.DeviceIdType.MESH
VMEM = 48 << 20
FORWARD_BLOCK = 512
BACK_BLOCK = 256
CHUNKS = (3, 1)


def left_trans(left, right):
    return lax.dot_general(
        left, right, (((0,), (0,)), ((), ())), preferred_element_type=F32
    )


def right_trans(left, right):
    return lax.dot_general(
        left, right, (((1,), (1,)), ((), ())), preferred_element_type=F32
    )


def product(left, right):
    return jnp.dot(left, right, preferred_element_type=F32)


def causal_tile(scores):
    size = scores.shape[0]
    key = lax.broadcasted_iota(jnp.int32, scores.shape, 0)
    query = lax.broadcasted_iota(jnp.int32, scores.shape, 1)
    return jnp.where(key <= query, scores, -1e30)


def head_parts(packed_ref, head, width):
    columns = [slice(part * width + head * HD, part * width + (head + 1) * HD) for part in range(3)]
    query, key, value = [packed_ref[:, part] for part in columns]
    return query * HD ** (-0.5), key, value


def attend_kernel(packed_ref, out_ref, lse_ref):
    width = out_ref.shape[1]
    for head in range(width // HD):
        query, key, value = head_parts(packed_ref, head, width)
        query = query.astype(BF16)
        value_t = value.T
        for top in range(0, LEN, FORWARD_BLOCK):
            keys = top + FORWARD_BLOCK
            scores = right_trans(key[:keys], query[top:keys])
            last = causal_tile(scores[top:])
            scores = jnp.concatenate([scores[:top], last]) if top else last
            highest = jnp.max(scores, axis=0, keepdims=True)
            exponent = jnp.exp(scores - highest)
            total = jnp.sum(exponent, axis=0, keepdims=True)
            mixed = product(value_t[:, :keys], exponent.astype(BF16)) / total
            out_ref[top:keys, head * HD : (head + 1) * HD] = mixed.T.astype(BF16)
            lse_ref[0, 0, head : head + 1, top:keys] = highest + jnp.log(total)


def attend_back_kernel(packed_ref, out_ref, grad_ref, lse_ref, grads_ref, key_acc, value_acc):
    width = out_ref.shape[1]
    for head in range(width // HD):
        lanes = slice(head * HD, (head + 1) * HD)
        query, key, value = head_parts(packed_ref, head, width)
        query = query.astype(BF16)
        key_t = key.T
        grad = grad_ref[:, lanes]
        inner = (out_ref[:, lanes].astype(F32) * grad.astype(F32)).T
        inner = jnp.sum(inner, axis=0, keepdims=True)
        for top in reversed(range(0, LEN, BACK_BLOCK)):
            keys = top + BACK_BLOCK
            scores = right_trans(key[:keys], query[top:keys])
            last = causal_tile(scores[top:])
            scores = jnp.concatenate([scores[:top], last]) if top else last
            probs = jnp.exp(scores - lse_ref[0, 0, head : head + 1, top:keys])
            grad_probs = right_trans(value[:keys], grad[top:keys])
            grad_scores = (probs * (grad_probs - inner[:, top:keys])).astype(BF16)
            value_term = product(probs.astype(BF16), grad[top:keys])
            key_term = product(grad_scores, query[top:keys])
            if keys == LEN:
                value_acc[...] = value_term
                key_acc[...] = key_term
            else:
                value_acc[:keys] += value_term
                key_acc[:keys] += key_term
            grad_query = product(key_t[:, :keys], grad_scores) * HD ** (-0.5)
            grads_ref[top:keys, lanes] = grad_query.T.astype(BF16)
        grads_ref[:, width + head * HD : width + (head + 1) * HD] = key_acc[...].astype(BF16)
        grads_ref[:, 2 * width + head * HD : 2 * width + (head + 1) * HD] = value_acc[...].astype(
            BF16
        )


def attend(packed):
    rows, columns = packed.shape
    width = 2 * HD
    sequences, pairs = rows // LEN, columns // (3 * width)
    return pl.pallas_call(
        attend_kernel,
        grid=(sequences, pairs),
        out_shape=(
            jax.ShapeDtypeStruct((rows, pairs * width), BF16),
            jax.ShapeDtypeStruct((sequences, pairs, 2, LEN), F32),
        ),
        in_specs=[pl.BlockSpec((LEN, 3 * width), lambda s, p: (s, p))],
        out_specs=(
            pl.BlockSpec((LEN, width), lambda s, p: (s, p)),
            pl.BlockSpec((1, 1, 2, LEN), lambda s, p: (s, p, 0, 0)),
        ),
        compiler_params=pltpu.CompilerParams(vmem_limit_bytes=VMEM),
        cost_estimate=pl.CostEstimate(
            flops=4 * rows * LEN * pairs * width // 2,
            transcendentals=rows * LEN * pairs,
            bytes_accessed=2 * rows * columns * 2,
        ),
        name="attend",
    )(packed)


def attend_back(packed, attended, grad_attended, lse):
    rows, columns = packed.shape
    width = 2 * HD
    sequences, pairs = rows // LEN, columns // (3 * width)
    narrow = pl.BlockSpec((LEN, width), lambda s, p: (s, p))
    return pl.pallas_call(
        attend_back_kernel,
        grid=(sequences, pairs),
        out_shape=jax.ShapeDtypeStruct((rows, columns), BF16),
        in_specs=[
            pl.BlockSpec((LEN, 3 * width), lambda s, p: (s, p)),
            narrow,
            narrow,
            pl.BlockSpec((1, 1, 2, LEN), lambda s, p: (s, p, 0, 0)),
        ],
        out_specs=pl.BlockSpec((LEN, 3 * width), lambda s, p: (s, p)),
        scratch_shapes=[pltpu.VMEM((LEN, HD), F32)] * 2,
        compiler_params=pltpu.CompilerParams(vmem_limit_bytes=VMEM),
        cost_estimate=pl.CostEstimate(
            flops=10 * rows * LEN * pairs * width // 2,
            transcendentals=rows * LEN * pairs,
            bytes_accessed=3 * rows * columns * 2,
        ),
        name="attend_back",
    )(packed, attended, grad_attended, lse)


SPREAD = (
    (0, 0, "y", None),
    (0, 1, "x", None),
    (0, 0, "x", None),
    (0, 1, "y", None),
    (0, 0, "core", None),
    (0, 1, "core", None),
    (4, 0, "x", 0),
    (2, 1, "y", 1),
    (4, 0, "core", 0),
    (2, 1, "core", 1),
    (2, 0, "core", 2),
    (4, 1, "core", 3),
    (6, 0, "core", 6),
    (6, 1, "core", 7),
)
BIT = {"y": 4, "x": 2, "core": 1}


def neighbours():
    token, feat = lax.axis_index("tok"), lax.axis_index("feat")
    return {
        "y": (token + 1 - 2 * lax.rem(token, 2), feat),
        "x": (token, lax.rem(feat + 2, 4)),
        "core": (token, feat + 1 - 2 * lax.rem(feat, 2)),
    }


def owner(r):
    member, slot = lax.rem(lax.axis_index("tok"), 2), lax.axis_index("feat")
    if r & 4:
        member = 1 - member
    if r & 2:
        slot = lax.rem(slot + 2, 4)
    if r & 1:
        slot = slot + 1 - 2 * lax.rem(slot, 2)
    return member, slot


def greet(others=()):
    barrier = pltpu.get_barrier_semaphore()
    peers = [*neighbours().values(), *others]
    for peer in peers:
        pl.semaphore_signal(barrier, inc=1, device_id=peer, device_id_type=MESH)
    pl.semaphore_wait(barrier, len(peers))


def ring_peer(ring, distance):
    token = lax.axis_index("tok")
    return lax.rem(token + 2 * distance, 2 * ring), lax.axis_index("feat")


class SumAll:
    def __init__(self, ring, ref, steps, arrived, slots, send, recv):
        self.ring, self.ref = ring, ref
        self.steps, self.arrived, self.slots = steps, arrived, slots
        self.send, self.recv = send, recv
        self.place = lax.div(lax.axis_index("tok"), 2)
        self.peers = neighbours()

    @staticmethod
    def scratch(ring, shape):
        return [
            pltpu.VMEM((3, *shape), F32),
            pltpu.VMEM((3, *shape), F32),
            pltpu.VMEM((ring, *shape), F32),
            pltpu.SemaphoreType.DMA((2 + ring,)),
            pltpu.SemaphoreType.DMA((2 + ring,)),
        ]

    def copy(self, k):
        if k < 3:
            source = self.ref if k == 0 else self.steps.at[k - 1]
            target, peer = self.arrived.at[k], self.peers[("core", "x", "y")[k]]
        else:
            source, target = self.steps.at[2], self.slots.at[self.place]
            peer = ring_peer(self.ring, k - 2)
        return pltpu.make_async_remote_copy(
            source, target, self.send.at[k], self.recv.at[k],
            device_id=peer, device_id_type=MESH,
        )

    def start(self):
        self.copy(0).start()

    def step(self, k):
        self.copy(k).wait_recv()
        before = self.ref[...] if k == 0 else self.steps[k - 1]
        self.steps[k] = before + self.arrived[k]
        if k < 2:
            self.copy(k + 1).start()
        else:
            for distance in range(1, self.ring):
                self.copy(2 + distance).start()
            self.slots[self.place] = self.steps[2]

    def finish(self):
        for distance in range(1, self.ring):
            source = lax.rem(self.place + self.ring - distance, self.ring)
            k = 2 + distance
            pltpu.make_async_remote_copy(
                self.slots.at[source], self.slots.at[source], self.send.at[k], self.recv.at[k],
                device_id=ring_peer(self.ring, distance), device_id_type=MESH,
            ).wait_recv()
        for k in range(2 + self.ring):
            self.copy(k).wait_send()
        total = self.slots[0]
        for place in range(1, self.ring):
            total = total + self.slots[place]
        return total


class Spread:
    def __init__(self, own, region, send, recv):
        self.own, self.region, self.send, self.recv = own, region, send, recv
        self.peers = neighbours()

    def copy(self, k):
        r, half, way, _ = SPREAD[k]
        source = self.own(half) if r == 0 else self.region(r, half)
        return pltpu.make_async_remote_copy(
            source, self.region(r, half), self.send.at[k], self.recv.at[k],
            device_id=self.peers[way], device_id_type=MESH,
        )

    def arrival(self, k):
        r, half, way, _ = SPREAD[k]
        place = self.region(r ^ BIT[way], half)
        return pltpu.make_async_remote_copy(
            place, place, self.send.at[k], self.recv.at[k],
            device_id=self.peers[way], device_id_type=MESH,
        )

    def start(self, half):
        for k, (r, which, _, after) in enumerate(SPREAD):
            if after is None and which == half:
                self.copy(k).start()

    def forward(self):
        for first in range(8):
            if first in (4, 5):
                continue
            self.arrival(first).wait_recv()
            for k, (_, _, _, after) in enumerate(SPREAD):
                if after == first:
                    self.copy(k).start()

    def finish(self):
        for k, (_, _, way, _) in enumerate(SPREAD):
            if way == "core":
                self.arrival(k).wait_recv()
        for k in range(len(SPREAD)):
            self.copy(k).wait_send()


SPREAD_SEMS = [pltpu.SemaphoreType.DMA((len(SPREAD),))] * 2


class Collect:
    def __init__(self, part, size, parts, near, from_x, from_y, last_y, last_x, sems):
        self.part, self.size, self.half = part, size, size // 2
        self.parts, self.near = parts, near
        self.from_x, self.from_y, self.last_y, self.last_x = from_x, from_y, last_y, last_x
        self.load, self.send, self.recv = sems
        self.peers = neighbours()

    @staticmethod
    def scratch(size, columns):
        half = size // 2
        return [
            pltpu.VMEM((4, size, columns), BF16),
            pltpu.VMEM((4, size, columns), BF16),
            pltpu.VMEM((2, half, columns), BF16),
            pltpu.VMEM((2, half, columns), BF16),
            pltpu.VMEM((half, columns), BF16),
            pltpu.VMEM((half, columns), BF16),
            pltpu.SemaphoreType.DMA((4,)),
            pltpu.SemaphoreType.DMA((10,)),
            pltpu.SemaphoreType.DMA((10,)),
        ]

    def remote(self, k, source, target, way):
        return pltpu.make_async_remote_copy(
            source, target, self.send.at[k], self.recv.at[k],
            device_id=self.peers[way], device_id_type=MESH,
        )

    def copy(self, k):
        low, high = pl.ds(0, self.half), pl.ds(self.half, self.half)
        if k < 4:
            return self.remote(k, self.part(2 * k + 1), self.near.at[k], "core")
        if k < 6:
            return self.remote(k, self.parts.at[(1, 3)[k - 4], low], self.from_x.at[k - 4], "x")
        if k < 8:
            return self.remote(k, self.parts.at[(2, 3)[k - 6], high], self.from_y.at[k - 6], "y")
        if k == 8:
            return self.remote(k, self.parts.at[2, low], self.last_y, "y")
        return self.remote(k, self.parts.at[1, high], self.last_x, "x")

    def add(self, index, start, count, other):
        step = 32

        def body(i, carry):
            here = pl.ds(pl.multiple_of(start + i * step, step), step)
            there = pl.ds(pl.multiple_of(i * step, step), step)
            total = self.parts[index, here].astype(F32) + other[there].astype(F32)
            self.parts[index, here] = total.astype(BF16)
            return carry

        lax.fori_loop(0, count // step, body, 0)

    def loads(self, k):
        return pltpu.make_async_copy(self.part(2 * k), self.parts.at[k], self.load.at[k])

    def start(self):
        for k in (3, 1, 2, 0):
            self.copy(k).start()
        for k in (3, 1, 2, 0):
            self.loads(k).start()

    def first(self):
        for k, following in ((3, (5, 7)), (1, (4,)), (2, (6,)), (0, ())):
            self.loads(k).wait()
            self.copy(k).wait_recv()
            self.add(k, 0, self.size, self.near.at[k])
            for after in following:
                self.copy(after).start()

    def second(self):
        self.copy(5).wait_recv()
        self.add(2, 0, self.half, self.from_x.at[1])
        self.copy(8).start()
        self.copy(7).wait_recv()
        self.add(1, self.half, self.half, self.from_y.at[1])
        self.copy(9).start()

    def total(self, half, rows):
        first, last = (self.from_x, self.last_y) if half == 0 else (self.from_y, self.last_x)
        own = self.parts[0, pl.ds(pl.multiple_of(half * self.half + rows.start, 32), rows.size)]
        return own.astype(F32) + first[0, rows].astype(F32) + last[rows].astype(F32)

    def ready(self, half):
        for k in ((4, 8) if half == 0 else (6, 9)):
            self.copy(k).wait_recv()

    def finish(self):
        for k in range(10):
            self.copy(k).wait_send()


def loop_rows(count, body):
    def step(i, carry):
        body(pl.ds(pl.multiple_of(i * 32, 32), 32))
        return carry

    lax.fori_loop(0, count // 32, step, 0)


def call(kernel, identity, operands, spaces, outputs, out_spaces, scratch, cost):
    return pl.pallas_call(
        kernel,
        out_shape=outputs,
        in_specs=[pl.BlockSpec(memory_space=space) for space in spaces],
        out_specs=jax.tree.map(lambda space: pl.BlockSpec(memory_space=space), out_spaces),
        scratch_shapes=scratch,
        compiler_params=pltpu.CompilerParams(
            collective_id=identity, has_side_effects=True, vmem_limit_bytes=VMEM
        ),
        cost_estimate=pl.CostEstimate(flops=cost, bytes_accessed=cost // 100, transcendentals=0),
        name=kernel.__name__,
    )(*operands)


class PairSwap:
    def __init__(self, sources, out_ref, pieces, local, send, recv):
        self.sources, self.out, self.pieces = sources, out_ref, pieces
        self.local, self.send, self.recv = local, send, recv
        self.peer = neighbours()["y"]
        self.member = lax.rem(lax.axis_index("tok"), 2)

    def block(self, i, half):
        source, start, width, _ = self.pieces[i]
        ref = self.sources[source]
        offset = half * (ref.shape[1] // 2) + start
        return ref.at[:, pl.ds(pl.multiple_of(offset, 128), width)]

    def place(self, i, member):
        _, _, width, column = self.pieces[i]
        rows = self.out.shape[0] // 2
        return self.out.at[pl.ds(pl.multiple_of(member * rows, rows), rows), pl.ds(column, width)]

    def remote(self, i, source, member):
        return pltpu.make_async_remote_copy(
            source, self.place(i, member), self.send.at[i], self.recv.at[i],
            device_id=self.peer, device_id_type=MESH,
        )

    def own(self, i):
        return pltpu.make_async_copy(
            self.block(i, self.member), self.place(i, self.member), self.local.at[i]
        )

    def away(self, i):
        return self.remote(i, self.block(i, 1 - self.member), self.member)

    def start(self):
        for i in range(len(self.pieces)):
            self.away(i).start()
        for i in range(len(self.pieces)):
            self.own(i).start()

    def finish(self):
        for i in range(len(self.pieces)):
            other = 1 - self.member
            self.remote(i, self.place(i, other), other).wait_recv()
            self.away(i).wait_send()
            self.own(i).wait()


def swap_and_gather(identity, weights, pieces, shard=None):
    count = len(weights)
    size = weights[0].shape[0]
    columns = sum(piece[2] for piece in pieces)
    operands = tuple(weights)
    outputs = [jax.ShapeDtypeStruct((2 * size, columns), weights[0].dtype)]
    scratch = [pltpu.SemaphoreType.DMA((len(pieces),))] * 3
    if shard is not None:
        rows, wide = shard.shape
        half = rows // 2
        operands += (shard,)
        outputs.append(jax.ShapeDtypeStruct((2 * rows, 4 * wide), shard.dtype))
        scratch += [pltpu.SemaphoreType.DMA((2,))] + SPREAD_SEMS

    def swap_gather(*refs):
        sources, refs = refs[:count], refs[count:]
        if shard is not None:
            shard_ref, start_ref, out_ref, *sems = refs
        else:
            start_ref, *sems = refs
        greet()
        pair = PairSwap(sources, start_ref, pieces, *sems[:3])
        pair.start()
        if shard is None:
            pair.finish()
            return

        def own(which):
            return shard_ref.at[pl.ds(which * half, half)]

        def region(r, which):
            member, slot = owner(r)
            return out_ref.at[
                pl.ds(pl.multiple_of(member * rows + which * half, half), half),
                pl.ds(pl.multiple_of(slot * wide, wide), wide),
            ]

        spread = Spread(own, region, *sems[4:])
        spread.start(0)
        spread.start(1)
        copies = [
            pltpu.make_async_copy(own(which), region(0, which), sems[3].at[which])
            for which in range(2)
        ]
        for copy in copies:
            copy.start()
        spread.forward()
        spread.finish()
        pair.finish()
        for copy in copies:
            copy.wait()

    return call(
        swap_gather, identity, operands, (pl.ANY,) * len(operands),
        outputs, [pl.ANY] * len(outputs), scratch,
        15_000_000_000 if shard is None else 50_000_000_000,
    )


def scatter_blocks(identity, ring, vector, *terms):
    rows, wide = terms[0].shape[0] // 2, terms[0].shape[1] // 4
    count = len(terms)

    def scatter_outputs(vector_ref, *refs):
        greet([ring_peer(ring, distance) for distance in range(1, ring)])
        small_ref = refs[2 * count]
        scratch = refs[2 * count + 1 :]
        small = SumAll(ring, vector_ref, *scratch[:5])
        collects = []
        for i in range(count):

            def part(r, terms_ref=refs[i]):
                member, slot = owner(r)
                return terms_ref.at[
                    pl.ds(pl.multiple_of(member * rows, rows), rows),
                    pl.ds(pl.multiple_of(slot * wide, wide), wide),
                ]

            mine = scratch[5 + 9 * i : 5 + 9 * (i + 1)]
            collects.append(Collect(part, rows, *mine[:6], mine[6:]))
        small.start()
        for collect in collects:
            collect.start()
        small.step(0)
        for collect in collects:
            collect.first()
        small.step(1)
        for collect in collects:
            collect.second()
        small.step(2)
        for collect, out_ref in zip(collects, refs[count:]):
            for which in range(2):
                collect.ready(which)

                def body(here, collect=collect, out_ref=out_ref):
                    there = pl.ds(pl.multiple_of(which * (rows // 2) + here.start, 32), 32)
                    out_ref[there] = collect.total(which, here).astype(BF16)

                loop_rows(rows // 2, body)
        for collect in collects:
            collect.finish()
        scratch[1][0] = small.finish()
        start = pl.multiple_of(lax.axis_index("feat") * wide, wide)
        small_ref[...] = scratch[1][0, :, pl.ds(start, wide)]

    return call(
        scatter_outputs, identity, (vector, *terms), (pltpu.VMEM,) + (pl.ANY,) * count,
        [jax.ShapeDtypeStruct((rows, wide), BF16)] * count
        + [jax.ShapeDtypeStruct((vector.shape[0], wide), F32)],
        [pltpu.VMEM] * (count + 1),
        SumAll.scratch(ring, vector.shape) + Collect.scratch(rows, wide) * count,
        30_000_000_000 * count,
    )


def row_parts(terms_ref, quarter):
    def part(r):
        member, slot = owner(r)
        return terms_ref.at[pl.ds(pl.multiple_of((member * 4 + slot) * quarter, quarter), quarter)]

    return part


def row_region(out_ref, quarter):
    half = quarter // 2

    def region(r, which):
        member, slot = owner(r)
        start = (member * 4 + slot) * quarter + which * half
        return out_ref.at[pl.ds(pl.multiple_of(start, half), half)]

    return region


def middle_norm(identity, terms, x_all, gain):
    total, model = terms.shape
    quarter = total // 8
    half = quarter // 2

    def middle_step(
        terms_ref, x_ref, gain_ref, out_ref, middle_ref, factor_ref,
        x_own, normed, local, send, recv, *scratch
    ):
        greet()
        x_copy = pltpu.make_async_copy(row_parts(x_ref, quarter)(0), x_own, local.at[0])
        x_copy.start()
        collect = Collect(row_parts(terms_ref, quarter), quarter, *scratch[:6], scratch[6:])
        region = row_region(out_ref, quarter)
        spread = Spread(
            lambda which: normed.at[pl.ds(which * half, half)], region, send, recv
        )
        collect.start()
        collect.first()
        collect.second()
        x_copy.wait()
        copies = []
        for which in range(2):
            collect.ready(which)

            def body(here):
                there = pl.ds(pl.multiple_of(which * half + here.start, 32), 32)
                middle = collect.total(which, here) + x_own[there].astype(F32)
                mean = jnp.mean(middle * middle, axis=1, keepdims=True)
                factor = lax.rsqrt(mean + EPSILON)
                middle_ref[there] = middle
                factor_ref[there] = jnp.broadcast_to(factor, (32, 128))
                normed[there] = (middle * factor * gain_ref[...]).astype(BF16)

            loop_rows(half, body)
            spread.start(which)
            copy = pltpu.make_async_copy(
                normed.at[pl.ds(which * half, half)], region(0, which), local.at[1 + which]
            )
            copy.start()
            copies.append(copy)
        spread.forward()
        spread.finish()
        collect.finish()
        for copy in copies:
            copy.wait()

    return call(
        middle_step, identity, (terms, x_all, gain), (pl.ANY, pl.ANY, pltpu.VMEM),
        (
            jax.ShapeDtypeStruct((total, model), BF16),
            jax.ShapeDtypeStruct((quarter, model), F32),
            jax.ShapeDtypeStruct((quarter, 128), F32),
        ),
        (pl.ANY, pltpu.VMEM, pltpu.VMEM),
        [
            pltpu.VMEM((quarter, model), BF16),
            pltpu.VMEM((quarter, model), BF16),
            pltpu.SemaphoreType.DMA((3,)),
        ]
        + SPREAD_SEMS
        + Collect.scratch(quarter, model),
        70_000_000_000,
    )


def middle_back(identity, terms, cot, middle, factor, gain):
    total, model = terms.shape
    quarter = total // 8
    half = quarter // 2

    def middle_back_step(
        terms_ref, cot_ref, middle_ref, factor_ref, gain_ref, out_ref, grad_ref, gain_grad_ref,
        cot_own, rounded, local, send, recv, *scratch
    ):
        greet()
        cot_copy = pltpu.make_async_copy(row_parts(cot_ref, quarter)(0), cot_own, local.at[0])
        cot_copy.start()
        collect = Collect(row_parts(terms_ref, quarter), quarter, *scratch[:6], scratch[6:])
        region = row_region(out_ref, quarter)
        spread = Spread(
            lambda which: rounded.at[pl.ds(which * half, half)], region, send, recv
        )
        collect.start()
        collect.first()
        collect.second()
        cot_copy.wait()
        gain_grad_ref[...] = jnp.zeros_like(gain_grad_ref)
        copies = []
        for which in range(2):
            collect.ready(which)

            def body(here):
                there = pl.ds(pl.multiple_of(which * half + here.start, 32), 32)
                grad_normed = collect.total(which, here)
                values = middle_ref[there]
                factor = factor_ref[there][:, :1]
                weighted = gain_ref[...] * grad_normed
                inner = jnp.mean(weighted * values, axis=1, keepdims=True)
                grad = (
                    cot_own[there].astype(F32)
                    + factor * weighted
                    - values * (factor * factor * factor * inner)
                )
                grad_ref[there] = grad
                rounded[there] = grad.astype(BF16)
                gain_grad_ref[...] += jnp.sum(grad_normed * values * factor, axis=0, keepdims=True)

            loop_rows(half, body)
            spread.start(which)
            copy = pltpu.make_async_copy(
                rounded.at[pl.ds(which * half, half)], region(0, which), local.at[1 + which]
            )
            copy.start()
            copies.append(copy)
        spread.forward()
        spread.finish()
        collect.finish()
        for copy in copies:
            copy.wait()

    return call(
        middle_back_step, identity, (terms, cot, middle, factor, gain),
        (pl.ANY, pl.ANY, pltpu.VMEM, pltpu.VMEM, pltpu.VMEM),
        (
            jax.ShapeDtypeStruct((total, model), BF16),
            jax.ShapeDtypeStruct((quarter, model), F32),
            jax.ShapeDtypeStruct((1, model), F32),
        ),
        (pl.ANY, pltpu.VMEM, pltpu.VMEM),
        [
            pltpu.VMEM((quarter, model), BF16),
            pltpu.VMEM((quarter, model), BF16),
            pltpu.SemaphoreType.DMA((3,)),
        ]
        + SPREAD_SEMS
        + Collect.scratch(quarter, model),
        70_000_000_000,
    )


def assemble(plan, flipped_out, totals, others, passed=()):
    count = len(totals)
    size = others[0].shape[0]
    shapes = []
    for index, pieces in enumerate(plan):
        wide = 2 * sum(piece[2] for piece in pieces)
        shapes.append((size, wide) if index < flipped_out else (wide, size))

    def assemble_grads(*refs):
        member = lax.rem(lax.axis_index("tok"), 2)
        outs = refs[2 * count + len(passed) :]
        for i in range(len(passed)):
            outs[len(plan) + i][...] = refs[2 * count + i][...]
        for index, pieces in enumerate(plan):
            half = sum(piece[2] for piece in pieces)
            for source, column, width, target in pieces:
                own_rows = pl.ds(pl.multiple_of(member * size, size), size)
                own = refs[source][own_rows, column : column + width]
                other = refs[count + source][:, column : column + width]
                for which, block in ((member, own), (1 - member, other)):
                    start = pl.multiple_of(which * half + target, 128)
                    if index < flipped_out:
                        outs[index][:, pl.ds(start, width)] = block.astype(F32)
                    else:
                        outs[index][pl.ds(start, width), :] = block.astype(F32).T

    return pl.pallas_call(
        assemble_grads,
        out_shape=[jax.ShapeDtypeStruct(shape, F32) for shape in shapes]
        + [jax.ShapeDtypeStruct(array.shape, array.dtype) for array in passed],
        in_specs=[pl.BlockSpec(memory_space=pltpu.VMEM)] * (2 * count + len(passed)),
        out_specs=[pl.BlockSpec(memory_space=pltpu.VMEM)] * (len(plan) + len(passed)),
        compiler_params=pltpu.CompilerParams(vmem_limit_bytes=VMEM),
        cost_estimate=pl.CostEstimate(
            flops=0, transcendentals=0, bytes_accessed=8 * size * 2 * sum(t.shape[1] for t in totals)
        ),
        name="assemble_grads",
    )(*totals, *others, *passed)


def input_terms(grad_packed, weights, x_all, gain, grad_middle, own):
    total, columns = grad_packed.shape
    model = x_all.shape[1]
    tile = grad_middle.shape[0]

    def input_terms_step(own_ref, grad_ref, qkv_ref, x_ref, gain_ref, middle_ref, out_ref, gain_grad_ref):
        step = pl.program_id(0)
        grad_normed = right_trans(grad_ref[...], qkv_ref[...])
        values = x_ref[...].astype(F32)
        factor = lax.rsqrt(jnp.mean(values * values, axis=1, keepdims=True) + EPSILON)
        weighted = grad_normed * gain_ref[...]
        inner = jnp.mean(weighted * values, axis=1, keepdims=True)
        terms = factor * weighted - values * (factor * factor * factor * inner)

        @pl.when(step == own_ref[0])
        def _():
            out_ref[...] = (terms + middle_ref[...]).astype(BF16)

        @pl.when(step != own_ref[0])
        def _():
            out_ref[...] = terms.astype(BF16)

        @pl.when(step == 0)
        def _():
            gain_grad_ref[...] = jnp.zeros_like(gain_grad_ref)

        gain_grad_ref[...] += jnp.sum(grad_normed * values * factor, axis=0, keepdims=True)

    return pl.pallas_call(
        input_terms_step,
        grid_spec=pltpu.PrefetchScalarGridSpec(
            num_scalar_prefetch=1,
            grid=(total // tile,),
            in_specs=[
                pl.BlockSpec((tile, columns), lambda i, own: (i, 0)),
                pl.BlockSpec((model, columns), lambda i, own: (0, 0)),
                pl.BlockSpec((tile, model), lambda i, own: (i, 0)),
                pl.BlockSpec((1, model), lambda i, own: (0, 0)),
                pl.BlockSpec((tile, model), lambda i, own: (0, 0)),
            ],
            out_specs=[
                pl.BlockSpec((tile, model), lambda i, own: (i, 0)),
                pl.BlockSpec((1, model), lambda i, own: (0, 0)),
            ],
        ),
        out_shape=[
            jax.ShapeDtypeStruct((total, model), BF16),
            jax.ShapeDtypeStruct((1, model), F32),
        ],
        compiler_params=pltpu.CompilerParams(vmem_limit_bytes=VMEM),
        cost_estimate=pl.CostEstimate(
            flops=2 * total * columns * model,
            transcendentals=total,
            bytes_accessed=6 * total * model,
        ),
        name="input_terms",
    )(own, grad_packed, weights, x_all, gain, grad_middle)


def feed_forward(normed, cot, weights, chunk):
    total, model = normed.shape
    tile = 512
    part = 256 if chunk % 256 == 0 else 128

    def feed_step(normed_ref, cot_ref, gate_ref, up_ref, down_ref, hidden_ref, grads_ref):
        for left in range(0, chunk, part):
            here = slice(left, left + part)
            gate = product(normed_ref[...], gate_ref[:, here])
            upward = product(normed_ref[...], up_ref[:, here])
            grad_hidden = product(cot_ref[...], down_ref[:, here])
            sigma = jax.nn.sigmoid(gate)
            active = gate * sigma
            hidden_ref[:, here] = (active * upward).astype(BF16)
            grads_ref[:, here] = (
                grad_hidden * upward * (sigma + active * (1.0 - sigma))
            ).astype(BF16)
            grads_ref[:, chunk + left : chunk + left + part] = (grad_hidden * active).astype(BF16)

    rows = pl.BlockSpec((tile, model), lambda i: (i, 0))

    def weight(part):
        return pl.BlockSpec((model, chunk), lambda i: (0, part), pipeline_mode=pl.Buffered(1))

    return pl.pallas_call(
        feed_step,
        grid=(total // tile,),
        in_specs=[rows, rows, weight(0), weight(1), weight(2)],
        out_specs=[
            pl.BlockSpec((tile, chunk), lambda i: (i, 0)),
            pl.BlockSpec((tile, 2 * chunk), lambda i: (i, 0)),
        ],
        out_shape=[
            jax.ShapeDtypeStruct((total, chunk), BF16),
            jax.ShapeDtypeStruct((total, 2 * chunk), BF16),
        ],
        compiler_params=pltpu.CompilerParams(vmem_limit_bytes=VMEM),
        cost_estimate=pl.CostEstimate(
            flops=6 * total * chunk * model,
            transcendentals=total * chunk,
            bytes_accessed=4 * total * model + 6 * chunk * (model + total),
        ),
        name="feed_forward",
    )(normed, cot, weights, weights, weights)


def columns_back(lefts, weights, place, own, base=None, middle=None):
    count = len(lefts)
    total = lefts[0].shape[0]
    model = weights[0].shape[0]
    tile, part = 512, 512

    def columns_step(own_ref, *refs):
        out_ref = refs[-1]
        for start in range(0, model, part):
            here = slice(start, start + part)
            value = sum(
                right_trans(refs[i][...], refs[count + i][here, :]) for i in range(count)
            )
            if base is not None:
                value = value + refs[2 * count][:, here].astype(F32)
            out_ref[:, here] = value.astype(BF16)
        if middle is not None:
            middle_ref = refs[-2]
            size = middle_ref.shape[0]
            inside = own_ref[0] * size - pl.program_id(0) * tile

            @pl.when((inside >= 0) & (inside < tile))
            def _():
                rows = pl.ds(pl.multiple_of(inside, size), size)
                out_ref[rows, :] = (out_ref[rows, :].astype(F32) + middle_ref[...]).astype(BF16)

    in_specs = [pl.BlockSpec((tile, left.shape[1]), lambda i, own: (i, 0)) for left in lefts]
    in_specs += [
        pl.BlockSpec(
            (model, left.shape[1]), lambda i, own: (0, place), pipeline_mode=pl.Buffered(1)
        )
        for left in lefts
    ]
    operands = [own, *lefts, *weights]
    if base is not None:
        in_specs.append(pl.BlockSpec((tile, model), lambda i, own: (i, 0)))
        operands.append(base)
    if middle is not None:
        in_specs.append(pl.BlockSpec(middle.shape, lambda i, own: (0, 0)))
        operands.append(middle)
    inner = sum(left.shape[1] for left in lefts)
    return pl.pallas_call(
        columns_step,
        grid_spec=pltpu.PrefetchScalarGridSpec(
            num_scalar_prefetch=1,
            grid=(total // tile,),
            in_specs=in_specs,
            out_specs=pl.BlockSpec((tile, model), lambda i, own: (i, 0)),
        ),
        out_shape=jax.ShapeDtypeStruct((total, model), BF16),
        compiler_params=pltpu.CompilerParams(vmem_limit_bytes=VMEM),
        cost_estimate=pl.CostEstimate(
            flops=2 * total * model * inner,
            transcendentals=0,
            bytes_accessed=2 * total * model + 2 * (total + model) * inner,
        ),
        name="columns_back",
    )(*operands)


def weight_terms(pairs, tile=256):
    rows, model = pairs[0][0].shape
    count = len(pairs)
    widths = [right.shape[1] for _, right in pairs]

    def terms_step(*refs):
        out_ref = refs[-1]
        start = 0
        for i, width in enumerate(widths):
            out_ref[:, start : start + width] = left_trans(refs[i][...], refs[count + i][...]).astype(
                BF16
            )
            start += width

    return pl.pallas_call(
        terms_step,
        grid=(model // tile,),
        in_specs=[pl.BlockSpec((rows, tile), lambda i: (0, i))] * count
        + [
            pl.BlockSpec((rows, width), lambda i: (0, 0), pipeline_mode=pl.Buffered(1))
            for width in widths
        ],
        out_specs=pl.BlockSpec((tile, sum(widths)), lambda i: (i, 0)),
        out_shape=jax.ShapeDtypeStruct((model, sum(widths)), BF16),
        compiler_params=pltpu.CompilerParams(vmem_limit_bytes=VMEM),
        cost_estimate=pl.CostEstimate(
            flops=2 * rows * model * sum(widths),
            transcendentals=0,
            bytes_accessed=2 * (rows * model * count + (rows + model) * sum(widths)),
        ),
        name="weight_terms",
    )(*[left for left, _ in pairs], *[right for _, right in pairs])


def program(
    tok_size,
    tokens, gain_attn, w_query, w_key, w_value, w_out, gain_ffn, w_gate, w_up, w_down, cotangent
):
    token = lax.axis_index("tok")
    feat = lax.axis_index("feat")
    member = token % 2
    rows, wide = tokens.shape
    model = 4 * wide
    quarter = rows // 4
    groups = [list(range(i, tok_size, 2)) for i in range(2)]
    pair_width = 2 * HD

    def swap(value):
        return lax.ppermute(value, "tok", [(i, i ^ 1) for i in range(tok_size)])

    def x_swap(value):
        return lax.ppermute(value, "feat", [(i, i ^ 2) for i in range(4)])

    def core_swap(value):
        return lax.ppermute(value, "feat", [(i, i ^ 1) for i in range(4)])

    def ring_gather(shard):
        return lax.all_gather(shard, "tok", axis=0, tiled=True, axis_index_groups=groups)

    def ring_scatter(terms):
        return lax.psum_scatter(
            terms, "tok", scatter_dimension=0, tiled=True, axis_index_groups=groups
        )

    def other_half(total):
        size = total.shape[0] // 2
        return swap(lax.dynamic_slice_in_dim(total, (1 - member) * size, size, 0))

    heads_wide = w_query.shape[1] // 2
    hidden_wide = w_gate.shape[1] // 2
    chunks = [hidden_wide * part // sum(CHUNKS) for part in CHUNKS]
    lefts = [sum(chunks[:c]) for c in range(len(chunks))]
    attention_pieces = [
        (part, left, pair_width, 3 * left + part * pair_width)
        for left in range(0, heads_wide, pair_width)
        for part in range(3)
    ]
    attention_pieces.append((3, 0, heads_wide, 3 * heads_wide))
    (attention_start,) = swap_and_gather(0, (w_query, w_key, w_value, w_out.T), attention_pieces)
    feed = (w_gate, w_up, w_down.T)
    tokens_after, attention_start = lax.optimization_barrier((tokens, attention_start))
    attention_weights = ring_gather(attention_start)
    feed_weights = []
    wholes = []
    for c, shard in enumerate((tokens_after, cotangent)):
        if c:
            shard, wholes[0] = lax.optimization_barrier((shard, wholes[0]))
        pieces = [(part, lefts[c], chunks[c], part * chunks[c]) for part in range(3)]
        start, whole = swap_and_gather(1 + c, feed, pieces, shard)
        wholes.append(whole)
        feed_weights.append(ring_gather(start))
    x_all, cot_rows = wholes
    qkv = attention_weights[:, : 3 * heads_wide]
    out_proj = attention_weights[:, 3 * heads_wide :]

    gains = jnp.stack([gain_attn, gain_ffn])
    gains = jnp.stack([gains, core_swap(gains)])
    gains = jnp.concatenate([gains, x_swap(gains)])
    gains = jnp.concatenate(
        [lax.dynamic_index_in_dim(gains, feat ^ j, 0, keepdims=False) for j in range(4)], axis=1
    )
    gain_one, gain_two = gains[:1], gains[1:]

    x_wide = x_all.astype(F32)
    factor_one = lax.rsqrt(jnp.mean(x_wide * x_wide, axis=1, keepdims=True) + EPSILON)
    normed = (x_wide * factor_one * gain_one).astype(BF16)
    packed = product(normed, qkv).astype(BF16)
    attended, log_sums = attend(packed)
    normed_two, middle, factor_two = middle_norm(
        3, right_trans(attended, out_proj).astype(BF16), x_all, gain_two
    )

    own = (member * 4 + feat).astype(jnp.int32).reshape(1)
    feed_sums = []
    grad_normed_two = out_rows = None

    hiddens = []
    for c in range(len(chunks)):
        if c:
            feed_weights[c], grad_normed_two = lax.optimization_barrier(
                (feed_weights[c], grad_normed_two)
            )
        hidden, grad_both = feed_forward(normed_two, cot_rows, feed_weights[c], chunks[c])
        hiddens.append(hidden)
        if c + 1 < len(chunks):
            feed_terms = weight_terms([(normed_two, grad_both), (cot_rows, hidden)])
            feed_terms, grad_both = lax.optimization_barrier((feed_terms, grad_both))
            feed_sums.append(ring_scatter(feed_terms))
        grad_normed_two = columns_back(
            [grad_both], [feed_weights[c]], 0, own, grad_normed_two
        )
    grad_mid_rows, grad_middle, gain_ffn_part = middle_back(
        4, grad_normed_two, cot_rows, middle, factor_two, gain_two
    )

    hidden, grad_both, grad_mid_rows = lax.optimization_barrier((hidden, grad_both, grad_mid_rows))
    feed_terms = weight_terms(
        [(normed_two, grad_both), (cot_rows, hidden), (grad_mid_rows, attended)]
    )
    grad_mid_rows, feed_terms = lax.optimization_barrier((grad_mid_rows, feed_terms))
    feed_sums.append(ring_scatter(feed_terms))

    grad_attended = product(grad_mid_rows, out_proj).astype(BF16)
    grad_packed = attend_back(packed, attended, grad_attended, log_sums)
    attention_terms = left_trans(normed, grad_packed).astype(BF16)
    attention_terms, grad_packed = lax.optimization_barrier((attention_terms, grad_packed))
    attention_sum = ring_scatter(attention_terms)
    terms, gain_attn_part = input_terms(grad_packed, attention_weights, x_all, gain_one, grad_middle, own)
    hiddens[0], terms, feed_sums[0] = lax.optimization_barrier((hiddens[0], terms, feed_sums[0]))
    out_rows = columns_back(hiddens, feed_weights, 2, own, None, middle)
    outcome, input_grad, gain_grads = scatter_blocks(
        5, tok_size // 2, jnp.concatenate([gain_attn_part, gain_ffn_part]), out_rows, terms
    )
    feed_others = [other_half(feed_sums[0])]
    outcome, feed_sums[1] = lax.optimization_barrier((outcome, feed_sums[1]))
    feed_others.append(other_half(feed_sums[1]))
    feed_others[1], attention_sum = lax.optimization_barrier((feed_others[1], attention_sum))
    feed_plan = [
        [(c, part * chunks[c], chunks[c], lefts[c]) for c in range(len(chunks))]
        for part in range(3)
    ]
    feed_plan.append([(len(chunks) - 1, 3 * chunks[-1], heads_wide, 0)])
    gate_grad, up_grad, down_grad, out_grad, outcome, input_grad = assemble(
        feed_plan, 2, feed_sums, feed_others, (outcome, input_grad)
    )
    attention_plan = [
        [
            (0, 3 * left + part * pair_width, pair_width, left)
            for left in range(0, heads_wide, pair_width)
        ]
        for part in range(3)
    ]
    attention_other = other_half(attention_sum)
    attention_other, gate_grad, up_grad, down_grad, outcome, input_grad = lax.optimization_barrier(
        (attention_other, gate_grad, up_grad, down_grad, outcome, input_grad)
    )
    part_grads = assemble(attention_plan, 3, [attention_sum], [attention_other])
    return (
        outcome,
        input_grad,
        gain_grads[0],
        gain_grads[1],
        *part_grads,
        out_grad,
        gate_grad,
        up_grad,
        down_grad,
    )


def solution(mesh):
    in_specs = (
        P("tok", "feat"),
        P("feat"),
        P("tok", "feat"),
        P("tok", "feat"),
        P("tok", "feat"),
        P("feat", "tok"),
        P("feat"),
        P("tok", "feat"),
        P("tok", "feat"),
        P("feat", "tok"),
        P("tok", "feat"),
    )
    out_specs = (
        P("tok", "feat"),
        P("tok", "feat"),
        P("feat"),
        P("feat"),
        P("tok", "feat"),
        P("tok", "feat"),
        P("tok", "feat"),
        P("feat", "tok"),
        P("tok", "feat"),
        P("tok", "feat"),
        P("feat", "tok"),
    )

    def on_device(*arrays):
        return program(mesh.shape["tok"], *arrays)

    return jax.shard_map(
        on_device, mesh=mesh, in_specs=in_specs, out_specs=out_specs, check_vma=False
    )
```

```python
import jax
import jax.numpy as jnp
from jax import lax
from jax.experimental import pallas as pl
from jax.experimental.pallas import tpu as pltpu
from jax.sharding import PartitionSpec as P

HD = 64
LEN = 1024
EPSILON = 1e-05
BF16 = jnp.bfloat16
F32 = jnp.float32
MESH = pl.DeviceIdType.MESH
VMEM = 48 << 20
FORWARD_BLOCK = 512
BACK_BLOCK = 256
CHUNKS = (3, 1)


def left_trans(left, right):
    return lax.dot_general(
        left, right, (((0,), (0,)), ((), ())), preferred_element_type=F32
    )


def right_trans(left, right):
    return lax.dot_general(
        left, right, (((1,), (1,)), ((), ())), preferred_element_type=F32
    )


def product(left, right):
    return jnp.dot(left, right, preferred_element_type=F32)


def causal_tile(scores):
    size = scores.shape[0]
    key = lax.broadcasted_iota(jnp.int32, scores.shape, 0)
    query = lax.broadcasted_iota(jnp.int32, scores.shape, 1)
    return jnp.where(key <= query, scores, -1e30)


def head_parts(packed_ref, head, width):
    columns = [slice(part * width + head * HD, part * width + (head + 1) * HD) for part in range(3)]
    query, key, value = [packed_ref[:, part] for part in columns]
    return query * HD ** (-0.5), key, value


def attend_kernel(packed_ref, out_ref, lse_ref):
    width = out_ref.shape[1]
    for head in range(width // HD):
        query, key, value = head_parts(packed_ref, head, width)
        query = query.astype(BF16)
        value_t = value.T
        for top in range(0, LEN, FORWARD_BLOCK):
            keys = top + FORWARD_BLOCK
            scores = right_trans(key[:keys], query[top:keys])
            last = causal_tile(scores[top:])
            scores = jnp.concatenate([scores[:top], last]) if top else last
            highest = jnp.max(scores, axis=0, keepdims=True)
            exponent = jnp.exp(scores - highest)
            total = jnp.sum(exponent, axis=0, keepdims=True)
            mixed = product(value_t[:, :keys], exponent.astype(BF16)) / total
            out_ref[top:keys, head * HD : (head + 1) * HD] = mixed.T.astype(BF16)
            lse_ref[0, 0, head : head + 1, top:keys] = highest + jnp.log(total)


def attend_back_kernel(packed_ref, out_ref, grad_ref, lse_ref, grads_ref, key_acc, value_acc):
    width = out_ref.shape[1]
    for head in range(width // HD):
        lanes = slice(head * HD, (head + 1) * HD)
        query, key, value = head_parts(packed_ref, head, width)
        query = query.astype(BF16)
        key_t = key.T
        grad = grad_ref[:, lanes]
        inner = (out_ref[:, lanes].astype(F32) * grad.astype(F32)).T
        inner = jnp.sum(inner, axis=0, keepdims=True)
        for top in reversed(range(0, LEN, BACK_BLOCK)):
            keys = top + BACK_BLOCK
            scores = right_trans(key[:keys], query[top:keys])
            last = causal_tile(scores[top:])
            scores = jnp.concatenate([scores[:top], last]) if top else last
            probs = jnp.exp(scores - lse_ref[0, 0, head : head + 1, top:keys])
            grad_probs = right_trans(value[:keys], grad[top:keys])
            grad_scores = (probs * (grad_probs - inner[:, top:keys])).astype(BF16)
            value_term = product(probs.astype(BF16), grad[top:keys])
            key_term = product(grad_scores, query[top:keys])
            if keys == LEN:
                value_acc[...] = value_term
                key_acc[...] = key_term
            else:
                value_acc[:keys] += value_term
                key_acc[:keys] += key_term
            grad_query = product(key_t[:, :keys], grad_scores) * HD ** (-0.5)
            grads_ref[top:keys, lanes] = grad_query.T.astype(BF16)
        grads_ref[:, width + head * HD : width + (head + 1) * HD] = key_acc[...].astype(BF16)
        grads_ref[:, 2 * width + head * HD : 2 * width + (head + 1) * HD] = value_acc[...].astype(
            BF16
        )


def attend(packed):
    rows, columns = packed.shape
    width = 2 * HD
    sequences, pairs = rows // LEN, columns // (3 * width)
    return pl.pallas_call(
        attend_kernel,
        grid=(sequences, pairs),
        out_shape=(
            jax.ShapeDtypeStruct((rows, pairs * width), BF16),
            jax.ShapeDtypeStruct((sequences, pairs, 2, LEN), F32),
        ),
        in_specs=[pl.BlockSpec((LEN, 3 * width), lambda s, p: (s, p))],
        out_specs=(
            pl.BlockSpec((LEN, width), lambda s, p: (s, p)),
            pl.BlockSpec((1, 1, 2, LEN), lambda s, p: (s, p, 0, 0)),
        ),
        compiler_params=pltpu.CompilerParams(vmem_limit_bytes=VMEM),
        cost_estimate=pl.CostEstimate(
            flops=4 * rows * LEN * pairs * width // 2,
            transcendentals=rows * LEN * pairs,
            bytes_accessed=2 * rows * columns * 2,
        ),
        name="attend",
    )(packed)


def attend_back(packed, attended, grad_attended, lse):
    rows, columns = packed.shape
    width = 2 * HD
    sequences, pairs = rows // LEN, columns // (3 * width)
    narrow = pl.BlockSpec((LEN, width), lambda s, p: (s, p))
    return pl.pallas_call(
        attend_back_kernel,
        grid=(sequences, pairs),
        out_shape=jax.ShapeDtypeStruct((rows, columns), BF16),
        in_specs=[
            pl.BlockSpec((LEN, 3 * width), lambda s, p: (s, p)),
            narrow,
            narrow,
            pl.BlockSpec((1, 1, 2, LEN), lambda s, p: (s, p, 0, 0)),
        ],
        out_specs=pl.BlockSpec((LEN, 3 * width), lambda s, p: (s, p)),
        scratch_shapes=[pltpu.VMEM((LEN, HD), F32)] * 2,
        compiler_params=pltpu.CompilerParams(vmem_limit_bytes=VMEM),
        cost_estimate=pl.CostEstimate(
            flops=10 * rows * LEN * pairs * width // 2,
            transcendentals=rows * LEN * pairs,
            bytes_accessed=3 * rows * columns * 2,
        ),
        name="attend_back",
    )(packed, attended, grad_attended, lse)


SPREAD = (
    (0, 0, "y", None),
    (0, 1, "x", None),
    (0, 0, "x", None),
    (0, 1, "y", None),
    (0, 0, "core", None),
    (0, 1, "core", None),
    (4, 0, "x", 0),
    (2, 1, "y", 1),
    (4, 0, "core", 0),
    (2, 1, "core", 1),
    (2, 0, "core", 2),
    (4, 1, "core", 3),
    (6, 0, "core", 6),
    (6, 1, "core", 7),
)
BIT = {"y": 4, "x": 2, "core": 1}


def neighbours():
    token, feat = lax.axis_index("tok"), lax.axis_index("feat")
    return {
        "y": (token + 1 - 2 * lax.rem(token, 2), feat),
        "x": (token, lax.rem(feat + 2, 4)),
        "core": (token, feat + 1 - 2 * lax.rem(feat, 2)),
    }


def owner(r):
    member, slot = lax.rem(lax.axis_index("tok"), 2), lax.axis_index("feat")
    if r & 4:
        member = 1 - member
    if r & 2:
        slot = lax.rem(slot + 2, 4)
    if r & 1:
        slot = slot + 1 - 2 * lax.rem(slot, 2)
    return member, slot


def greet(others=()):
    barrier = pltpu.get_barrier_semaphore()
    peers = [*neighbours().values(), *others]
    for peer in peers:
        pl.semaphore_signal(barrier, inc=1, device_id=peer, device_id_type=MESH)
    pl.semaphore_wait(barrier, len(peers))


def ring_peer(ring, distance):
    token = lax.axis_index("tok")
    return lax.rem(token + 2 * distance, 2 * ring), lax.axis_index("feat")


class SumAll:
    def __init__(self, ring, ref, steps, arrived, slots, send, recv):
        self.ring, self.ref = ring, ref
        self.steps, self.arrived, self.slots = steps, arrived, slots
        self.send, self.recv = send, recv
        self.place = lax.div(lax.axis_index("tok"), 2)
        self.peers = neighbours()

    @staticmethod
    def scratch(ring, shape):
        return [
            pltpu.VMEM((3, *shape), F32),
            pltpu.VMEM((3, *shape), F32),
            pltpu.VMEM((ring, *shape), F32),
            pltpu.SemaphoreType.DMA((2 + ring,)),
            pltpu.SemaphoreType.DMA((2 + ring,)),
        ]

    def copy(self, k):
        if k < 3:
            source = self.ref if k == 0 else self.steps.at[k - 1]
            target, peer = self.arrived.at[k], self.peers[("core", "x", "y")[k]]
        else:
            source, target = self.steps.at[2], self.slots.at[self.place]
            peer = ring_peer(self.ring, k - 2)
        return pltpu.make_async_remote_copy(
            source, target, self.send.at[k], self.recv.at[k],
            device_id=peer, device_id_type=MESH,
        )

    def start(self):
        self.copy(0).start()

    def step(self, k):
        self.copy(k).wait_recv()
        before = self.ref[...] if k == 0 else self.steps[k - 1]
        self.steps[k] = before + self.arrived[k]
        if k < 2:
            self.copy(k + 1).start()
        else:
            for distance in range(1, self.ring):
                self.copy(2 + distance).start()
            self.slots[self.place] = self.steps[2]

    def finish(self):
        for distance in range(1, self.ring):
            source = lax.rem(self.place + self.ring - distance, self.ring)
            k = 2 + distance
            pltpu.make_async_remote_copy(
                self.slots.at[source], self.slots.at[source], self.send.at[k], self.recv.at[k],
                device_id=ring_peer(self.ring, distance), device_id_type=MESH,
            ).wait_recv()
        for k in range(2 + self.ring):
            self.copy(k).wait_send()
        total = self.slots[0]
        for place in range(1, self.ring):
            total = total + self.slots[place]
        return total


class Spread:
    def __init__(self, own, region, send, recv):
        self.own, self.region, self.send, self.recv = own, region, send, recv
        self.peers = neighbours()

    def copy(self, k):
        r, half, way, _ = SPREAD[k]
        source = self.own(half) if r == 0 else self.region(r, half)
        return pltpu.make_async_remote_copy(
            source, self.region(r, half), self.send.at[k], self.recv.at[k],
            device_id=self.peers[way], device_id_type=MESH,
        )

    def arrival(self, k):
        r, half, way, _ = SPREAD[k]
        place = self.region(r ^ BIT[way], half)
        return pltpu.make_async_remote_copy(
            place, place, self.send.at[k], self.recv.at[k],
            device_id=self.peers[way], device_id_type=MESH,
        )

    def start(self, half):
        for k, (r, which, _, after) in enumerate(SPREAD):
            if after is None and which == half:
                self.copy(k).start()

    def forward(self, arrivals=(0, 1, 2, 3, 6, 7)):
        for first in arrivals:
            self.arrival(first).wait_recv()
            for k, (_, _, _, after) in enumerate(SPREAD):
                if after == first:
                    self.copy(k).start()

    def finish(self):
        for k, (_, _, way, _) in enumerate(SPREAD):
            if way == "core":
                self.arrival(k).wait_recv()
        for k in range(len(SPREAD)):
            self.copy(k).wait_send()


SPREAD_SEMS = [pltpu.SemaphoreType.DMA((len(SPREAD),))] * 2


def block_spread(shard_ref, out_ref, local, send, recv):
    rows, wide = shard_ref.shape
    half = rows // 2

    def own(which):
        return shard_ref.at[pl.ds(which * half, half)]

    def region(r, which):
        member, slot = owner(r)
        return out_ref.at[
            pl.ds(pl.multiple_of(member * rows + which * half, half), half),
            pl.ds(pl.multiple_of(slot * wide, wide), wide),
        ]

    copies = [
        pltpu.make_async_copy(own(which), region(0, which), local.at[which]) for which in range(2)
    ]
    return Spread(own, region, send, recv), copies


class Collect:
    def __init__(self, part, size, parts, near, from_x, from_y, last_y, last_x, sems):
        self.part, self.size, self.half = part, size, size // 2
        self.parts, self.near = parts, near
        self.from_x, self.from_y, self.last_y, self.last_x = from_x, from_y, last_y, last_x
        self.load, self.send, self.recv = sems
        self.peers = neighbours()

    @staticmethod
    def scratch(size, columns):
        half = size // 2
        return [
            pltpu.VMEM((4, size, columns), BF16),
            pltpu.VMEM((4, size, columns), BF16),
            pltpu.VMEM((2, half, columns), BF16),
            pltpu.VMEM((2, half, columns), BF16),
            pltpu.VMEM((half, columns), BF16),
            pltpu.VMEM((half, columns), BF16),
            pltpu.SemaphoreType.DMA((4,)),
            pltpu.SemaphoreType.DMA((10,)),
            pltpu.SemaphoreType.DMA((10,)),
        ]

    def remote(self, k, source, target, way):
        return pltpu.make_async_remote_copy(
            source, target, self.send.at[k], self.recv.at[k],
            device_id=self.peers[way], device_id_type=MESH,
        )

    def copy(self, k):
        low, high = pl.ds(0, self.half), pl.ds(self.half, self.half)
        if k < 4:
            return self.remote(k, self.part(2 * k + 1), self.near.at[k], "core")
        if k < 6:
            return self.remote(k, self.parts.at[(1, 3)[k - 4], low], self.from_x.at[k - 4], "x")
        if k < 8:
            return self.remote(k, self.parts.at[(2, 3)[k - 6], high], self.from_y.at[k - 6], "y")
        if k == 8:
            return self.remote(k, self.parts.at[2, low], self.last_y, "y")
        return self.remote(k, self.parts.at[1, high], self.last_x, "x")

    def add(self, index, start, count, other):
        step = 32

        def body(i, carry):
            here = pl.ds(pl.multiple_of(start + i * step, step), step)
            there = pl.ds(pl.multiple_of(i * step, step), step)
            total = self.parts[index, here].astype(F32) + other[there].astype(F32)
            self.parts[index, here] = total.astype(BF16)
            return carry

        lax.fori_loop(0, count // step, body, 0)

    def loads(self, k):
        return pltpu.make_async_copy(self.part(2 * k), self.parts.at[k], self.load.at[k])

    def start(self):
        for k in (3, 1, 2, 0):
            self.copy(k).start()
        for k in (3, 1, 2, 0):
            self.loads(k).start()

    def first(self):
        for k, following in ((3, (5, 7)), (1, (4,)), (2, (6,)), (0, ())):
            self.loads(k).wait()
            self.copy(k).wait_recv()
            self.add(k, 0, self.size, self.near.at[k])
            for after in following:
                self.copy(after).start()

    def second(self):
        self.copy(5).wait_recv()
        self.add(2, 0, self.half, self.from_x.at[1])
        self.copy(8).start()
        self.copy(7).wait_recv()
        self.add(1, self.half, self.half, self.from_y.at[1])
        self.copy(9).start()

    def total(self, half, rows):
        first, last = (self.from_x, self.last_y) if half == 0 else (self.from_y, self.last_x)
        own = self.parts[0, pl.ds(pl.multiple_of(half * self.half + rows.start, 32), rows.size)]
        return own.astype(F32) + first[0, rows].astype(F32) + last[rows].astype(F32)

    def ready(self, half):
        for k in ((4, 8) if half == 0 else (6, 9)):
            self.copy(k).wait_recv()

    def finish(self):
        for k in range(10):
            self.copy(k).wait_send()


def loop_rows(count, body):
    def step(i, carry):
        body(pl.ds(pl.multiple_of(i * 32, 32), 32))
        return carry

    lax.fori_loop(0, count // 32, step, 0)


def call(kernel, identity, operands, spaces, outputs, out_spaces, scratch, cost):
    return pl.pallas_call(
        kernel,
        out_shape=outputs,
        in_specs=[pl.BlockSpec(memory_space=space) for space in spaces],
        out_specs=jax.tree.map(lambda space: pl.BlockSpec(memory_space=space), out_spaces),
        scratch_shapes=scratch,
        compiler_params=pltpu.CompilerParams(
            collective_id=identity, has_side_effects=True, vmem_limit_bytes=VMEM
        ),
        cost_estimate=pl.CostEstimate(flops=cost, bytes_accessed=cost // 100, transcendentals=0),
        name=kernel.__name__,
    )(*operands)


class RingBlocks:
    def __init__(self, ring, source, out_ref, send, recv):
        self.ring, self.source, self.out, self.send, self.recv = ring, source, out_ref, send, recv
        self.count = out_ref.shape[0]
        self.stage = 0

    def copy(self, k):
        source = self.source if k == 0 else self.out.at[k - 1]
        return pltpu.make_async_remote_copy(
            source, self.out.at[k], self.send.at[k], self.recv.at[k],
            device_id=ring_peer(self.ring, 1), device_id_type=MESH,
        )

    def start(self):
        self.copy(0).start()

    def advance(self):
        if self.stage + 1 < self.count:
            self.copy(self.stage).wait_recv()
            self.stage += 1
            self.copy(self.stage).start()

    def finish(self):
        while self.stage + 1 < self.count:
            self.advance()
        self.copy(self.count - 1).wait_recv()
        for k in range(self.count):
            self.copy(k).wait_send()


class RowsSwap:
    def __init__(self, ring, blocks, out_ref, local, send, recv):
        self.ring, self.blocks, self.out = ring, blocks, out_ref
        self.local, self.send, self.recv = local, send, recv
        token = lax.axis_index("tok")
        self.place, self.member = lax.div(token, 2), lax.rem(token, 2)
        self.peer = neighbours()["y"]

    def block(self, s, half):
        width = self.out.shape[1]
        return self.blocks[s].at[:, pl.ds(pl.multiple_of(half * width, width), width)]

    def target(self, s, member):
        size = self.out.shape[0] // self.ring // 2
        place = lax.rem(self.place + self.ring - s, self.ring)
        return self.out.at[pl.ds(pl.multiple_of((2 * place + member) * size, size), size)]

    def remote(self, s, source, member):
        return pltpu.make_async_remote_copy(
            source, self.target(s, member), self.send.at[s], self.recv.at[s],
            device_id=self.peer, device_id_type=MESH,
        )

    def own(self, s):
        return pltpu.make_async_copy(
            self.block(s, self.member), self.target(s, self.member), self.local.at[s]
        )

    def away(self, s):
        return self.remote(s, self.block(s, 1 - self.member), self.member)

    def start(self):
        for s in range(self.ring):
            self.away(s).start()
        for s in range(self.ring):
            self.own(s).start()

    def finish(self):
        for s in range(self.ring):
            other = 1 - self.member
            self.remote(s, self.target(s, other), other).wait_recv()
            self.away(s).wait_send()
            self.own(s).wait()


class PairSwap:
    def __init__(self, sources, out_ref, pieces, local, send, recv):
        self.sources, self.out, self.pieces = sources, out_ref, pieces
        self.local, self.send, self.recv = local, send, recv
        self.peer = neighbours()["y"]
        self.member = lax.rem(lax.axis_index("tok"), 2)

    def block(self, i, half):
        source, start, width, _ = self.pieces[i]
        ref = self.sources[source]
        offset = half * (ref.shape[1] // 2) + start
        return ref.at[:, pl.ds(pl.multiple_of(offset, 128), width)]

    def place(self, i, member):
        _, _, width, column = self.pieces[i]
        rows = self.out.shape[0] // 2
        return self.out.at[pl.ds(pl.multiple_of(member * rows, rows), rows), pl.ds(column, width)]

    def remote(self, i, source, member):
        return pltpu.make_async_remote_copy(
            source, self.place(i, member), self.send.at[i], self.recv.at[i],
            device_id=self.peer, device_id_type=MESH,
        )

    def own(self, i):
        return pltpu.make_async_copy(
            self.block(i, self.member), self.place(i, self.member), self.local.at[i]
        )

    def away(self, i):
        return self.remote(i, self.block(i, 1 - self.member), self.member)

    def start(self):
        for i in range(len(self.pieces)):
            self.away(i).start()
        for i in range(len(self.pieces)):
            self.own(i).start()

    def finish(self):
        for i in range(len(self.pieces)):
            other = 1 - self.member
            self.remote(i, self.place(i, other), other).wait_recv()
            self.away(i).wait_send()
            self.own(i).wait()


def swap_first(identity, weights, pieces, ring, block, count):
    size = weights[0].shape[0]
    outputs = [
        jax.ShapeDtypeStruct((2 * size, sum(piece[2] for piece in pieces)), weights[0].dtype),
        jax.ShapeDtypeStruct((count, *block.shape), block.dtype),
    ]

    def swap_start(*refs):
        sources, (block_ref, start_ref, blocks_ref, *sems) = refs[: len(weights)], refs[len(weights) :]
        greet([ring_peer(ring, 1), ring_peer(ring, ring - 1)])
        around = RingBlocks(ring, block_ref, blocks_ref, *sems[3:])
        pair = PairSwap(sources, start_ref, pieces, *sems[:3])
        around.start()
        pair.start()
        around.finish()
        pair.finish()

    operands = (*weights, block)
    return call(
        swap_start, identity, operands, (pl.ANY,) * len(operands),
        outputs, [pl.ANY] * len(outputs),
        [pltpu.SemaphoreType.DMA((len(pieces),))] * 3 + [pltpu.SemaphoreType.DMA((count,))] * 2,
        15_000_000_000,
    )


def swap_and_gather(identity, weights, pieces, shard, ring, blocks, steps, small):
    count = len(weights)
    size = weights[0].shape[0]
    columns = sum(piece[2] for piece in pieces)
    rows, wide = shard.shape
    operands = (*weights, shard, blocks, small)
    small_rows, small_wide = small.shape
    outputs = [
        jax.ShapeDtypeStruct((2 * size, columns), weights[0].dtype),
        jax.ShapeDtypeStruct((2 * rows, 4 * wide), shard.dtype),
        jax.ShapeDtypeStruct((steps, *blocks.shape[1:]), shard.dtype),
        jax.ShapeDtypeStruct((small_rows, 4 * small_wide), small.dtype),
    ]

    def swap_gather(*refs):
        sources, refs = refs[:count], refs[count:]
        shard_ref, blocks_ref, small_ref, start_ref, out_ref, around_ref, whole_ref, *sems = refs
        small_send, small_recv = sems[8:]
        greet([ring_peer(ring, 1), ring_peer(ring, ring - 1)])

        def small_place(r):
            _, slot = owner(r)
            return whole_ref.at[:, pl.ds(pl.multiple_of(slot * small_wide, small_wide), small_wide)]

        def small_copy(k, source, place):
            return pltpu.make_async_remote_copy(
                source, place, small_send.at[k], small_recv.at[k],
                device_id=neighbours()[("core", "x", "core")[k]], device_id_type=MESH,
            )

        small_copies = [
            small_copy(0, small_ref, small_place(0)),
            small_copy(1, small_ref, small_place(0)),
            small_copy(2, small_place(2), small_place(2)),
        ]
        small_copies[0].start()
        small_copies[1].start()
        last = blocks_ref.at[blocks.shape[0] - 1]
        around = RingBlocks(ring, last, around_ref, *sems[6:8])
        around.start()
        pair = PairSwap(sources, start_ref, pieces, *sems[:3])
        pair.start()
        spread, copies = block_spread(shard_ref, out_ref, *sems[3:6])
        spread.start(0)
        spread.start(1)
        for copy in copies:
            copy.start()
        small_copy(1, small_place(2), small_place(2)).wait_recv()
        small_copies[2].start()
        whole_ref[:, pl.ds(pl.multiple_of(owner(0)[1] * small_wide, small_wide), small_wide)] = (
            small_ref[...]
        )
        spread.forward((0, 1, 2, 3))
        around.advance()
        spread.forward((6, 7))
        spread.finish()
        pair.finish()
        around.finish()
        small_copy(0, small_place(1), small_place(1)).wait_recv()
        small_copy(2, small_place(3), small_place(3)).wait_recv()
        for copy in small_copies:
            copy.wait_send()
        for copy in copies:
            copy.wait()

    return call(
        swap_gather, identity, operands, (pl.ANY,) * (len(operands) - 1) + (pltpu.VMEM,),
        outputs, [pl.ANY] * (len(outputs) - 1) + [pltpu.VMEM],
        [pltpu.SemaphoreType.DMA((len(pieces),))] * 3
        + [pltpu.SemaphoreType.DMA((2,))]
        + SPREAD_SEMS
        + [pltpu.SemaphoreType.DMA((steps,))] * 2
        + [pltpu.SemaphoreType.DMA((3,))] * 2,
        50_000_000_000,
    )


def swap_pairs(identity, weights, pieces, ring, blocks):
    count = len(weights)
    size = weights[0].shape[0]
    columns = sum(piece[2] for piece in pieces)
    block_size, block_wide = blocks[0].shape[-2:]
    operands = (*weights, *blocks)
    outputs = [
        jax.ShapeDtypeStruct((2 * size, columns), weights[0].dtype),
        jax.ShapeDtypeStruct((2 * ring * block_size, block_wide // 2), weights[0].dtype),
    ]

    def swap_last(*refs):
        greet()
        start_ref, out_ref, *sems = refs[len(operands) :]
        parts = []
        for ref in refs[count : len(operands)]:
            parts += [ref] if len(ref.shape) == 2 else [ref.at[k] for k in range(ref.shape[0])]
        around = RowsSwap(ring, parts, out_ref, *sems[3:])
        around.start()
        pair = PairSwap(refs[:count], start_ref, pieces, *sems[:3])
        pair.start()
        around.finish()
        pair.finish()

    return call(
        swap_last, identity, operands, (pl.ANY,) * len(operands),
        outputs, [pl.ANY] * len(outputs),
        [pltpu.SemaphoreType.DMA((len(pieces),))] * 3 + [pltpu.SemaphoreType.DMA((ring,))] * 3,
        20_000_000_000,
    )


def scatter_blocks(identity, ring, vector, *terms):
    rows, wide = terms[0].shape[0] // 2, terms[0].shape[1] // 4
    count = len(terms)

    def scatter_outputs(vector_ref, *refs):
        greet([ring_peer(ring, distance) for distance in range(1, ring)])
        small_ref = refs[2 * count]
        scratch = refs[2 * count + 1 :]
        small = SumAll(ring, vector_ref, *scratch[:5])
        collects = []
        for i in range(count):

            def part(r, terms_ref=refs[i]):
                member, slot = owner(r)
                return terms_ref.at[
                    pl.ds(pl.multiple_of(member * rows, rows), rows),
                    pl.ds(pl.multiple_of(slot * wide, wide), wide),
                ]

            mine = scratch[5 + 9 * i : 5 + 9 * (i + 1)]
            collects.append(Collect(part, rows, *mine[:6], mine[6:]))
        small.start()
        for collect in collects:
            collect.start()
        small.step(0)
        for collect in collects:
            collect.first()
        small.step(1)
        for collect in collects:
            collect.second()
        small.step(2)
        for collect, out_ref in zip(collects, refs[count:]):
            for which in range(2):
                collect.ready(which)

                def body(here, collect=collect, out_ref=out_ref):
                    there = pl.ds(pl.multiple_of(which * (rows // 2) + here.start, 32), 32)
                    out_ref[there] = collect.total(which, here).astype(BF16)

                loop_rows(rows // 2, body)
        for collect in collects:
            collect.finish()
        scratch[1][0] = small.finish()
        start = pl.multiple_of(lax.axis_index("feat") * wide, wide)
        small_ref[...] = scratch[1][0, :, pl.ds(start, wide)]

    return call(
        scatter_outputs, identity, (vector, *terms), (pltpu.VMEM,) + (pl.ANY,) * count,
        [jax.ShapeDtypeStruct((rows, wide), BF16)] * count
        + [jax.ShapeDtypeStruct((vector.shape[0], wide), F32)],
        [pltpu.VMEM] * (count + 1),
        SumAll.scratch(ring, vector.shape) + Collect.scratch(rows, wide) * count,
        30_000_000_000 * count,
    )


def row_parts(terms_ref, quarter):
    def part(r):
        member, slot = owner(r)
        return terms_ref.at[pl.ds(pl.multiple_of((member * 4 + slot) * quarter, quarter), quarter)]

    return part


def row_region(out_ref, quarter):
    half = quarter // 2

    def region(r, which):
        member, slot = owner(r)
        start = (member * 4 + slot) * quarter + which * half
        return out_ref.at[pl.ds(pl.multiple_of(start, half), half)]

    return region


def middle_norm(identity, terms, x_all, gain, cotangent):
    total, model = terms.shape
    quarter = total // 8
    half = quarter // 2

    def middle_step(
        terms_ref, x_ref, gain_ref, shard_ref, out_ref, middle_ref, factor_ref, cot_ref,
        x_own, normed, local, send, recv, cot_local, cot_send, cot_recv, *scratch
    ):
        greet()
        beside, copies = block_spread(shard_ref, cot_ref, cot_local, cot_send, cot_recv)
        x_copy = pltpu.make_async_copy(row_parts(x_ref, quarter)(0), x_own, local.at[0])
        x_copy.start()
        collect = Collect(row_parts(terms_ref, quarter), quarter, *scratch[:6], scratch[6:])
        region = row_region(out_ref, quarter)
        spread = Spread(
            lambda which: normed.at[pl.ds(which * half, half)], region, send, recv
        )
        collect.start()
        beside.start(0)
        beside.start(1)
        for copy in copies:
            copy.start()
        collect.first()
        beside.forward((0, 1, 2, 3))
        collect.second()
        x_copy.wait()
        for which in range(2):
            collect.ready(which)

            def body(here):
                there = pl.ds(pl.multiple_of(which * half + here.start, 32), 32)
                middle = collect.total(which, here) + x_own[there].astype(F32)
                mean = jnp.mean(middle * middle, axis=1, keepdims=True)
                factor = lax.rsqrt(mean + EPSILON)
                middle_ref[there] = middle
                factor_ref[there] = jnp.broadcast_to(factor, (32, 128))
                normed[there] = (middle * factor * gain_ref[...]).astype(BF16)

            loop_rows(half, body)
            spread.start(which)
            copy = pltpu.make_async_copy(
                normed.at[pl.ds(which * half, half)], region(0, which), local.at[1 + which]
            )
            copy.start()
            copies.append(copy)
        beside.forward((6, 7))
        spread.forward()
        spread.finish()
        beside.finish()
        collect.finish()
        for copy in copies:
            copy.wait()

    return call(
        middle_step, identity, (terms, x_all, gain, cotangent),
        (pl.ANY, pl.ANY, pltpu.VMEM, pl.ANY),
        (
            jax.ShapeDtypeStruct((total, model), BF16),
            jax.ShapeDtypeStruct((quarter, model), F32),
            jax.ShapeDtypeStruct((quarter, 128), F32),
            jax.ShapeDtypeStruct((total, model), BF16),
        ),
        (pl.ANY, pltpu.VMEM, pltpu.VMEM, pl.ANY),
        [
            pltpu.VMEM((quarter, model), BF16),
            pltpu.VMEM((quarter, model), BF16),
            pltpu.SemaphoreType.DMA((3,)),
        ]
        + SPREAD_SEMS
        + [pltpu.SemaphoreType.DMA((2,))]
        + SPREAD_SEMS
        + Collect.scratch(quarter, model),
        100_000_000_000,
    )


def middle_back(identity, terms, cot, middle, factor, gain):
    total, model = terms.shape
    quarter = total // 8
    half = quarter // 2

    def middle_back_step(
        terms_ref, cot_ref, middle_ref, factor_ref, gain_ref, out_ref, grad_ref, gain_grad_ref,
        cot_own, rounded, local, send, recv, *scratch
    ):
        greet()
        cot_copy = pltpu.make_async_copy(row_parts(cot_ref, quarter)(0), cot_own, local.at[0])
        cot_copy.start()
        collect = Collect(row_parts(terms_ref, quarter), quarter, *scratch[:6], scratch[6:])
        region = row_region(out_ref, quarter)
        spread = Spread(
            lambda which: rounded.at[pl.ds(which * half, half)], region, send, recv
        )
        collect.start()
        collect.first()
        collect.second()
        cot_copy.wait()
        gain_grad_ref[...] = jnp.zeros_like(gain_grad_ref)
        copies = []
        for which in range(2):
            collect.ready(which)

            def body(here):
                there = pl.ds(pl.multiple_of(which * half + here.start, 32), 32)
                grad_normed = collect.total(which, here)
                values = middle_ref[there]
                factor = factor_ref[there][:, :1]
                weighted = gain_ref[...] * grad_normed
                inner = jnp.mean(weighted * values, axis=1, keepdims=True)
                grad = (
                    cot_own[there].astype(F32)
                    + factor * weighted
                    - values * (factor * factor * factor * inner)
                )
                grad_ref[there] = grad
                rounded[there] = grad.astype(BF16)
                gain_grad_ref[...] += jnp.sum(grad_normed * values * factor, axis=0, keepdims=True)

            loop_rows(half, body)
            spread.start(which)
            copy = pltpu.make_async_copy(
                rounded.at[pl.ds(which * half, half)], region(0, which), local.at[1 + which]
            )
            copy.start()
            copies.append(copy)
        spread.forward()
        spread.finish()
        collect.finish()
        for copy in copies:
            copy.wait()

    return call(
        middle_back_step, identity, (terms, cot, middle, factor, gain),
        (pl.ANY, pl.ANY, pltpu.VMEM, pltpu.VMEM, pltpu.VMEM),
        (
            jax.ShapeDtypeStruct((total, model), BF16),
            jax.ShapeDtypeStruct((quarter, model), F32),
            jax.ShapeDtypeStruct((1, model), F32),
        ),
        (pl.ANY, pltpu.VMEM, pltpu.VMEM),
        [
            pltpu.VMEM((quarter, model), BF16),
            pltpu.VMEM((quarter, model), BF16),
            pltpu.SemaphoreType.DMA((3,)),
        ]
        + SPREAD_SEMS
        + Collect.scratch(quarter, model),
        70_000_000_000,
    )


def assemble(plan, flipped_out, totals, others, passed=()):
    count = len(totals)
    size = others[0].shape[0]
    shapes = []
    for index, pieces in enumerate(plan):
        wide = 2 * sum(piece[2] for piece in pieces)
        shapes.append((size, wide) if index < flipped_out else (wide, size))

    def assemble_grads(*refs):
        member = lax.rem(lax.axis_index("tok"), 2)
        outs = refs[2 * count + len(passed) :]
        for i in range(len(passed)):
            outs[len(plan) + i][...] = refs[2 * count + i][...]
        for index, pieces in enumerate(plan):
            half = sum(piece[2] for piece in pieces)
            for source, column, width, target in pieces:
                own_rows = pl.ds(pl.multiple_of(member * size, size), size)
                own = refs[source][own_rows, column : column + width]
                other = refs[count + source][:, column : column + width]
                for which, block in ((member, own), (1 - member, other)):
                    start = pl.multiple_of(which * half + target, 128)
                    if index < flipped_out:
                        outs[index][:, pl.ds(start, width)] = block.astype(F32)
                    else:
                        outs[index][pl.ds(start, width), :] = block.astype(F32).T

    return pl.pallas_call(
        assemble_grads,
        out_shape=[jax.ShapeDtypeStruct(shape, F32) for shape in shapes]
        + [jax.ShapeDtypeStruct(array.shape, array.dtype) for array in passed],
        in_specs=[pl.BlockSpec(memory_space=pltpu.VMEM)] * (2 * count + len(passed)),
        out_specs=[pl.BlockSpec(memory_space=pltpu.VMEM)] * (len(plan) + len(passed)),
        compiler_params=pltpu.CompilerParams(vmem_limit_bytes=VMEM),
        cost_estimate=pl.CostEstimate(
            flops=0, transcendentals=0, bytes_accessed=8 * size * 2 * sum(t.shape[1] for t in totals)
        ),
        name="assemble_grads",
    )(*totals, *others, *passed)


def input_terms(grad_packed, weights, x_all, gain, grad_middle, own):
    total, columns = grad_packed.shape
    model = x_all.shape[1]
    tile = grad_middle.shape[0]

    def input_terms_step(own_ref, grad_ref, qkv_ref, x_ref, gain_ref, middle_ref, out_ref, gain_grad_ref):
        step = pl.program_id(0)
        grad_normed = right_trans(grad_ref[...], qkv_ref[...])
        values = x_ref[...].astype(F32)
        factor = lax.rsqrt(jnp.mean(values * values, axis=1, keepdims=True) + EPSILON)
        weighted = grad_normed * gain_ref[...]
        inner = jnp.mean(weighted * values, axis=1, keepdims=True)
        terms = factor * weighted - values * (factor * factor * factor * inner)

        @pl.when(step == own_ref[0])
        def _():
            out_ref[...] = (terms + middle_ref[...]).astype(BF16)

        @pl.when(step != own_ref[0])
        def _():
            out_ref[...] = terms.astype(BF16)

        @pl.when(step == 0)
        def _():
            gain_grad_ref[...] = jnp.zeros_like(gain_grad_ref)

        gain_grad_ref[...] += jnp.sum(grad_normed * values * factor, axis=0, keepdims=True)

    return pl.pallas_call(
        input_terms_step,
        grid_spec=pltpu.PrefetchScalarGridSpec(
            num_scalar_prefetch=1,
            grid=(total // tile,),
            in_specs=[
                pl.BlockSpec((tile, columns), lambda i, own: (i, 0)),
                pl.BlockSpec((model, columns), lambda i, own: (0, 0)),
                pl.BlockSpec((tile, model), lambda i, own: (i, 0)),
                pl.BlockSpec((1, model), lambda i, own: (0, 0)),
                pl.BlockSpec((tile, model), lambda i, own: (0, 0)),
            ],
            out_specs=[
                pl.BlockSpec((tile, model), lambda i, own: (i, 0)),
                pl.BlockSpec((1, model), lambda i, own: (0, 0)),
            ],
        ),
        out_shape=[
            jax.ShapeDtypeStruct((total, model), BF16),
            jax.ShapeDtypeStruct((1, model), F32),
        ],
        compiler_params=pltpu.CompilerParams(vmem_limit_bytes=VMEM),
        cost_estimate=pl.CostEstimate(
            flops=2 * total * columns * model,
            transcendentals=total,
            bytes_accessed=6 * total * model,
        ),
        name="input_terms",
    )(own, grad_packed, weights, x_all, gain, grad_middle)


def feed_forward(normed, cot, weights, chunk):
    total, model = normed.shape
    tile = 512
    part = 256 if chunk % 256 == 0 else 128

    def feed_step(normed_ref, cot_ref, gate_ref, up_ref, down_ref, hidden_ref, grads_ref):
        for left in range(0, chunk, part):
            here = slice(left, left + part)
            gate = product(normed_ref[...], gate_ref[:, here])
            upward = product(normed_ref[...], up_ref[:, here])
            grad_hidden = product(cot_ref[...], down_ref[:, here])
            sigma = jax.nn.sigmoid(gate)
            active = gate * sigma
            hidden_ref[:, here] = (active * upward).astype(BF16)
            grads_ref[:, here] = (
                grad_hidden * upward * (sigma + active * (1.0 - sigma))
            ).astype(BF16)
            grads_ref[:, chunk + left : chunk + left + part] = (grad_hidden * active).astype(BF16)

    rows = pl.BlockSpec((tile, model), lambda i: (i, 0))

    def weight(part):
        return pl.BlockSpec((model, chunk), lambda i: (0, part), pipeline_mode=pl.Buffered(1))

    return pl.pallas_call(
        feed_step,
        grid=(total // tile,),
        in_specs=[rows, rows, weight(0), weight(1), weight(2)],
        out_specs=[
            pl.BlockSpec((tile, chunk), lambda i: (i, 0)),
            pl.BlockSpec((tile, 2 * chunk), lambda i: (i, 0)),
        ],
        out_shape=[
            jax.ShapeDtypeStruct((total, chunk), BF16),
            jax.ShapeDtypeStruct((total, 2 * chunk), BF16),
        ],
        compiler_params=pltpu.CompilerParams(vmem_limit_bytes=VMEM),
        cost_estimate=pl.CostEstimate(
            flops=6 * total * chunk * model,
            transcendentals=total * chunk,
            bytes_accessed=4 * total * model + 6 * chunk * (model + total),
        ),
        name="feed_forward",
    )(normed, cot, weights, weights, weights)


def columns_back(lefts, weights, place, own, base=None, middle=None):
    count = len(lefts)
    total = lefts[0].shape[0]
    model = weights[0].shape[0]
    tile, part = 512, 512

    def columns_step(own_ref, *refs):
        out_ref = refs[-1]
        for start in range(0, model, part):
            here = slice(start, start + part)
            value = sum(
                right_trans(refs[i][...], refs[count + i][here, :]) for i in range(count)
            )
            if base is not None:
                value = value + refs[2 * count][:, here].astype(F32)
            out_ref[:, here] = value.astype(BF16)
        if middle is not None:
            middle_ref = refs[-2]
            size = middle_ref.shape[0]
            inside = own_ref[0] * size - pl.program_id(0) * tile

            @pl.when((inside >= 0) & (inside < tile))
            def _():
                rows = pl.ds(pl.multiple_of(inside, size), size)
                out_ref[rows, :] = (out_ref[rows, :].astype(F32) + middle_ref[...]).astype(BF16)

    in_specs = [pl.BlockSpec((tile, left.shape[1]), lambda i, own: (i, 0)) for left in lefts]
    in_specs += [
        pl.BlockSpec(
            (model, left.shape[1]), lambda i, own: (0, place), pipeline_mode=pl.Buffered(1)
        )
        for left in lefts
    ]
    operands = [own, *lefts, *weights]
    if base is not None:
        in_specs.append(pl.BlockSpec((tile, model), lambda i, own: (i, 0)))
        operands.append(base)
    if middle is not None:
        in_specs.append(pl.BlockSpec(middle.shape, lambda i, own: (0, 0)))
        operands.append(middle)
    inner = sum(left.shape[1] for left in lefts)
    return pl.pallas_call(
        columns_step,
        grid_spec=pltpu.PrefetchScalarGridSpec(
            num_scalar_prefetch=1,
            grid=(total // tile,),
            in_specs=in_specs,
            out_specs=pl.BlockSpec((tile, model), lambda i, own: (i, 0)),
        ),
        out_shape=jax.ShapeDtypeStruct((total, model), BF16),
        compiler_params=pltpu.CompilerParams(vmem_limit_bytes=VMEM),
        cost_estimate=pl.CostEstimate(
            flops=2 * total * model * inner,
            transcendentals=0,
            bytes_accessed=2 * total * model + 2 * (total + model) * inner,
        ),
        name="columns_back",
    )(*operands)


def weight_terms(pairs, tile=256):
    rows, model = pairs[0][0].shape
    count = len(pairs)
    widths = [right.shape[1] for _, right in pairs]

    def terms_step(*refs):
        out_ref = refs[-1]
        start = 0
        for i, width in enumerate(widths):
            out_ref[:, start : start + width] = left_trans(refs[i][...], refs[count + i][...]).astype(
                BF16
            )
            start += width

    return pl.pallas_call(
        terms_step,
        grid=(model // tile,),
        in_specs=[pl.BlockSpec((rows, tile), lambda i: (0, i))] * count
        + [
            pl.BlockSpec((rows, width), lambda i: (0, 0), pipeline_mode=pl.Buffered(1))
            for width in widths
        ],
        out_specs=pl.BlockSpec((tile, sum(widths)), lambda i: (i, 0)),
        out_shape=jax.ShapeDtypeStruct((model, sum(widths)), BF16),
        compiler_params=pltpu.CompilerParams(vmem_limit_bytes=VMEM),
        cost_estimate=pl.CostEstimate(
            flops=2 * rows * model * sum(widths),
            transcendentals=0,
            bytes_accessed=2 * (rows * model * count + (rows + model) * sum(widths)),
        ),
        name="weight_terms",
    )(*[left for left, _ in pairs], *[right for _, right in pairs])


def program(
    tok_size,
    tokens, gain_attn, w_query, w_key, w_value, w_out, gain_ffn, w_gate, w_up, w_down, cotangent
):
    token = lax.axis_index("tok")
    feat = lax.axis_index("feat")
    member = token % 2
    rows, wide = tokens.shape
    model = 4 * wide
    quarter = rows // 4
    groups = [list(range(i, tok_size, 2)) for i in range(2)]
    pair_width = 2 * HD

    def swap(value):
        return lax.ppermute(value, "tok", [(i, i ^ 1) for i in range(tok_size)])

    def ring_gather(shard):
        return lax.all_gather(shard, "tok", axis=0, tiled=True, axis_index_groups=groups)

    def ring_scatter(terms):
        return lax.psum_scatter(
            terms, "tok", scatter_dimension=0, tiled=True, axis_index_groups=groups
        )

    def other_half(total):
        size = total.shape[0] // 2
        return swap(lax.dynamic_slice_in_dim(total, (1 - member) * size, size, 0))

    heads_wide = w_query.shape[1] // 2
    hidden_wide = w_gate.shape[1] // 2
    chunks = [hidden_wide * part // sum(CHUNKS) for part in CHUNKS]
    lefts = [sum(chunks[:c]) for c in range(len(chunks))]
    attention_pieces = [
        (part, left, pair_width, 3 * left + part * pair_width)
        for left in range(0, heads_wide, pair_width)
        for part in range(3)
    ]
    ring = tok_size // 2
    early = 1
    out_blocks = [w_out.T]
    attention_start, block = swap_first(
        0, (w_query, w_key, w_value), attention_pieces, ring, out_blocks[0], early
    )
    out_blocks.append(block)
    feed = (w_gate, w_up, w_down.T)
    tokens_after, attention_start = lax.optimization_barrier((tokens, attention_start))
    qkv = ring_gather(attention_start)
    plans = [
        [(part, left, size, part * size) for part in range(3)] for left, size in zip(lefts, chunks)
    ]
    first_start, x_all, block, gains = swap_and_gather(
        1,
        feed,
        plans[0],
        tokens_after,
        ring,
        out_blocks[-1],
        ring - 1 - early,
        jnp.stack([gain_attn, gain_ffn]),
    )
    gain_one, gain_two = gains[:1], gains[1:]
    out_blocks.append(block)
    feed_weights = [ring_gather(first_start)]
    w_gate, x_all = lax.optimization_barrier((w_gate, x_all))
    last_start, out_proj = swap_pairs(2, (w_gate, *feed[1:]), plans[1], ring, out_blocks)
    feed_weights.append(ring_gather(last_start))

    x_wide = x_all.astype(F32)
    factor_one = lax.rsqrt(jnp.mean(x_wide * x_wide, axis=1, keepdims=True) + EPSILON)
    normed = (x_wide * factor_one * gain_one).astype(BF16)
    packed = product(normed, qkv).astype(BF16)
    attended, log_sums = attend(packed)
    normed_two, middle, factor_two, cot_rows = middle_norm(
        3, right_trans(attended, out_proj).astype(BF16), x_all, gain_two, cotangent
    )

    own = (member * 4 + feat).astype(jnp.int32).reshape(1)
    feed_sums = []
    grad_normed_two = out_rows = None

    hiddens = []
    for c in range(len(chunks)):
        if c:
            feed_weights[c], grad_normed_two = lax.optimization_barrier(
                (feed_weights[c], grad_normed_two)
            )
        hidden, grad_both = feed_forward(normed_two, cot_rows, feed_weights[c], chunks[c])
        hiddens.append(hidden)
        if c + 1 < len(chunks):
            feed_terms = weight_terms([(normed_two, grad_both), (cot_rows, hidden)])
            feed_terms, grad_both = lax.optimization_barrier((feed_terms, grad_both))
            feed_sums.append(ring_scatter(feed_terms))
        grad_normed_two = columns_back(
            [grad_both], [feed_weights[c]], 0, own, grad_normed_two
        )
    grad_mid_rows, grad_middle, gain_ffn_part = middle_back(
        4, grad_normed_two, cot_rows, middle, factor_two, gain_two
    )

    hidden, grad_both, grad_mid_rows = lax.optimization_barrier((hidden, grad_both, grad_mid_rows))
    feed_terms = weight_terms(
        [(normed_two, grad_both), (cot_rows, hidden), (grad_mid_rows, attended)]
    )
    grad_mid_rows, feed_terms = lax.optimization_barrier((grad_mid_rows, feed_terms))
    feed_sums.append(ring_scatter(feed_terms))

    grad_attended = product(grad_mid_rows, out_proj).astype(BF16)
    grad_packed = attend_back(packed, attended, grad_attended, log_sums)
    attention_terms = left_trans(normed, grad_packed).astype(BF16)
    attention_terms, grad_packed = lax.optimization_barrier((attention_terms, grad_packed))
    attention_sum = ring_scatter(attention_terms)
    terms, gain_attn_part = input_terms(grad_packed, qkv, x_all, gain_one, grad_middle, own)
    hiddens[0], terms, feed_sums[0] = lax.optimization_barrier((hiddens[0], terms, feed_sums[0]))
    out_rows = columns_back(hiddens, feed_weights, 2, own, None, middle)
    outcome, input_grad, gain_grads = scatter_blocks(
        5, tok_size // 2, jnp.concatenate([gain_attn_part, gain_ffn_part]), out_rows, terms
    )
    feed_others = [other_half(feed_sums[0])]
    outcome, feed_sums[1] = lax.optimization_barrier((outcome, feed_sums[1]))
    feed_others.append(other_half(feed_sums[1]))
    feed_others[1], attention_sum = lax.optimization_barrier((feed_others[1], attention_sum))
    feed_plan = [
        [(c, part * chunks[c], chunks[c], lefts[c]) for c in range(len(chunks))]
        for part in range(3)
    ]
    feed_plan.append([(len(chunks) - 1, 3 * chunks[-1], heads_wide, 0)])
    gate_grad, up_grad, down_grad, out_grad, outcome, input_grad = assemble(
        feed_plan, 2, feed_sums, feed_others, (outcome, input_grad)
    )
    attention_plan = [
        [
            (0, 3 * left + part * pair_width, pair_width, left)
            for left in range(0, heads_wide, pair_width)
        ]
        for part in range(3)
    ]
    attention_other = other_half(attention_sum)
    attention_other, gate_grad, up_grad, down_grad, outcome, input_grad = lax.optimization_barrier(
        (attention_other, gate_grad, up_grad, down_grad, outcome, input_grad)
    )
    part_grads = assemble(attention_plan, 3, [attention_sum], [attention_other])
    return (
        outcome,
        input_grad,
        gain_grads[0],
        gain_grads[1],
        *part_grads,
        out_grad,
        gate_grad,
        up_grad,
        down_grad,
    )


def solution(mesh):
    in_specs = (
        P("tok", "feat"),
        P("feat"),
        P("tok", "feat"),
        P("tok", "feat"),
        P("tok", "feat"),
        P("feat", "tok"),
        P("feat"),
        P("tok", "feat"),
        P("tok", "feat"),
        P("feat", "tok"),
        P("tok", "feat"),
    )
    out_specs = (
        P("tok", "feat"),
        P("tok", "feat"),
        P("feat"),
        P("feat"),
        P("tok", "feat"),
        P("tok", "feat"),
        P("tok", "feat"),
        P("feat", "tok"),
        P("tok", "feat"),
        P("tok", "feat"),
        P("feat", "tok"),
    )

    def on_device(*arrays):
        return program(mesh.shape["tok"], *arrays)

    return jax.shard_map(
        on_device, mesh=mesh, in_specs=in_specs, out_specs=out_specs, check_vma=False
    )
```

```python
import jax
import jax.numpy as jnp
from jax import lax
from jax.experimental import pallas as pl
from jax.experimental.pallas import tpu as pltpu
from jax.sharding import PartitionSpec as P

HD = 64
LEN = 1024
EPSILON = 1e-05
BF16 = jnp.bfloat16
F32 = jnp.float32
MESH = pl.DeviceIdType.MESH
VMEM = 48 << 20
FORWARD_BLOCK = 512
BACK_BLOCK = 256
CHUNKS = (3, 1)


def left_trans(left, right):
    return lax.dot_general(
        left, right, (((0,), (0,)), ((), ())), preferred_element_type=F32
    )


def right_trans(left, right):
    return lax.dot_general(
        left, right, (((1,), (1,)), ((), ())), preferred_element_type=F32
    )


def product(left, right):
    return jnp.dot(left, right, preferred_element_type=F32)


def causal_tile(scores):
    size = scores.shape[0]
    key = lax.broadcasted_iota(jnp.int32, scores.shape, 0)
    query = lax.broadcasted_iota(jnp.int32, scores.shape, 1)
    return jnp.where(key <= query, scores, -1e30)


def head_parts(packed_ref, head, width):
    columns = [slice(part * width + head * HD, part * width + (head + 1) * HD) for part in range(3)]
    query, key, value = [packed_ref[:, part] for part in columns]
    return query * HD ** (-0.5), key, value


def attend_kernel(packed_ref, out_ref, lse_ref):
    width = out_ref.shape[1]
    for head in range(width // HD):
        query, key, value = head_parts(packed_ref, head, width)
        query = query.astype(BF16)
        value_t = value.T
        for top in range(0, LEN, FORWARD_BLOCK):
            keys = top + FORWARD_BLOCK
            scores = right_trans(key[:keys], query[top:keys])
            last = causal_tile(scores[top:])
            scores = jnp.concatenate([scores[:top], last]) if top else last
            highest = jnp.max(scores, axis=0, keepdims=True)
            exponent = jnp.exp(scores - highest)
            total = jnp.sum(exponent, axis=0, keepdims=True)
            mixed = product(value_t[:, :keys], exponent.astype(BF16)) / total
            out_ref[top:keys, head * HD : (head + 1) * HD] = mixed.T.astype(BF16)
            lse_ref[0, 0, head : head + 1, top:keys] = highest + jnp.log(total)


def attend_back_kernel(packed_ref, out_ref, grad_ref, lse_ref, grads_ref, key_acc, value_acc):
    width = out_ref.shape[1]
    for head in range(width // HD):
        lanes = slice(head * HD, (head + 1) * HD)
        query, key, value = head_parts(packed_ref, head, width)
        query = query.astype(BF16)
        key_t = key.T
        grad = grad_ref[:, lanes]
        inner = (out_ref[:, lanes].astype(F32) * grad.astype(F32)).T
        inner = jnp.sum(inner, axis=0, keepdims=True)
        for top in reversed(range(0, LEN, BACK_BLOCK)):
            keys = top + BACK_BLOCK
            scores = right_trans(key[:keys], query[top:keys])
            last = causal_tile(scores[top:])
            scores = jnp.concatenate([scores[:top], last]) if top else last
            probs = jnp.exp(scores - lse_ref[0, 0, head : head + 1, top:keys])
            grad_probs = right_trans(value[:keys], grad[top:keys])
            grad_scores = (probs * (grad_probs - inner[:, top:keys])).astype(BF16)
            value_term = product(probs.astype(BF16), grad[top:keys])
            key_term = product(grad_scores, query[top:keys])
            if keys == LEN:
                value_acc[...] = value_term
                key_acc[...] = key_term
            else:
                value_acc[:keys] += value_term
                key_acc[:keys] += key_term
            grad_query = product(key_t[:, :keys], grad_scores) * HD ** (-0.5)
            grads_ref[top:keys, lanes] = grad_query.T.astype(BF16)
        grads_ref[:, width + head * HD : width + (head + 1) * HD] = key_acc[...].astype(BF16)
        grads_ref[:, 2 * width + head * HD : 2 * width + (head + 1) * HD] = value_acc[...].astype(
            BF16
        )


def attend(packed):
    rows, columns = packed.shape
    width = 2 * HD
    sequences, pairs = rows // LEN, columns // (3 * width)
    return pl.pallas_call(
        attend_kernel,
        grid=(sequences, pairs),
        out_shape=(
            jax.ShapeDtypeStruct((rows, pairs * width), BF16),
            jax.ShapeDtypeStruct((sequences, pairs, 2, LEN), F32),
        ),
        in_specs=[pl.BlockSpec((LEN, 3 * width), lambda s, p: (s, p))],
        out_specs=(
            pl.BlockSpec((LEN, width), lambda s, p: (s, p)),
            pl.BlockSpec((1, 1, 2, LEN), lambda s, p: (s, p, 0, 0)),
        ),
        compiler_params=pltpu.CompilerParams(vmem_limit_bytes=VMEM),
        cost_estimate=pl.CostEstimate(
            flops=4 * rows * LEN * pairs * width // 2,
            transcendentals=rows * LEN * pairs,
            bytes_accessed=2 * rows * columns * 2,
        ),
        name="attend",
    )(packed)


def attend_back(packed, attended, grad_attended, lse):
    rows, columns = packed.shape
    width = 2 * HD
    sequences, pairs = rows // LEN, columns // (3 * width)
    narrow = pl.BlockSpec((LEN, width), lambda s, p: (s, p))
    return pl.pallas_call(
        attend_back_kernel,
        grid=(sequences, pairs),
        out_shape=jax.ShapeDtypeStruct((rows, columns), BF16),
        in_specs=[
            pl.BlockSpec((LEN, 3 * width), lambda s, p: (s, p)),
            narrow,
            narrow,
            pl.BlockSpec((1, 1, 2, LEN), lambda s, p: (s, p, 0, 0)),
        ],
        out_specs=pl.BlockSpec((LEN, 3 * width), lambda s, p: (s, p)),
        scratch_shapes=[pltpu.VMEM((LEN, HD), F32)] * 2,
        compiler_params=pltpu.CompilerParams(vmem_limit_bytes=VMEM),
        cost_estimate=pl.CostEstimate(
            flops=10 * rows * LEN * pairs * width // 2,
            transcendentals=rows * LEN * pairs,
            bytes_accessed=3 * rows * columns * 2,
        ),
        name="attend_back",
    )(packed, attended, grad_attended, lse)


SPREAD = (
    (0, 0, "y", None),
    (0, 1, "x", None),
    (0, 0, "x", None),
    (0, 1, "y", None),
    (0, 0, "core", None),
    (0, 1, "core", None),
    (4, 0, "x", 0),
    (2, 1, "y", 1),
    (4, 0, "core", 0),
    (2, 1, "core", 1),
    (2, 0, "core", 2),
    (4, 1, "core", 3),
    (6, 0, "core", 6),
    (6, 1, "core", 7),
)
BIT = {"y": 4, "x": 2, "core": 1}


def neighbours():
    token, feat = lax.axis_index("tok"), lax.axis_index("feat")
    return {
        "y": (token + 1 - 2 * lax.rem(token, 2), feat),
        "x": (token, lax.rem(feat + 2, 4)),
        "core": (token, feat + 1 - 2 * lax.rem(feat, 2)),
    }


def owner(r):
    member, slot = lax.rem(lax.axis_index("tok"), 2), lax.axis_index("feat")
    if r & 4:
        member = 1 - member
    if r & 2:
        slot = lax.rem(slot + 2, 4)
    if r & 1:
        slot = slot + 1 - 2 * lax.rem(slot, 2)
    return member, slot


def greet(others=()):
    barrier = pltpu.get_barrier_semaphore()
    peers = [*neighbours().values(), *others]
    for peer in peers:
        pl.semaphore_signal(barrier, inc=1, device_id=peer, device_id_type=MESH)
    pl.semaphore_wait(barrier, len(peers))


def ring_peer(ring, distance):
    token = lax.axis_index("tok")
    return lax.rem(token + 2 * distance, 2 * ring), lax.axis_index("feat")


class SumAll:
    def __init__(self, ring, ref, steps, arrived, slots, send, recv):
        self.ring, self.ref = ring, ref
        self.steps, self.arrived, self.slots = steps, arrived, slots
        self.send, self.recv = send, recv
        self.place = lax.div(lax.axis_index("tok"), 2)
        self.peers = neighbours()

    @staticmethod
    def scratch(ring, shape):
        return [
            pltpu.VMEM((3, *shape), F32),
            pltpu.VMEM((3, *shape), F32),
            pltpu.VMEM((ring, *shape), F32),
            pltpu.SemaphoreType.DMA((2 + ring,)),
            pltpu.SemaphoreType.DMA((2 + ring,)),
        ]

    def copy(self, k):
        if k < 3:
            source = self.ref if k == 0 else self.steps.at[k - 1]
            target, peer = self.arrived.at[k], self.peers[("core", "x", "y")[k]]
        else:
            source, target = self.steps.at[2], self.slots.at[self.place]
            peer = ring_peer(self.ring, k - 2)
        return pltpu.make_async_remote_copy(
            source, target, self.send.at[k], self.recv.at[k],
            device_id=peer, device_id_type=MESH,
        )

    def start(self):
        self.copy(0).start()

    def step(self, k):
        self.copy(k).wait_recv()
        before = self.ref[...] if k == 0 else self.steps[k - 1]
        self.steps[k] = before + self.arrived[k]
        if k < 2:
            self.copy(k + 1).start()
        else:
            for distance in range(1, self.ring):
                self.copy(2 + distance).start()
            self.slots[self.place] = self.steps[2]

    def finish(self):
        for distance in range(1, self.ring):
            source = lax.rem(self.place + self.ring - distance, self.ring)
            k = 2 + distance
            pltpu.make_async_remote_copy(
                self.slots.at[source], self.slots.at[source], self.send.at[k], self.recv.at[k],
                device_id=ring_peer(self.ring, distance), device_id_type=MESH,
            ).wait_recv()
        for k in range(2 + self.ring):
            self.copy(k).wait_send()
        total = self.slots[0]
        for place in range(1, self.ring):
            total = total + self.slots[place]
        return total


class Spread:
    def __init__(self, own, region, send, recv):
        self.own, self.region, self.send, self.recv = own, region, send, recv
        self.peers = neighbours()

    def copy(self, k):
        r, half, way, _ = SPREAD[k]
        source = self.own(half) if r == 0 else self.region(r, half)
        return pltpu.make_async_remote_copy(
            source, self.region(r, half), self.send.at[k], self.recv.at[k],
            device_id=self.peers[way], device_id_type=MESH,
        )

    def arrival(self, k):
        r, half, way, _ = SPREAD[k]
        place = self.region(r ^ BIT[way], half)
        return pltpu.make_async_remote_copy(
            place, place, self.send.at[k], self.recv.at[k],
            device_id=self.peers[way], device_id_type=MESH,
        )

    def start(self, half):
        for k, (r, which, _, after) in enumerate(SPREAD):
            if after is None and which == half:
                self.copy(k).start()

    def forward(self, arrivals=(0, 1, 2, 3, 6, 7)):
        for first in arrivals:
            self.arrival(first).wait_recv()
            for k, (_, _, _, after) in enumerate(SPREAD):
                if after == first:
                    self.copy(k).start()

    def finish(self):
        for k, (_, _, way, _) in enumerate(SPREAD):
            if way == "core":
                self.arrival(k).wait_recv()
        for k in range(len(SPREAD)):
            self.copy(k).wait_send()


SPREAD_SEMS = [pltpu.SemaphoreType.DMA((len(SPREAD),))] * 2


def block_spread(shard_ref, out_ref, local, send, recv):
    rows, wide = shard_ref.shape
    half = rows // 2

    def own(which):
        return shard_ref.at[pl.ds(which * half, half)]

    def region(r, which):
        member, slot = owner(r)
        return out_ref.at[
            pl.ds(pl.multiple_of(member * rows + which * half, half), half),
            pl.ds(pl.multiple_of(slot * wide, wide), wide),
        ]

    copies = [
        pltpu.make_async_copy(own(which), region(0, which), local.at[which]) for which in range(2)
    ]
    return Spread(own, region, send, recv), copies


class Collect:
    def __init__(self, part, size, parts, near, from_x, from_y, last_y, last_x, sems):
        self.part, self.size, self.half = part, size, size // 2
        self.parts, self.near = parts, near
        self.from_x, self.from_y, self.last_y, self.last_x = from_x, from_y, last_y, last_x
        self.load, self.send, self.recv = sems
        self.peers = neighbours()

    @staticmethod
    def scratch(size, columns):
        half = size // 2
        return [
            pltpu.VMEM((4, size, columns), BF16),
            pltpu.VMEM((4, size, columns), BF16),
            pltpu.VMEM((2, half, columns), BF16),
            pltpu.VMEM((2, half, columns), BF16),
            pltpu.VMEM((half, columns), BF16),
            pltpu.VMEM((half, columns), BF16),
            pltpu.SemaphoreType.DMA((4,)),
            pltpu.SemaphoreType.DMA((10,)),
            pltpu.SemaphoreType.DMA((10,)),
        ]

    def remote(self, k, source, target, way):
        return pltpu.make_async_remote_copy(
            source, target, self.send.at[k], self.recv.at[k],
            device_id=self.peers[way], device_id_type=MESH,
        )

    def copy(self, k):
        low, high = pl.ds(0, self.half), pl.ds(self.half, self.half)
        if k < 4:
            return self.remote(k, self.part(2 * k + 1), self.near.at[k], "core")
        if k < 6:
            return self.remote(k, self.parts.at[(1, 3)[k - 4], low], self.from_x.at[k - 4], "x")
        if k < 8:
            return self.remote(k, self.parts.at[(2, 3)[k - 6], high], self.from_y.at[k - 6], "y")
        if k == 8:
            return self.remote(k, self.parts.at[2, low], self.last_y, "y")
        return self.remote(k, self.parts.at[1, high], self.last_x, "x")

    def add(self, index, start, count, other):
        step = 32

        def body(i, carry):
            here = pl.ds(pl.multiple_of(start + i * step, step), step)
            there = pl.ds(pl.multiple_of(i * step, step), step)
            total = self.parts[index, here].astype(F32) + other[there].astype(F32)
            self.parts[index, here] = total.astype(BF16)
            return carry

        lax.fori_loop(0, count // step, body, 0)

    def loads(self, k):
        return pltpu.make_async_copy(self.part(2 * k), self.parts.at[k], self.load.at[k])

    def start(self):
        for k in (3, 1, 2, 0):
            self.copy(k).start()
        for k in (3, 1, 2, 0):
            self.loads(k).start()

    def first(self):
        for k, following in ((3, (5, 7)), (1, (4,)), (2, (6,)), (0, ())):
            self.loads(k).wait()
            self.copy(k).wait_recv()
            self.add(k, 0, self.size, self.near.at[k])
            for after in following:
                self.copy(after).start()

    def second(self):
        self.copy(5).wait_recv()
        self.add(2, 0, self.half, self.from_x.at[1])
        self.copy(8).start()
        self.copy(7).wait_recv()
        self.add(1, self.half, self.half, self.from_y.at[1])
        self.copy(9).start()

    def total(self, half, rows):
        first, last = (self.from_x, self.last_y) if half == 0 else (self.from_y, self.last_x)
        own = self.parts[0, pl.ds(pl.multiple_of(half * self.half + rows.start, 32), rows.size)]
        return own.astype(F32) + first[0, rows].astype(F32) + last[rows].astype(F32)

    def ready(self, half):
        for k in ((4, 8) if half == 0 else (6, 9)):
            self.copy(k).wait_recv()

    def finish(self):
        for k in range(10):
            self.copy(k).wait_send()


def loop_rows(count, body):
    def step(i, carry):
        body(pl.ds(pl.multiple_of(i * 32, 32), 32))
        return carry

    lax.fori_loop(0, count // 32, step, 0)


def call(kernel, identity, operands, spaces, outputs, out_spaces, scratch, cost):
    return pl.pallas_call(
        kernel,
        out_shape=outputs,
        in_specs=[pl.BlockSpec(memory_space=space) for space in spaces],
        out_specs=jax.tree.map(lambda space: pl.BlockSpec(memory_space=space), out_spaces),
        scratch_shapes=scratch,
        compiler_params=pltpu.CompilerParams(
            collective_id=identity, has_side_effects=True, vmem_limit_bytes=VMEM
        ),
        cost_estimate=pl.CostEstimate(flops=cost, bytes_accessed=cost // 100, transcendentals=0),
        name=kernel.__name__,
    )(*operands)


class RingBlocks:
    def __init__(self, ring, source, out_ref, send, recv):
        self.ring, self.source, self.out, self.send, self.recv = ring, source, out_ref, send, recv
        self.count = out_ref.shape[0]
        self.stage = 0

    def copy(self, k):
        source = self.source if k == 0 else self.out.at[k - 1]
        return pltpu.make_async_remote_copy(
            source, self.out.at[k], self.send.at[k], self.recv.at[k],
            device_id=ring_peer(self.ring, 1), device_id_type=MESH,
        )

    def start(self):
        self.copy(0).start()

    def advance(self):
        if self.stage + 1 < self.count:
            self.copy(self.stage).wait_recv()
            self.stage += 1
            self.copy(self.stage).start()

    def finish(self):
        while self.stage + 1 < self.count:
            self.advance()
        self.copy(self.count - 1).wait_recv()
        for k in range(self.count):
            self.copy(k).wait_send()


class RowsSwap:
    def __init__(self, ring, blocks, out_ref, local, send, recv):
        self.ring, self.blocks, self.out = ring, blocks, out_ref
        self.local, self.send, self.recv = local, send, recv
        token = lax.axis_index("tok")
        self.place, self.member = lax.div(token, 2), lax.rem(token, 2)
        self.peer = neighbours()["y"]

    def block(self, s, half):
        width = self.out.shape[1]
        return self.blocks[s].at[:, pl.ds(pl.multiple_of(half * width, width), width)]

    def target(self, s, member):
        size = self.out.shape[0] // self.ring // 2
        place = lax.rem(self.place + self.ring - s, self.ring)
        return self.out.at[pl.ds(pl.multiple_of((2 * place + member) * size, size), size)]

    def remote(self, s, source, member):
        return pltpu.make_async_remote_copy(
            source, self.target(s, member), self.send.at[s], self.recv.at[s],
            device_id=self.peer, device_id_type=MESH,
        )

    def own(self, s):
        return pltpu.make_async_copy(
            self.block(s, self.member), self.target(s, self.member), self.local.at[s]
        )

    def away(self, s):
        return self.remote(s, self.block(s, 1 - self.member), self.member)

    def start(self):
        for s in range(self.ring):
            self.away(s).start()
        for s in range(self.ring):
            self.own(s).start()

    def finish(self):
        for s in range(self.ring):
            other = 1 - self.member
            self.remote(s, self.target(s, other), other).wait_recv()
            self.away(s).wait_send()
            self.own(s).wait()


class PairSwap:
    def __init__(self, sources, out_ref, pieces, local, send, recv):
        self.sources, self.out, self.pieces = sources, out_ref, pieces
        self.local, self.send, self.recv = local, send, recv
        self.peer = neighbours()["y"]
        self.member = lax.rem(lax.axis_index("tok"), 2)

    def block(self, i, half):
        source, start, width, _ = self.pieces[i]
        ref = self.sources[source]
        offset = half * (ref.shape[1] // 2) + start
        return ref.at[:, pl.ds(pl.multiple_of(offset, 128), width)]

    def place(self, i, member):
        _, _, width, column = self.pieces[i]
        rows = self.out.shape[0] // 2
        return self.out.at[pl.ds(pl.multiple_of(member * rows, rows), rows), pl.ds(column, width)]

    def remote(self, i, source, member):
        return pltpu.make_async_remote_copy(
            source, self.place(i, member), self.send.at[i], self.recv.at[i],
            device_id=self.peer, device_id_type=MESH,
        )

    def own(self, i):
        return pltpu.make_async_copy(
            self.block(i, self.member), self.place(i, self.member), self.local.at[i]
        )

    def away(self, i):
        return self.remote(i, self.block(i, 1 - self.member), self.member)

    def start(self):
        for i in range(len(self.pieces)):
            self.away(i).start()
        for i in range(len(self.pieces)):
            self.own(i).start()

    def finish(self):
        for i in range(len(self.pieces)):
            other = 1 - self.member
            self.remote(i, self.place(i, other), other).wait_recv()
            self.away(i).wait_send()
            self.own(i).wait()


def swap_ring(identity, weights, pieces, ring, block, count):
    size = weights[0].shape[0]
    outputs = [
        jax.ShapeDtypeStruct((2 * size, sum(piece[2] for piece in pieces)), weights[0].dtype),
        jax.ShapeDtypeStruct((count, *block.shape[-2:]), block.dtype),
    ]

    def swap_start(*refs):
        sources, (block_ref, start_ref, blocks_ref, *sems) = refs[: len(weights)], refs[len(weights) :]
        greet([ring_peer(ring, 1), ring_peer(ring, ring - 1)])
        if len(block.shape) == 3:
            block_ref = block_ref.at[block.shape[0] - 1]
        around = RingBlocks(ring, block_ref, blocks_ref, *sems[3:])
        pair = PairSwap(sources, start_ref, pieces, *sems[:3])
        around.start()
        pair.start()
        around.finish()
        pair.finish()

    operands = (*weights, block)
    return call(
        swap_start, identity, operands, (pl.ANY,) * len(operands),
        outputs, [pl.ANY] * len(outputs),
        [pltpu.SemaphoreType.DMA((len(pieces),))] * 3 + [pltpu.SemaphoreType.DMA((count,))] * 2,
        15_000_000_000,
    )


def swap_and_gather(identity, weights, pieces, shard, ring, blocks, small):
    count = len(weights)
    size = weights[0].shape[0]
    columns = sum(piece[2] for piece in pieces)
    rows, wide = shard.shape
    operands = (*weights, shard, *blocks, small)
    small_rows, small_wide = small.shape
    block_size, block_wide = blocks[0].shape[-2:]
    outputs = [
        jax.ShapeDtypeStruct((2 * size, columns), weights[0].dtype),
        jax.ShapeDtypeStruct((2 * rows, 4 * wide), shard.dtype),
        jax.ShapeDtypeStruct((2 * ring * block_size, block_wide // 2), shard.dtype),
        jax.ShapeDtypeStruct((small_rows, 4 * small_wide), small.dtype),
    ]

    def swap_gather(*refs):
        sources, shard_ref = refs[:count], refs[count]
        block_refs = refs[count + 1 : count + 1 + len(blocks)]
        small_ref, start_ref, out_ref, around_ref, whole_ref, *sems = refs[
            count + 1 + len(blocks) :
        ]
        small_send, small_recv = sems[9:]
        greet()

        def small_place(r):
            _, slot = owner(r)
            return whole_ref.at[:, pl.ds(pl.multiple_of(slot * small_wide, small_wide), small_wide)]

        def small_copy(k, source, place):
            return pltpu.make_async_remote_copy(
                source, place, small_send.at[k], small_recv.at[k],
                device_id=neighbours()[("core", "x", "core")[k]], device_id_type=MESH,
            )

        small_copies = [
            small_copy(0, small_ref, small_place(0)),
            small_copy(1, small_ref, small_place(0)),
            small_copy(2, small_place(2), small_place(2)),
        ]
        small_copies[0].start()
        small_copies[1].start()
        spread, copies = block_spread(shard_ref, out_ref, *sems[3:6])
        spread.start(0)
        spread.start(1)
        pair = PairSwap(sources, start_ref, pieces, *sems[:3])
        parts = []
        for ref in block_refs:
            parts += [ref] if len(ref.shape) == 2 else [ref.at[k] for k in range(ref.shape[0])]
        around = RowsSwap(ring, parts, around_ref, *sems[6:9])
        for copy in copies:
            copy.start()
        small_copy(1, small_place(2), small_place(2)).wait_recv()
        small_copies[2].start()
        whole_ref[:, pl.ds(pl.multiple_of(owner(0)[1] * small_wide, small_wide), small_wide)] = (
            small_ref[...]
        )
        spread.forward((0, 1, 2, 3))
        around.start()
        pair.start()
        spread.forward((6, 7))
        spread.finish()
        around.finish()
        pair.finish()
        small_copy(0, small_place(1), small_place(1)).wait_recv()
        small_copy(2, small_place(3), small_place(3)).wait_recv()
        for copy in small_copies:
            copy.wait_send()
        for copy in copies:
            copy.wait()

    return call(
        swap_gather, identity, operands, (pl.ANY,) * (len(operands) - 1) + (pltpu.VMEM,),
        outputs, [pl.ANY] * (len(outputs) - 1) + [pltpu.VMEM],
        [pltpu.SemaphoreType.DMA((len(pieces),))] * 3
        + [pltpu.SemaphoreType.DMA((2,))]
        + SPREAD_SEMS
        + [pltpu.SemaphoreType.DMA((ring,))] * 3
        + [pltpu.SemaphoreType.DMA((3,))] * 2,
        55_000_000_000,
    )


def scatter_blocks(identity, ring, vector, *terms):
    rows, wide = terms[0].shape[0] // 2, terms[0].shape[1] // 4
    count = len(terms)

    def scatter_outputs(vector_ref, *refs):
        greet([ring_peer(ring, distance) for distance in range(1, ring)])
        small_ref = refs[2 * count]
        scratch = refs[2 * count + 1 :]
        small = SumAll(ring, vector_ref, *scratch[:5])
        collects = []
        for i in range(count):

            def part(r, terms_ref=refs[i]):
                member, slot = owner(r)
                return terms_ref.at[
                    pl.ds(pl.multiple_of(member * rows, rows), rows),
                    pl.ds(pl.multiple_of(slot * wide, wide), wide),
                ]

            mine = scratch[5 + 9 * i : 5 + 9 * (i + 1)]
            collects.append(Collect(part, rows, *mine[:6], mine[6:]))
        small.start()
        for collect in collects:
            collect.start()
        small.step(0)
        for collect in collects:
            collect.first()
        small.step(1)
        for collect in collects:
            collect.second()
        small.step(2)
        for collect, out_ref in zip(collects, refs[count:]):
            for which in range(2):
                collect.ready(which)

                def body(here, collect=collect, out_ref=out_ref):
                    there = pl.ds(pl.multiple_of(which * (rows // 2) + here.start, 32), 32)
                    out_ref[there] = collect.total(which, here).astype(BF16)

                loop_rows(rows // 2, body)
        for collect in collects:
            collect.finish()
        scratch[1][0] = small.finish()
        start = pl.multiple_of(lax.axis_index("feat") * wide, wide)
        small_ref[...] = scratch[1][0, :, pl.ds(start, wide)]

    return call(
        scatter_outputs, identity, (vector, *terms), (pltpu.VMEM,) + (pl.ANY,) * count,
        [jax.ShapeDtypeStruct((rows, wide), BF16)] * count
        + [jax.ShapeDtypeStruct((vector.shape[0], wide), F32)],
        [pltpu.VMEM] * (count + 1),
        SumAll.scratch(ring, vector.shape) + Collect.scratch(rows, wide) * count,
        30_000_000_000 * count,
    )


def row_parts(terms_ref, quarter):
    def part(r):
        member, slot = owner(r)
        return terms_ref.at[pl.ds(pl.multiple_of((member * 4 + slot) * quarter, quarter), quarter)]

    return part


def row_region(out_ref, quarter):
    half = quarter // 2

    def region(r, which):
        member, slot = owner(r)
        start = (member * 4 + slot) * quarter + which * half
        return out_ref.at[pl.ds(pl.multiple_of(start, half), half)]

    return region


def middle_norm(identity, terms, x_all, gain, cotangent):
    total, model = terms.shape
    quarter = total // 8
    half = quarter // 2

    def middle_step(
        terms_ref, x_ref, gain_ref, shard_ref, out_ref, middle_ref, factor_ref, cot_ref,
        x_own, normed, local, send, recv, cot_local, cot_send, cot_recv, *scratch
    ):
        greet()
        beside, copies = block_spread(shard_ref, cot_ref, cot_local, cot_send, cot_recv)
        x_copy = pltpu.make_async_copy(row_parts(x_ref, quarter)(0), x_own, local.at[0])
        x_copy.start()
        collect = Collect(row_parts(terms_ref, quarter), quarter, *scratch[:6], scratch[6:])
        region = row_region(out_ref, quarter)
        spread = Spread(
            lambda which: normed.at[pl.ds(which * half, half)], region, send, recv
        )
        collect.start()
        beside.start(0)
        beside.start(1)
        for copy in copies:
            copy.start()
        collect.first()
        beside.forward((0, 1, 2, 3))
        collect.second()
        x_copy.wait()
        for which in range(2):
            collect.ready(which)

            def body(here):
                there = pl.ds(pl.multiple_of(which * half + here.start, 32), 32)
                middle = collect.total(which, here) + x_own[there].astype(F32)
                mean = jnp.mean(middle * middle, axis=1, keepdims=True)
                factor = lax.rsqrt(mean + EPSILON)
                middle_ref[there] = middle
                factor_ref[there] = jnp.broadcast_to(factor, (32, 128))
                normed[there] = (middle * factor * gain_ref[...]).astype(BF16)

            loop_rows(half, body)
            spread.start(which)
            copy = pltpu.make_async_copy(
                normed.at[pl.ds(which * half, half)], region(0, which), local.at[1 + which]
            )
            copy.start()
            copies.append(copy)
        beside.forward((6, 7))
        spread.forward()
        spread.finish()
        beside.finish()
        collect.finish()
        for copy in copies:
            copy.wait()

    return call(
        middle_step, identity, (terms, x_all, gain, cotangent),
        (pl.ANY, pl.ANY, pltpu.VMEM, pl.ANY),
        (
            jax.ShapeDtypeStruct((total, model), BF16),
            jax.ShapeDtypeStruct((quarter, model), F32),
            jax.ShapeDtypeStruct((quarter, 128), F32),
            jax.ShapeDtypeStruct((total, model), BF16),
        ),
        (pl.ANY, pltpu.VMEM, pltpu.VMEM, pl.ANY),
        [
            pltpu.VMEM((quarter, model), BF16),
            pltpu.VMEM((quarter, model), BF16),
            pltpu.SemaphoreType.DMA((3,)),
        ]
        + SPREAD_SEMS
        + [pltpu.SemaphoreType.DMA((2,))]
        + SPREAD_SEMS
        + Collect.scratch(quarter, model),
        100_000_000_000,
    )


def middle_back(identity, terms, cot, middle, factor, gain, hiddens, weights):
    total, model = terms.shape
    widths = [hidden.shape[1] for hidden in hiddens]
    inner_width = sum(widths)
    count = len(hiddens)
    quarter = total // 8
    half = quarter // 2

    def middle_back_step(
        terms_ref, cot_ref, middle_ref, factor_ref, gain_ref, *refs
    ):
        parts_refs, refs = refs[: 2 * count], refs[2 * count :]
        out_ref, grad_ref, gain_grad_ref, rows_ref, *refs = refs
        hidden_all, down_all, tiles, load_sems, tile_sems, *refs = refs
        cot_own, rounded, local, send, recv, *scratch = refs
        greet()
        loads = []
        left = 0
        for k, width in enumerate(widths):
            place = pl.ds(left, width)
            loads.append(
                pltpu.make_async_copy(parts_refs[k], hidden_all.at[:, place], load_sems.at[2 * k])
            )
            down = parts_refs[count + k].at[:, pl.ds(2 * width, width)]
            loads.append(
                pltpu.make_async_copy(down, down_all.at[:, place], load_sems.at[2 * k + 1])
            )
            left += width
        for load in loads:
            load.start()
        member, slot = owner(0)

        def tile_copy(index):
            start = pl.multiple_of(index * quarter, quarter)
            kept = lax.rem(index, 2)
            return pltpu.make_async_copy(
                tiles.at[kept], rows_ref.at[pl.ds(start, quarter)], tile_sems.at[kept]
            )

        def result_tiles(first, last):
            def step(index, carry):
                @pl.when(index >= 2)
                def _():
                    tile_copy(index - 2).wait()

                kept = lax.rem(index, 2)
                rows = pl.ds(pl.multiple_of(index * quarter, quarter), quarter)
                for start in range(0, model, 512):
                    here = slice(start, start + 512)
                    value = right_trans(hidden_all[rows, :], down_all[here, :])
                    tiles[kept, :, here] = value.astype(BF16)

                @pl.when(index == member * 4 + slot)
                def _():
                    tiles[kept] = (tiles[kept].astype(F32) + middle_ref[...]).astype(BF16)

                tile_copy(index).start()
                return carry

            lax.fori_loop(first, last, step, 0)

        cot_copy = pltpu.make_async_copy(row_parts(cot_ref, quarter)(0), cot_own, local.at[0])
        cot_copy.start()
        collect = Collect(row_parts(terms_ref, quarter), quarter, *scratch[:6], scratch[6:])
        region = row_region(out_ref, quarter)
        spread = Spread(
            lambda which: rounded.at[pl.ds(which * half, half)], region, send, recv
        )
        collect.start()
        collect.first()
        for load in loads:
            load.wait()
        result_tiles(0, 4)
        collect.second()
        result_tiles(4, 6)
        cot_copy.wait()
        gain_grad_ref[...] = jnp.zeros_like(gain_grad_ref)
        copies = []
        for which in range(2):
            collect.ready(which)

            def body(here):
                there = pl.ds(pl.multiple_of(which * half + here.start, 32), 32)
                grad_normed = collect.total(which, here)
                values = middle_ref[there]
                factor = factor_ref[there][:, :1]
                weighted = gain_ref[...] * grad_normed
                inner = jnp.mean(weighted * values, axis=1, keepdims=True)
                grad = (
                    cot_own[there].astype(F32)
                    + factor * weighted
                    - values * (factor * factor * factor * inner)
                )
                grad_ref[there] = grad
                rounded[there] = grad.astype(BF16)
                gain_grad_ref[...] += jnp.sum(grad_normed * values * factor, axis=0, keepdims=True)

            loop_rows(half, body)
            spread.start(which)
            copy = pltpu.make_async_copy(
                rounded.at[pl.ds(which * half, half)], region(0, which), local.at[1 + which]
            )
            copy.start()
            copies.append(copy)
        result_tiles(6, 8)
        spread.forward()
        spread.finish()
        collect.finish()
        tile_copy(6).wait()
        tile_copy(7).wait()
        for copy in copies:
            copy.wait()

    return call(
        middle_back_step, identity, (terms, cot, middle, factor, gain, *hiddens, *weights),
        (pl.ANY, pl.ANY, pltpu.VMEM, pltpu.VMEM, pltpu.VMEM) + (pl.ANY,) * (2 * count),
        (
            jax.ShapeDtypeStruct((total, model), BF16),
            jax.ShapeDtypeStruct((quarter, model), F32),
            jax.ShapeDtypeStruct((1, model), F32),
            jax.ShapeDtypeStruct((total, model), BF16),
        ),
        (pl.ANY, pltpu.VMEM, pltpu.VMEM, pl.ANY),
        [
            pltpu.VMEM((total, inner_width), BF16),
            pltpu.VMEM((model, inner_width), BF16),
            pltpu.VMEM((2, quarter, model), BF16),
            pltpu.SemaphoreType.DMA((2 * count,)),
            pltpu.SemaphoreType.DMA((2,)),
            pltpu.VMEM((quarter, model), BF16),
            pltpu.VMEM((quarter, model), BF16),
            pltpu.SemaphoreType.DMA((3,)),
        ]
        + SPREAD_SEMS
        + Collect.scratch(quarter, model),
        70_000_000_000,
    )


def assemble(plan, flipped_out, totals, others, passed=()):
    count = len(totals)
    size = others[0].shape[0]
    shapes = []
    for index, pieces in enumerate(plan):
        wide = 2 * sum(piece[2] for piece in pieces)
        shapes.append((size, wide) if index < flipped_out else (wide, size))

    def assemble_grads(*refs):
        member = lax.rem(lax.axis_index("tok"), 2)
        outs = refs[2 * count + len(passed) :]
        for i in range(len(passed)):
            outs[len(plan) + i][...] = refs[2 * count + i][...]
        for index, pieces in enumerate(plan):
            half = sum(piece[2] for piece in pieces)
            for source, column, width, target in pieces:
                own_rows = pl.ds(pl.multiple_of(member * size, size), size)
                own = refs[source][own_rows, column : column + width]
                other = refs[count + source][:, column : column + width]
                for which, block in ((member, own), (1 - member, other)):
                    start = pl.multiple_of(which * half + target, 128)
                    if index < flipped_out:
                        outs[index][:, pl.ds(start, width)] = block.astype(F32)
                    else:
                        outs[index][pl.ds(start, width), :] = block.astype(F32).T

    return pl.pallas_call(
        assemble_grads,
        out_shape=[jax.ShapeDtypeStruct(shape, F32) for shape in shapes]
        + [jax.ShapeDtypeStruct(array.shape, array.dtype) for array in passed],
        in_specs=[pl.BlockSpec(memory_space=pltpu.VMEM)] * (2 * count + len(passed)),
        out_specs=[pl.BlockSpec(memory_space=pltpu.VMEM)] * (len(plan) + len(passed)),
        compiler_params=pltpu.CompilerParams(vmem_limit_bytes=VMEM),
        cost_estimate=pl.CostEstimate(
            flops=0, transcendentals=0, bytes_accessed=8 * size * 2 * sum(t.shape[1] for t in totals)
        ),
        name="assemble_grads",
    )(*totals, *others, *passed)


def input_terms(grad_packed, weights, x_all, gain, grad_middle, own):
    total, columns = grad_packed.shape
    model = x_all.shape[1]
    tile = grad_middle.shape[0]

    def input_terms_step(own_ref, grad_ref, qkv_ref, x_ref, gain_ref, middle_ref, out_ref, gain_grad_ref):
        step = pl.program_id(0)
        grad_normed = right_trans(grad_ref[...], qkv_ref[...])
        values = x_ref[...].astype(F32)
        factor = lax.rsqrt(jnp.mean(values * values, axis=1, keepdims=True) + EPSILON)
        weighted = grad_normed * gain_ref[...]
        inner = jnp.mean(weighted * values, axis=1, keepdims=True)
        terms = factor * weighted - values * (factor * factor * factor * inner)

        @pl.when(step == own_ref[0])
        def _():
            out_ref[...] = (terms + middle_ref[...]).astype(BF16)

        @pl.when(step != own_ref[0])
        def _():
            out_ref[...] = terms.astype(BF16)

        @pl.when(step == 0)
        def _():
            gain_grad_ref[...] = jnp.zeros_like(gain_grad_ref)

        gain_grad_ref[...] += jnp.sum(grad_normed * values * factor, axis=0, keepdims=True)

    return pl.pallas_call(
        input_terms_step,
        grid_spec=pltpu.PrefetchScalarGridSpec(
            num_scalar_prefetch=1,
            grid=(total // tile,),
            in_specs=[
                pl.BlockSpec((tile, columns), lambda i, own: (i, 0)),
                pl.BlockSpec((model, columns), lambda i, own: (0, 0)),
                pl.BlockSpec((tile, model), lambda i, own: (i, 0)),
                pl.BlockSpec((1, model), lambda i, own: (0, 0)),
                pl.BlockSpec((tile, model), lambda i, own: (0, 0)),
            ],
            out_specs=[
                pl.BlockSpec((tile, model), lambda i, own: (i, 0)),
                pl.BlockSpec((1, model), lambda i, own: (0, 0)),
            ],
        ),
        out_shape=[
            jax.ShapeDtypeStruct((total, model), BF16),
            jax.ShapeDtypeStruct((1, model), F32),
        ],
        compiler_params=pltpu.CompilerParams(vmem_limit_bytes=VMEM),
        cost_estimate=pl.CostEstimate(
            flops=2 * total * columns * model,
            transcendentals=total,
            bytes_accessed=6 * total * model,
        ),
        name="input_terms",
    )(own, grad_packed, weights, x_all, gain, grad_middle)


def feed_forward(normed, cot, weights, chunk):
    total, model = normed.shape
    tile = 256
    part = 256 if chunk % 256 == 0 else 128

    def feed_step(normed_ref, cot_ref, gate_ref, up_ref, down_ref, hidden_ref, grads_ref):
        for left in range(0, chunk, part):
            here = slice(left, left + part)
            gate = product(normed_ref[...], gate_ref[:, here])
            upward = product(normed_ref[...], up_ref[:, here])
            grad_hidden = product(cot_ref[...], down_ref[:, here])
            sigma = jax.nn.sigmoid(gate)
            active = gate * sigma
            hidden_ref[:, here] = (active * upward).astype(BF16)
            grads_ref[:, here] = (
                grad_hidden * upward * (sigma + active * (1.0 - sigma))
            ).astype(BF16)
            grads_ref[:, chunk + left : chunk + left + part] = (grad_hidden * active).astype(BF16)

    rows = pl.BlockSpec((tile, model), lambda i: (i, 0))

    def weight(part):
        return pl.BlockSpec((model, chunk), lambda i: (0, part), pipeline_mode=pl.Buffered(1))

    return pl.pallas_call(
        feed_step,
        grid=(total // tile,),
        in_specs=[rows, rows, weight(0), weight(1), weight(2)],
        out_specs=[
            pl.BlockSpec((tile, chunk), lambda i: (i, 0)),
            pl.BlockSpec((tile, 2 * chunk), lambda i: (i, 0)),
        ],
        out_shape=[
            jax.ShapeDtypeStruct((total, chunk), BF16),
            jax.ShapeDtypeStruct((total, 2 * chunk), BF16),
        ],
        compiler_params=pltpu.CompilerParams(vmem_limit_bytes=VMEM),
        cost_estimate=pl.CostEstimate(
            flops=6 * total * chunk * model,
            transcendentals=total * chunk,
            bytes_accessed=4 * total * model + 6 * chunk * (model + total),
        ),
        name="feed_forward",
    )(normed, cot, weights, weights, weights)


def columns_back(lefts, weights, place, own, base=None, middle=None):
    count = len(lefts)
    total = lefts[0].shape[0]
    model = weights[0].shape[0]
    tile, part = 512, 512

    def columns_step(own_ref, *refs):
        out_ref = refs[-1]
        for start in range(0, model, part):
            here = slice(start, start + part)
            value = sum(
                right_trans(refs[i][...], refs[count + i][here, :]) for i in range(count)
            )
            if base is not None:
                value = value + refs[2 * count][:, here].astype(F32)
            out_ref[:, here] = value.astype(BF16)
        if middle is not None:
            middle_ref = refs[-2]
            size = middle_ref.shape[0]
            inside = own_ref[0] * size - pl.program_id(0) * tile

            @pl.when((inside >= 0) & (inside < tile))
            def _():
                rows = pl.ds(pl.multiple_of(inside, size), size)
                out_ref[rows, :] = (out_ref[rows, :].astype(F32) + middle_ref[...]).astype(BF16)

    in_specs = [pl.BlockSpec((tile, left.shape[1]), lambda i, own: (i, 0)) for left in lefts]
    in_specs += [
        pl.BlockSpec(
            (model, left.shape[1]), lambda i, own: (0, place), pipeline_mode=pl.Buffered(1)
        )
        for left in lefts
    ]
    operands = [own, *lefts, *weights]
    if base is not None:
        in_specs.append(pl.BlockSpec((tile, model), lambda i, own: (i, 0)))
        operands.append(base)
    if middle is not None:
        in_specs.append(pl.BlockSpec(middle.shape, lambda i, own: (0, 0)))
        operands.append(middle)
    inner = sum(left.shape[1] for left in lefts)
    return pl.pallas_call(
        columns_step,
        grid_spec=pltpu.PrefetchScalarGridSpec(
            num_scalar_prefetch=1,
            grid=(total // tile,),
            in_specs=in_specs,
            out_specs=pl.BlockSpec((tile, model), lambda i, own: (i, 0)),
        ),
        out_shape=jax.ShapeDtypeStruct((total, model), BF16),
        compiler_params=pltpu.CompilerParams(vmem_limit_bytes=VMEM),
        cost_estimate=pl.CostEstimate(
            flops=2 * total * model * inner,
            transcendentals=0,
            bytes_accessed=2 * total * model + 2 * (total + model) * inner,
        ),
        name="columns_back",
    )(*operands)


def weight_terms(pairs, tile=256):
    rows, model = pairs[0][0].shape
    count = len(pairs)
    widths = [right.shape[1] for _, right in pairs]

    def terms_step(*refs):
        out_ref = refs[-1]
        start = 0
        for i, width in enumerate(widths):
            out_ref[:, start : start + width] = left_trans(refs[i][...], refs[count + i][...]).astype(
                BF16
            )
            start += width

    return pl.pallas_call(
        terms_step,
        grid=(model // tile,),
        in_specs=[pl.BlockSpec((rows, tile), lambda i: (0, i))] * count
        + [
            pl.BlockSpec((rows, width), lambda i: (0, 0), pipeline_mode=pl.Buffered(1))
            for width in widths
        ],
        out_specs=pl.BlockSpec((tile, sum(widths)), lambda i: (i, 0)),
        out_shape=jax.ShapeDtypeStruct((model, sum(widths)), BF16),
        compiler_params=pltpu.CompilerParams(vmem_limit_bytes=VMEM),
        cost_estimate=pl.CostEstimate(
            flops=2 * rows * model * sum(widths),
            transcendentals=0,
            bytes_accessed=2 * (rows * model * count + (rows + model) * sum(widths)),
        ),
        name="weight_terms",
    )(*[left for left, _ in pairs], *[right for _, right in pairs])


def program(
    tok_size,
    tokens, gain_attn, w_query, w_key, w_value, w_out, gain_ffn, w_gate, w_up, w_down, cotangent
):
    token = lax.axis_index("tok")
    feat = lax.axis_index("feat")
    member = token % 2
    rows, wide = tokens.shape
    model = 4 * wide
    quarter = rows // 4
    groups = [list(range(i, tok_size, 2)) for i in range(2)]
    pair_width = 2 * HD

    def swap(value):
        return lax.ppermute(value, "tok", [(i, i ^ 1) for i in range(tok_size)])

    def ring_gather(shard):
        return lax.all_gather(shard, "tok", axis=0, tiled=True, axis_index_groups=groups)

    def ring_scatter(terms):
        return lax.psum_scatter(
            terms, "tok", scatter_dimension=0, tiled=True, axis_index_groups=groups
        )

    def other_half(total):
        size = total.shape[0] // 2
        return swap(lax.dynamic_slice_in_dim(total, (1 - member) * size, size, 0))

    heads_wide = w_query.shape[1] // 2
    hidden_wide = w_gate.shape[1] // 2
    chunks = [hidden_wide * part // sum(CHUNKS) for part in CHUNKS]
    lefts = [sum(chunks[:c]) for c in range(len(chunks))]
    attention_pieces = [
        (part, left, pair_width, 3 * left + part * pair_width)
        for left in range(0, heads_wide, pair_width)
        for part in range(3)
    ]
    ring = tok_size // 2
    early = 1
    out_blocks = [w_out.T]
    attention_start, block = swap_ring(
        0, (w_query, w_key, w_value), attention_pieces, ring, out_blocks[0], early
    )
    out_blocks.append(block)
    feed = (w_gate, w_up, w_down.T)
    block, attention_start = lax.optimization_barrier((block, attention_start))
    qkv = ring_gather(attention_start)
    plans = [
        [(part, left, size, part * size) for part in range(3)] for left, size in zip(lefts, chunks)
    ]
    first_start, block = swap_ring(1, feed, plans[0], ring, block, ring - 1 - early)
    out_blocks.append(block)
    feed_weights = [ring_gather(first_start)]
    tokens, block = lax.optimization_barrier((tokens, block))
    last_start, x_all, out_proj, gains = swap_and_gather(
        2, feed, plans[1], tokens, ring, out_blocks, jnp.stack([gain_attn, gain_ffn])
    )
    gain_one, gain_two = gains[:1], gains[1:]
    feed_weights.append(ring_gather(last_start))

    x_wide = x_all.astype(F32)
    factor_one = lax.rsqrt(jnp.mean(x_wide * x_wide, axis=1, keepdims=True) + EPSILON)
    normed = (x_wide * factor_one * gain_one).astype(BF16)
    packed = product(normed, qkv).astype(BF16)
    attended, log_sums = attend(packed)
    normed_two, middle, factor_two, cot_rows = middle_norm(
        3, right_trans(attended, out_proj).astype(BF16), x_all, gain_two, cotangent
    )

    own = (member * 4 + feat).astype(jnp.int32).reshape(1)
    feed_sums = []
    grad_normed_two = out_rows = None

    hiddens = []
    for c in range(len(chunks)):
        if c:
            feed_weights[c], grad_normed_two = lax.optimization_barrier(
                (feed_weights[c], grad_normed_two)
            )
        hidden, grad_both = feed_forward(normed_two, cot_rows, feed_weights[c], chunks[c])
        hiddens.append(hidden)
        if c + 1 < len(chunks):
            feed_terms = weight_terms([(normed_two, grad_both), (cot_rows, hidden)])
            feed_terms, grad_both = lax.optimization_barrier((feed_terms, grad_both))
            feed_sums.append(ring_scatter(feed_terms))
        grad_normed_two = columns_back(
            [grad_both], [feed_weights[c]], 0, own, grad_normed_two
        )
    grad_mid_rows, grad_middle, gain_ffn_part, out_rows = middle_back(
        4, grad_normed_two, cot_rows, middle, factor_two, gain_two, hiddens, feed_weights
    )

    hidden, grad_both, grad_mid_rows = lax.optimization_barrier((hidden, grad_both, grad_mid_rows))
    feed_terms = weight_terms(
        [(normed_two, grad_both), (cot_rows, hidden), (grad_mid_rows, attended)]
    )
    grad_mid_rows, feed_terms = lax.optimization_barrier((grad_mid_rows, feed_terms))
    feed_sums.append(ring_scatter(feed_terms))

    grad_attended = product(grad_mid_rows, out_proj).astype(BF16)
    grad_packed = attend_back(packed, attended, grad_attended, log_sums)
    attention_terms = left_trans(normed, grad_packed).astype(BF16)
    attention_terms, grad_packed = lax.optimization_barrier((attention_terms, grad_packed))
    attention_sum = ring_scatter(attention_terms)
    grad_packed, feed_sums[0] = lax.optimization_barrier((grad_packed, feed_sums[0]))
    first_other = other_half(feed_sums[0])
    terms, gain_attn_part = input_terms(grad_packed, qkv, x_all, gain_one, grad_middle, own)
    terms, first_other = lax.optimization_barrier((terms, first_other))
    outcome, input_grad, gain_grads = scatter_blocks(
        5, tok_size // 2, jnp.concatenate([gain_attn_part, gain_ffn_part]), out_rows, terms
    )
    feed_others = [first_other]
    outcome, feed_sums[1] = lax.optimization_barrier((outcome, feed_sums[1]))
    feed_others.append(other_half(feed_sums[1]))
    feed_others[1], attention_sum = lax.optimization_barrier((feed_others[1], attention_sum))
    feed_plan = [
        [(c, part * chunks[c], chunks[c], lefts[c]) for c in range(len(chunks))]
        for part in range(3)
    ]
    feed_plan.append([(len(chunks) - 1, 3 * chunks[-1], heads_wide, 0)])
    gate_grad, up_grad, down_grad, out_grad, outcome, input_grad = assemble(
        feed_plan, 2, feed_sums, feed_others, (outcome, input_grad)
    )
    attention_plan = [
        [
            (0, 3 * left + part * pair_width, pair_width, left)
            for left in range(0, heads_wide, pair_width)
        ]
        for part in range(3)
    ]
    attention_other = other_half(attention_sum)
    attention_other, gate_grad, up_grad, down_grad, outcome, input_grad = lax.optimization_barrier(
        (attention_other, gate_grad, up_grad, down_grad, outcome, input_grad)
    )
    part_grads = assemble(attention_plan, 3, [attention_sum], [attention_other])
    return (
        outcome,
        input_grad,
        gain_grads[0],
        gain_grads[1],
        *part_grads,
        out_grad,
        gate_grad,
        up_grad,
        down_grad,
    )


def solution(mesh):
    in_specs = (
        P("tok", "feat"),
        P("feat"),
        P("tok", "feat"),
        P("tok", "feat"),
        P("tok", "feat"),
        P("feat", "tok"),
        P("feat"),
        P("tok", "feat"),
        P("tok", "feat"),
        P("feat", "tok"),
        P("tok", "feat"),
    )
    out_specs = (
        P("tok", "feat"),
        P("tok", "feat"),
        P("feat"),
        P("feat"),
        P("tok", "feat"),
        P("tok", "feat"),
        P("tok", "feat"),
        P("feat", "tok"),
        P("tok", "feat"),
        P("tok", "feat"),
        P("feat", "tok"),
    )

    def on_device(*arrays):
        return program(mesh.shape["tok"], *arrays)

    return jax.shard_map(
        on_device, mesh=mesh, in_specs=in_specs, out_specs=out_specs, check_vma=False
    )
```

```python
import jax
import jax.numpy as jnp
from jax import lax
from jax.experimental import pallas as pl
from jax.experimental.pallas import tpu as pltpu
from jax.sharding import PartitionSpec as P

HD = 64
LEN = 1024
EPSILON = 1e-05
BF16 = jnp.bfloat16
F32 = jnp.float32
MESH = pl.DeviceIdType.MESH
VMEM = 48 << 20
FORWARD_BLOCK = 512
BACK_BLOCK = 256
CHUNKS = (3, 1)


def left_trans(left, right):
    return lax.dot_general(
        left, right, (((0,), (0,)), ((), ())), preferred_element_type=F32
    )


def right_trans(left, right):
    return lax.dot_general(
        left, right, (((1,), (1,)), ((), ())), preferred_element_type=F32
    )


def product(left, right):
    return jnp.dot(left, right, preferred_element_type=F32)


def causal_tile(scores):
    size = scores.shape[0]
    key = lax.broadcasted_iota(jnp.int32, scores.shape, 0)
    query = lax.broadcasted_iota(jnp.int32, scores.shape, 1)
    return jnp.where(key <= query, scores, -1e30)


def head_parts(packed_ref, head, width):
    columns = [slice(part * width + head * HD, part * width + (head + 1) * HD) for part in range(3)]
    query, key, value = [packed_ref[:, part] for part in columns]
    return query * HD ** (-0.5), key, value


def attend_kernel(packed_ref, out_ref, lse_ref):
    width = out_ref.shape[1]
    for head in range(width // HD):
        query, key, value = head_parts(packed_ref, head, width)
        query = query.astype(BF16)
        value_t = value.T
        for top in range(0, LEN, FORWARD_BLOCK):
            keys = top + FORWARD_BLOCK
            scores = right_trans(key[:keys], query[top:keys])
            last = causal_tile(scores[top:])
            scores = jnp.concatenate([scores[:top], last]) if top else last
            highest = jnp.max(scores, axis=0, keepdims=True)
            exponent = jnp.exp(scores - highest)
            total = jnp.sum(exponent, axis=0, keepdims=True)
            mixed = product(value_t[:, :keys], exponent.astype(BF16)) / total
            out_ref[top:keys, head * HD : (head + 1) * HD] = mixed.T.astype(BF16)
            lse_ref[0, 0, head : head + 1, top:keys] = highest + jnp.log(total)


def attend_back_kernel(packed_ref, out_ref, grad_ref, lse_ref, grads_ref, key_acc, value_acc):
    width = out_ref.shape[1]
    for head in range(width // HD):
        lanes = slice(head * HD, (head + 1) * HD)
        query, key, value = head_parts(packed_ref, head, width)
        query = query.astype(BF16)
        key_t = key.T
        grad = grad_ref[:, lanes]
        inner = (out_ref[:, lanes].astype(F32) * grad.astype(F32)).T
        inner = jnp.sum(inner, axis=0, keepdims=True)
        for top in reversed(range(0, LEN, BACK_BLOCK)):
            keys = top + BACK_BLOCK
            scores = right_trans(key[:keys], query[top:keys])
            last = causal_tile(scores[top:])
            scores = jnp.concatenate([scores[:top], last]) if top else last
            probs = jnp.exp(scores - lse_ref[0, 0, head : head + 1, top:keys])
            grad_probs = right_trans(value[:keys], grad[top:keys])
            grad_scores = (probs * (grad_probs - inner[:, top:keys])).astype(BF16)
            value_term = product(probs.astype(BF16), grad[top:keys])
            key_term = product(grad_scores, query[top:keys])
            if keys == LEN:
                value_acc[...] = value_term
                key_acc[...] = key_term
            else:
                value_acc[:keys] += value_term
                key_acc[:keys] += key_term
            grad_query = product(key_t[:, :keys], grad_scores) * HD ** (-0.5)
            grads_ref[top:keys, lanes] = grad_query.T.astype(BF16)
        grads_ref[:, width + head * HD : width + (head + 1) * HD] = key_acc[...].astype(BF16)
        grads_ref[:, 2 * width + head * HD : 2 * width + (head + 1) * HD] = value_acc[...].astype(
            BF16
        )


def attend(packed):
    rows, columns = packed.shape
    width = 2 * HD
    sequences, pairs = rows // LEN, columns // (3 * width)
    return pl.pallas_call(
        attend_kernel,
        grid=(sequences, pairs),
        out_shape=(
            jax.ShapeDtypeStruct((rows, pairs * width), BF16),
            jax.ShapeDtypeStruct((sequences, pairs, 2, LEN), F32),
        ),
        in_specs=[pl.BlockSpec((LEN, 3 * width), lambda s, p: (s, p))],
        out_specs=(
            pl.BlockSpec((LEN, width), lambda s, p: (s, p)),
            pl.BlockSpec((1, 1, 2, LEN), lambda s, p: (s, p, 0, 0)),
        ),
        compiler_params=pltpu.CompilerParams(vmem_limit_bytes=VMEM),
        cost_estimate=pl.CostEstimate(
            flops=4 * rows * LEN * pairs * width // 2,
            transcendentals=rows * LEN * pairs,
            bytes_accessed=2 * rows * columns * 2,
        ),
        name="attend",
    )(packed)


def attend_back(packed, attended, grad_attended, lse):
    rows, columns = packed.shape
    width = 2 * HD
    sequences, pairs = rows // LEN, columns // (3 * width)
    narrow = pl.BlockSpec((LEN, width), lambda s, p: (s, p))
    return pl.pallas_call(
        attend_back_kernel,
        grid=(sequences, pairs),
        out_shape=jax.ShapeDtypeStruct((rows, columns), BF16),
        in_specs=[
            pl.BlockSpec((LEN, 3 * width), lambda s, p: (s, p)),
            narrow,
            narrow,
            pl.BlockSpec((1, 1, 2, LEN), lambda s, p: (s, p, 0, 0)),
        ],
        out_specs=pl.BlockSpec((LEN, 3 * width), lambda s, p: (s, p)),
        scratch_shapes=[pltpu.VMEM((LEN, HD), F32)] * 2,
        compiler_params=pltpu.CompilerParams(vmem_limit_bytes=VMEM),
        cost_estimate=pl.CostEstimate(
            flops=10 * rows * LEN * pairs * width // 2,
            transcendentals=rows * LEN * pairs,
            bytes_accessed=3 * rows * columns * 2,
        ),
        name="attend_back",
    )(packed, attended, grad_attended, lse)


SPREAD = (
    (0, 0, "y", None),
    (0, 1, "x", None),
    (0, 0, "x", None),
    (0, 1, "y", None),
    (0, 0, "core", None),
    (0, 1, "core", None),
    (4, 0, "x", 0),
    (2, 1, "y", 1),
    (4, 0, "core", 0),
    (2, 1, "core", 1),
    (2, 0, "core", 2),
    (4, 1, "core", 3),
    (6, 0, "core", 6),
    (6, 1, "core", 7),
)
BIT = {"y": 4, "x": 2, "core": 1}


def neighbours():
    token, feat = lax.axis_index("tok"), lax.axis_index("feat")
    return {
        "y": (token + 1 - 2 * lax.rem(token, 2), feat),
        "x": (token, lax.rem(feat + 2, 4)),
        "core": (token, feat + 1 - 2 * lax.rem(feat, 2)),
    }


def owner(r):
    member, slot = lax.rem(lax.axis_index("tok"), 2), lax.axis_index("feat")
    if r & 4:
        member = 1 - member
    if r & 2:
        slot = lax.rem(slot + 2, 4)
    if r & 1:
        slot = slot + 1 - 2 * lax.rem(slot, 2)
    return member, slot


def greet(others=()):
    barrier = pltpu.get_barrier_semaphore()
    peers = [*neighbours().values(), *others]
    for peer in peers:
        pl.semaphore_signal(barrier, inc=1, device_id=peer, device_id_type=MESH)
    pl.semaphore_wait(barrier, len(peers))


def ring_peer(ring, distance):
    token = lax.axis_index("tok")
    return lax.rem(token + 2 * distance, 2 * ring), lax.axis_index("feat")


class SumAll:
    def __init__(self, ring, ref, steps, arrived, slots, send, recv):
        self.ring, self.ref = ring, ref
        self.steps, self.arrived, self.slots = steps, arrived, slots
        self.send, self.recv = send, recv
        self.place = lax.div(lax.axis_index("tok"), 2)
        self.peers = neighbours()

    @staticmethod
    def scratch(ring, shape):
        return [
            pltpu.VMEM((3, *shape), F32),
            pltpu.VMEM((3, *shape), F32),
            pltpu.VMEM((ring, *shape), F32),
            pltpu.SemaphoreType.DMA((2 + ring,)),
            pltpu.SemaphoreType.DMA((2 + ring,)),
        ]

    def copy(self, k):
        if k < 3:
            source = self.ref if k == 0 else self.steps.at[k - 1]
            target, peer = self.arrived.at[k], self.peers[("core", "x", "y")[k]]
        else:
            source, target = self.steps.at[2], self.slots.at[self.place]
            peer = ring_peer(self.ring, k - 2)
        return pltpu.make_async_remote_copy(
            source, target, self.send.at[k], self.recv.at[k],
            device_id=peer, device_id_type=MESH,
        )

    def start(self):
        self.copy(0).start()

    def step(self, k):
        self.copy(k).wait_recv()
        before = self.ref[...] if k == 0 else self.steps[k - 1]
        self.steps[k] = before + self.arrived[k]
        if k < 2:
            self.copy(k + 1).start()
        else:
            for distance in range(1, self.ring):
                self.copy(2 + distance).start()
            self.slots[self.place] = self.steps[2]

    def finish(self):
        for distance in range(1, self.ring):
            source = lax.rem(self.place + self.ring - distance, self.ring)
            k = 2 + distance
            pltpu.make_async_remote_copy(
                self.slots.at[source], self.slots.at[source], self.send.at[k], self.recv.at[k],
                device_id=ring_peer(self.ring, distance), device_id_type=MESH,
            ).wait_recv()
        for k in range(2 + self.ring):
            self.copy(k).wait_send()
        total = self.slots[0]
        for place in range(1, self.ring):
            total = total + self.slots[place]
        return total


class Spread:
    def __init__(self, own, region, send, recv):
        self.own, self.region, self.send, self.recv = own, region, send, recv
        self.peers = neighbours()

    def copy(self, k):
        r, half, way, _ = SPREAD[k]
        source = self.own(half) if r == 0 else self.region(r, half)
        return pltpu.make_async_remote_copy(
            source, self.region(r, half), self.send.at[k], self.recv.at[k],
            device_id=self.peers[way], device_id_type=MESH,
        )

    def arrival(self, k):
        r, half, way, _ = SPREAD[k]
        place = self.region(r ^ BIT[way], half)
        return pltpu.make_async_remote_copy(
            place, place, self.send.at[k], self.recv.at[k],
            device_id=self.peers[way], device_id_type=MESH,
        )

    def start(self, half):
        for k, (r, which, _, after) in enumerate(SPREAD):
            if after is None and which == half:
                self.copy(k).start()

    def forward(self, arrivals=(0, 1, 2, 3, 6, 7)):
        for first in arrivals:
            self.arrival(first).wait_recv()
            for k, (_, _, _, after) in enumerate(SPREAD):
                if after == first:
                    self.copy(k).start()

    def finish(self):
        for k, (_, _, way, _) in enumerate(SPREAD):
            if way == "core":
                self.arrival(k).wait_recv()
        for k in range(len(SPREAD)):
            self.copy(k).wait_send()


SPREAD_SEMS = [pltpu.SemaphoreType.DMA((len(SPREAD),))] * 2


def block_spread(shard_ref, out_ref, local, send, recv):
    rows, wide = shard_ref.shape
    half = rows // 2

    def own(which):
        return shard_ref.at[pl.ds(which * half, half)]

    def region(r, which):
        member, slot = owner(r)
        return out_ref.at[
            pl.ds(pl.multiple_of(member * rows + which * half, half), half),
            pl.ds(pl.multiple_of(slot * wide, wide), wide),
        ]

    copies = [
        pltpu.make_async_copy(own(which), region(0, which), local.at[which]) for which in range(2)
    ]
    return Spread(own, region, send, recv), copies


class Collect:
    def __init__(self, part, size, parts, near, from_x, from_y, last_y, last_x, sems):
        self.part, self.size, self.half = part, size, size // 2
        self.parts, self.near = parts, near
        self.from_x, self.from_y, self.last_y, self.last_x = from_x, from_y, last_y, last_x
        self.load, self.send, self.recv = sems
        self.peers = neighbours()

    @staticmethod
    def scratch(size, columns):
        half = size // 2
        return [
            pltpu.VMEM((4, size, columns), BF16),
            pltpu.VMEM((4, size, columns), BF16),
            pltpu.VMEM((2, half, columns), BF16),
            pltpu.VMEM((2, half, columns), BF16),
            pltpu.VMEM((half, columns), BF16),
            pltpu.VMEM((half, columns), BF16),
            pltpu.SemaphoreType.DMA((4,)),
            pltpu.SemaphoreType.DMA((10,)),
            pltpu.SemaphoreType.DMA((10,)),
        ]

    def remote(self, k, source, target, way):
        return pltpu.make_async_remote_copy(
            source, target, self.send.at[k], self.recv.at[k],
            device_id=self.peers[way], device_id_type=MESH,
        )

    def copy(self, k):
        low, high = pl.ds(0, self.half), pl.ds(self.half, self.half)
        if k < 4:
            return self.remote(k, self.part(2 * k + 1), self.near.at[k], "core")
        if k < 6:
            return self.remote(k, self.parts.at[(1, 3)[k - 4], low], self.from_x.at[k - 4], "x")
        if k < 8:
            return self.remote(k, self.parts.at[(2, 3)[k - 6], high], self.from_y.at[k - 6], "y")
        if k == 8:
            return self.remote(k, self.parts.at[2, low], self.last_y, "y")
        return self.remote(k, self.parts.at[1, high], self.last_x, "x")

    def add(self, index, start, count, other):
        step = 32

        def body(i, carry):
            here = pl.ds(pl.multiple_of(start + i * step, step), step)
            there = pl.ds(pl.multiple_of(i * step, step), step)
            total = self.parts[index, here].astype(F32) + other[there].astype(F32)
            self.parts[index, here] = total.astype(BF16)
            return carry

        lax.fori_loop(0, count // step, body, 0)

    def loads(self, k):
        return pltpu.make_async_copy(self.part(2 * k), self.parts.at[k], self.load.at[k])

    def start(self):
        for k in (3, 1, 2, 0):
            self.copy(k).start()
        for k in (3, 1, 2, 0):
            self.loads(k).start()

    def first(self):
        for k, following in ((3, (5, 7)), (1, (4,)), (2, (6,)), (0, ())):
            self.loads(k).wait()
            self.copy(k).wait_recv()
            self.add(k, 0, self.size, self.near.at[k])
            for after in following:
                self.copy(after).start()

    def second(self):
        self.copy(5).wait_recv()
        self.add(2, 0, self.half, self.from_x.at[1])
        self.copy(8).start()
        self.copy(7).wait_recv()
        self.add(1, self.half, self.half, self.from_y.at[1])
        self.copy(9).start()

    def total(self, half, rows):
        first, last = (self.from_x, self.last_y) if half == 0 else (self.from_y, self.last_x)
        own = self.parts[0, pl.ds(pl.multiple_of(half * self.half + rows.start, 32), rows.size)]
        return own.astype(F32) + first[0, rows].astype(F32) + last[rows].astype(F32)

    def ready(self, half):
        for k in ((4, 8) if half == 0 else (6, 9)):
            self.copy(k).wait_recv()

    def finish(self):
        for k in range(10):
            self.copy(k).wait_send()


def loop_rows(count, body):
    def step(i, carry):
        body(pl.ds(pl.multiple_of(i * 32, 32), 32))
        return carry

    lax.fori_loop(0, count // 32, step, 0)


def call(kernel, identity, operands, spaces, outputs, out_spaces, scratch, cost, limit=VMEM):
    return pl.pallas_call(
        kernel,
        out_shape=outputs,
        in_specs=[pl.BlockSpec(memory_space=space) for space in spaces],
        out_specs=jax.tree.map(lambda space: pl.BlockSpec(memory_space=space), out_spaces),
        scratch_shapes=scratch,
        compiler_params=pltpu.CompilerParams(
            collective_id=identity, has_side_effects=True, vmem_limit_bytes=limit
        ),
        cost_estimate=pl.CostEstimate(flops=cost, bytes_accessed=cost // 100, transcendentals=0),
        name=kernel.__name__,
    )(*operands)


class RingBlocks:
    def __init__(self, ring, source, out_ref, send, recv):
        self.ring, self.source, self.out, self.send, self.recv = ring, source, out_ref, send, recv
        self.count = out_ref.shape[0]
        self.stage = 0

    def copy(self, k):
        source = self.source if k == 0 else self.out.at[k - 1]
        return pltpu.make_async_remote_copy(
            source, self.out.at[k], self.send.at[k], self.recv.at[k],
            device_id=ring_peer(self.ring, 1), device_id_type=MESH,
        )

    def start(self):
        self.copy(0).start()

    def advance(self):
        if self.stage + 1 < self.count:
            self.copy(self.stage).wait_recv()
            self.stage += 1
            self.copy(self.stage).start()

    def finish(self):
        while self.stage + 1 < self.count:
            self.advance()
        self.copy(self.count - 1).wait_recv()
        for k in range(self.count):
            self.copy(k).wait_send()


class RowsSwap:
    def __init__(self, ring, blocks, out_ref, local, send, recv):
        self.ring, self.blocks, self.out = ring, blocks, out_ref
        self.local, self.send, self.recv = local, send, recv
        token = lax.axis_index("tok")
        self.place, self.member = lax.div(token, 2), lax.rem(token, 2)
        self.peer = neighbours()["y"]

    def block(self, s, half):
        width = self.out.shape[1]
        return self.blocks[s].at[:, pl.ds(pl.multiple_of(half * width, width), width)]

    def target(self, s, member):
        size = self.out.shape[0] // self.ring // 2
        place = lax.rem(self.place + self.ring - s, self.ring)
        return self.out.at[pl.ds(pl.multiple_of((2 * place + member) * size, size), size)]

    def remote(self, s, source, member):
        return pltpu.make_async_remote_copy(
            source, self.target(s, member), self.send.at[s], self.recv.at[s],
            device_id=self.peer, device_id_type=MESH,
        )

    def own(self, s):
        return pltpu.make_async_copy(
            self.block(s, self.member), self.target(s, self.member), self.local.at[s]
        )

    def away(self, s):
        return self.remote(s, self.block(s, 1 - self.member), self.member)

    def start(self):
        for s in range(self.ring):
            self.away(s).start()
        for s in range(self.ring):
            self.own(s).start()

    def finish(self):
        for s in range(self.ring):
            other = 1 - self.member
            self.remote(s, self.target(s, other), other).wait_recv()
            self.away(s).wait_send()
            self.own(s).wait()


class PairSwap:
    def __init__(self, sources, out_ref, pieces, local, send, recv):
        self.sources, self.out, self.pieces = sources, out_ref, pieces
        self.local, self.send, self.recv = local, send, recv
        self.peer = neighbours()["y"]
        self.member = lax.rem(lax.axis_index("tok"), 2)

    def block(self, i, half):
        source, start, width, _ = self.pieces[i]
        ref = self.sources[source]
        offset = half * (ref.shape[1] // 2) + start
        return ref.at[:, pl.ds(pl.multiple_of(offset, 128), width)]

    def place(self, i, member):
        _, _, width, column = self.pieces[i]
        rows = self.out.shape[0] // 2
        return self.out.at[pl.ds(pl.multiple_of(member * rows, rows), rows), pl.ds(column, width)]

    def remote(self, i, source, member):
        return pltpu.make_async_remote_copy(
            source, self.place(i, member), self.send.at[i], self.recv.at[i],
            device_id=self.peer, device_id_type=MESH,
        )

    def own(self, i):
        return pltpu.make_async_copy(
            self.block(i, self.member), self.place(i, self.member), self.local.at[i]
        )

    def away(self, i):
        return self.remote(i, self.block(i, 1 - self.member), self.member)

    def start(self):
        for i in range(len(self.pieces)):
            self.away(i).start()
        for i in range(len(self.pieces)):
            self.own(i).start()

    def finish(self):
        for i in range(len(self.pieces)):
            other = 1 - self.member
            self.remote(i, self.place(i, other), other).wait_recv()
            self.away(i).wait_send()
            self.own(i).wait()


def swap_ring(identity, weights, pieces, ring, block, count, load=False):
    size = weights[0].shape[0]
    outputs = [
        jax.ShapeDtypeStruct((2 * size, sum(piece[2] for piece in pieces)), weights[0].dtype),
        jax.ShapeDtypeStruct((count, *block.shape[-2:]), block.dtype),
    ]

    def swap_start(*refs):
        sources, (block_ref, start_ref, blocks_ref, *sems) = refs[: len(weights)], refs[len(weights) :]
        if load:
            held, load_sems = sems[5:-1], sems[-1]
            loads = [
                pltpu.make_async_copy(source, kept, load_sems.at[k])
                for k, (source, kept) in enumerate(zip(sources, held))
            ]
            for copy in loads:
                copy.start()
            sources = held
        greet([ring_peer(ring, 1), ring_peer(ring, ring - 1)])
        if len(block.shape) == 3:
            block_ref = block_ref.at[block.shape[0] - 1]
        around = RingBlocks(ring, block_ref, blocks_ref, *sems[3:5])
        pair = PairSwap(sources, start_ref, pieces, *sems[:3])
        around.start()
        if load:
            for copy in loads:
                copy.wait()
        pair.start()
        around.finish()
        pair.finish()

    operands = (*weights, block)
    scratch = [pltpu.SemaphoreType.DMA((len(pieces),))] * 3
    scratch += [pltpu.SemaphoreType.DMA((count,))] * 2
    if load:
        scratch += [pltpu.VMEM(weight.shape, weight.dtype) for weight in weights]
        scratch.append(pltpu.SemaphoreType.DMA((len(weights),)))
    return call(
        swap_start, identity, operands, (pl.ANY,) * len(operands),
        outputs, [pl.ANY] * len(outputs),
        scratch, 15_000_000_000, (62 << 20) if load else VMEM,
    )


def swap_and_gather(identity, weights, pieces, shard, ring, blocks, small):
    count = len(weights)
    size = weights[0].shape[0]
    columns = sum(piece[2] for piece in pieces)
    rows, wide = shard.shape
    operands = (*weights, shard, *blocks, small)
    small_rows, small_wide = small.shape
    block_size, block_wide = blocks[0].shape[-2:]
    outputs = [
        jax.ShapeDtypeStruct((2 * size, columns), weights[0].dtype),
        jax.ShapeDtypeStruct((2 * rows, 4 * wide), shard.dtype),
        jax.ShapeDtypeStruct((2 * ring * block_size, block_wide // 2), shard.dtype),
        jax.ShapeDtypeStruct((small_rows, 4 * small_wide), small.dtype),
    ]

    def swap_gather(*refs):
        sources, shard_ref = refs[:count], refs[count]
        block_refs = refs[count + 1 : count + 1 + len(blocks)]
        small_ref, start_ref, out_ref, around_ref, whole_ref, *sems = refs[
            count + 1 + len(blocks) :
        ]
        small_send, small_recv = sems[9:]
        greet()

        def small_place(r):
            _, slot = owner(r)
            return whole_ref.at[:, pl.ds(pl.multiple_of(slot * small_wide, small_wide), small_wide)]

        def small_copy(k, source, place):
            return pltpu.make_async_remote_copy(
                source, place, small_send.at[k], small_recv.at[k],
                device_id=neighbours()[("core", "x", "core")[k]], device_id_type=MESH,
            )

        small_copies = [
            small_copy(0, small_ref, small_place(0)),
            small_copy(1, small_ref, small_place(0)),
            small_copy(2, small_place(2), small_place(2)),
        ]
        small_copies[0].start()
        small_copies[1].start()
        spread, copies = block_spread(shard_ref, out_ref, *sems[3:6])
        spread.start(0)
        spread.start(1)
        pair = PairSwap(sources, start_ref, pieces, *sems[:3])
        parts = []
        for ref in block_refs:
            parts += [ref] if len(ref.shape) == 2 else [ref.at[k] for k in range(ref.shape[0])]
        around = RowsSwap(ring, parts, around_ref, *sems[6:9])
        for copy in copies:
            copy.start()
        small_copy(1, small_place(2), small_place(2)).wait_recv()
        small_copies[2].start()
        whole_ref[:, pl.ds(pl.multiple_of(owner(0)[1] * small_wide, small_wide), small_wide)] = (
            small_ref[...]
        )
        spread.forward((0, 1, 2, 3))
        around.start()
        pair.start()
        spread.forward((6, 7))
        spread.finish()
        around.finish()
        pair.finish()
        small_copy(0, small_place(1), small_place(1)).wait_recv()
        small_copy(2, small_place(3), small_place(3)).wait_recv()
        for copy in small_copies:
            copy.wait_send()
        for copy in copies:
            copy.wait()

    return call(
        swap_gather, identity, operands, (pl.ANY,) * (len(operands) - 1) + (pltpu.VMEM,),
        outputs, [pl.ANY] * (len(outputs) - 1) + [pltpu.VMEM],
        [pltpu.SemaphoreType.DMA((len(pieces),))] * 3
        + [pltpu.SemaphoreType.DMA((2,))]
        + SPREAD_SEMS
        + [pltpu.SemaphoreType.DMA((ring,))] * 3
        + [pltpu.SemaphoreType.DMA((3,))] * 2,
        55_000_000_000,
    )


def scatter_blocks(identity, ring, vector, *terms):
    rows, wide = terms[0].shape[0] // 2, terms[0].shape[1] // 4
    count = len(terms)

    def scatter_outputs(vector_ref, *refs):
        greet([ring_peer(ring, distance) for distance in range(1, ring)])
        small_ref = refs[2 * count]
        scratch = refs[2 * count + 1 :]
        small = SumAll(ring, vector_ref, *scratch[:5])
        collects = []
        for i in range(count):

            def part(r, terms_ref=refs[i]):
                member, slot = owner(r)
                return terms_ref.at[
                    pl.ds(pl.multiple_of(member * rows, rows), rows),
                    pl.ds(pl.multiple_of(slot * wide, wide), wide),
                ]

            mine = scratch[5 + 9 * i : 5 + 9 * (i + 1)]
            collects.append(Collect(part, rows, *mine[:6], mine[6:]))
        small.start()
        for collect in collects:
            collect.start()
        small.step(0)
        for collect in collects:
            collect.first()
        small.step(1)
        for collect in collects:
            collect.second()
        small.step(2)
        for collect, out_ref in zip(collects, refs[count:]):
            for which in range(2):
                collect.ready(which)

                def body(here, collect=collect, out_ref=out_ref):
                    there = pl.ds(pl.multiple_of(which * (rows // 2) + here.start, 32), 32)
                    out_ref[there] = collect.total(which, here).astype(BF16)

                loop_rows(rows // 2, body)
        for collect in collects:
            collect.finish()
        scratch[1][0] = small.finish()
        start = pl.multiple_of(lax.axis_index("feat") * wide, wide)
        small_ref[...] = scratch[1][0, :, pl.ds(start, wide)]

    return call(
        scatter_outputs, identity, (vector, *terms), (pltpu.VMEM,) + (pl.ANY,) * count,
        [jax.ShapeDtypeStruct((rows, wide), BF16)] * count
        + [jax.ShapeDtypeStruct((vector.shape[0], wide), F32)],
        [pltpu.VMEM] * (count + 1),
        SumAll.scratch(ring, vector.shape) + Collect.scratch(rows, wide) * count,
        30_000_000_000 * count,
    )


def row_parts(terms_ref, quarter):
    def part(r):
        member, slot = owner(r)
        return terms_ref.at[pl.ds(pl.multiple_of((member * 4 + slot) * quarter, quarter), quarter)]

    return part


def row_region(out_ref, quarter):
    half = quarter // 2

    def region(r, which):
        member, slot = owner(r)
        start = (member * 4 + slot) * quarter + which * half
        return out_ref.at[pl.ds(pl.multiple_of(start, half), half)]

    return region


def middle_norm(identity, terms, x_all, gain, cotangent):
    total, model = terms.shape
    quarter = total // 8
    half = quarter // 2

    def middle_step(
        terms_ref, x_ref, gain_ref, shard_ref, out_ref, middle_ref, factor_ref, cot_ref,
        x_own, normed, local, send, recv, cot_local, cot_send, cot_recv, *scratch
    ):
        greet()
        beside, copies = block_spread(shard_ref, cot_ref, cot_local, cot_send, cot_recv)
        x_copy = pltpu.make_async_copy(row_parts(x_ref, quarter)(0), x_own, local.at[0])
        x_copy.start()
        collect = Collect(row_parts(terms_ref, quarter), quarter, *scratch[:6], scratch[6:])
        region = row_region(out_ref, quarter)
        spread = Spread(
            lambda which: normed.at[pl.ds(which * half, half)], region, send, recv
        )
        collect.start()
        beside.start(0)
        beside.start(1)
        for copy in copies:
            copy.start()
        collect.first()
        beside.forward((0, 1, 2, 3))
        collect.second()
        x_copy.wait()
        for which in range(2):
            collect.ready(which)

            def body(here):
                there = pl.ds(pl.multiple_of(which * half + here.start, 32), 32)
                middle = collect.total(which, here) + x_own[there].astype(F32)
                mean = jnp.mean(middle * middle, axis=1, keepdims=True)
                factor = lax.rsqrt(mean + EPSILON)
                middle_ref[there] = middle
                factor_ref[there] = jnp.broadcast_to(factor, (32, 128))
                normed[there] = (middle * factor * gain_ref[...]).astype(BF16)

            loop_rows(half, body)
            spread.start(which)
            copy = pltpu.make_async_copy(
                normed.at[pl.ds(which * half, half)], region(0, which), local.at[1 + which]
            )
            copy.start()
            copies.append(copy)
        beside.forward((6, 7))
        spread.forward()
        spread.finish()
        beside.finish()
        collect.finish()
        for copy in copies:
            copy.wait()

    return call(
        middle_step, identity, (terms, x_all, gain, cotangent),
        (pl.ANY, pl.ANY, pltpu.VMEM, pl.ANY),
        (
            jax.ShapeDtypeStruct((total, model), BF16),
            jax.ShapeDtypeStruct((quarter, model), F32),
            jax.ShapeDtypeStruct((quarter, 128), F32),
            jax.ShapeDtypeStruct((total, model), BF16),
        ),
        (pl.ANY, pltpu.VMEM, pltpu.VMEM, pl.ANY),
        [
            pltpu.VMEM((quarter, model), BF16),
            pltpu.VMEM((quarter, model), BF16),
            pltpu.SemaphoreType.DMA((3,)),
        ]
        + SPREAD_SEMS
        + [pltpu.SemaphoreType.DMA((2,))]
        + SPREAD_SEMS
        + Collect.scratch(quarter, model),
        100_000_000_000,
    )


def middle_back(identity, terms, cot, middle, factor, gain, hiddens, weights):
    total, model = terms.shape
    widths = [hidden.shape[1] for hidden in hiddens]
    inner_width = sum(widths)
    count = len(hiddens)
    quarter = total // 8
    half = quarter // 2

    def middle_back_step(
        terms_ref, cot_ref, middle_ref, factor_ref, gain_ref, *refs
    ):
        parts_refs, refs = refs[: 2 * count], refs[2 * count :]
        out_ref, grad_ref, gain_grad_ref, rows_ref, *refs = refs
        hidden_all, down_all, tiles, load_sems, tile_sems, *refs = refs
        cot_own, rounded, local, send, recv, *scratch = refs
        greet()
        loads = []
        left = 0
        for k, width in enumerate(widths):
            place = pl.ds(left, width)
            loads.append(
                pltpu.make_async_copy(parts_refs[k], hidden_all.at[:, place], load_sems.at[2 * k])
            )
            down = parts_refs[count + k].at[:, pl.ds(2 * width, width)]
            loads.append(
                pltpu.make_async_copy(down, down_all.at[:, place], load_sems.at[2 * k + 1])
            )
            left += width
        for load in loads:
            load.start()
        member, slot = owner(0)

        def tile_copy(index):
            start = pl.multiple_of(index * quarter, quarter)
            kept = lax.rem(index, 2)
            return pltpu.make_async_copy(
                tiles.at[kept], rows_ref.at[pl.ds(start, quarter)], tile_sems.at[kept]
            )

        def result_tiles(first, last):
            def step(index, carry):
                @pl.when(index >= 2)
                def _():
                    tile_copy(index - 2).wait()

                kept = lax.rem(index, 2)
                rows = pl.ds(pl.multiple_of(index * quarter, quarter), quarter)
                for start in range(0, model, 512):
                    here = slice(start, start + 512)
                    value = right_trans(hidden_all[rows, :], down_all[here, :])
                    tiles[kept, :, here] = value.astype(BF16)

                @pl.when(index == member * 4 + slot)
                def _():
                    tiles[kept] = (tiles[kept].astype(F32) + middle_ref[...]).astype(BF16)

                tile_copy(index).start()
                return carry

            lax.fori_loop(first, last, step, 0)

        cot_copy = pltpu.make_async_copy(row_parts(cot_ref, quarter)(0), cot_own, local.at[0])
        cot_copy.start()
        collect = Collect(row_parts(terms_ref, quarter), quarter, *scratch[:6], scratch[6:])
        region = row_region(out_ref, quarter)
        spread = Spread(
            lambda which: rounded.at[pl.ds(which * half, half)], region, send, recv
        )
        collect.start()
        collect.first()
        for load in loads:
            load.wait()
        result_tiles(0, 4)
        collect.second()
        result_tiles(4, 6)
        cot_copy.wait()
        gain_grad_ref[...] = jnp.zeros_like(gain_grad_ref)
        copies = []
        for which in range(2):
            collect.ready(which)

            def body(here):
                there = pl.ds(pl.multiple_of(which * half + here.start, 32), 32)
                grad_normed = collect.total(which, here)
                values = middle_ref[there]
                factor = factor_ref[there][:, :1]
                weighted = gain_ref[...] * grad_normed
                inner = jnp.mean(weighted * values, axis=1, keepdims=True)
                grad = (
                    cot_own[there].astype(F32)
                    + factor * weighted
                    - values * (factor * factor * factor * inner)
                )
                grad_ref[there] = grad
                rounded[there] = grad.astype(BF16)
                gain_grad_ref[...] += jnp.sum(grad_normed * values * factor, axis=0, keepdims=True)

            loop_rows(half, body)
            spread.start(which)
            copy = pltpu.make_async_copy(
                rounded.at[pl.ds(which * half, half)], region(0, which), local.at[1 + which]
            )
            copy.start()
            copies.append(copy)
        result_tiles(6, 8)
        spread.forward()
        spread.finish()
        collect.finish()
        tile_copy(6).wait()
        tile_copy(7).wait()
        for copy in copies:
            copy.wait()

    return call(
        middle_back_step, identity, (terms, cot, middle, factor, gain, *hiddens, *weights),
        (pl.ANY, pl.ANY, pltpu.VMEM, pltpu.VMEM, pltpu.VMEM) + (pl.ANY,) * (2 * count),
        (
            jax.ShapeDtypeStruct((total, model), BF16),
            jax.ShapeDtypeStruct((quarter, model), F32),
            jax.ShapeDtypeStruct((1, model), F32),
            jax.ShapeDtypeStruct((total, model), BF16),
        ),
        (pl.ANY, pltpu.VMEM, pltpu.VMEM, pl.ANY),
        [
            pltpu.VMEM((total, inner_width), BF16),
            pltpu.VMEM((model, inner_width), BF16),
            pltpu.VMEM((2, quarter, model), BF16),
            pltpu.SemaphoreType.DMA((2 * count,)),
            pltpu.SemaphoreType.DMA((2,)),
            pltpu.VMEM((quarter, model), BF16),
            pltpu.VMEM((quarter, model), BF16),
            pltpu.SemaphoreType.DMA((3,)),
        ]
        + SPREAD_SEMS
        + Collect.scratch(quarter, model),
        70_000_000_000,
    )


def assemble(plan, flipped_out, totals, others, passed=()):
    count = len(totals)
    size = others[0].shape[0]
    shapes = []
    for index, pieces in enumerate(plan):
        wide = 2 * sum(piece[2] for piece in pieces)
        shapes.append((size, wide) if index < flipped_out else (wide, size))

    def assemble_grads(*refs):
        member = lax.rem(lax.axis_index("tok"), 2)
        outs = refs[2 * count + len(passed) :]
        for i in range(len(passed)):
            outs[len(plan) + i][...] = refs[2 * count + i][...]
        for index, pieces in enumerate(plan):
            half = sum(piece[2] for piece in pieces)
            for source, column, width, target in pieces:
                own_rows = pl.ds(pl.multiple_of(member * size, size), size)
                own = refs[source][own_rows, column : column + width]
                other = refs[count + source][:, column : column + width]
                for which, block in ((member, own), (1 - member, other)):
                    start = pl.multiple_of(which * half + target, 128)
                    if index < flipped_out:
                        outs[index][:, pl.ds(start, width)] = block.astype(F32)
                    else:
                        outs[index][pl.ds(start, width), :] = block.astype(F32).T

    return pl.pallas_call(
        assemble_grads,
        out_shape=[jax.ShapeDtypeStruct(shape, F32) for shape in shapes]
        + [jax.ShapeDtypeStruct(array.shape, array.dtype) for array in passed],
        in_specs=[pl.BlockSpec(memory_space=pltpu.VMEM)] * (2 * count + len(passed)),
        out_specs=[pl.BlockSpec(memory_space=pltpu.VMEM)] * (len(plan) + len(passed)),
        compiler_params=pltpu.CompilerParams(vmem_limit_bytes=VMEM),
        cost_estimate=pl.CostEstimate(
            flops=0, transcendentals=0, bytes_accessed=8 * size * 2 * sum(t.shape[1] for t in totals)
        ),
        name="assemble_grads",
    )(*totals, *others, *passed)


def input_terms(grad_packed, weights, x_all, gain, grad_middle, own):
    total, columns = grad_packed.shape
    model = x_all.shape[1]
    tile = grad_middle.shape[0]

    def input_terms_step(own_ref, grad_ref, qkv_ref, x_ref, gain_ref, middle_ref, out_ref, gain_grad_ref):
        step = pl.program_id(0)
        grad_normed = right_trans(grad_ref[...], qkv_ref[...])
        values = x_ref[...].astype(F32)
        factor = lax.rsqrt(jnp.mean(values * values, axis=1, keepdims=True) + EPSILON)
        weighted = grad_normed * gain_ref[...]
        inner = jnp.mean(weighted * values, axis=1, keepdims=True)
        terms = factor * weighted - values * (factor * factor * factor * inner)

        @pl.when(step == own_ref[0])
        def _():
            out_ref[...] = (terms + middle_ref[...]).astype(BF16)

        @pl.when(step != own_ref[0])
        def _():
            out_ref[...] = terms.astype(BF16)

        @pl.when(step == 0)
        def _():
            gain_grad_ref[...] = jnp.zeros_like(gain_grad_ref)

        gain_grad_ref[...] += jnp.sum(grad_normed * values * factor, axis=0, keepdims=True)

    return pl.pallas_call(
        input_terms_step,
        grid_spec=pltpu.PrefetchScalarGridSpec(
            num_scalar_prefetch=1,
            grid=(total // tile,),
            in_specs=[
                pl.BlockSpec((tile, columns), lambda i, own: (i, 0)),
                pl.BlockSpec((model, columns), lambda i, own: (0, 0)),
                pl.BlockSpec((tile, model), lambda i, own: (i, 0)),
                pl.BlockSpec((1, model), lambda i, own: (0, 0)),
                pl.BlockSpec((tile, model), lambda i, own: (0, 0)),
            ],
            out_specs=[
                pl.BlockSpec((tile, model), lambda i, own: (i, 0)),
                pl.BlockSpec((1, model), lambda i, own: (0, 0)),
            ],
        ),
        out_shape=[
            jax.ShapeDtypeStruct((total, model), BF16),
            jax.ShapeDtypeStruct((1, model), F32),
        ],
        compiler_params=pltpu.CompilerParams(vmem_limit_bytes=VMEM),
        cost_estimate=pl.CostEstimate(
            flops=2 * total * columns * model,
            transcendentals=total,
            bytes_accessed=6 * total * model,
        ),
        name="input_terms",
    )(own, grad_packed, weights, x_all, gain, grad_middle)


def feed_forward(normed, cot, weights, chunk):
    total, model = normed.shape
    tile = 256
    part = 256 if chunk % 256 == 0 else 128

    def feed_step(normed_ref, cot_ref, gate_ref, up_ref, down_ref, hidden_ref, grads_ref):
        for left in range(0, chunk, part):
            here = slice(left, left + part)
            gate = product(normed_ref[...], gate_ref[:, here])
            upward = product(normed_ref[...], up_ref[:, here])
            grad_hidden = product(cot_ref[...], down_ref[:, here])
            sigma = jax.nn.sigmoid(gate)
            active = gate * sigma
            hidden_ref[:, here] = (active * upward).astype(BF16)
            grads_ref[:, here] = (
                grad_hidden * upward * (sigma + active * (1.0 - sigma))
            ).astype(BF16)
            grads_ref[:, chunk + left : chunk + left + part] = (grad_hidden * active).astype(BF16)

    rows = pl.BlockSpec((tile, model), lambda i: (i, 0))

    def weight(part):
        return pl.BlockSpec((model, chunk), lambda i: (0, part), pipeline_mode=pl.Buffered(1))

    return pl.pallas_call(
        feed_step,
        grid=(total // tile,),
        in_specs=[rows, rows, weight(0), weight(1), weight(2)],
        out_specs=[
            pl.BlockSpec((tile, chunk), lambda i: (i, 0)),
            pl.BlockSpec((tile, 2 * chunk), lambda i: (i, 0)),
        ],
        out_shape=[
            jax.ShapeDtypeStruct((total, chunk), BF16),
            jax.ShapeDtypeStruct((total, 2 * chunk), BF16),
        ],
        compiler_params=pltpu.CompilerParams(vmem_limit_bytes=VMEM),
        cost_estimate=pl.CostEstimate(
            flops=6 * total * chunk * model,
            transcendentals=total * chunk,
            bytes_accessed=4 * total * model + 6 * chunk * (model + total),
        ),
        name="feed_forward",
    )(normed, cot, weights, weights, weights)


def columns_back(lefts, weights, place, own, base=None, middle=None):
    count = len(lefts)
    total = lefts[0].shape[0]
    model = weights[0].shape[0]
    tile, part = 512, 512

    def columns_step(own_ref, *refs):
        out_ref = refs[-1]
        for start in range(0, model, part):
            here = slice(start, start + part)
            value = sum(
                right_trans(refs[i][...], refs[count + i][here, :]) for i in range(count)
            )
            if base is not None:
                value = value + refs[2 * count][:, here].astype(F32)
            out_ref[:, here] = value.astype(BF16)
        if middle is not None:
            middle_ref = refs[-2]
            size = middle_ref.shape[0]
            inside = own_ref[0] * size - pl.program_id(0) * tile

            @pl.when((inside >= 0) & (inside < tile))
            def _():
                rows = pl.ds(pl.multiple_of(inside, size), size)
                out_ref[rows, :] = (out_ref[rows, :].astype(F32) + middle_ref[...]).astype(BF16)

    in_specs = [pl.BlockSpec((tile, left.shape[1]), lambda i, own: (i, 0)) for left in lefts]
    in_specs += [
        pl.BlockSpec(
            (model, left.shape[1]), lambda i, own: (0, place), pipeline_mode=pl.Buffered(1)
        )
        for left in lefts
    ]
    operands = [own, *lefts, *weights]
    if base is not None:
        in_specs.append(pl.BlockSpec((tile, model), lambda i, own: (i, 0)))
        operands.append(base)
    if middle is not None:
        in_specs.append(pl.BlockSpec(middle.shape, lambda i, own: (0, 0)))
        operands.append(middle)
    inner = sum(left.shape[1] for left in lefts)
    return pl.pallas_call(
        columns_step,
        grid_spec=pltpu.PrefetchScalarGridSpec(
            num_scalar_prefetch=1,
            grid=(total // tile,),
            in_specs=in_specs,
            out_specs=pl.BlockSpec((tile, model), lambda i, own: (i, 0)),
        ),
        out_shape=jax.ShapeDtypeStruct((total, model), BF16),
        compiler_params=pltpu.CompilerParams(vmem_limit_bytes=VMEM),
        cost_estimate=pl.CostEstimate(
            flops=2 * total * model * inner,
            transcendentals=0,
            bytes_accessed=2 * total * model + 2 * (total + model) * inner,
        ),
        name="columns_back",
    )(*operands)


def weight_terms(pairs, tile=256):
    rows, model = pairs[0][0].shape
    count = len(pairs)
    widths = [right.shape[1] for _, right in pairs]

    def terms_step(*refs):
        out_ref = refs[-1]
        start = 0
        for i, width in enumerate(widths):
            out_ref[:, start : start + width] = left_trans(refs[i][...], refs[count + i][...]).astype(
                BF16
            )
            start += width

    return pl.pallas_call(
        terms_step,
        grid=(model // tile,),
        in_specs=[pl.BlockSpec((rows, tile), lambda i: (0, i))] * count
        + [
            pl.BlockSpec((rows, width), lambda i: (0, 0), pipeline_mode=pl.Buffered(1))
            for width in widths
        ],
        out_specs=pl.BlockSpec((tile, sum(widths)), lambda i: (i, 0)),
        out_shape=jax.ShapeDtypeStruct((model, sum(widths)), BF16),
        compiler_params=pltpu.CompilerParams(vmem_limit_bytes=VMEM),
        cost_estimate=pl.CostEstimate(
            flops=2 * rows * model * sum(widths),
            transcendentals=0,
            bytes_accessed=2 * (rows * model * count + (rows + model) * sum(widths)),
        ),
        name="weight_terms",
    )(*[left for left, _ in pairs], *[right for _, right in pairs])


def program(
    tok_size,
    tokens, gain_attn, w_query, w_key, w_value, w_out, gain_ffn, w_gate, w_up, w_down, cotangent
):
    token = lax.axis_index("tok")
    feat = lax.axis_index("feat")
    member = token % 2
    rows, wide = tokens.shape
    model = 4 * wide
    quarter = rows // 4
    groups = [list(range(i, tok_size, 2)) for i in range(2)]
    pair_width = 2 * HD

    def swap(value):
        return lax.ppermute(value, "tok", [(i, i ^ 1) for i in range(tok_size)])

    def ring_gather(shard):
        return lax.all_gather(shard, "tok", axis=0, tiled=True, axis_index_groups=groups)

    def ring_scatter(terms):
        return lax.psum_scatter(
            terms, "tok", scatter_dimension=0, tiled=True, axis_index_groups=groups
        )

    def other_half(total):
        size = total.shape[0] // 2
        return swap(lax.dynamic_slice_in_dim(total, (1 - member) * size, size, 0))

    heads_wide = w_query.shape[1] // 2
    hidden_wide = w_gate.shape[1] // 2
    chunks = [hidden_wide * part // sum(CHUNKS) for part in CHUNKS]
    lefts = [sum(chunks[:c]) for c in range(len(chunks))]
    attention_pieces = [
        (part, left, pair_width, 3 * left + part * pair_width)
        for left in range(0, heads_wide, pair_width)
        for part in range(3)
    ]
    ring = tok_size // 2
    early = min(2, ring - 2)
    out_blocks = [w_out.T]
    attention_start, block = swap_ring(
        0, (w_query, w_key, w_value), attention_pieces, ring, out_blocks[0], early, True
    )
    out_blocks.append(block)
    feed = (w_gate, w_up, w_down.T)
    block, attention_start = lax.optimization_barrier((block, attention_start))
    qkv = ring_gather(attention_start)
    plans = [
        [(part, left, size, part * size) for part in range(3)] for left, size in zip(lefts, chunks)
    ]
    first_start, block = swap_ring(1, feed, plans[0], ring, block, ring - 1 - early)
    out_blocks.append(block)
    feed_weights = [ring_gather(first_start)]
    tokens, block = lax.optimization_barrier((tokens, block))
    last_start, x_all, out_proj, gains = swap_and_gather(
        2, feed, plans[1], tokens, ring, out_blocks, jnp.stack([gain_attn, gain_ffn])
    )
    gain_one, gain_two = gains[:1], gains[1:]
    feed_weights.append(ring_gather(last_start))

    x_wide = x_all.astype(F32)
    factor_one = lax.rsqrt(jnp.mean(x_wide * x_wide, axis=1, keepdims=True) + EPSILON)
    normed = (x_wide * factor_one * gain_one).astype(BF16)
    packed = product(normed, qkv).astype(BF16)
    attended, log_sums = attend(packed)
    normed_two, middle, factor_two, cot_rows = middle_norm(
        3, right_trans(attended, out_proj).astype(BF16), x_all, gain_two, cotangent
    )

    own = (member * 4 + feat).astype(jnp.int32).reshape(1)
    feed_sums = []
    grad_normed_two = out_rows = None

    hiddens = []
    for c in range(len(chunks)):
        if c:
            feed_weights[c], grad_normed_two = lax.optimization_barrier(
                (feed_weights[c], grad_normed_two)
            )
        hidden, grad_both = feed_forward(normed_two, cot_rows, feed_weights[c], chunks[c])
        hiddens.append(hidden)
        if c + 1 < len(chunks):
            feed_terms = weight_terms([(normed_two, grad_both), (cot_rows, hidden)])
            feed_terms, grad_both = lax.optimization_barrier((feed_terms, grad_both))
            feed_sums.append(ring_scatter(feed_terms))
        grad_normed_two = columns_back(
            [grad_both], [feed_weights[c]], 0, own, grad_normed_two
        )
    grad_mid_rows, grad_middle, gain_ffn_part, out_rows = middle_back(
        4, grad_normed_two, cot_rows, middle, factor_two, gain_two, hiddens, feed_weights
    )

    hidden, grad_both, grad_mid_rows = lax.optimization_barrier((hidden, grad_both, grad_mid_rows))
    feed_terms = weight_terms(
        [(normed_two, grad_both), (cot_rows, hidden), (grad_mid_rows, attended)]
    )
    grad_mid_rows, feed_terms = lax.optimization_barrier((grad_mid_rows, feed_terms))
    feed_sums.append(ring_scatter(feed_terms))

    grad_attended = product(grad_mid_rows, out_proj).astype(BF16)
    grad_packed = attend_back(packed, attended, grad_attended, log_sums)
    attention_terms = left_trans(normed, grad_packed).astype(BF16)
    attention_terms, grad_packed = lax.optimization_barrier((attention_terms, grad_packed))
    attention_sum = ring_scatter(attention_terms)
    grad_packed, feed_sums[0] = lax.optimization_barrier((grad_packed, feed_sums[0]))
    first_other = other_half(feed_sums[0])
    terms, gain_attn_part = input_terms(grad_packed, qkv, x_all, gain_one, grad_middle, own)
    terms, first_other = lax.optimization_barrier((terms, first_other))
    outcome, input_grad, gain_grads = scatter_blocks(
        5, tok_size // 2, jnp.concatenate([gain_attn_part, gain_ffn_part]), out_rows, terms
    )
    feed_others = [first_other]
    outcome, feed_sums[1] = lax.optimization_barrier((outcome, feed_sums[1]))
    feed_others.append(other_half(feed_sums[1]))
    feed_others[1], attention_sum = lax.optimization_barrier((feed_others[1], attention_sum))
    feed_plan = [
        [(c, part * chunks[c], chunks[c], lefts[c]) for c in range(len(chunks))]
        for part in range(3)
    ]
    feed_plan.append([(len(chunks) - 1, 3 * chunks[-1], heads_wide, 0)])
    gate_grad, up_grad, down_grad, out_grad, outcome, input_grad = assemble(
        feed_plan, 2, feed_sums, feed_others, (outcome, input_grad)
    )
    attention_plan = [
        [
            (0, 3 * left + part * pair_width, pair_width, left)
            for left in range(0, heads_wide, pair_width)
        ]
        for part in range(3)
    ]
    attention_other = other_half(attention_sum)
    attention_other, gate_grad, up_grad, down_grad, outcome, input_grad = lax.optimization_barrier(
        (attention_other, gate_grad, up_grad, down_grad, outcome, input_grad)
    )
    part_grads = assemble(attention_plan, 3, [attention_sum], [attention_other])
    return (
        outcome,
        input_grad,
        gain_grads[0],
        gain_grads[1],
        *part_grads,
        out_grad,
        gate_grad,
        up_grad,
        down_grad,
    )


def solution(mesh):
    in_specs = (
        P("tok", "feat"),
        P("feat"),
        P("tok", "feat"),
        P("tok", "feat"),
        P("tok", "feat"),
        P("feat", "tok"),
        P("feat"),
        P("tok", "feat"),
        P("tok", "feat"),
        P("feat", "tok"),
        P("tok", "feat"),
    )
    out_specs = (
        P("tok", "feat"),
        P("tok", "feat"),
        P("feat"),
        P("feat"),
        P("tok", "feat"),
        P("tok", "feat"),
        P("tok", "feat"),
        P("feat", "tok"),
        P("tok", "feat"),
        P("tok", "feat"),
        P("feat", "tok"),
    )

    def on_device(*arrays):
        return program(mesh.shape["tok"], *arrays)

    return jax.shard_map(
        on_device, mesh=mesh, in_specs=in_specs, out_specs=out_specs, check_vma=False
    )
```

```python
import jax
import jax.numpy as jnp
from jax import lax
from jax.experimental import pallas as pl
from jax.experimental.pallas import tpu as pltpu
from jax.sharding import PartitionSpec as P

HD = 64
LEN = 1024
EPSILON = 1e-05
BF16 = jnp.bfloat16
F32 = jnp.float32
MESH = pl.DeviceIdType.MESH
VMEM = 48 << 20
FORWARD_BLOCK = 512
BACK_BLOCK = 256
CHUNKS = (3, 1)


def left_trans(left, right):
    return lax.dot_general(
        left, right, (((0,), (0,)), ((), ())), preferred_element_type=F32
    )


def right_trans(left, right):
    return lax.dot_general(
        left, right, (((1,), (1,)), ((), ())), preferred_element_type=F32
    )


def product(left, right):
    return jnp.dot(left, right, preferred_element_type=F32)


def causal_tile(scores):
    size = scores.shape[0]
    key = lax.broadcasted_iota(jnp.int32, scores.shape, 0)
    query = lax.broadcasted_iota(jnp.int32, scores.shape, 1)
    return jnp.where(key <= query, scores, -1e30)


def head_parts(packed_ref, head, width):
    columns = [slice(part * width + head * HD, part * width + (head + 1) * HD) for part in range(3)]
    query, key, value = [packed_ref[:, part] for part in columns]
    return query * HD ** (-0.5), key, value


def attend_kernel(packed_ref, out_ref, lse_ref):
    width = out_ref.shape[1]
    for head in range(width // HD):
        query, key, value = head_parts(packed_ref, head, width)
        query = query.astype(BF16)
        value_t = value.T
        for top in range(0, LEN, FORWARD_BLOCK):
            keys = top + FORWARD_BLOCK
            scores = right_trans(key[:keys], query[top:keys])
            last = causal_tile(scores[top:])
            scores = jnp.concatenate([scores[:top], last]) if top else last
            highest = jnp.max(scores, axis=0, keepdims=True)
            exponent = jnp.exp(scores - highest)
            total = jnp.sum(exponent, axis=0, keepdims=True)
            mixed = product(value_t[:, :keys], exponent.astype(BF16)) / total
            out_ref[top:keys, head * HD : (head + 1) * HD] = mixed.T.astype(BF16)
            lse_ref[0, 0, head : head + 1, top:keys] = highest + jnp.log(total)


def attend_back_kernel(packed_ref, out_ref, grad_ref, lse_ref, grads_ref, key_acc, value_acc):
    width = out_ref.shape[1]
    for head in range(width // HD):
        lanes = slice(head * HD, (head + 1) * HD)
        query, key, value = head_parts(packed_ref, head, width)
        query = query.astype(BF16)
        key_t = key.T
        grad = grad_ref[:, lanes]
        inner = (out_ref[:, lanes].astype(F32) * grad.astype(F32)).T
        inner = jnp.sum(inner, axis=0, keepdims=True)
        for top in reversed(range(0, LEN, BACK_BLOCK)):
            keys = top + BACK_BLOCK
            scores = right_trans(key[:keys], query[top:keys])
            last = causal_tile(scores[top:])
            scores = jnp.concatenate([scores[:top], last]) if top else last
            probs = jnp.exp(scores - lse_ref[0, 0, head : head + 1, top:keys])
            grad_probs = right_trans(value[:keys], grad[top:keys])
            grad_scores = (probs * (grad_probs - inner[:, top:keys])).astype(BF16)
            value_term = product(probs.astype(BF16), grad[top:keys])
            key_term = product(grad_scores, query[top:keys])
            if keys == LEN:
                value_acc[...] = value_term
                key_acc[...] = key_term
            else:
                value_acc[:keys] += value_term
                key_acc[:keys] += key_term
            grad_query = product(key_t[:, :keys], grad_scores) * HD ** (-0.5)
            grads_ref[top:keys, lanes] = grad_query.T.astype(BF16)
        grads_ref[:, width + head * HD : width + (head + 1) * HD] = key_acc[...].astype(BF16)
        grads_ref[:, 2 * width + head * HD : 2 * width + (head + 1) * HD] = value_acc[...].astype(
            BF16
        )


def attend(packed):
    rows, columns = packed.shape
    width = 2 * HD
    sequences, pairs = rows // LEN, columns // (3 * width)
    return pl.pallas_call(
        attend_kernel,
        grid=(sequences, pairs),
        out_shape=(
            jax.ShapeDtypeStruct((rows, pairs * width), BF16),
            jax.ShapeDtypeStruct((sequences, pairs, 2, LEN), F32),
        ),
        in_specs=[pl.BlockSpec((LEN, 3 * width), lambda s, p: (s, p))],
        out_specs=(
            pl.BlockSpec((LEN, width), lambda s, p: (s, p)),
            pl.BlockSpec((1, 1, 2, LEN), lambda s, p: (s, p, 0, 0)),
        ),
        compiler_params=pltpu.CompilerParams(vmem_limit_bytes=VMEM),
        cost_estimate=pl.CostEstimate(
            flops=4 * rows * LEN * pairs * width // 2,
            transcendentals=rows * LEN * pairs,
            bytes_accessed=2 * rows * columns * 2,
        ),
        name="attend",
    )(packed)


def attend_back(packed, attended, grad_attended, lse):
    rows, columns = packed.shape
    width = 2 * HD
    sequences, pairs = rows // LEN, columns // (3 * width)
    narrow = pl.BlockSpec((LEN, width), lambda s, p: (s, p))
    return pl.pallas_call(
        attend_back_kernel,
        grid=(sequences, pairs),
        out_shape=jax.ShapeDtypeStruct((rows, columns), BF16),
        in_specs=[
            pl.BlockSpec((LEN, 3 * width), lambda s, p: (s, p)),
            narrow,
            narrow,
            pl.BlockSpec((1, 1, 2, LEN), lambda s, p: (s, p, 0, 0)),
        ],
        out_specs=pl.BlockSpec((LEN, 3 * width), lambda s, p: (s, p)),
        scratch_shapes=[pltpu.VMEM((LEN, HD), F32)] * 2,
        compiler_params=pltpu.CompilerParams(vmem_limit_bytes=VMEM),
        cost_estimate=pl.CostEstimate(
            flops=10 * rows * LEN * pairs * width // 2,
            transcendentals=rows * LEN * pairs,
            bytes_accessed=3 * rows * columns * 2,
        ),
        name="attend_back",
    )(packed, attended, grad_attended, lse)


SPREAD = (
    (0, 0, "y", None),
    (0, 1, "x", None),
    (0, 0, "x", None),
    (0, 1, "y", None),
    (0, 0, "core", None),
    (0, 1, "core", None),
    (4, 0, "x", 0),
    (2, 1, "y", 1),
    (4, 0, "core", 0),
    (2, 1, "core", 1),
    (2, 0, "core", 2),
    (4, 1, "core", 3),
    (6, 0, "core", 6),
    (6, 1, "core", 7),
)
BIT = {"y": 4, "x": 2, "core": 1}


def neighbours():
    token, feat = lax.axis_index("tok"), lax.axis_index("feat")
    return {
        "y": (token + 1 - 2 * lax.rem(token, 2), feat),
        "x": (token, lax.rem(feat + 2, 4)),
        "core": (token, feat + 1 - 2 * lax.rem(feat, 2)),
    }


def owner(r):
    member, slot = lax.rem(lax.axis_index("tok"), 2), lax.axis_index("feat")
    if r & 4:
        member = 1 - member
    if r & 2:
        slot = lax.rem(slot + 2, 4)
    if r & 1:
        slot = slot + 1 - 2 * lax.rem(slot, 2)
    return member, slot


def greet(others=()):
    barrier = pltpu.get_barrier_semaphore()
    peers = [*neighbours().values(), *others]
    for peer in peers:
        pl.semaphore_signal(barrier, inc=1, device_id=peer, device_id_type=MESH)
    pl.semaphore_wait(barrier, len(peers))


def ring_peer(ring, distance):
    token = lax.axis_index("tok")
    return lax.rem(token + 2 * distance, 2 * ring), lax.axis_index("feat")


class SumAll:
    def __init__(self, ring, ref, steps, arrived, slots, send, recv):
        self.ring, self.ref = ring, ref
        self.steps, self.arrived, self.slots = steps, arrived, slots
        self.send, self.recv = send, recv
        self.place = lax.div(lax.axis_index("tok"), 2)
        self.peers = neighbours()

    @staticmethod
    def scratch(ring, shape):
        return [
            pltpu.VMEM((3, *shape), F32),
            pltpu.VMEM((3, *shape), F32),
            pltpu.VMEM((ring, *shape), F32),
            pltpu.SemaphoreType.DMA((2 + ring,)),
            pltpu.SemaphoreType.DMA((2 + ring,)),
        ]

    def copy(self, k):
        if k < 3:
            source = self.ref if k == 0 else self.steps.at[k - 1]
            target, peer = self.arrived.at[k], self.peers[("core", "x", "y")[k]]
        else:
            source, target = self.steps.at[2], self.slots.at[self.place]
            peer = ring_peer(self.ring, k - 2)
        return pltpu.make_async_remote_copy(
            source, target, self.send.at[k], self.recv.at[k],
            device_id=peer, device_id_type=MESH,
        )

    def start(self):
        self.copy(0).start()

    def step(self, k):
        self.copy(k).wait_recv()
        before = self.ref[...] if k == 0 else self.steps[k - 1]
        self.steps[k] = before + self.arrived[k]
        if k < 2:
            self.copy(k + 1).start()
        else:
            for distance in range(1, self.ring):
                self.copy(2 + distance).start()
            self.slots[self.place] = self.steps[2]

    def finish(self):
        for distance in range(1, self.ring):
            source = lax.rem(self.place + self.ring - distance, self.ring)
            k = 2 + distance
            pltpu.make_async_remote_copy(
                self.slots.at[source], self.slots.at[source], self.send.at[k], self.recv.at[k],
                device_id=ring_peer(self.ring, distance), device_id_type=MESH,
            ).wait_recv()
        for k in range(2 + self.ring):
            self.copy(k).wait_send()
        total = self.slots[0]
        for place in range(1, self.ring):
            total = total + self.slots[place]
        return total


class Spread:
    def __init__(self, own, region, send, recv):
        self.own, self.region, self.send, self.recv = own, region, send, recv
        self.peers = neighbours()

    def copy(self, k):
        r, half, way, _ = SPREAD[k]
        source = self.own(half) if r == 0 else self.region(r, half)
        return pltpu.make_async_remote_copy(
            source, self.region(r, half), self.send.at[k], self.recv.at[k],
            device_id=self.peers[way], device_id_type=MESH,
        )

    def arrival(self, k):
        r, half, way, _ = SPREAD[k]
        place = self.region(r ^ BIT[way], half)
        return pltpu.make_async_remote_copy(
            place, place, self.send.at[k], self.recv.at[k],
            device_id=self.peers[way], device_id_type=MESH,
        )

    def start(self, half):
        for k, (r, which, _, after) in enumerate(SPREAD):
            if after is None and which == half:
                self.copy(k).start()

    def forward(self, arrivals=(0, 1, 2, 3, 6, 7)):
        for first in arrivals:
            self.arrival(first).wait_recv()
            for k, (_, _, _, after) in enumerate(SPREAD):
                if after == first:
                    self.copy(k).start()

    def finish(self):
        for k, (_, _, way, _) in enumerate(SPREAD):
            if way == "core":
                self.arrival(k).wait_recv()
        for k in range(len(SPREAD)):
            self.copy(k).wait_send()


SPREAD_SEMS = [pltpu.SemaphoreType.DMA((len(SPREAD),))] * 2


def block_spread(shard_ref, out_ref, local, send, recv):
    rows, wide = shard_ref.shape
    half = rows // 2

    def own(which):
        return shard_ref.at[pl.ds(which * half, half)]

    def region(r, which):
        member, slot = owner(r)
        return out_ref.at[
            pl.ds(pl.multiple_of(member * rows + which * half, half), half),
            pl.ds(pl.multiple_of(slot * wide, wide), wide),
        ]

    copies = [
        pltpu.make_async_copy(own(which), region(0, which), local.at[which]) for which in range(2)
    ]
    return Spread(own, region, send, recv), copies


class Collect:
    def __init__(self, part, size, parts, near, from_x, from_y, last_y, last_x, sems):
        self.part, self.size, self.half = part, size, size // 2
        self.parts, self.near = parts, near
        self.from_x, self.from_y, self.last_y, self.last_x = from_x, from_y, last_y, last_x
        self.load, self.send, self.recv = sems
        self.peers = neighbours()

    @staticmethod
    def scratch(size, columns):
        half = size // 2
        return [
            pltpu.VMEM((4, size, columns), BF16),
            pltpu.VMEM((4, size, columns), BF16),
            pltpu.VMEM((2, half, columns), BF16),
            pltpu.VMEM((2, half, columns), BF16),
            pltpu.VMEM((half, columns), BF16),
            pltpu.VMEM((half, columns), BF16),
            pltpu.SemaphoreType.DMA((4,)),
            pltpu.SemaphoreType.DMA((10,)),
            pltpu.SemaphoreType.DMA((10,)),
        ]

    def remote(self, k, source, target, way):
        return pltpu.make_async_remote_copy(
            source, target, self.send.at[k], self.recv.at[k],
            device_id=self.peers[way], device_id_type=MESH,
        )

    def copy(self, k):
        low, high = pl.ds(0, self.half), pl.ds(self.half, self.half)
        if k < 4:
            return self.remote(k, self.part(2 * k + 1), self.near.at[k], "core")
        if k < 6:
            return self.remote(k, self.parts.at[(1, 3)[k - 4], low], self.from_x.at[k - 4], "x")
        if k < 8:
            return self.remote(k, self.parts.at[(2, 3)[k - 6], high], self.from_y.at[k - 6], "y")
        if k == 8:
            return self.remote(k, self.parts.at[2, low], self.last_y, "y")
        return self.remote(k, self.parts.at[1, high], self.last_x, "x")

    def add(self, index, start, count, other):
        step = 32

        def body(i, carry):
            here = pl.ds(pl.multiple_of(start + i * step, step), step)
            there = pl.ds(pl.multiple_of(i * step, step), step)
            total = self.parts[index, here].astype(F32) + other[there].astype(F32)
            self.parts[index, here] = total.astype(BF16)
            return carry

        lax.fori_loop(0, count // step, body, 0)

    def loads(self, k):
        return pltpu.make_async_copy(self.part(2 * k), self.parts.at[k], self.load.at[k])

    def start(self):
        for k in (3, 1, 2, 0):
            self.copy(k).start()
        for k in (3, 1, 2, 0):
            self.loads(k).start()

    def first(self):
        for k, following in ((3, (5, 7)), (1, (4,)), (2, (6,)), (0, ())):
            self.loads(k).wait()
            self.copy(k).wait_recv()
            self.add(k, 0, self.size, self.near.at[k])
            for after in following:
                self.copy(after).start()

    def second(self):
        self.copy(5).wait_recv()
        self.add(2, 0, self.half, self.from_x.at[1])
        self.copy(8).start()
        self.copy(7).wait_recv()
        self.add(1, self.half, self.half, self.from_y.at[1])
        self.copy(9).start()

    def total(self, half, rows):
        first, last = (self.from_x, self.last_y) if half == 0 else (self.from_y, self.last_x)
        own = self.parts[0, pl.ds(pl.multiple_of(half * self.half + rows.start, 32), rows.size)]
        return own.astype(F32) + first[0, rows].astype(F32) + last[rows].astype(F32)

    def ready(self, half):
        for k in ((4, 8) if half == 0 else (6, 9)):
            self.copy(k).wait_recv()

    def finish(self):
        for k in range(10):
            self.copy(k).wait_send()


def loop_rows(count, body):
    def step(i, carry):
        body(pl.ds(pl.multiple_of(i * 32, 32), 32))
        return carry

    lax.fori_loop(0, count // 32, step, 0)


def call(kernel, identity, operands, spaces, outputs, out_spaces, scratch, cost, limit=VMEM):
    return pl.pallas_call(
        kernel,
        out_shape=outputs,
        in_specs=[pl.BlockSpec(memory_space=space) for space in spaces],
        out_specs=jax.tree.map(lambda space: pl.BlockSpec(memory_space=space), out_spaces),
        scratch_shapes=scratch,
        compiler_params=pltpu.CompilerParams(
            collective_id=identity, has_side_effects=True, vmem_limit_bytes=limit
        ),
        cost_estimate=pl.CostEstimate(flops=cost, bytes_accessed=cost // 100, transcendentals=0),
        name=kernel.__name__,
    )(*operands)


class RingBlocks:
    def __init__(self, ring, source, out_ref, send, recv):
        self.ring, self.source, self.out, self.send, self.recv = ring, source, out_ref, send, recv
        self.count = out_ref.shape[0]
        self.stage = 0

    def copy(self, k):
        source = self.source if k == 0 else self.out.at[k - 1]
        return pltpu.make_async_remote_copy(
            source, self.out.at[k], self.send.at[k], self.recv.at[k],
            device_id=ring_peer(self.ring, 1), device_id_type=MESH,
        )

    def start(self):
        self.copy(0).start()

    def advance(self):
        if self.stage + 1 < self.count:
            self.copy(self.stage).wait_recv()
            self.stage += 1
            self.copy(self.stage).start()

    def finish(self):
        while self.stage + 1 < self.count:
            self.advance()
        self.copy(self.count - 1).wait_recv()
        for k in range(self.count):
            self.copy(k).wait_send()


class RowsSwap:
    def __init__(self, ring, blocks, out_ref, local, send, recv):
        self.ring, self.blocks, self.out = ring, blocks, out_ref
        self.local, self.send, self.recv = local, send, recv
        token = lax.axis_index("tok")
        self.place, self.member = lax.div(token, 2), lax.rem(token, 2)
        self.peer = neighbours()["y"]

    def block(self, s, half):
        width = self.out.shape[1]
        return self.blocks[s].at[:, pl.ds(pl.multiple_of(half * width, width), width)]

    def target(self, s, member):
        size = self.out.shape[0] // self.ring // 2
        place = lax.rem(self.place + self.ring - s, self.ring)
        return self.out.at[pl.ds(pl.multiple_of((2 * place + member) * size, size), size)]

    def remote(self, s, source, member):
        return pltpu.make_async_remote_copy(
            source, self.target(s, member), self.send.at[s], self.recv.at[s],
            device_id=self.peer, device_id_type=MESH,
        )

    def own(self, s):
        return pltpu.make_async_copy(
            self.block(s, self.member), self.target(s, self.member), self.local.at[s]
        )

    def away(self, s):
        return self.remote(s, self.block(s, 1 - self.member), self.member)

    def start(self):
        for s in range(self.ring):
            self.away(s).start()
        for s in range(self.ring):
            self.own(s).start()

    def finish(self):
        for s in range(self.ring):
            other = 1 - self.member
            self.remote(s, self.target(s, other), other).wait_recv()
            self.away(s).wait_send()
            self.own(s).wait()


class PairSwap:
    def __init__(self, sources, out_ref, pieces, local, send, recv):
        self.sources, self.out, self.pieces = sources, out_ref, pieces
        self.local, self.send, self.recv = local, send, recv
        self.peer = neighbours()["y"]
        self.member = lax.rem(lax.axis_index("tok"), 2)

    def block(self, i, half):
        source, start, width, _ = self.pieces[i]
        ref = self.sources[source]
        offset = half * (ref.shape[1] // 2) + start
        return ref.at[:, pl.ds(pl.multiple_of(offset, 128), width)]

    def place(self, i, member):
        _, _, width, column = self.pieces[i]
        rows = self.out.shape[0] // 2
        return self.out.at[pl.ds(pl.multiple_of(member * rows, rows), rows), pl.ds(column, width)]

    def remote(self, i, source, member):
        return pltpu.make_async_remote_copy(
            source, self.place(i, member), self.send.at[i], self.recv.at[i],
            device_id=self.peer, device_id_type=MESH,
        )

    def own(self, i):
        return pltpu.make_async_copy(
            self.block(i, self.member), self.place(i, self.member), self.local.at[i]
        )

    def away(self, i):
        return self.remote(i, self.block(i, 1 - self.member), self.member)

    def start(self):
        for i in range(len(self.pieces)):
            self.away(i).start()
        for i in range(len(self.pieces)):
            self.own(i).start()

    def finish(self):
        for i in range(len(self.pieces)):
            other = 1 - self.member
            self.remote(i, self.place(i, other), other).wait_recv()
            self.away(i).wait_send()
            self.own(i).wait()


def swap_ring(identity, weights, pieces, ring, block, count, load=False):
    size = weights[0].shape[0]
    block_shape = block.shape[::-1] if load else block.shape[-2:]
    outputs = [
        jax.ShapeDtypeStruct((2 * size, sum(piece[2] for piece in pieces)), weights[0].dtype),
        jax.ShapeDtypeStruct((count, *block_shape), block.dtype),
    ]

    def swap_start(*refs):
        sources, (block_ref, start_ref, blocks_ref, *sems) = refs[: len(weights)], refs[len(weights) :]
        if load:
            held, raw, turned, load_sems = sems[5:-3], sems[-3], sems[-2], sems[-1]
            loads = [
                pltpu.make_async_copy(source, kept, load_sems.at[k])
                for k, (source, kept) in enumerate(zip([*sources, block_ref], [*held, raw]))
            ]
            for copy in loads:
                copy.start()
            sources, block_ref = held, turned
            loads.pop().wait()
            turned[...] = raw[...].T
        greet([ring_peer(ring, 1), ring_peer(ring, ring - 1)])
        if len(block.shape) == 3:
            block_ref = block_ref.at[block.shape[0] - 1]
        around = RingBlocks(ring, block_ref, blocks_ref, *sems[3:5])
        pair = PairSwap(sources, start_ref, pieces, *sems[:3])
        around.start()
        if load:
            for copy in loads:
                copy.wait()
        pair.start()
        around.finish()
        pair.finish()

    operands = (*weights, block)
    scratch = [pltpu.SemaphoreType.DMA((len(pieces),))] * 3
    scratch += [pltpu.SemaphoreType.DMA((count,))] * 2
    if load:
        scratch += [pltpu.VMEM(weight.shape, weight.dtype) for weight in weights]
        scratch += [pltpu.VMEM(block.shape, block.dtype), pltpu.VMEM(block_shape, block.dtype)]
        scratch.append(pltpu.SemaphoreType.DMA((len(weights) + 1,)))
    return call(
        swap_start, identity, operands, (pl.ANY,) * len(operands),
        outputs, [pl.ANY] * len(outputs),
        scratch, 15_000_000_000, (62 << 20) if load else VMEM,
    )


def swap_and_gather(identity, weights, pieces, shard, ring, blocks, small):
    count = len(weights)
    size = weights[0].shape[0]
    columns = sum(piece[2] for piece in pieces)
    rows, wide = shard.shape
    operands = (*weights, shard, *blocks, small)
    small_rows, small_wide = small.shape
    block_size, block_wide = blocks[0].shape[-2:]
    outputs = [
        jax.ShapeDtypeStruct((2 * size, columns), weights[0].dtype),
        jax.ShapeDtypeStruct((2 * rows, 4 * wide), shard.dtype),
        jax.ShapeDtypeStruct((2 * ring * block_size, block_wide // 2), shard.dtype),
        jax.ShapeDtypeStruct((small_rows, 4 * small_wide), small.dtype),
    ]

    def swap_gather(*refs):
        sources, shard_ref = refs[:count], refs[count]
        block_refs = refs[count + 1 : count + 1 + len(blocks)]
        small_ref, start_ref, out_ref, around_ref, whole_ref, *sems = refs[
            count + 1 + len(blocks) :
        ]
        small_send, small_recv = sems[9:]
        greet()

        def small_place(r):
            _, slot = owner(r)
            return whole_ref.at[:, pl.ds(pl.multiple_of(slot * small_wide, small_wide), small_wide)]

        def small_copy(k, source, place):
            return pltpu.make_async_remote_copy(
                source, place, small_send.at[k], small_recv.at[k],
                device_id=neighbours()[("core", "x", "core")[k]], device_id_type=MESH,
            )

        small_copies = [
            small_copy(0, small_ref, small_place(0)),
            small_copy(1, small_ref, small_place(0)),
            small_copy(2, small_place(2), small_place(2)),
        ]
        small_copies[0].start()
        small_copies[1].start()
        spread, copies = block_spread(shard_ref, out_ref, *sems[3:6])
        spread.start(0)
        spread.start(1)
        pair = PairSwap(sources, start_ref, pieces, *sems[:3])
        parts = []
        for ref in block_refs:
            parts += [ref] if len(ref.shape) == 2 else [ref.at[k] for k in range(ref.shape[0])]
        around = RowsSwap(ring, parts, around_ref, *sems[6:9])
        for copy in copies:
            copy.start()
        small_copy(1, small_place(2), small_place(2)).wait_recv()
        small_copies[2].start()
        whole_ref[:, pl.ds(pl.multiple_of(owner(0)[1] * small_wide, small_wide), small_wide)] = (
            small_ref[...]
        )
        spread.forward((0, 1, 2, 3))
        around.start()
        pair.start()
        spread.forward((6, 7))
        spread.finish()
        around.finish()
        pair.finish()
        small_copy(0, small_place(1), small_place(1)).wait_recv()
        small_copy(2, small_place(3), small_place(3)).wait_recv()
        for copy in small_copies:
            copy.wait_send()
        for copy in copies:
            copy.wait()

    return call(
        swap_gather, identity, operands, (pl.ANY,) * (len(operands) - 1) + (pltpu.VMEM,),
        outputs, [pl.ANY] * (len(outputs) - 1) + [pltpu.VMEM],
        [pltpu.SemaphoreType.DMA((len(pieces),))] * 3
        + [pltpu.SemaphoreType.DMA((2,))]
        + SPREAD_SEMS
        + [pltpu.SemaphoreType.DMA((ring,))] * 3
        + [pltpu.SemaphoreType.DMA((3,))] * 2,
        55_000_000_000,
    )


def scatter_blocks(identity, ring, vector, *terms):
    rows, wide = terms[0].shape[0] // 2, terms[0].shape[1] // 4
    count = len(terms)

    def scatter_outputs(vector_ref, *refs):
        greet([ring_peer(ring, distance) for distance in range(1, ring)])
        small_ref = refs[2 * count]
        scratch = refs[2 * count + 1 :]
        small = SumAll(ring, vector_ref, *scratch[:5])
        collects = []
        for i in range(count):

            def part(r, terms_ref=refs[i]):
                member, slot = owner(r)
                return terms_ref.at[
                    pl.ds(pl.multiple_of(member * rows, rows), rows),
                    pl.ds(pl.multiple_of(slot * wide, wide), wide),
                ]

            mine = scratch[5 + 9 * i : 5 + 9 * (i + 1)]
            collects.append(Collect(part, rows, *mine[:6], mine[6:]))
        small.start()
        for collect in collects:
            collect.start()
        small.step(0)
        for collect in collects:
            collect.first()
        small.step(1)
        for collect in collects:
            collect.second()
        small.step(2)
        for collect, out_ref in zip(collects, refs[count:]):
            for which in range(2):
                collect.ready(which)

                def body(here, collect=collect, out_ref=out_ref):
                    there = pl.ds(pl.multiple_of(which * (rows // 2) + here.start, 32), 32)
                    out_ref[there] = collect.total(which, here).astype(BF16)

                loop_rows(rows // 2, body)
        for collect in collects:
            collect.finish()
        scratch[1][0] = small.finish()
        start = pl.multiple_of(lax.axis_index("feat") * wide, wide)
        small_ref[...] = scratch[1][0, :, pl.ds(start, wide)]

    return call(
        scatter_outputs, identity, (vector, *terms), (pltpu.VMEM,) + (pl.ANY,) * count,
        [jax.ShapeDtypeStruct((rows, wide), BF16)] * count
        + [jax.ShapeDtypeStruct((vector.shape[0], wide), F32)],
        [pltpu.VMEM] * (count + 1),
        SumAll.scratch(ring, vector.shape) + Collect.scratch(rows, wide) * count,
        30_000_000_000 * count,
    )


def row_parts(terms_ref, quarter):
    def part(r):
        member, slot = owner(r)
        return terms_ref.at[pl.ds(pl.multiple_of((member * 4 + slot) * quarter, quarter), quarter)]

    return part


def row_region(out_ref, quarter):
    half = quarter // 2

    def region(r, which):
        member, slot = owner(r)
        start = (member * 4 + slot) * quarter + which * half
        return out_ref.at[pl.ds(pl.multiple_of(start, half), half)]

    return region


def middle_norm(identity, terms, x_all, gain, cotangent):
    total, model = terms.shape
    quarter = total // 8
    half = quarter // 2

    def middle_step(
        terms_ref, x_ref, gain_ref, shard_ref, out_ref, middle_ref, factor_ref, cot_ref,
        x_own, normed, local, send, recv, cot_local, cot_send, cot_recv, *scratch
    ):
        greet()
        beside, copies = block_spread(shard_ref, cot_ref, cot_local, cot_send, cot_recv)
        x_copy = pltpu.make_async_copy(row_parts(x_ref, quarter)(0), x_own, local.at[0])
        x_copy.start()
        collect = Collect(row_parts(terms_ref, quarter), quarter, *scratch[:6], scratch[6:])
        region = row_region(out_ref, quarter)
        spread = Spread(
            lambda which: normed.at[pl.ds(which * half, half)], region, send, recv
        )
        collect.start()
        beside.start(0)
        beside.start(1)
        for copy in copies:
            copy.start()
        collect.first()
        beside.forward((0, 1, 2, 3))
        collect.second()
        x_copy.wait()
        for which in range(2):
            collect.ready(which)

            def body(here):
                there = pl.ds(pl.multiple_of(which * half + here.start, 32), 32)
                middle = collect.total(which, here) + x_own[there].astype(F32)
                mean = jnp.mean(middle * middle, axis=1, keepdims=True)
                factor = lax.rsqrt(mean + EPSILON)
                middle_ref[there] = middle
                factor_ref[there] = jnp.broadcast_to(factor, (32, 128))
                normed[there] = (middle * factor * gain_ref[...]).astype(BF16)

            loop_rows(half, body)
            spread.start(which)
            copy = pltpu.make_async_copy(
                normed.at[pl.ds(which * half, half)], region(0, which), local.at[1 + which]
            )
            copy.start()
            copies.append(copy)
        beside.forward((6, 7))
        spread.forward()
        spread.finish()
        beside.finish()
        collect.finish()
        for copy in copies:
            copy.wait()

    return call(
        middle_step, identity, (terms, x_all, gain, cotangent),
        (pl.ANY, pl.ANY, pltpu.VMEM, pl.ANY),
        (
            jax.ShapeDtypeStruct((total, model), BF16),
            jax.ShapeDtypeStruct((quarter, model), F32),
            jax.ShapeDtypeStruct((quarter, 128), F32),
            jax.ShapeDtypeStruct((total, model), BF16),
        ),
        (pl.ANY, pltpu.VMEM, pltpu.VMEM, pl.ANY),
        [
            pltpu.VMEM((quarter, model), BF16),
            pltpu.VMEM((quarter, model), BF16),
            pltpu.SemaphoreType.DMA((3,)),
        ]
        + SPREAD_SEMS
        + [pltpu.SemaphoreType.DMA((2,))]
        + SPREAD_SEMS
        + Collect.scratch(quarter, model),
        100_000_000_000,
    )


def middle_back(identity, terms, cot, middle, factor, gain, hiddens, weights):
    total, model = terms.shape
    widths = [hidden.shape[1] for hidden in hiddens]
    inner_width = sum(widths)
    count = len(hiddens)
    quarter = total // 8
    half = quarter // 2

    def middle_back_step(
        terms_ref, cot_ref, middle_ref, factor_ref, gain_ref, *refs
    ):
        parts_refs, refs = refs[: 2 * count], refs[2 * count :]
        out_ref, grad_ref, gain_grad_ref, rows_ref, *refs = refs
        hidden_all, down_all, tiles, load_sems, tile_sems, *refs = refs
        cot_own, rounded, local, send, recv, *scratch = refs
        greet()
        loads = []
        left = 0
        for k, width in enumerate(widths):
            place = pl.ds(left, width)
            loads.append(
                pltpu.make_async_copy(parts_refs[k], hidden_all.at[:, place], load_sems.at[2 * k])
            )
            down = parts_refs[count + k].at[:, pl.ds(2 * width, width)]
            loads.append(
                pltpu.make_async_copy(down, down_all.at[:, place], load_sems.at[2 * k + 1])
            )
            left += width
        for load in loads:
            load.start()
        member, slot = owner(0)

        def tile_copy(index):
            start = pl.multiple_of(index * quarter, quarter)
            kept = lax.rem(index, 2)
            return pltpu.make_async_copy(
                tiles.at[kept], rows_ref.at[pl.ds(start, quarter)], tile_sems.at[kept]
            )

        def result_tiles(first, last):
            def step(index, carry):
                @pl.when(index >= 2)
                def _():
                    tile_copy(index - 2).wait()

                kept = lax.rem(index, 2)
                rows = pl.ds(pl.multiple_of(index * quarter, quarter), quarter)
                for start in range(0, model, 512):
                    here = slice(start, start + 512)
                    value = right_trans(hidden_all[rows, :], down_all[here, :])
                    tiles[kept, :, here] = value.astype(BF16)

                @pl.when(index == member * 4 + slot)
                def _():
                    tiles[kept] = (tiles[kept].astype(F32) + middle_ref[...]).astype(BF16)

                tile_copy(index).start()
                return carry

            lax.fori_loop(first, last, step, 0)

        cot_copy = pltpu.make_async_copy(row_parts(cot_ref, quarter)(0), cot_own, local.at[0])
        cot_copy.start()
        collect = Collect(row_parts(terms_ref, quarter), quarter, *scratch[:6], scratch[6:])
        region = row_region(out_ref, quarter)
        spread = Spread(
            lambda which: rounded.at[pl.ds(which * half, half)], region, send, recv
        )
        collect.start()
        collect.first()
        for load in loads:
            load.wait()
        result_tiles(0, 4)
        collect.second()
        result_tiles(4, 6)
        cot_copy.wait()
        gain_grad_ref[...] = jnp.zeros_like(gain_grad_ref)
        copies = []
        for which in range(2):
            collect.ready(which)

            def body(here):
                there = pl.ds(pl.multiple_of(which * half + here.start, 32), 32)
                grad_normed = collect.total(which, here)
                values = middle_ref[there]
                factor = factor_ref[there][:, :1]
                weighted = gain_ref[...] * grad_normed
                inner = jnp.mean(weighted * values, axis=1, keepdims=True)
                grad = (
                    cot_own[there].astype(F32)
                    + factor * weighted
                    - values * (factor * factor * factor * inner)
                )
                grad_ref[there] = grad
                rounded[there] = grad.astype(BF16)
                gain_grad_ref[...] += jnp.sum(grad_normed * values * factor, axis=0, keepdims=True)

            loop_rows(half, body)
            spread.start(which)
            copy = pltpu.make_async_copy(
                rounded.at[pl.ds(which * half, half)], region(0, which), local.at[1 + which]
            )
            copy.start()
            copies.append(copy)
        result_tiles(6, 8)
        spread.forward()
        spread.finish()
        collect.finish()
        tile_copy(6).wait()
        tile_copy(7).wait()
        for copy in copies:
            copy.wait()

    return call(
        middle_back_step, identity, (terms, cot, middle, factor, gain, *hiddens, *weights),
        (pl.ANY, pl.ANY, pltpu.VMEM, pltpu.VMEM, pltpu.VMEM) + (pl.ANY,) * (2 * count),
        (
            jax.ShapeDtypeStruct((total, model), BF16),
            jax.ShapeDtypeStruct((quarter, model), F32),
            jax.ShapeDtypeStruct((1, model), F32),
            jax.ShapeDtypeStruct((total, model), BF16),
        ),
        (pl.ANY, pltpu.VMEM, pltpu.VMEM, pl.ANY),
        [
            pltpu.VMEM((total, inner_width), BF16),
            pltpu.VMEM((model, inner_width), BF16),
            pltpu.VMEM((2, quarter, model), BF16),
            pltpu.SemaphoreType.DMA((2 * count,)),
            pltpu.SemaphoreType.DMA((2,)),
            pltpu.VMEM((quarter, model), BF16),
            pltpu.VMEM((quarter, model), BF16),
            pltpu.SemaphoreType.DMA((3,)),
        ]
        + SPREAD_SEMS
        + Collect.scratch(quarter, model),
        70_000_000_000,
    )


def assemble(plan, flipped_out, totals, others, passed=()):
    count = len(totals)
    size = others[0].shape[0]
    shapes = []
    for index, pieces in enumerate(plan):
        wide = 2 * sum(piece[2] for piece in pieces)
        shapes.append((size, wide) if index < flipped_out else (wide, size))

    def assemble_grads(*refs):
        member = lax.rem(lax.axis_index("tok"), 2)
        outs = refs[2 * count + len(passed) :]
        for i in range(len(passed)):
            outs[len(plan) + i][...] = refs[2 * count + i][...]
        for index, pieces in enumerate(plan):
            half = sum(piece[2] for piece in pieces)
            for source, column, width, target in pieces:
                own_rows = pl.ds(pl.multiple_of(member * size, size), size)
                own = refs[source][own_rows, column : column + width]
                other = refs[count + source][:, column : column + width]
                for which, block in ((member, own), (1 - member, other)):
                    start = pl.multiple_of(which * half + target, 128)
                    if index < flipped_out:
                        outs[index][:, pl.ds(start, width)] = block.astype(F32)
                    else:
                        outs[index][pl.ds(start, width), :] = block.astype(F32).T

    return pl.pallas_call(
        assemble_grads,
        out_shape=[jax.ShapeDtypeStruct(shape, F32) for shape in shapes]
        + [jax.ShapeDtypeStruct(array.shape, array.dtype) for array in passed],
        in_specs=[pl.BlockSpec(memory_space=pltpu.VMEM)] * (2 * count + len(passed)),
        out_specs=[pl.BlockSpec(memory_space=pltpu.VMEM)] * (len(plan) + len(passed)),
        compiler_params=pltpu.CompilerParams(vmem_limit_bytes=VMEM),
        cost_estimate=pl.CostEstimate(
            flops=0, transcendentals=0, bytes_accessed=8 * size * 2 * sum(t.shape[1] for t in totals)
        ),
        name="assemble_grads",
    )(*totals, *others, *passed)


def input_terms(grad_packed, weights, x_all, gain, grad_middle, own):
    total, columns = grad_packed.shape
    model = x_all.shape[1]
    tile = grad_middle.shape[0]

    def input_terms_step(own_ref, grad_ref, qkv_ref, x_ref, gain_ref, middle_ref, out_ref, gain_grad_ref):
        step = pl.program_id(0)
        grad_normed = right_trans(grad_ref[...], qkv_ref[...])
        values = x_ref[...].astype(F32)
        factor = lax.rsqrt(jnp.mean(values * values, axis=1, keepdims=True) + EPSILON)
        weighted = grad_normed * gain_ref[...]
        inner = jnp.mean(weighted * values, axis=1, keepdims=True)
        terms = factor * weighted - values * (factor * factor * factor * inner)

        @pl.when(step == own_ref[0])
        def _():
            out_ref[...] = (terms + middle_ref[...]).astype(BF16)

        @pl.when(step != own_ref[0])
        def _():
            out_ref[...] = terms.astype(BF16)

        @pl.when(step == 0)
        def _():
            gain_grad_ref[...] = jnp.zeros_like(gain_grad_ref)

        gain_grad_ref[...] += jnp.sum(grad_normed * values * factor, axis=0, keepdims=True)

    return pl.pallas_call(
        input_terms_step,
        grid_spec=pltpu.PrefetchScalarGridSpec(
            num_scalar_prefetch=1,
            grid=(total // tile,),
            in_specs=[
                pl.BlockSpec((tile, columns), lambda i, own: (i, 0)),
                pl.BlockSpec((model, columns), lambda i, own: (0, 0)),
                pl.BlockSpec((tile, model), lambda i, own: (i, 0)),
                pl.BlockSpec((1, model), lambda i, own: (0, 0)),
                pl.BlockSpec((tile, model), lambda i, own: (0, 0)),
            ],
            out_specs=[
                pl.BlockSpec((tile, model), lambda i, own: (i, 0)),
                pl.BlockSpec((1, model), lambda i, own: (0, 0)),
            ],
        ),
        out_shape=[
            jax.ShapeDtypeStruct((total, model), BF16),
            jax.ShapeDtypeStruct((1, model), F32),
        ],
        compiler_params=pltpu.CompilerParams(vmem_limit_bytes=VMEM),
        cost_estimate=pl.CostEstimate(
            flops=2 * total * columns * model,
            transcendentals=total,
            bytes_accessed=6 * total * model,
        ),
        name="input_terms",
    )(own, grad_packed, weights, x_all, gain, grad_middle)


def feed_forward(normed, cot, weights, chunk):
    total, model = normed.shape
    tile = 256
    part = 256 if chunk % 256 == 0 else 128

    def feed_step(normed_ref, cot_ref, gate_ref, up_ref, down_ref, hidden_ref, grads_ref):
        for left in range(0, chunk, part):
            here = slice(left, left + part)
            gate = product(normed_ref[...], gate_ref[:, here])
            upward = product(normed_ref[...], up_ref[:, here])
            grad_hidden = product(cot_ref[...], down_ref[:, here])
            sigma = jax.nn.sigmoid(gate)
            active = gate * sigma
            hidden_ref[:, here] = (active * upward).astype(BF16)
            grads_ref[:, here] = (
                grad_hidden * upward * (sigma + active * (1.0 - sigma))
            ).astype(BF16)
            grads_ref[:, chunk + left : chunk + left + part] = (grad_hidden * active).astype(BF16)

    rows = pl.BlockSpec((tile, model), lambda i: (i, 0))

    def weight(part):
        return pl.BlockSpec((model, chunk), lambda i: (0, part), pipeline_mode=pl.Buffered(1))

    return pl.pallas_call(
        feed_step,
        grid=(total // tile,),
        in_specs=[rows, rows, weight(0), weight(1), weight(2)],
        out_specs=[
            pl.BlockSpec((tile, chunk), lambda i: (i, 0)),
            pl.BlockSpec((tile, 2 * chunk), lambda i: (i, 0)),
        ],
        out_shape=[
            jax.ShapeDtypeStruct((total, chunk), BF16),
            jax.ShapeDtypeStruct((total, 2 * chunk), BF16),
        ],
        compiler_params=pltpu.CompilerParams(vmem_limit_bytes=VMEM),
        cost_estimate=pl.CostEstimate(
            flops=6 * total * chunk * model,
            transcendentals=total * chunk,
            bytes_accessed=4 * total * model + 6 * chunk * (model + total),
        ),
        name="feed_forward",
    )(normed, cot, weights, weights, weights)


def columns_back(lefts, weights, place, own, base=None, middle=None):
    count = len(lefts)
    total = lefts[0].shape[0]
    model = weights[0].shape[0]
    tile, part = 512, 512

    def columns_step(own_ref, *refs):
        out_ref = refs[-1]
        for start in range(0, model, part):
            here = slice(start, start + part)
            value = sum(
                right_trans(refs[i][...], refs[count + i][here, :]) for i in range(count)
            )
            if base is not None:
                value = value + refs[2 * count][:, here].astype(F32)
            out_ref[:, here] = value.astype(BF16)
        if middle is not None:
            middle_ref = refs[-2]
            size = middle_ref.shape[0]
            inside = own_ref[0] * size - pl.program_id(0) * tile

            @pl.when((inside >= 0) & (inside < tile))
            def _():
                rows = pl.ds(pl.multiple_of(inside, size), size)
                out_ref[rows, :] = (out_ref[rows, :].astype(F32) + middle_ref[...]).astype(BF16)

    in_specs = [pl.BlockSpec((tile, left.shape[1]), lambda i, own: (i, 0)) for left in lefts]
    in_specs += [
        pl.BlockSpec(
            (model, left.shape[1]), lambda i, own: (0, place), pipeline_mode=pl.Buffered(1)
        )
        for left in lefts
    ]
    operands = [own, *lefts, *weights]
    if base is not None:
        in_specs.append(pl.BlockSpec((tile, model), lambda i, own: (i, 0)))
        operands.append(base)
    if middle is not None:
        in_specs.append(pl.BlockSpec(middle.shape, lambda i, own: (0, 0)))
        operands.append(middle)
    inner = sum(left.shape[1] for left in lefts)
    return pl.pallas_call(
        columns_step,
        grid_spec=pltpu.PrefetchScalarGridSpec(
            num_scalar_prefetch=1,
            grid=(total // tile,),
            in_specs=in_specs,
            out_specs=pl.BlockSpec((tile, model), lambda i, own: (i, 0)),
        ),
        out_shape=jax.ShapeDtypeStruct((total, model), BF16),
        compiler_params=pltpu.CompilerParams(vmem_limit_bytes=VMEM),
        cost_estimate=pl.CostEstimate(
            flops=2 * total * model * inner,
            transcendentals=0,
            bytes_accessed=2 * total * model + 2 * (total + model) * inner,
        ),
        name="columns_back",
    )(*operands)


def weight_terms(pairs, tile=256):
    rows, model = pairs[0][0].shape
    count = len(pairs)
    widths = [right.shape[1] for _, right in pairs]

    def terms_step(*refs):
        out_ref = refs[-1]
        start = 0
        for i, width in enumerate(widths):
            out_ref[:, start : start + width] = left_trans(refs[i][...], refs[count + i][...]).astype(
                BF16
            )
            start += width

    return pl.pallas_call(
        terms_step,
        grid=(model // tile,),
        in_specs=[pl.BlockSpec((rows, tile), lambda i: (0, i))] * count
        + [
            pl.BlockSpec((rows, width), lambda i: (0, 0), pipeline_mode=pl.Buffered(1))
            for width in widths
        ],
        out_specs=pl.BlockSpec((tile, sum(widths)), lambda i: (i, 0)),
        out_shape=jax.ShapeDtypeStruct((model, sum(widths)), BF16),
        compiler_params=pltpu.CompilerParams(vmem_limit_bytes=VMEM),
        cost_estimate=pl.CostEstimate(
            flops=2 * rows * model * sum(widths),
            transcendentals=0,
            bytes_accessed=2 * (rows * model * count + (rows + model) * sum(widths)),
        ),
        name="weight_terms",
    )(*[left for left, _ in pairs], *[right for _, right in pairs])


def program(
    tok_size,
    tokens, gain_attn, w_query, w_key, w_value, w_out, gain_ffn, w_gate, w_up, w_down, cotangent
):
    token = lax.axis_index("tok")
    feat = lax.axis_index("feat")
    member = token % 2
    rows, wide = tokens.shape
    model = 4 * wide
    quarter = rows // 4
    groups = [list(range(i, tok_size, 2)) for i in range(2)]
    pair_width = 2 * HD

    def swap(value):
        return lax.ppermute(value, "tok", [(i, i ^ 1) for i in range(tok_size)])

    def ring_gather(shard):
        return lax.all_gather(shard, "tok", axis=0, tiled=True, axis_index_groups=groups)

    def ring_scatter(terms):
        return lax.psum_scatter(
            terms, "tok", scatter_dimension=0, tiled=True, axis_index_groups=groups
        )

    def other_half(total):
        size = total.shape[0] // 2
        return swap(lax.dynamic_slice_in_dim(total, (1 - member) * size, size, 0))

    heads_wide = w_query.shape[1] // 2
    hidden_wide = w_gate.shape[1] // 2
    chunks = [hidden_wide * part // sum(CHUNKS) for part in CHUNKS]
    lefts = [sum(chunks[:c]) for c in range(len(chunks))]
    attention_pieces = [
        (part, left, pair_width, 3 * left + part * pair_width)
        for left in range(0, heads_wide, pair_width)
        for part in range(3)
    ]
    ring = tok_size // 2
    early = min(2, ring - 2)
    out_blocks = [w_out.T]
    attention_start, block = swap_ring(
        0, (w_query, w_key, w_value), attention_pieces, ring, w_out, early, True
    )
    out_blocks.append(block)
    feed = (w_gate, w_up, w_down.T)
    block, attention_start = lax.optimization_barrier((block, attention_start))
    qkv = ring_gather(attention_start)
    plans = [
        [(part, left, size, part * size) for part in range(3)] for left, size in zip(lefts, chunks)
    ]
    first_start, block = swap_ring(1, feed, plans[0], ring, block, ring - 1 - early)
    out_blocks.append(block)
    feed_weights = [ring_gather(first_start)]
    tokens, block = lax.optimization_barrier((tokens, block))
    last_start, x_all, out_proj, gains = swap_and_gather(
        2, feed, plans[1], tokens, ring, out_blocks, jnp.stack([gain_attn, gain_ffn])
    )
    gain_one, gain_two = gains[:1], gains[1:]
    feed_weights.append(ring_gather(last_start))

    x_wide = x_all.astype(F32)
    factor_one = lax.rsqrt(jnp.mean(x_wide * x_wide, axis=1, keepdims=True) + EPSILON)
    normed = (x_wide * factor_one * gain_one).astype(BF16)
    packed = product(normed, qkv).astype(BF16)
    attended, log_sums = attend(packed)
    normed_two, middle, factor_two, cot_rows = middle_norm(
        3, right_trans(attended, out_proj).astype(BF16), x_all, gain_two, cotangent
    )

    own = (member * 4 + feat).astype(jnp.int32).reshape(1)
    feed_sums = []
    grad_normed_two = out_rows = None

    hiddens = []
    for c in range(len(chunks)):
        if c:
            feed_weights[c], grad_normed_two = lax.optimization_barrier(
                (feed_weights[c], grad_normed_two)
            )
        hidden, grad_both = feed_forward(normed_two, cot_rows, feed_weights[c], chunks[c])
        hiddens.append(hidden)
        if c + 1 < len(chunks):
            feed_terms = weight_terms([(normed_two, grad_both), (cot_rows, hidden)])
            feed_terms, grad_both = lax.optimization_barrier((feed_terms, grad_both))
            feed_sums.append(ring_scatter(feed_terms))
        grad_normed_two = columns_back(
            [grad_both], [feed_weights[c]], 0, own, grad_normed_two
        )
    grad_mid_rows, grad_middle, gain_ffn_part, out_rows = middle_back(
        4, grad_normed_two, cot_rows, middle, factor_two, gain_two, hiddens, feed_weights
    )

    hidden, grad_both, grad_mid_rows = lax.optimization_barrier((hidden, grad_both, grad_mid_rows))
    feed_terms = weight_terms(
        [(normed_two, grad_both), (cot_rows, hidden), (grad_mid_rows, attended)]
    )
    grad_mid_rows, feed_terms = lax.optimization_barrier((grad_mid_rows, feed_terms))
    feed_sums.append(ring_scatter(feed_terms))

    grad_attended = product(grad_mid_rows, out_proj).astype(BF16)
    grad_packed = attend_back(packed, attended, grad_attended, log_sums)
    attention_terms = left_trans(normed, grad_packed).astype(BF16)
    attention_terms, grad_packed = lax.optimization_barrier((attention_terms, grad_packed))
    attention_sum = ring_scatter(attention_terms)
    grad_packed, feed_sums[0] = lax.optimization_barrier((grad_packed, feed_sums[0]))
    first_other = other_half(feed_sums[0])
    terms, gain_attn_part = input_terms(grad_packed, qkv, x_all, gain_one, grad_middle, own)
    terms, first_other = lax.optimization_barrier((terms, first_other))
    outcome, input_grad, gain_grads = scatter_blocks(
        5, tok_size // 2, jnp.concatenate([gain_attn_part, gain_ffn_part]), out_rows, terms
    )
    feed_others = [first_other]
    outcome, feed_sums[1] = lax.optimization_barrier((outcome, feed_sums[1]))
    feed_others.append(other_half(feed_sums[1]))
    feed_others[1], attention_sum = lax.optimization_barrier((feed_others[1], attention_sum))
    feed_plan = [
        [(c, part * chunks[c], chunks[c], lefts[c]) for c in range(len(chunks))]
        for part in range(3)
    ]
    feed_plan.append([(len(chunks) - 1, 3 * chunks[-1], heads_wide, 0)])
    gate_grad, up_grad, down_grad, out_grad, outcome, input_grad = assemble(
        feed_plan, 2, feed_sums, feed_others, (outcome, input_grad)
    )
    attention_plan = [
        [
            (0, 3 * left + part * pair_width, pair_width, left)
            for left in range(0, heads_wide, pair_width)
        ]
        for part in range(3)
    ]
    attention_other = other_half(attention_sum)
    attention_other, gate_grad, up_grad, down_grad, outcome, input_grad = lax.optimization_barrier(
        (attention_other, gate_grad, up_grad, down_grad, outcome, input_grad)
    )
    part_grads = assemble(attention_plan, 3, [attention_sum], [attention_other])
    return (
        outcome,
        input_grad,
        gain_grads[0],
        gain_grads[1],
        *part_grads,
        out_grad,
        gate_grad,
        up_grad,
        down_grad,
    )


def solution(mesh):
    in_specs = (
        P("tok", "feat"),
        P("feat"),
        P("tok", "feat"),
        P("tok", "feat"),
        P("tok", "feat"),
        P("feat", "tok"),
        P("feat"),
        P("tok", "feat"),
        P("tok", "feat"),
        P("feat", "tok"),
        P("tok", "feat"),
    )
    out_specs = (
        P("tok", "feat"),
        P("tok", "feat"),
        P("feat"),
        P("feat"),
        P("tok", "feat"),
        P("tok", "feat"),
        P("tok", "feat"),
        P("feat", "tok"),
        P("tok", "feat"),
        P("tok", "feat"),
        P("feat", "tok"),
    )

    def on_device(*arrays):
        return program(mesh.shape["tok"], *arrays)

    return jax.shard_map(
        on_device, mesh=mesh, in_specs=in_specs, out_specs=out_specs, check_vma=False
    )
```
